32 devices in a mesh: seq: 8 (over y, x, core), head: 4 (over z).
Axes of the slice: x: 2, y: 2, z: 4, core: 2. Of those that a mesh axis runs over, the one named last changes fastest.
Arguments:
- tokens: bfloat16 [24576, 768], P(('seq', 'head')), may hold values from -6 to 6
- cotangent: bfloat16 [24576, 768], P(('seq', 'head')), may hold values from -6 to 6
- lengths: int32 [8, 24], P('seq'), may hold values from 1 to 512, 3072 in all within a row
- labels: int32 [8, 24], P('seq'), may hold values from 0 to 2
- w_qkv: bfloat16 [768, 2304], replicated, may hold values from -0.3125 to 0.3125
- b_query: float32 [768], replicated, may hold values from -3 to 3
- b_value: float32 [768], replicated, may hold values from -3 to 3
- w_out: bfloat16 [768, 768], replicated, may hold values from -0.625 to 0.625
- b_out: float32 [768], replicated, may hold values from -3 to 3
- gain_attn: float32 [768], replicated, may hold values from 0.1 to 1.9
- shift_attn: float32 [768], replicated, may hold values from -3 to 3
- w_in: bfloat16 [768, 3072], replicated, may hold values from -0.21875 to 0.21875
- b_in: float32 [3072], replicated, may hold values from -3 to 3
- w_back: bfloat16 [3072, 768], replicated, may hold values from -0.15625 to 0.15625
- b_back: float32 [768], replicated, may hold values from -3 to 3
- gain_ffn: float32 [768], replicated, may hold values from 0.1 to 1.9
- shift_ffn: float32 [768], replicated, may hold values from -3 to 3
- w_pool: bfloat16 [768, 768], replicated, may hold values from -0.21875 to 0.21875
- b_pool: float32 [768], replicated, may hold values from -3 to 3
- w_class: float32 [768, 3], replicated, may hold values from -0.625 to 0.625
Outputs:
- output: bfloat16 [24576, 768], P(('seq', 'head'))
- grad_tokens: float32 [24576, 768], P(('seq', 'head'))
- grad_w_qkv: float32 [768, 2304], P(('seq', 'head'))
- grad_b_query: float32 [768], P(('seq', 'head'))
- grad_b_value: float32 [768], P(('seq', 'head'))
- grad_w_out: float32 [768, 768], P(('seq', 'head'))
- grad_b_out: float32 [768], P(('seq', 'head'))
- grad_gain_attn: float32 [768], P(('seq', 'head'))
- grad_shift_attn: float32 [768], P(('seq', 'head'))
- grad_w_in: float32 [768, 3072], P(('seq', 'head'))
- grad_b_in: float32 [3072], P(('seq', 'head'))
- grad_w_back: float32 [3072, 768], P(('seq', 'head'))
- grad_b_back: float32 [768], P(('seq', 'head'))
- grad_gain_ffn: float32 [768], P(('seq', 'head'))
- grad_shift_ffn: float32 [768], P(('seq', 'head'))
- grad_w_pool: float32 [768, 768], P(('seq', 'head'))
- grad_b_pool: float32 [768], P(('seq', 'head'))
- grad_w_class: float32 [768, 3], P(('seq', 'head'))
- entropy: float32 [], replicated
The draws below stay inside these ranges and needn't reach their ends.
Inputs may be any that keep to these rules, and one draw needn't show every extreme that they name: Each row of 24 lengths sums to 3072, and its largest length is 512.
All inputs are finite; a program needn't handle non-finite values.
Results may differ from the reference program's by a relative error of at most 0.014.
The reference program's roundings to bfloat16 on the way count: a program that leaves them out, or rounds other values in their place, can miss the bound.
Values may be sent and summed in bfloat16 or wider, within the bound.
A program may use at most 192 MiB of HBM per device.

```python
import math
import jax
import jax.numpy as jnp
import numpy as np
from jax import lax

D = 768
HEADS = 12
HEAD_DIM = 64
FF = 3072
CLASSES = 3
TOK_DEV = 768
MAXLEN = 512
GRP_TOK = 3072
SEQ_GRP = 24
GROUPS = 8
TOKENS = 24576
N_HEAD = 4


def set_ends(drawn, key, least, largest):
    longest = drawn.shape.index(max(drawn.shape))
    spots = []
    for shift in (0, 1):
        where = [jax.random.randint(jax.random.fold_in(key, axis), (), 0, length) for axis, length in enumerate(drawn.shape)]
        where[longest] = (where[longest] + shift) % drawn.shape[longest]
        spots.append(tuple(where))
    return drawn.at[spots[0]].set(least).at[spots[1]].set(largest)


def with_spikes(values, own_key, source, target, parts, factor):
    owner, partner = [(jnp.arange(values.shape[dim]) // (values.shape[dim] // parts)).reshape([-1 if axis == dim else 1 for axis in range(values.ndim)]) for dim in (source, target)]
    chosen = jax.random.permutation(own_key, parts)[partner]
    strong = (owner == chosen) | (owner == (partner + parts // 2) % parts)
    return jnp.where(strong, factor * values, values)


def block_levels(rng, shape, shards, low, high):
    level, own = 1.0, jax.random.fold_in(rng, 6)
    for axis_at, parts in shards:
        draws = jnp.exp(jax.random.uniform(jax.random.fold_in(own, axis_at), (parts,), jnp.float32, low / len(shards), high / len(shards)))
        level = level * jnp.repeat(draws, shape[axis_at] // parts).reshape([-1 if axis == axis_at else 1 for axis in range(len(shape))])
    return level


def length_profile(amount, total, most, lean):
    loads = [(1 << 20) // math.isqrt(grade ** lean) + 1 for grade in range(2, amount + 1)]
    surplus, holding = total - most - (amount - 1), [1] * (amount - 1)
    while surplus > 0:
        candidates = [i for i in range(amount - 1) if holding[i] < most]
        whole, left = sum([loads[i] for i in candidates]), surplus
        for i in candidates:
            extra = min(most - holding[i], max(1, left * loads[i] // whole), surplus)
            holding[i] = holding[i] + extra
            surplus = surplus - extra
    return np.array([most] + holding)


def uneven_parts(key, number_of, total, limit, slope):
    if number_of == 2:
        one = jax.random.randint(key, (), max(1, total - limit), min(limit, total - 1) + 1)
        return jnp.stack([one, total - one])
    sizes = jnp.asarray(length_profile(number_of, total, limit, slope), jnp.int32)
    twos = (number_of - 1) // 2
    giver, sink = sizes[1:1 + 2 * twos:2], sizes[2:2 + 2 * twos:2]
    margin = jnp.minimum(giver - 1, limit - sink)
    passed = jax.random.randint(jax.random.fold_in(key, 1), (twos,), 0, 1 << 20) % (margin + 1)
    sizes = sizes.at[1:1 + 2 * twos:2].set(giver - passed).at[2:2 + 2 * twos:2].set(sink + passed)
    return sizes[jax.random.permutation(jax.random.fold_in(key, 2), number_of)]


def bell_draw(stream_key, extent, deviation, most, split=(), kind=jnp.bfloat16):
    drawn = deviation * jax.random.normal(stream_key, extent, jnp.float32)
    if split:
        drawn = drawn * block_levels(stream_key, extent, split, -0.22, 0.18)
    return jnp.clip(drawn, -most, most).astype(kind)


def noise_with(own_key, shape, scale, limit, split, heavy, kind=jnp.bfloat16):
    entries = scale * jax.random.normal(own_key, shape, jnp.float32)
    if split:
        entries = entries * block_levels(own_key, shape, split, -0.22, 0.18)
    return jnp.clip(with_spikes(entries, jax.random.fold_in(own_key, 3), *heavy), -limit, limit).astype(kind)


def setup_inputs(seed: int = 0) -> dict:
    seeds = jax.random.split(jax.random.key(seed), 21)
    return {
        "tokens": noise_with(seeds[0], (TOKENS, D), 1.0, 6.0, ((0, 32),), (0, 1, 32, 2.75)),
        "cotangent": bell_draw(seeds[1], (TOKENS, D), 1.0, 6.0, ((0, 32),)),
        "lengths": jax.vmap(lambda own: uneven_parts(own, SEQ_GRP, GRP_TOK, MAXLEN, 2))(jax.random.split(seeds[2], GROUPS)).reshape((GROUPS, SEQ_GRP)).astype(jnp.int32),
        "labels": set_ends(jax.random.randint(seeds[3], (GROUPS, SEQ_GRP), 0, CLASSES), jax.random.fold_in(seeds[3], 1), 0, CLASSES - 1).astype(jnp.int32),
        "w_qkv": bell_draw(seeds[4], (D, 3 * D), (D // 2) ** -0.5, 0.3125),
        "b_query": bell_draw(seeds[5], (D,), 0.5, 3.0, (), jnp.float32),
        "b_value": bell_draw(seeds[6], (D,), 0.5, 3.0, (), jnp.float32),
        "w_out": bell_draw(seeds[7], (D, D), (D // 8) ** -0.5, 0.625),
        "b_out": bell_draw(seeds[8], (D,), 0.5, 3.0, (), jnp.float32),
        "gain_attn": jnp.clip(1.0 + 0.18 * jax.random.normal(seeds[9], (D,), jnp.float32), 0.1, 1.9),
        "shift_attn": bell_draw(seeds[10], (D,), 0.5, 3.0, (), jnp.float32),
        "w_in": bell_draw(seeds[11], (D, FF), D ** -0.5, 0.21875),
        "b_in": bell_draw(seeds[12], (FF,), 0.5, 3.0, (), jnp.float32),
        "w_back": bell_draw(seeds[13], (FF, D), (FF // 2) ** -0.5, 0.15625),
        "b_back": bell_draw(seeds[14], (D,), 0.5, 3.0, (), jnp.float32),
        "gain_ffn": jnp.clip(1.0 + 0.18 * jax.random.normal(seeds[15], (D,), jnp.float32), 0.1, 1.9),
        "shift_ffn": bell_draw(seeds[16], (D,), 0.5, 3.0, (), jnp.float32),
        "w_pool": bell_draw(seeds[17], (D, D), D ** -0.5, 0.21875),
        "b_pool": bell_draw(seeds[18], (D,), 0.5, 3.0, (), jnp.float32),
        "w_class": bell_draw(seeds[19], (D, CLASSES), 0.1, 0.625, (), jnp.float32),
    }


@jax.custom_vjp
def low(v):
    return lax.optimization_barrier(v.astype(jnp.bfloat16)).astype(jnp.float32)

@jax.custom_vjp
def low_back(v):
    return v

def low_keep(v):
    return (low(v), None)

def low_pass(kept, grad):
    return (grad,)

def back_keep(v):
    return (v, None)

def back_low(kept, grad):
    return (low(grad),)
low.defvjp(low_keep, low_pass)
low_back.defvjp(back_keep, back_low)
eps = 1e-05
big_neg = -1e+30
highest = lax.Precision.HIGHEST

def rounded(values):
    return low(low_back(values))

def matmul(left_op, right_op):
    return jnp.dot(left_op, right_op, precision=highest)

def layer_norm(hidden, gain_vec, shift_vec):
    centred = hidden - lax.optimization_barrier(jnp.mean(hidden, axis=-1, keepdims=True))
    return centred * lax.rsqrt(lax.optimization_barrier(jnp.mean(centred * centred, axis=-1, keepdims=True)) + eps) * gain_vec + shift_vec

def group_forward(tok_f, params, group_cot, seq_lengths, seq_labels):
    w_qkv, b_query, b_value, w_out, b_out, gain_attn, shift_attn, w_in, b_in, w_back, b_back, gain_ffn, shift_ffn, w_pool, b_pool, w_class = params
    group_rows = tok_f.shape[0]
    block_len = MAXLEN
    starts = (jnp.cumsum(seq_lengths) - seq_lengths).astype(jnp.int32)
    positions = jnp.arange(group_rows, dtype=jnp.int32)
    seg_all = lax.optimization_barrier(jnp.sum((starts[None, :] <= positions[:, None]).astype(jnp.int32), axis=1)) - 1
    projected = matmul(tok_f, w_qkv)
    q_all = rounded(projected[:, :D] + b_query).reshape(group_rows, HEADS, HEAD_DIM)
    k_all = rounded(projected[:, D:2 * D]).reshape(group_rows, HEADS, HEAD_DIM)
    v_all = rounded(projected[:, 2 * D:] + b_value).reshape(group_rows, HEADS, HEAD_DIM)
    k_pad = jnp.pad(k_all, ((block_len, block_len), (0, 0), (0, 0)))
    v_pad = jnp.pad(v_all, ((block_len, block_len), (0, 0), (0, 0)))
    seg_pad = jnp.pad(seg_all, (block_len, block_len), constant_values=-1)

    def block_attend(block_index):
        offset = (block_index * block_len).astype(jnp.int32)
        q_block = lax.dynamic_slice_in_dim(q_all, offset, block_len, 0)
        k_window = lax.dynamic_slice_in_dim(k_pad, offset, 3 * block_len, 0)
        v_window = lax.dynamic_slice_in_dim(v_pad, offset, 3 * block_len, 0)
        seg_query = lax.dynamic_slice_in_dim(seg_all, offset, block_len, 0)
        seg_key = lax.dynamic_slice_in_dim(seg_pad, offset, 3 * block_len, 0)
        raw_scores = low_back(jnp.einsum('qhd,khd->hqk', q_block, k_window, precision=highest)) * HEAD_DIM ** (-0.5)
        same_seq = seg_query[:, None] == seg_key[None, :]
        scores = jnp.where(same_seq[None], raw_scores, big_neg)
        weights = low(jax.nn.softmax(scores, axis=-1))
        return jnp.einsum('hqk,khd->qhd', weights, v_window, precision=highest)
    blocks = lax.map(jax.checkpoint(block_attend), jnp.arange(group_rows // block_len, dtype=jnp.int32))
    context = rounded(blocks.reshape(group_rows, D))
    attn_out = low_back(matmul(context, w_out) + b_out)
    middle = low(layer_norm(tok_f + attn_out, gain_attn, shift_attn))
    pre_act = low_back(matmul(middle, w_in) + b_in)
    activated = low(jax.nn.gelu(pre_act, approximate=False))
    ffn_out = low_back(matmul(activated, w_back) + b_back)
    output = low(layer_norm(middle + ffn_out, gain_ffn, shift_ffn))
    cls_rows = jnp.take(output, starts, axis=0)
    pre_pool = low_back(matmul(cls_rows, w_pool) + b_pool)
    pooled = jnp.tanh(pre_pool)
    logits = matmul(pooled, w_class)
    log_norm = jax.nn.logsumexp(logits, axis=-1)
    picked = jnp.take_along_axis(logits, seq_labels[:, None].astype(jnp.int32), axis=1)[:, 0]
    class_probs = jax.nn.softmax(logits, axis=-1)
    entropy = jnp.sum(log_norm - lax.optimization_barrier(jnp.sum(class_probs * logits, axis=-1)))
    objective = jnp.sum(group_cot * output) + jnp.sum(log_norm - picked)
    return (objective, (output, entropy))

def reference(tokens, cotangent, lengths, labels, w_qkv, b_query, b_value, w_out, b_out, gain_attn, shift_attn, w_in, b_in, w_back, b_back, gain_ffn, shift_ffn, w_pool, b_pool, w_class):
    params = tuple((weight_arr.astype(jnp.float32) for weight_arr in (w_qkv, b_query, b_value, w_out, b_out, gain_attn, shift_attn, w_in, b_in, w_back, b_back, gain_ffn, shift_ffn, w_pool, b_pool, w_class)))
    group_rows = TOK_DEV * N_HEAD
    token_groups = tokens.astype(jnp.float32).reshape(GROUPS, group_rows, D)
    cot_groups = cotangent.astype(jnp.float32).reshape(GROUPS, group_rows, D)

    def one_group(totals, inputs):
        group_tokens, group_cot, seq_lengths, seq_labels = inputs

        def objective_fn(tok_f, param_f):
            return group_forward(tok_f, param_f, group_cot, seq_lengths, seq_labels)
        objective_value, pullback, extras = jax.vjp(objective_fn, group_tokens, params, has_aux=True)
        grad_group, grad_params = pullback(jnp.ones_like(objective_value))
        totals = jax.tree.map(lambda running, adding: running + adding, totals, grad_params)
        return (totals, (extras[0], grad_group, extras[1]))
    zero_grads = jax.tree.map(jnp.zeros_like, params)
    totals, (outs_rows, grads_rows, entropies) = lax.scan(one_group, zero_grads, (token_groups, cot_groups, lengths, labels))
    entropy_mean = (jnp.sum(entropies) / (GROUPS * SEQ_GRP)).astype(jnp.float32)
    return (outs_rows.reshape(TOKENS, D).astype(jnp.bfloat16), grads_rows.reshape(TOKENS, D).astype(jnp.float32), totals[0], totals[1], totals[2], totals[3], totals[4], totals[5], totals[6], totals[7], totals[8], totals[9], totals[10], totals[11], totals[12], totals[13], totals[14], totals[15], entropy_mean)
```

```python
import functools

import jax
import jax.numpy as jnp
from jax import lax
from jax.experimental import pallas as pl
from jax.experimental.pallas import tpu as pltpu
from jax.sharding import PartitionSpec as P

HEAD_DIM = 64
MAXLEN = 512
PAIR = 2 * HEAD_DIM
QBLK = 128
KCHUNK = 256
PAD = KCHUNK - 128
LSE0 = 32
SIDE = 128

eps = 1e-05
BIG = 1e30
highest = lax.Precision.HIGHEST
f32 = jnp.float32
bf16 = jnp.bfloat16
NT = (((1,), (1,)), ((), ()))
NN = (((1,), (0,)), ((), ()))
TN = (((0,), (0,)), ((), ()))


def dot(left, right, dims):
    return lax.dot_general(left, right, dims, preferred_element_type=f32)


def pair_rows(rows, side):
    lane = lax.broadcasted_iota(jnp.int32, rows.shape, 1)
    zero = jnp.zeros_like(rows)
    first = jnp.where(lane < HEAD_DIM, rows, zero)
    second = jnp.where(lane >= HEAD_DIM, rows, zero)
    return jnp.concatenate(
        [jnp.concatenate([first, side[0]], axis=1), jnp.concatenate([second, side[1]], axis=1)],
        axis=0,
    )


def unpair(both):
    row = lax.broadcasted_iota(jnp.int32, (PAIR, QBLK), 0)
    return jnp.where(row < HEAD_DIM, both[:, :QBLK], both[:, QBLK:])


def attend_kernel(bounds, q_ref, k_ref, v_ref, hot_ref, mask_ref, ctx_ref, lse_ref, kcat, vt):
    window = k_ref.shape[0]
    own = ctx_ref.shape[0]

    @pl.when(pl.program_id(0) == 0)
    def _():
        kcat[:, PAIR:] = mask_ref[...]
        kcat[pl.ds(window, PAD), :PAIR] = jnp.zeros((PAD, PAIR), bf16)
        vt[:, pl.ds(window, PAD)] = jnp.zeros((PAIR, PAD), bf16)

    kcat[pl.ds(0, window), :PAIR] = k_ref[...]
    for at in range(0, window, 256):
        vt[:, pl.ds(at, 256)] = v_ref[pl.ds(at, 256), :].T

    def block(i, carry):
        row0 = pl.multiple_of(i * QBLK, QBLK)
        hot = hot_ref[pl.ds(MAXLEN + row0, QBLK), :]
        qcat = pair_rows(q_ref[pl.ds(MAXLEN + row0, QBLK), :], (hot, hot))
        first = bounds[0, i]

        def step(c, state):
            peak, total, acc = state
            start = pl.multiple_of(first + c * KCHUNK, 128)
            s = dot(kcat[pl.ds(start, KCHUNK), :], qcat, NT)
            new_peak = jnp.maximum(peak, jnp.max(s, axis=0, keepdims=True))
            scale = jnp.exp(peak - new_peak)
            p = jnp.exp(s - new_peak)
            total = total * scale + jnp.sum(p, axis=0, keepdims=True)
            acc = acc * scale + dot(vt[:, pl.ds(start, KCHUNK)], p.astype(bf16), NN)
            return new_peak, total, acc

        peak, total, acc = lax.fori_loop(
            0,
            bounds[1, i],
            step,
            (
                jnp.full((1, 2 * QBLK), -BIG, f32),
                jnp.zeros((1, 2 * QBLK), f32),
                jnp.zeros((PAIR, 2 * QBLK), f32),
            ),
        )
        ctx_ref[pl.ds(row0, QBLK), :] = unpair(acc / total).T.astype(bf16)
        lse = peak + jnp.log(total)
        lse_ref[0, :, pl.ds(row0, QBLK)] = jnp.concatenate([lse[:, :QBLK], lse[:, QBLK:]], axis=0)
        return carry

    lax.fori_loop(0, own // QBLK, block, 0)


def attend(bounds, qkv, hot, mask, own):
    window, wide = qkv.shape
    width = wide // 3
    pairs = width // PAIR
    column = lambda part: pl.BlockSpec((window, PAIR), lambda g, b: (0, part * pairs + g))
    whole = lambda a: pl.BlockSpec(a.shape, lambda g, b: (0, 0))
    return pl.pallas_call(
        attend_kernel,
        grid_spec=pltpu.PrefetchScalarGridSpec(
            num_scalar_prefetch=1,
            grid=(pairs,),
            in_specs=[column(0), column(1), column(2), whole(hot), whole(mask)],
            out_specs=[
                pl.BlockSpec((own, PAIR), lambda g, b: (0, g)),
                pl.BlockSpec((1, 2, own), lambda g, b: (g, 0, 0)),
            ],
            scratch_shapes=[
                pltpu.VMEM((window + PAD, 2 * PAIR), bf16),
                pltpu.VMEM((PAIR, window + PAD), bf16),
            ],
        ),
        out_shape=[
            jax.ShapeDtypeStruct((own, width), bf16),
            jax.ShapeDtypeStruct((pairs, 2, own), f32),
        ],
        name="attend",
    )(bounds, qkv, qkv, qkv, hot, mask)


def attend_back_kernel(
    bounds, q_ref, k_ref, v_ref, do_ref, side_ref, hot_ref, mask_ref,
    gqkv_ref, kcat, vcat, kt, dk, dv,
):
    window = k_ref.shape[0]
    own = gqkv_ref.shape[1]
    heads = LSE0 + 3 * 2 * pl.num_programs(0)
    g = pl.program_id(0)

    @pl.when(g == 0)
    def _():
        kcat[:, PAIR:] = mask_ref[...]
        vcat[:, PAIR:] = jnp.ones((window + PAD, SIDE), bf16)
        kcat[pl.ds(window, PAD), :PAIR] = jnp.zeros((PAD, PAIR), bf16)
        vcat[pl.ds(window, PAD), :PAIR] = jnp.zeros((PAD, PAIR), bf16)
        kt[:, pl.ds(window, PAD)] = jnp.zeros((PAIR, PAD), bf16)

    kcat[pl.ds(0, window), :PAIR] = k_ref[...]
    vcat[pl.ds(0, window), :PAIR] = v_ref[...]
    for at in range(0, window, 256):
        kt[:, pl.ds(at, 256)] = k_ref[pl.ds(at, 256), :].T
    dk[...] = jnp.zeros_like(dk)
    dv[...] = jnp.zeros_like(dv)
    lane = lax.broadcasted_iota(jnp.int32, (QBLK, SIDE), 1)
    low = LSE0 + 6 * g

    def side_lanes(side, first):
        return jnp.where((lane >= first) & (lane < first + 3), side, jnp.zeros_like(side))

    def block(i, carry):
        row0 = pl.multiple_of(i * QBLK, QBLK)
        hot = hot_ref[pl.ds(row0, QBLK), :]
        side = side_ref[pl.ds(row0, QBLK), :]
        qcat = pair_rows(
            q_ref[pl.ds(row0, QBLK), :],
            (hot + side_lanes(side, low), hot + side_lanes(side, low + 3)),
        )
        gap = heads - LSE0
        docat = pair_rows(
            do_ref[pl.ds(row0, QBLK), :],
            (side_lanes(side, low + gap), side_lanes(side, low + gap + 3)),
        )
        first = bounds[0, i]

        def step(c, dq):
            start = pl.multiple_of(first + c * KCHUNK, 128)
            here = pl.ds(start, KCHUNK)
            p = jnp.exp(dot(kcat[here, :], qcat, NT))
            dp = dot(vcat[here, :], docat, NT)
            ds = (p * dp).astype(bf16)
            dv[here, :] += dot(p.astype(bf16), docat[:, :PAIR], NN)
            dk[here, :] += dot(ds, qcat[:, :PAIR], NN)
            return dq + dot(kt[:, here], ds, NN)

        dq = lax.fori_loop(0, bounds[1, i], step, jnp.zeros((PAIR, 2 * QBLK), f32))

        @pl.when((i >= MAXLEN // QBLK) & (i < (MAXLEN + own) // QBLK))
        def _():
            gqkv_ref[0, pl.ds(pl.multiple_of(row0 - MAXLEN, QBLK), QBLK), :] = (
                (unpair(dq) * HEAD_DIM**-0.5).T.astype(bf16)
            )

        return carry

    lax.fori_loop(0, window // QBLK, block, 0)
    gqkv_ref[1, :, :] = dk[pl.ds(MAXLEN, own), :].astype(bf16)
    gqkv_ref[2, :, :] = dv[pl.ds(MAXLEN, own), :].astype(bf16)


def attend_back(bounds, qkv, grads, hot, mask, own):
    window, wide = qkv.shape
    width = wide // 3
    pairs = width // PAIR
    column = lambda part: pl.BlockSpec((window, PAIR), lambda g, b: (0, part * pairs + g))
    whole = lambda a: pl.BlockSpec(a.shape, lambda g, b: (0, 0))
    return pl.pallas_call(
        attend_back_kernel,
        grid_spec=pltpu.PrefetchScalarGridSpec(
            num_scalar_prefetch=1,
            grid=(pairs,),
            in_specs=[
                column(0),
                column(1),
                column(2),
                pl.BlockSpec((window, PAIR), lambda g, b: (0, g)),
                pl.BlockSpec((window, SIDE), lambda g, b: (0, pairs)),
                whole(hot),
                whole(mask),
            ],
            out_specs=pl.BlockSpec((3, own, PAIR), lambda g, b: (0, 0, g)),
            scratch_shapes=[
                pltpu.VMEM((window + PAD, 2 * PAIR), bf16),
                pltpu.VMEM((window + PAD, 2 * PAIR), bf16),
                pltpu.VMEM((PAIR, window + PAD), bf16),
                pltpu.VMEM((window + PAD, PAIR), f32),
                pltpu.VMEM((window + PAD, PAIR), f32),
            ],
        ),
        out_shape=jax.ShapeDtypeStruct((3, own, width), bf16),
        name="attend_back",
    )(bounds, qkv, qkv, qkv, grads, grads, hot, mask)


def parts3(values):
    round_low = lambda v: lax.reduce_precision(v, 8, 7)
    high = round_low(values)
    mid = round_low(values - high)
    return jnp.stack([high, mid, values - high - mid], axis=-1).astype(bf16)


def halo(rows, left_axis, n_head):
    up = [(i, i + 1) for i in range(n_head - 1)]
    down = [(i + 1, i) for i in range(n_head - 1)]
    from_left = lax.ppermute(rows[-MAXLEN:], left_axis, up)
    from_right = lax.ppermute(rows[:MAXLEN], left_axis, down)
    return jnp.concatenate([from_left, rows, from_right], axis=0)


def pick(values, axis, index):
    return lax.dynamic_index_in_dim(values, index, axis, keepdims=False)


def scatter_sum(values, n_seq, n_head, order):
    seq_bits, head_bits = n_seq.bit_length() - 1, n_head.bit_length() - 1
    bits = seq_bits + head_bits
    shard = values.shape[0] // (n_seq * n_head)
    values = values.reshape((2,) * bits + (shard,) + values.shape[1:])
    axes = list(range(bits))
    seq, head = lax.axis_index("seq"), lax.axis_index("head")
    for name, bit in order:
        where = seq_bits - 1 - bit if name == "seq" else bits - 1 - bit
        count = n_seq if name == "seq" else n_head
        mine = ((seq if name == "seq" else head) >> bit) & 1
        at = axes.index(where)
        axes.pop(at)
        other = pick(values, at, 1 - mine).astype(bf16)
        own = pick(values, at, mine).astype(f32)
        got = lax.ppermute(other, name, [(i, i ^ (1 << bit)) for i in range(count)])
        values = own + got.astype(f32)
    return values


def orders(n_seq, n_head):
    seq_bits, head_bits = n_seq.bit_length() - 1, n_head.bit_length() - 1
    core = [("seq", 0)]
    planar = [("seq", b) for b in range(1, seq_bits)]
    along = [("head", b) for b in range(head_bits)]
    return (
        core + planar + along,
        core + planar[::-1] + along,
        core + along + planar,
    )


def layer_norm(hidden, gain_vec, shift_vec):
    centred = hidden - jnp.mean(hidden, axis=-1, keepdims=True)
    inv_std = lax.rsqrt(jnp.mean(centred * centred, axis=-1, keepdims=True) + eps)
    normed = centred * inv_std
    return (normed * gain_vec + shift_vec, normed, inv_std)


def norm_back(grad_out, normed, inv_std, gain_vec):
    grad_norm = grad_out * gain_vec
    inner = grad_norm - jnp.mean(grad_norm, axis=-1, keepdims=True)
    inner = inner - normed * jnp.mean(grad_norm * normed, axis=-1, keepdims=True)
    return (inv_std * inner, jnp.sum(grad_out * normed, axis=0), jnp.sum(grad_out, axis=0))


def local(
    tokens, cotangent, lengths, labels, w_qkv, b_query, b_value, w_out, b_out, gain_attn,
    shift_attn, w_in, b_in, w_back, b_back, gain_ffn, shift_ffn, w_pool, b_pool, w_class,
):
    n_head = lax.axis_size("head")
    n_seq = lax.axis_size("seq")
    head_index = lax.axis_index("head")
    own, width = tokens.shape
    heads = width // HEAD_DIM
    window = own + 2 * MAXLEN
    group = own * n_head

    seq_lengths = lengths[0]
    ends = jnp.cumsum(seq_lengths)
    starts = ends - seq_lengths
    base = head_index * own - MAXLEN
    pos = base + jnp.arange(window, dtype=jnp.int32)
    n_in_group = seq_lengths.shape[0]
    lane_pad = (0, SIDE - n_in_group)
    starts_w = jnp.pad(starts, lane_pad, constant_values=group + MAXLEN)
    ends_w = jnp.pad(ends, lane_pad, constant_values=-MAXLEN)
    inside = (starts_w[None, :] <= pos[:, None]) & (pos[:, None] < ends_w[None, :])
    hot = inside.astype(bf16)
    lane = jnp.arange(SIDE, dtype=jnp.int32)[None, :]
    mask = jnp.where(lane < n_in_group, jnp.where(inside, 0.0, -BIG), 1.0).astype(bf16)
    mask = jnp.concatenate(
        [mask, jnp.broadcast_to(jnp.where(lane < n_in_group, -BIG, 1.0).astype(bf16), (PAD, SIDE))]
    )
    blk = base + QBLK * jnp.arange(window // QBLK, dtype=jnp.int32)
    low = jnp.max(jnp.where(starts[None, :] <= blk[:, None], starts[None, :], -1), axis=1)
    high = jnp.min(
        jnp.where(ends[None, :] > blk[:, None] + QBLK - 1, ends[None, :], group), axis=1
    )
    is_own = (blk >= base + MAXLEN) & (blk < base + MAXLEN + own)
    low = jnp.where(is_own, low - base, jnp.maximum(low - base, MAXLEN))
    high = jnp.where(is_own, high - base, jnp.minimum(high - base, MAXLEN + own))
    valid = (blk >= 0) & (blk < group)
    low = low // 128 * 128
    steps = jnp.where(valid, jnp.maximum((high - low + KCHUNK - 1) // KCHUNK, 0), 0)
    bounds = jnp.stack([low, steps]).astype(jnp.int32)
    own_bounds = bounds[:, MAXLEN // QBLK : (MAXLEN + own) // QBLK]

    tokens_w = halo(tokens, "head", n_head)
    bias = jnp.concatenate([b_query, jnp.zeros_like(b_query), b_value])[None, :]
    qscale = jnp.where(jnp.arange(3 * width) < width, HEAD_DIM**-0.5, 1.0).astype(f32)[None, :]
    qkv = ((dot(tokens_w, w_qkv, NN) + bias) * qscale).astype(bf16)
    context, lse = attend(own_bounds, qkv, hot, mask, own)

    attn_out = dot(context, w_out, NN) + b_out
    normed_attn, unit_attn, inv_attn = layer_norm(
        tokens.astype(f32) + attn_out, gain_attn, shift_attn
    )
    middle = normed_attn.astype(bf16)
    pre_act = dot(middle, w_in, NN) + b_in
    cdf = 0.5 * (1.0 + lax.erf(pre_act * (0.5**0.5)))
    activated = (pre_act * cdf).astype(bf16)
    gelu_slope = cdf + pre_act * (jnp.exp(-0.5 * pre_act * pre_act) * 0.3989422804014327)
    ffn_out = dot(activated, w_back, NN) + b_back
    normed_ffn, unit_ffn, inv_ffn = layer_norm(
        middle.astype(f32) + ffn_out, gain_ffn, shift_ffn
    )
    output = normed_ffn.astype(bf16)

    my_rows = head_index * own + jnp.arange(own, dtype=jnp.int32)
    owner_sel = (starts[:, None] == my_rows[None, :]).astype(bf16)
    owned = jnp.sum(owner_sel.astype(f32), axis=1)
    cls_low = dot(owner_sel, output, NN).astype(bf16)
    pooled = jnp.tanh(dot(cls_low, w_pool, NN) + b_pool)
    logits = jnp.dot(pooled, w_class, precision=highest)
    class_peak = jnp.max(logits, axis=-1, keepdims=True)
    class_exp = jnp.exp(logits - class_peak)
    class_total = jnp.sum(class_exp, axis=-1, keepdims=True)
    class_probs = class_exp / class_total
    ramp_norm = (class_peak + jnp.log(class_total))[:, 0]
    entropy_terms = owned * (ramp_norm - jnp.sum(class_probs * logits, axis=-1))
    entropy_own = jnp.sum(entropy_terms)
    onehot = (labels[0][:, None] == jnp.arange(w_class.shape[1], dtype=jnp.int32)[None, :]).astype(
        f32
    )
    grad_logits = (class_probs - onehot) * owned[:, None]
    grad_class = lax.dot_general(pooled, grad_logits, TN, precision=highest)
    grad_pooled = lax.dot_general(grad_logits, w_class, NT, precision=highest)
    grad_pre_pool = (grad_pooled * (1.0 - pooled * pooled)).astype(bf16)
    grad_pool = dot(cls_low, grad_pre_pool, TN)
    grad_bpool = jnp.sum(grad_pre_pool.astype(f32), axis=0)
    grad_cls = dot(grad_pre_pool, w_pool, NT)
    cls_back = lax.dot_general(owner_sel.astype(f32), grad_cls, TN, precision=highest)
    grad_result = cotangent.astype(f32) + cls_back

    grad_ffn_res, grad_gain_ffn, grad_shift_ffn = norm_back(
        grad_result, unit_ffn, inv_ffn, gain_ffn
    )
    grad_ffn = grad_ffn_res.astype(bf16)
    grad_bback = jnp.sum(grad_ffn.astype(f32), axis=0)
    grad_act = dot(grad_ffn, w_back, NT)
    grad_pre = (grad_act * gelu_slope).astype(bf16)
    grad_bin = jnp.sum(grad_pre.astype(f32), axis=0)
    grad_middle = grad_ffn_res + dot(grad_pre, w_in, NT)
    grad_attn_res, grad_gain_attn, grad_shift_attn = norm_back(
        grad_middle, unit_attn, inv_attn, gain_attn
    )
    grad_attn = grad_attn_res.astype(bf16)
    grad_bout = jnp.sum(grad_attn.astype(f32), axis=0)
    grad_ctx = dot(grad_attn, w_out, NT).astype(bf16)

    head_of = (jnp.arange(width)[:, None] // HEAD_DIM == jnp.arange(heads)[None, :]).astype(f32)
    delta = jnp.dot(
        grad_ctx.astype(f32) * context.astype(f32), head_of, precision=highest
    )
    lse_rows = lse.reshape(heads, own).T
    side = jnp.concatenate(
        [
            jnp.zeros((own, LSE0), bf16),
            parts3(-lse_rows).reshape(own, 3 * heads),
            parts3(-delta).reshape(own, 3 * heads),
            jnp.zeros((own, SIDE - LSE0 - 6 * heads), bf16),
        ],
        axis=1,
    )
    grads_w = halo(jnp.concatenate([grad_ctx, side], axis=1), "head", n_head)

    grad_wback = dot(activated, grad_ffn, TN)
    grad_win = dot(middle, grad_pre, TN)
    grad_wout = dot(context, grad_attn, TN)
    order_a, order_b, order_c = orders(n_seq, n_head)
    sum_wback = scatter_sum(grad_wback, n_seq, n_head, order_a)
    sum_win = scatter_sum(grad_win, n_seq, n_head, order_b)
    sum_wout_pool = scatter_sum(jnp.concatenate([grad_wout, grad_pool], axis=1), n_seq, n_head, order_c)
    sum_wout, sum_pool = sum_wout_pool[:, :width], sum_wout_pool[:, width:]

    gqkv = attend_back(bounds, qkv, grads_w, hot, mask, own)
    grad_qkv = jnp.concatenate([gqkv[0], gqkv[1], gqkv[2]], axis=1)
    grad_tokens = grad_attn_res + dot(grad_qkv, w_qkv, NT)
    grad_wqkv = dot(tokens, grad_qkv, TN)
    grad_bquery = jnp.sum(gqkv[0].astype(f32), axis=0)
    grad_bvalue = jnp.sum(gqkv[2].astype(f32), axis=0)
    sum_wqkv = scatter_sum(grad_wqkv, n_seq, n_head, order_b)

    shards = n_seq * n_head
    small = [
        grad_bquery, grad_bvalue, grad_bout, grad_gain_attn, grad_shift_attn, grad_bin, grad_bback,
        grad_gain_ffn, grad_shift_ffn, grad_bpool, grad_class.reshape(-1),
        jnp.broadcast_to(entropy_own, (shards,)),
    ]
    packed = jnp.concatenate([v.reshape(shards, -1) for v in small], axis=1)
    summed = lax.psum_scatter(packed, ("seq", "head"), scatter_dimension=0, tiled=True)[0]
    out, at = [], 0
    for v in small:
        size = v.shape[0] // shards
        out.append(summed[at : at + size])
        at += size
    entropy_mean = out[11][0] / (n_seq * labels.shape[1])
    return (
        output, grad_tokens, sum_wqkv, out[0], out[1], sum_wout, out[2], out[3], out[4], sum_win,
        out[5], sum_wback, out[6], out[7], out[8], sum_pool, out[9],
        out[10].reshape(-1, w_class.shape[1]), entropy_mean,
    )


def solution(mesh):
    rows = P(("seq", "head"), None)
    vec = P(("seq", "head"))
    return jax.shard_map(
        local,
        mesh=mesh,
        in_specs=(rows, rows, P("seq", None), P("seq", None)) + (P(),) * 16,
        out_specs=(
            rows, rows, rows, vec, vec, rows, vec, vec, vec, rows, vec, rows, vec, vec, vec, rows,
            vec, rows, P(),
        ),
        check_vma=False,
    )
```

```python
import functools

import jax
import jax.numpy as jnp
from jax import lax
from jax.experimental import pallas as pl
from jax.experimental.pallas import tpu as pltpu
from jax.sharding import PartitionSpec as P

HEAD_DIM = 64
MAXLEN = 512
PAIR = 2 * HEAD_DIM
QBLK = 128
KCHUNK = 256
PAD = KCHUNK - 128
LSE0 = 32
SIDE = 128

eps = 1e-05
BIG = 1e30
highest = lax.Precision.HIGHEST
f32 = jnp.float32
bf16 = jnp.bfloat16
NT = (((1,), (1,)), ((), ()))
NN = (((1,), (0,)), ((), ()))
TN = (((0,), (0,)), ((), ()))


def dot(left, right, dims):
    return lax.dot_general(left, right, dims, preferred_element_type=f32)


def pair_rows(rows, side):
    lane = lax.broadcasted_iota(jnp.int32, rows.shape, 1)
    zero = jnp.zeros_like(rows)
    first = jnp.where(lane < HEAD_DIM, rows, zero)
    second = jnp.where(lane >= HEAD_DIM, rows, zero)
    return jnp.concatenate(
        [jnp.concatenate([first, side[0]], axis=1), jnp.concatenate([second, side[1]], axis=1)],
        axis=0,
    )


def unpair(both):
    row = lax.broadcasted_iota(jnp.int32, (PAIR, QBLK), 0)
    return jnp.where(row < HEAD_DIM, both[:, :QBLK], both[:, QBLK:])


def attend_kernel(bounds, q_ref, k_ref, v_ref, hot_ref, mask_ref, ctx_ref, lse_ref, kcat, vt):
    window = k_ref.shape[0]
    own = ctx_ref.shape[0]
    fold = kcat.shape[0]

    @pl.when(pl.program_id(0) == 0)
    def _():
        for j in range(fold):
            kcat[j, :, PAIR:] = mask_ref[...]
            kcat[j, pl.ds(window, PAD), :PAIR] = jnp.zeros((PAD, PAIR), bf16)
            vt[j, :, pl.ds(window, PAD)] = jnp.zeros((PAIR, PAD), bf16)

    lse_ref[...] = jnp.zeros_like(lse_ref)
    for j in range(fold):
        cols = pl.ds(j * PAIR, PAIR)
        kcat[j, pl.ds(0, window), :PAIR] = k_ref[:, cols]
        for at in range(0, window, 256):
            vt[j, :, pl.ds(at, 256)] = v_ref[pl.ds(at, 256), cols].T

    def block(i, carry):
        row0 = pl.multiple_of(i * QBLK, QBLK)
        hot = hot_ref[pl.ds(MAXLEN + row0, QBLK), :]
        rows = q_ref[pl.ds(MAXLEN + row0, QBLK), :]
        qcat = [pair_rows(rows[:, j * PAIR : (j + 1) * PAIR], (hot, hot)) for j in range(fold)]
        first = bounds[0, i]

        def step(c, state):
            start = pl.multiple_of(first + c * KCHUNK, 128)
            scores = [dot(kcat[j, pl.ds(start, KCHUNK), :], qcat[j], NT) for j in range(fold)]
            out = []
            for j, s in enumerate(scores):
                peak, total, acc = state[j]
                new_peak = jnp.maximum(peak, jnp.max(s, axis=0, keepdims=True))
                scale = jnp.exp(peak - new_peak)
                p = jnp.exp(s - new_peak)
                total = total * scale + jnp.sum(p, axis=0, keepdims=True)
                acc = acc * scale + dot(vt[j, :, pl.ds(start, KCHUNK)], p.astype(bf16), NN)
                out.append((new_peak, total, acc))
            return tuple(out)

        empty = (
            jnp.full((1, 2 * QBLK), -BIG, f32),
            jnp.zeros((1, 2 * QBLK), f32),
            jnp.zeros((PAIR, 2 * QBLK), f32),
        )
        state = lax.fori_loop(0, bounds[1, i], step, (empty,) * fold)
        for j, (peak, total, acc) in enumerate(state):
            ctx_ref[pl.ds(row0, QBLK), pl.ds(j * PAIR, PAIR)] = unpair(acc / total).T.astype(bf16)
            lse = peak + jnp.log(total)
            lse_ref[2 * j : 2 * j + 1, pl.ds(row0, QBLK)] = lse[:, :QBLK]
            lse_ref[2 * j + 1 : 2 * j + 2, pl.ds(row0, QBLK)] = lse[:, QBLK:]
        return carry

    lax.fori_loop(0, own // QBLK, block, 0)


def fold_of(pairs, most):
    return max(n for n in range(1, most + 1) if pairs % n == 0)


def attend(bounds, qkv, hot, mask, own):
    window, wide = qkv.shape
    width = wide // 3
    pairs = width // PAIR
    fold = fold_of(pairs, 3)
    parts = pairs // fold
    column = lambda part: pl.BlockSpec((window, fold * PAIR), lambda g, b: (0, part * parts + g))
    whole = lambda a: pl.BlockSpec(a.shape, lambda g, b: (0, 0))
    return pl.pallas_call(
        attend_kernel,
        grid_spec=pltpu.PrefetchScalarGridSpec(
            num_scalar_prefetch=1,
            grid=(parts,),
            in_specs=[column(0), column(1), column(2), whole(hot), whole(mask)],
            out_specs=[
                pl.BlockSpec((own, fold * PAIR), lambda g, b: (0, g)),
                pl.BlockSpec((8, own), lambda g, b: (g, 0)),
            ],
            scratch_shapes=[
                pltpu.VMEM((fold, window + PAD, 2 * PAIR), bf16),
                pltpu.VMEM((fold, PAIR, window + PAD), bf16),
            ],
        ),
        out_shape=[
            jax.ShapeDtypeStruct((own, width), bf16),
            jax.ShapeDtypeStruct((8 * parts, own), f32),
        ],
        cost_estimate=pl.CostEstimate(
            flops=own * 600 * width * 4, bytes_accessed=window * wide * 2, transcendentals=0
        ),
        name="attend",
    )(bounds, qkv, qkv, qkv, hot, mask)


def attend_back_kernel(
    side0, bounds, q_ref, k_ref, v_ref, do_ref, side_ref, hot_ref, mask_ref,
    gqkv_ref, kcat, vcat, kt, dk, dv,
):
    window = k_ref.shape[0]
    own = gqkv_ref.shape[1]
    fold = kcat.shape[0]
    low0, gap = side0

    for j in range(fold):
        cols = pl.ds(j * PAIR, PAIR)
        kcat[j, :, PAIR:] = mask_ref[...]
        vcat[j, :, PAIR:] = jnp.ones((window + PAD, SIDE), bf16)
        kcat[j, pl.ds(window, PAD), :PAIR] = jnp.zeros((PAD, PAIR), bf16)
        vcat[j, pl.ds(window, PAD), :PAIR] = jnp.zeros((PAD, PAIR), bf16)
        kt[j, :, pl.ds(window, PAD)] = jnp.zeros((PAIR, PAD), bf16)
        kcat[j, pl.ds(0, window), :PAIR] = k_ref[:, cols]
        vcat[j, pl.ds(0, window), :PAIR] = v_ref[:, cols]
        for at in range(0, window, 256):
            kt[j, :, pl.ds(at, 256)] = k_ref[pl.ds(at, 256), cols].T
    dk[...] = jnp.zeros_like(dk)
    dv[...] = jnp.zeros_like(dv)
    lane = lax.broadcasted_iota(jnp.int32, (QBLK, SIDE), 1)

    def side_lanes(side, first):
        return jnp.where((lane >= first) & (lane < first + 3), side, jnp.zeros_like(side))

    def block(i, carry):
        row0 = pl.multiple_of(i * QBLK, QBLK)
        hot = hot_ref[pl.ds(row0, QBLK), :]
        side = side_ref[pl.ds(row0, QBLK), :]
        rows = q_ref[pl.ds(row0, QBLK), :]
        grads = do_ref[pl.ds(row0, QBLK), :]
        qcat, docat = [], []
        for j in range(fold):
            cols = slice(j * PAIR, (j + 1) * PAIR)
            low = low0 + 6 * j
            qcat.append(
                pair_rows(
                    rows[:, cols],
                    (hot + side_lanes(side, low), hot + side_lanes(side, low + 3)),
                )
            )
            docat.append(
                pair_rows(
                    grads[:, cols],
                    (side_lanes(side, low + gap), side_lanes(side, low + gap + 3)),
                )
            )
        first = bounds[0, i]

        def step(c, dq):
            start = pl.multiple_of(first + c * KCHUNK, 128)
            here = pl.ds(start, KCHUNK)
            scores = [dot(kcat[j, here, :], qcat[j], NT) for j in range(fold)]
            slopes = [dot(vcat[j, here, :], docat[j], NT) for j in range(fold)]
            out = []
            for j in range(fold):
                p = jnp.exp(scores[j])
                ds = (p * slopes[j]).astype(bf16)
                dv[j, here, :] += dot(p.astype(bf16), docat[j][:, :PAIR], NN)
                dk[j, here, :] += dot(ds, qcat[j][:, :PAIR], NN)
                out.append(dq[j] + dot(kt[j, :, here], ds, NN))
            return tuple(out)

        dq = lax.fori_loop(
            0, bounds[1, i], step, (jnp.zeros((PAIR, 2 * QBLK), f32),) * fold
        )

        @pl.when((i >= MAXLEN // QBLK) & (i < (MAXLEN + own) // QBLK))
        def _():
            for j in range(fold):
                gqkv_ref[
                    0, pl.ds(pl.multiple_of(row0 - MAXLEN, QBLK), QBLK), pl.ds(j * PAIR, PAIR)
                ] = (unpair(dq[j]) * HEAD_DIM**-0.5).T.astype(bf16)

        return carry

    lax.fori_loop(0, window // QBLK, block, 0)
    for j in range(fold):
        cols = pl.ds(j * PAIR, PAIR)
        gqkv_ref[1, :, cols] = dk[j, pl.ds(MAXLEN, own), :].astype(bf16)
        gqkv_ref[2, :, cols] = dv[j, pl.ds(MAXLEN, own), :].astype(bf16)


def attend_back(part, fold, bounds, qkv, grads, hot, mask, own):
    window, wide = qkv.shape
    width = wide // 3
    pairs = width // PAIR
    parts = pairs // fold
    column = lambda c: pl.BlockSpec((window, fold * PAIR), lambda g, b: (0, c * parts + part))
    whole = lambda a: pl.BlockSpec(a.shape, lambda g, b: (0, 0))
    side0 = (LSE0 + 6 * fold * part, 6 * pairs)
    return pl.pallas_call(
        functools.partial(attend_back_kernel, side0),
        grid_spec=pltpu.PrefetchScalarGridSpec(
            num_scalar_prefetch=1,
            grid=(1,),
            in_specs=[
                column(0),
                column(1),
                column(2),
                pl.BlockSpec((window, fold * PAIR), lambda g, b: (0, part)),
                pl.BlockSpec((window, SIDE), lambda g, b: (0, pairs)),
                whole(hot),
                whole(mask),
            ],
            out_specs=pl.BlockSpec((3, own, fold * PAIR), lambda g, b: (0, 0, 0)),
            scratch_shapes=[
                pltpu.VMEM((fold, window + PAD, 2 * PAIR), bf16),
                pltpu.VMEM((fold, window + PAD, 2 * PAIR), bf16),
                pltpu.VMEM((fold, PAIR, window + PAD), bf16),
                pltpu.VMEM((fold, window + PAD, PAIR), f32),
                pltpu.VMEM((fold, window + PAD, PAIR), f32),
            ],
        ),
        out_shape=jax.ShapeDtypeStruct((3, own, fold * PAIR), bf16),
        cost_estimate=pl.CostEstimate(
            flops=own * 900 * PAIR * fold * 16,
            bytes_accessed=window * PAIR * fold * 8,
            transcendentals=0,
        ),
        name=f"attend_back{part}",
    )(bounds, qkv, qkv, qkv, grads, grads, hot, mask)


def low3(values):
    high = values.astype(bf16)
    rest = values - high.astype(f32)
    mid = rest.astype(bf16)
    return high, mid, (rest - mid.astype(f32)).astype(bf16)


def dot3(values, chosen, dims):
    return sum(dot(part, chosen, dims) for part in low3(values))


def iota(shape, axis):
    return lax.broadcasted_iota(jnp.int32, shape, axis)


def mean_row(values):
    return jnp.mean(values, axis=-1, keepdims=True)


def col_sum(values):
    return jnp.sum(values, axis=0, keepdims=True)


def norm_back(grad_out, normed, inv_std, gain_vec):
    grad_norm = grad_out * gain_vec
    inner = grad_norm - mean_row(grad_norm) - normed * mean_row(grad_norm * normed)
    return inv_std * inner, col_sum(grad_out * normed), col_sum(grad_out)


ROWS = 256
VECTORS = 24


def middle_kernel(
    heads_part, place, w_in_hbm, w_back_hbm, w_pool_hbm, tok, ctx, lse, cot, w_out, b_out, gain_a, shift_a, b_in,
    b_back, gain_f, shift_f, b_pool, w_class, starts, labels,
    out, gar, gs, act_hbm, gpre_hbm, gffn, mid, gattn, cls, gpool, vec,
    w_in, w_back, w_pool, act, gpre, slope, unit_a, unit_f, inv_a, inv_f, acc, sems,
):
    own, width = tok.shape
    chunks, _, wide = act.shape
    blocks = own // ROWS
    n_class = w_class.shape[0]
    loads = [
        pltpu.make_async_copy(w_in_hbm, w_in, sems.at[0]),
        pltpu.make_async_copy(w_back_hbm, w_back, sems.at[1]),
        pltpu.make_async_copy(w_pool_hbm, w_pool, sems.at[2]),
    ]
    for load in loads:
        load.start()

    def at(b):
        return pl.ds(pl.multiple_of(b * ROWS, ROWS), ROWS)

    def cols(c):
        return pl.ds(pl.multiple_of(c * wide, wide), wide)

    def norm(hidden, rows, unit, inv, gain, shift):
        centred = hidden - mean_row(hidden)
        inv_std = lax.rsqrt(mean_row(centred * centred) + eps)
        normed = centred * inv_std
        unit[rows, :] = normed
        inv[rows, :] = inv_std
        return (normed * gain[...] + shift[...]).astype(bf16)

    def first_norm(b, carry):
        rows = at(b)
        hidden = tok[rows, :].astype(f32) + dot(ctx[rows, :], w_out[...], NN) + b_out[...]
        mid[rows, :] = norm(hidden, rows, unit_a, inv_a, gain_a, shift_a)
        return carry

    lax.fori_loop(0, blocks, first_norm, 0)
    loads[0].wait()
    loads[1].wait()
    acc[...] = jnp.zeros_like(acc)

    def forward(c, carry):
        for b in range(blocks):
            rows = slice(b * ROWS, (b + 1) * ROWS)
            pre = dot(mid[rows, :], w_in[:, cols(c)], NN) + b_in[:, cols(c)]
            cdf = 0.5 * (1.0 + lax.erf(pre * (0.5**0.5)))
            low = (pre * cdf).astype(bf16)
            act[c, rows, :] = low
            slope[c, rows, :] = cdf + pre * (jnp.exp(-0.5 * pre * pre) * 0.3989422804014327)
            acc[rows, :] += dot(low, w_back[cols(c), :], NN)
        pltpu.make_async_copy(act.at[c], act_hbm.at[c], sems.at[3 + c]).start()
        return carry

    lax.fori_loop(0, chunks, forward, 0)

    def second_norm(b, carry):
        rows = at(b)
        hidden = mid[rows, :].astype(f32) + (acc[rows, :] + b_back[...])
        out[rows, :] = norm(hidden, rows, unit_f, inv_f, gain_f, shift_f)
        return carry

    lax.fori_loop(0, blocks, second_norm, 0)

    loads[2].wait()
    seqs = starts.shape[0]
    picked = (iota((seqs, own), 1) + place[0] * own == starts[...]).astype(f32)
    sel = picked.astype(bf16)
    owned = jnp.sum(picked, axis=1, keepdims=True)
    cls_low = dot(sel, out[...], NN).astype(bf16)
    cls[...] = cls_low
    pooled = jnp.tanh(dot(cls_low, w_pool[...], NN) + b_pool[...])
    logits = [jnp.sum(pooled * w_class[c : c + 1, :], axis=1, keepdims=True) for c in range(n_class)]
    peak = functools.reduce(jnp.maximum, logits)
    expo = [jnp.exp(x - peak) for x in logits]
    total = sum(expo)
    probs = [x / total for x in expo]
    terms = owned * (peak + jnp.log(total) - sum(p * x for p, x in zip(probs, logits)))
    entropy = jnp.sum(terms, axis=0, keepdims=True)
    g_logits = [
        (probs[c] - (labels[...] == c).astype(f32)) * owned for c in range(n_class)
    ]
    g_pooled = sum(g_logits[c] * w_class[c : c + 1, :] for c in range(n_class))
    g_low = (g_pooled * (1.0 - pooled * pooled)).astype(bf16)
    gpool[...] = g_low
    grad_cls = dot(g_low, w_pool[...], NT)

    def second_back(b, carry):
        rows = at(b)
        here = (
            iota((seqs, ROWS), 1) + (place[0] * own + b * ROWS) == starts[...]
        ).astype(f32).astype(bf16)
        back = sum(dot(here, part, TN) for part in low3(grad_cls))
        grad_out = cot[rows, :].astype(f32) + back
        res, g_gain, g_shift = norm_back(grad_out, unit_f[rows, :], inv_f[rows, :], gain_f[...])
        low = res.astype(bf16)
        gar[rows, :] = res
        gffn[rows, :] = low
        return carry[0] + g_gain, carry[1] + g_shift, carry[2] + col_sum(low.astype(f32))

    zero = jnp.zeros((1, width), f32)
    sums_f = lax.fori_loop(0, blocks, second_back, (zero, zero, zero))
    acc[...] = jnp.zeros_like(acc)

    def backward(c, carry):
        g_b_in = jnp.zeros((1, wide), f32)
        for b in range(blocks):
            rows = slice(b * ROWS, (b + 1) * ROWS)
            grad_act = dot(gffn[rows, :], w_back[cols(c), :], NT)
            low = (grad_act * slope[c, rows, :]).astype(bf16)
            gpre[c, rows, :] = low
            g_b_in += col_sum(low.astype(f32))
            acc[rows, :] += dot(low, w_in[:, cols(c)], NT)
        vec[pl.ds(8 + c, 1), :] = g_b_in
        pltpu.make_async_copy(gpre.at[c], gpre_hbm.at[c], sems.at[3 + chunks + c]).start()
        return carry

    lax.fori_loop(0, chunks, backward, 0)

    heads = width // HEAD_DIM
    lane = iota((1, SIDE), 1)
    gap = LSE0 + 3 * heads
    feature, flane = iota((width, SIDE), 0), iota((width, SIDE), 1)
    third = flane - gap - 3 * (feature // HEAD_DIM)
    head_sum = ((third >= 0) & (third < 3)).astype(f32).astype(bf16)
    lrow, llane = iota((lse.shape[0], SIDE), 0), iota((lse.shape[0], SIDE), 1)
    lhead = (lrow // 8) * heads_part + lrow % 8
    spread = [
        ((llane == LSE0 + 3 * lhead + p) & (lrow % 8 < heads_part)).astype(f32).astype(bf16)
        for p in range(3)
    ]
    which = lax.rem(lane - gap + 3 * heads, 3)

    def first_back(b, carry):
        rows = at(b)
        grad_mid = gar[rows, :] + acc[rows, :]
        res, g_gain, g_shift = norm_back(grad_mid, unit_a[rows, :], inv_a[rows, :], gain_a[...])
        low = res.astype(bf16)
        gar[rows, :] = res
        gattn[rows, :] = low
        grad_ctx = dot(low, w_out[...], NT).astype(bf16)
        gs[rows, :width] = grad_ctx
        delta = dot3(grad_ctx.astype(f32) * ctx[rows, :].astype(f32), head_sum, NN)
        high, mid_part, rest = low3(-delta)
        side = jnp.where(which == 0, high, jnp.where(which == 1, mid_part, rest))
        lse_parts = low3(-lse[:, rows])
        side_lse = sum(dot(part, spread[p], TN) for p, part in enumerate(lse_parts))
        gs[rows, width:] = side + side_lse.astype(bf16)
        return carry[0] + g_gain, carry[1] + g_shift, carry[2] + col_sum(low.astype(f32))

    sums_a = lax.fori_loop(0, blocks, first_back, (zero, zero, zero))
    for row, value in enumerate((sums_a[2], sums_a[0], sums_a[1], sums_f[2], sums_f[0], sums_f[1])):
        vec[row : row + 1, :] = value
    vec[6:7, :] = col_sum(g_low.astype(f32))
    vec[7:8, :] = jnp.broadcast_to(entropy, (1, width))
    for c in range(n_class):
        vec[8 + chunks + c : 9 + chunks + c, :] = col_sum(pooled * g_logits[c])
    done = 8 + chunks + n_class
    vec[done:, :] = jnp.zeros((VECTORS - done, width), f32)
    for c in range(chunks):
        pltpu.make_async_copy(act.at[c], act_hbm.at[c], sems.at[3 + c]).wait()
        pltpu.make_async_copy(gpre.at[c], gpre_hbm.at[c], sems.at[3 + chunks + c]).wait()


def middle_layer(heads_part, place, w_in, w_back, w_pool, tok, ctx, lse, cot, w_out, rest, starts, labels):
    own, width = tok.shape
    ff = w_in.shape[1]
    chunks = ff // width
    seqs = starts.shape[0]
    vmem = pl.BlockSpec(memory_space=pltpu.VMEM)
    hbm = pl.BlockSpec(memory_space=pl.ANY)
    shape = jax.ShapeDtypeStruct
    flops = 2 * own * width * (6 * width + 4 * ff)
    return pl.pallas_call(
        functools.partial(middle_kernel, heads_part),
        in_specs=[pl.BlockSpec(memory_space=pltpu.SMEM), hbm, hbm, hbm] + [vmem] * (5 + len(rest) + 2),
        out_specs=[vmem, vmem, vmem, hbm, hbm] + [vmem] * 6,
        out_shape=[
            shape((own, width), bf16),
            shape((own, width), f32),
            shape((own, width + SIDE), bf16),
            shape((chunks, own, width), bf16),
            shape((chunks, own, width), bf16),
            shape((own, width), bf16),
            shape((own, width), bf16),
            shape((own, width), bf16),
            shape((seqs, width), bf16),
            shape((seqs, width), bf16),
            shape((VECTORS, width), f32),
        ],
        scratch_shapes=[
            pltpu.VMEM(w_in.shape, bf16),
            pltpu.VMEM(w_back.shape, bf16),
            pltpu.VMEM(w_pool.shape, bf16),
            pltpu.VMEM((chunks, own, width), bf16),
            pltpu.VMEM((chunks, own, width), bf16),
            pltpu.VMEM((chunks, own, width), f32),
            pltpu.VMEM((own, width), f32),
            pltpu.VMEM((own, width), f32),
            pltpu.VMEM((own, 1), f32),
            pltpu.VMEM((own, 1), f32),
            pltpu.VMEM((own, width), f32),
            pltpu.SemaphoreType.DMA((3 + 2 * chunks,)),
        ],
        compiler_params=pltpu.CompilerParams(vmem_limit_bytes=62 * 2**20),
        cost_estimate=pl.CostEstimate(flops=flops, bytes_accessed=30 * 2**20, transcendentals=0),
        name="middle_layer",
    )(place, w_in, w_back, w_pool, tok, ctx, lse, cot, w_out, *rest, starts, labels)


def split_core(tile, core, half, keep, send, first):
    for n in range(tile.shape[0] // (2 * half)):
        even = tile[2 * n * half : (2 * n + 1) * half, :]
        odd = tile[(2 * n + 1) * half : (2 * n + 2) * half, :]
        keep[first + n, :, :] = jnp.where(core == 0, even, odd).astype(bf16)
        send[first + n, :, :] = jnp.where(core == 0, odd, even).astype(bf16)


def weight_grads_kernel(
    core, act, gpre, gffn, mid, ctx, gattn, cls, gpool,
    back_keep, back_send, in_keep, in_send, out_keep, out_send, mid_t,
):
    y = pl.program_id(0)

    @pl.when(y == 0)
    def _():
        mid_t[...] = mid[...].T
        split_core(dot(ctx[...], gattn[...], TN), core[0], out_keep.shape[1], out_keep, out_send, 0)

    @pl.when(y == 1)
    def _():
        split_core(dot(cls[...], gpool[...], TN), core[0], out_keep.shape[1], out_keep, out_send, 0)

    split_core(dot(act[0], gffn[...], TN), core[0], back_keep.shape[1], back_keep, back_send, 0)
    split_core(dot(mid_t[...], gpre[0], NN), core[0], in_keep.shape[1], in_keep, in_send, 0)


def weight_grads(core, n_seq, act, gpre, gffn, mid, ctx, gattn, cls, gpool):
    chunks, own, width = act.shape
    groups = n_seq // 2
    half_b, half_w = chunks * width // n_seq, width // n_seq
    shape = jax.ShapeDtypeStruct
    whole = lambda a: pl.BlockSpec(a.shape, lambda y, c: (0, 0))
    tile = pl.BlockSpec((1, own, width), lambda y, c: (y, 0, 0))
    back = pl.BlockSpec((groups // chunks, half_b, width), lambda y, c: (y, 0, 0))
    inner = pl.BlockSpec((groups, half_w, width), lambda y, c: (0, 0, y))
    outer = pl.BlockSpec((groups, half_w, width), lambda y, c: (0, 0, jnp.minimum(y, 1)))
    return pl.pallas_call(
        weight_grads_kernel,
        grid_spec=pltpu.PrefetchScalarGridSpec(
            num_scalar_prefetch=1,
            grid=(chunks,),
            in_specs=[tile, tile] + [whole(a) for a in (gffn, mid, ctx, gattn, cls, gpool)],
            out_specs=[back, back, inner, inner, outer, outer],
            scratch_shapes=[pltpu.VMEM((width, own), bf16)],
        ),
        out_shape=[shape((groups, half_b, width), bf16)] * 2
        + [shape((groups, half_w, chunks * width), bf16)] * 2
        + [shape((groups, half_w, 2 * width), bf16)] * 2,
        compiler_params=pltpu.CompilerParams(vmem_limit_bytes=48 * 2**20),
        cost_estimate=pl.CostEstimate(
            flops=2 * own * width * width * (2 * chunks + 1), bytes_accessed=30 * 2**20, transcendentals=0
        ),
        name="weight_grads",
    )(core, act, gpre, gffn, mid, ctx, gattn, cls, gpool)


def last_kernel(n_parts, core, *refs):
    tok, gar, w_qkv = refs[:3]
    parts = refs[3 : 3 + n_parts]
    gtok, vec = refs[3 + n_parts : 5 + n_parts]
    pairs = refs[5 + n_parts : 11 + n_parts]
    tok_t = refs[11 + n_parts]
    c = pl.program_id(0)

    @pl.when(c == 0)
    def _():
        tok_t[...] = tok[...].T
        gtok[...] = gar[...]
        vec[...] = jnp.zeros_like(vec)

    grads = jnp.concatenate([p[0] for p in parts], axis=1)
    gtok[...] += dot(grads, w_qkv[...], NT)
    vec[pl.ds(c, 1), :] = col_sum(grads.astype(f32))
    tile = dot(tok_t[...], grads, NN)
    for n in range(3):

        @pl.when(c == n)
        def _():
            keep, send = pairs[2 * n], pairs[2 * n + 1]
            split_core(tile, core[0], keep.shape[1], keep, send, 0)


def last_layer(core, n_seq, tok, gar, w_qkv, parts):
    own, width = tok.shape
    groups, half = n_seq // 2, width // n_seq
    shape = jax.ShapeDtypeStruct
    whole = lambda a: pl.BlockSpec(a.shape, lambda c, k: (0,) * len(a.shape))
    pair = pl.BlockSpec((groups, half, width), lambda c, k: (0, 0, 0))
    return pl.pallas_call(
        functools.partial(last_kernel, len(parts)),
        grid_spec=pltpu.PrefetchScalarGridSpec(
            num_scalar_prefetch=1,
            grid=(3,),
            in_specs=[whole(tok), whole(gar), pl.BlockSpec((width, width), lambda c, k: (0, c))]
            + [pl.BlockSpec((1,) + p.shape[1:], lambda c, k: (c, 0, 0)) for p in parts],
            out_specs=[whole(gar), pl.BlockSpec((8, width), lambda c, k: (0, 0))] + [pair] * 6,
            scratch_shapes=[pltpu.VMEM((width, own), bf16)],
        ),
        out_shape=[shape((own, width), f32), shape((8, width), f32)]
        + [shape((groups, half, width), bf16)] * 6,
        compiler_params=pltpu.CompilerParams(vmem_limit_bytes=40 * 2**20),
        cost_estimate=pl.CostEstimate(
            flops=12 * own * width * width, bytes_accessed=12 * 2**20, transcendentals=0
        ),
        name="last_layer",
    )(core, tok, gar, w_qkv, *parts)


def halo(rows, left_axis, n_head):
    up = [(i, i + 1) for i in range(n_head - 1)]
    down = [(i + 1, i) for i in range(n_head - 1)]
    from_left = lax.ppermute(rows[-MAXLEN:], left_axis, up)
    from_right = lax.ppermute(rows[:MAXLEN], left_axis, down)
    return jnp.concatenate([from_left, rows, from_right], axis=0)


def pick(values, axis, index):
    return lax.dynamic_index_in_dim(values, index, axis, keepdims=False)


class Sums:
    def __init__(self, pairs, orders, n_seq, n_head, vectors):
        self.count = {"seq": n_seq, "head": n_head}
        self.bits = {"seq": n_seq.bit_length() - 1, "head": n_head.bit_length() - 1}
        self.stages = sum(self.bits.values())
        self.orders = orders
        self.vectors = vectors
        self.axes = [[n for n in range(self.stages) if n != self.bits["seq"] - 1] for _ in pairs]
        shape = lambda a: a.reshape(
            (2,) * (self.stages - 1) + (a.shape[1] // n_head,) + a.shape[2:]
        )
        self.kept = [shape(keep) for keep, _ in pairs]
        self.sent = [shape(send) for _, send in pairs]
        self.stage = 0
        self.send()

    def send(self):
        self.got = [
            self.swap(v, *self.orders[n][self.stage]) for n, v in enumerate(self.sent)
        ]
        self.vectors = self.vectors + self.swap(self.vectors, *self.orders[0][self.stage])

    def swap(self, values, name, bit):
        return lax.ppermute(values, name, [(i, i ^ (1 << bit)) for i in range(self.count[name])])

    def split(self):
        self.stage += 1
        kept, sent = [], []
        for n, (keep, got) in enumerate(zip(self.kept, self.got)):
            name, bit = self.orders[n][self.stage]
            where = (self.stages if name == "head" else self.bits["seq"]) - 1 - bit
            at = self.axes[n].index(where)
            self.axes[n].pop(at)
            mine = (lax.axis_index(name) >> bit) & 1
            half = lambda m: pick(keep, at, m).astype(f32) + pick(got, at, m).astype(f32)
            sent.append(half(1 - mine).astype(bf16))
            kept.append(half(mine))
        self.kept, self.sent = kept, sent

    def rest(self):
        while self.stage < self.stages - 1:
            self.split()
            self.send()
        return [k.astype(f32) + g.astype(f32) for k, g in zip(self.kept, self.got)]


def after(value, *others):
    return lax.optimization_barrier((value, *others))[0]


def orders(n_seq, n_head):
    seq_bits, head_bits = n_seq.bit_length() - 1, n_head.bit_length() - 1
    core = [("seq", 0)]
    planar = [("seq", b) for b in range(1, seq_bits)]
    along = [("head", b) for b in range(head_bits)]
    return (
        core + planar + along,
        core + planar[::-1] + along,
        core + along + planar,
    )


def local(
    tokens, cotangent, lengths, labels, w_qkv, b_query, b_value, w_out, b_out, gain_attn,
    shift_attn, w_in, b_in, w_back, b_back, gain_ffn, shift_ffn, w_pool, b_pool, w_class,
):
    n_head = lax.axis_size("head")
    n_seq = lax.axis_size("seq")
    head_index = lax.axis_index("head")
    own, width = tokens.shape
    window = own + 2 * MAXLEN
    group = own * n_head

    seq_lengths = lengths[0]
    ends = jnp.cumsum(seq_lengths)
    starts = ends - seq_lengths
    base = head_index * own - MAXLEN
    pos = base + jnp.arange(window, dtype=jnp.int32)
    n_in_group = seq_lengths.shape[0]
    lane_pad = (0, SIDE - n_in_group)
    starts_w = jnp.pad(starts, lane_pad, constant_values=group + MAXLEN)
    ends_w = jnp.pad(ends, lane_pad, constant_values=-MAXLEN)
    inside = (starts_w[None, :] <= pos[:, None]) & (pos[:, None] < ends_w[None, :])
    hot = inside.astype(bf16)
    lane = jnp.arange(SIDE, dtype=jnp.int32)[None, :]
    mask = jnp.where(lane < n_in_group, jnp.where(inside, 0.0, -BIG), 1.0).astype(bf16)
    mask = jnp.concatenate(
        [mask, jnp.broadcast_to(jnp.where(lane < n_in_group, -BIG, 1.0).astype(bf16), (PAD, SIDE))]
    )
    blk = base + QBLK * jnp.arange(window // QBLK, dtype=jnp.int32)
    low = jnp.max(jnp.where(starts[None, :] <= blk[:, None], starts[None, :], -1), axis=1)
    high = jnp.min(
        jnp.where(ends[None, :] > blk[:, None] + QBLK - 1, ends[None, :], group), axis=1
    )
    is_own = (blk >= base + MAXLEN) & (blk < base + MAXLEN + own)
    low = jnp.where(is_own, low - base, jnp.maximum(low - base, MAXLEN))
    high = jnp.where(is_own, high - base, jnp.minimum(high - base, MAXLEN + own))
    valid = (blk >= 0) & (blk < group)
    low = low // 128 * 128
    steps = jnp.where(valid, jnp.maximum((high - low + KCHUNK - 1) // KCHUNK, 0), 0)
    bounds = jnp.stack([low, steps]).astype(jnp.int32)
    own_bounds = bounds[:, MAXLEN // QBLK : (MAXLEN + own) // QBLK]

    tokens_w = halo(tokens, "head", n_head)
    bias = jnp.concatenate([b_query, jnp.zeros_like(b_query), b_value])[None, :]
    qscale = jnp.where(jnp.arange(3 * width) < width, HEAD_DIM**-0.5, 1.0).astype(f32)[None, :]
    qkv = ((dot(tokens_w, w_qkv, NN) + bias) * qscale).astype(bf16)
    context, lse = attend(own_bounds, qkv, hot, mask, own)

    shards = n_seq * n_head
    shard = head_index + n_head * lax.axis_index("seq")
    core = (lax.axis_index("seq") & 1).reshape(1)
    row = lambda v: v.reshape(1, -1)
    seq_pad = (0, -n_in_group % 16)
    column = lambda v, fill: jnp.pad(v, seq_pad, constant_values=fill).reshape(-1, 1)
    rest = [
        row(v) for v in (b_out, gain_attn, shift_attn, b_in, b_back, gain_ffn, shift_ffn, b_pool)
    ] + [w_class.T]
    (output, gar, gs, act, gpre, gffn, mid, gattn, cls, gpool, vec) = middle_layer(
        2 * fold_of(width // PAIR, 3), head_index.reshape(1), w_in, w_back, w_pool, tokens, context, lse, cotangent, w_out,
        rest, column(starts, -1), column(labels[0], 0),
    )
    grads_w = halo(gs, "head", n_head)

    pieces = weight_grads(core, n_seq, act, gpre, gffn, mid, context, gattn, cls, gpool)
    orders_all = orders(n_seq, n_head)
    first = Sums(
        [pieces[0:2], pieces[2:4], pieces[4:6]], orders_all, n_seq, n_head, vec
    )
    pairs = width // PAIR
    fold = fold_of(pairs, 2)
    parts = pairs // fold
    gqkv = []
    for part in range(parts):
        gqkv.append(attend_back(part, fold, bounds, qkv, grads_w, hot, mask, own))
        bounds = after(bounds, gqkv[-1][0, :8, :128])
        if part + 1 < parts:
            first.split()
            sums = lax.optimization_barrier(tuple(first.sent) + (bounds, first.vectors))
            first.sent, bounds, first.vectors = list(sums[:3]), sums[3], sums[4]
            first.send()
    last_out = last_layer(core, n_seq, tokens, gar, w_qkv, gqkv)
    grad_tokens, vec_qkv = last_out[:2]
    last = Sums(
        [last_out[2:4], last_out[4:6], last_out[6:8]], orders_all, n_seq, n_head, vec_qkv
    )
    sum_wback, sum_win, sum_c = first.rest()
    sum_wout, sum_pool = sum_c[:, :width], sum_c[:, width:]
    sum_q, sum_k, sum_v = last.rest()
    sum_wqkv = jnp.concatenate([sum_q, sum_k, sum_v], axis=1)

    vectors, vectors_qkv = first.vectors, last.vectors
    size = width // shards
    mine = lax.dynamic_slice_in_dim(vectors, shard * size, size, 1)
    mine_qkv = lax.dynamic_slice_in_dim(vectors_qkv, shard * size, size, 1)
    chunks = w_in.shape[1] // width
    n_class = w_class.shape[1]
    grad_bin = lax.dynamic_slice_in_dim(
        vectors[8 : 8 + chunks].reshape(-1), shard * size * chunks, size * chunks, 0
    )
    grad_class = mine[8 + chunks : 8 + chunks + n_class].T
    entropy_mean = vectors[7, 0] / (n_seq * labels.shape[1])
    return (
        output, grad_tokens, sum_wqkv, mine_qkv[0], mine_qkv[2], sum_wout, mine[0], mine[1], mine[2],
        sum_win, grad_bin, sum_wback, mine[3], mine[4], mine[5], sum_pool, mine[6], grad_class,
        entropy_mean,
    )


def solution(mesh):
    rows = P(("seq", "head"), None)
    vec = P(("seq", "head"))
    return jax.shard_map(
        local,
        mesh=mesh,
        in_specs=(rows, rows, P("seq", None), P("seq", None)) + (P(),) * 16,
        out_specs=(
            rows, rows, rows, vec, vec, rows, vec, vec, vec, rows, vec, rows, vec, vec, vec, rows,
            vec, rows, P(),
        ),
        check_vma=False,
    )
```

```python
import functools

import jax
import jax.numpy as jnp
from jax import lax
from jax.experimental import pallas as pl
from jax.experimental.pallas import tpu as pltpu
from jax.sharding import PartitionSpec as P

HEAD_DIM = 64
MAXLEN = 512
PAIR = 2 * HEAD_DIM
QBLK = 128
KCHUNK = 256
PAD = KCHUNK - 128
LSE0 = 32
SIDE = 128

eps = 1e-05
BIG = 1e30
highest = lax.Precision.HIGHEST
f32 = jnp.float32
bf16 = jnp.bfloat16
NT = (((1,), (1,)), ((), ()))
NN = (((1,), (0,)), ((), ()))
TN = (((0,), (0,)), ((), ()))


def dot(left, right, dims):
    return lax.dot_general(left, right, dims, preferred_element_type=f32)


def pair_rows(rows, side):
    lane = lax.broadcasted_iota(jnp.int32, rows.shape, 1)
    zero = jnp.zeros_like(rows)
    first = jnp.where(lane < HEAD_DIM, rows, zero)
    second = jnp.where(lane >= HEAD_DIM, rows, zero)
    return jnp.concatenate(
        [jnp.concatenate([first, side[0]], axis=1), jnp.concatenate([second, side[1]], axis=1)],
        axis=0,
    )


def unpair(both):
    row = lax.broadcasted_iota(jnp.int32, (PAIR, QBLK), 0)
    return jnp.where(row < HEAD_DIM, both[:, :QBLK], both[:, QBLK:])


def attend_kernel(bounds, q_ref, k_ref, v_ref, hot_ref, mask_ref, ctx_ref, lse_ref, kcat, vt):
    window = k_ref.shape[0]
    own = ctx_ref.shape[0]
    fold = kcat.shape[0]

    @pl.when(pl.program_id(0) == 0)
    def _():
        for j in range(fold):
            kcat[j, :, PAIR:] = mask_ref[...]
            kcat[j, pl.ds(window, PAD), :PAIR] = jnp.zeros((PAD, PAIR), bf16)
            vt[j, :, pl.ds(window, PAD)] = jnp.zeros((PAIR, PAD), bf16)

    lse_ref[...] = jnp.zeros_like(lse_ref)
    for j in range(fold):
        cols = pl.ds(j * PAIR, PAIR)
        kcat[j, pl.ds(0, window), :PAIR] = k_ref[:, cols]
        for at in range(0, window, 256):
            vt[j, :, pl.ds(at, 256)] = v_ref[pl.ds(at, 256), cols].T

    def block(i, carry):
        row0 = pl.multiple_of(i * QBLK, QBLK)
        hot = hot_ref[pl.ds(MAXLEN + row0, QBLK), :]
        rows = q_ref[pl.ds(MAXLEN + row0, QBLK), :]
        qcat = [pair_rows(rows[:, j * PAIR : (j + 1) * PAIR], (hot, hot)) for j in range(fold)]
        first = bounds[0, i]

        def step(c, state):
            start = pl.multiple_of(first + c * KCHUNK, 128)
            scores = [dot(kcat[j, pl.ds(start, KCHUNK), :], qcat[j], NT) for j in range(fold)]
            out = []
            for j, s in enumerate(scores):
                peak, total, acc = state[j]
                new_peak = jnp.maximum(peak, jnp.max(s, axis=0, keepdims=True))
                scale = jnp.exp(peak - new_peak)
                p = jnp.exp(s - new_peak)
                total = total * scale + jnp.sum(p, axis=0, keepdims=True)
                acc = acc * scale + dot(vt[j, :, pl.ds(start, KCHUNK)], p.astype(bf16), NN)
                out.append((new_peak, total, acc))
            return tuple(out)

        empty = (
            jnp.full((1, 2 * QBLK), -BIG, f32),
            jnp.zeros((1, 2 * QBLK), f32),
            jnp.zeros((PAIR, 2 * QBLK), f32),
        )
        state = lax.fori_loop(0, bounds[1, i], step, (empty,) * fold)
        for j, (peak, total, acc) in enumerate(state):
            ctx_ref[pl.ds(row0, QBLK), pl.ds(j * PAIR, PAIR)] = unpair(acc / total).T.astype(bf16)
            lse = peak + jnp.log(total)
            lse_ref[2 * j : 2 * j + 1, pl.ds(row0, QBLK)] = lse[:, :QBLK]
            lse_ref[2 * j + 1 : 2 * j + 2, pl.ds(row0, QBLK)] = lse[:, QBLK:]
        return carry

    lax.fori_loop(0, own // QBLK, block, 0)


def fold_of(pairs, most):
    return max(n for n in range(1, most + 1) if pairs % n == 0)


def attend(bounds, qkv, hot, mask, own):
    window, wide = qkv.shape
    width = wide // 3
    pairs = width // PAIR
    fold = fold_of(pairs, 3)
    parts = pairs // fold
    column = lambda part: pl.BlockSpec((window, fold * PAIR), lambda g, b: (0, part * parts + g))
    whole = lambda a: pl.BlockSpec(a.shape, lambda g, b: (0, 0))
    return pl.pallas_call(
        attend_kernel,
        grid_spec=pltpu.PrefetchScalarGridSpec(
            num_scalar_prefetch=1,
            grid=(parts,),
            in_specs=[column(0), column(1), column(2), whole(hot), whole(mask)],
            out_specs=[
                pl.BlockSpec((own, fold * PAIR), lambda g, b: (0, g)),
                pl.BlockSpec((8, own), lambda g, b: (g, 0)),
            ],
            scratch_shapes=[
                pltpu.VMEM((fold, window + PAD, 2 * PAIR), bf16),
                pltpu.VMEM((fold, PAIR, window + PAD), bf16),
            ],
        ),
        out_shape=[
            jax.ShapeDtypeStruct((own, width), bf16),
            jax.ShapeDtypeStruct((8 * parts, own), f32),
        ],
        cost_estimate=pl.CostEstimate(
            flops=own * 600 * width * 4, bytes_accessed=window * wide * 2, transcendentals=0
        ),
        name="attend",
    )(bounds, qkv, qkv, qkv, hot, mask)


def attend_back_kernel(
    side0, bounds, q_ref, k_ref, v_ref, do_ref, side_ref, hot_ref, mask_ref,
    gqkv_ref, kcat, vcat, kt, dk, dv,
):
    window = k_ref.shape[0]
    own = gqkv_ref.shape[1]
    fold = kcat.shape[0]
    low0, gap = side0

    for j in range(fold):
        cols = pl.ds(j * PAIR, PAIR)
        kcat[j, :, PAIR:] = mask_ref[...]
        vcat[j, :, PAIR:] = jnp.ones((window + PAD, SIDE), bf16)
        kcat[j, pl.ds(window, PAD), :PAIR] = jnp.zeros((PAD, PAIR), bf16)
        vcat[j, pl.ds(window, PAD), :PAIR] = jnp.zeros((PAD, PAIR), bf16)
        kt[j, :, pl.ds(window, PAD)] = jnp.zeros((PAIR, PAD), bf16)
        kcat[j, pl.ds(0, window), :PAIR] = k_ref[:, cols]
        vcat[j, pl.ds(0, window), :PAIR] = v_ref[:, cols]
        for at in range(0, window, 256):
            kt[j, :, pl.ds(at, 256)] = k_ref[pl.ds(at, 256), cols].T
    dk[...] = jnp.zeros_like(dk)
    dv[...] = jnp.zeros_like(dv)
    lane = lax.broadcasted_iota(jnp.int32, (QBLK, SIDE), 1)

    def side_lanes(side, first):
        return jnp.where((lane >= first) & (lane < first + 3), side, jnp.zeros_like(side))

    def block(i, carry):
        row0 = pl.multiple_of(i * QBLK, QBLK)
        hot = hot_ref[pl.ds(row0, QBLK), :]
        side = side_ref[pl.ds(row0, QBLK), :]
        rows = q_ref[pl.ds(row0, QBLK), :]
        grads = do_ref[pl.ds(row0, QBLK), :]
        qcat, docat = [], []
        for j in range(fold):
            cols = slice(j * PAIR, (j + 1) * PAIR)
            low = low0 + 6 * j
            qcat.append(
                pair_rows(
                    rows[:, cols],
                    (hot + side_lanes(side, low), hot + side_lanes(side, low + 3)),
                )
            )
            docat.append(
                pair_rows(
                    grads[:, cols],
                    (side_lanes(side, low + gap), side_lanes(side, low + gap + 3)),
                )
            )
        first = bounds[0, i]

        def step(c, dq):
            start = pl.multiple_of(first + c * KCHUNK, 128)
            here = pl.ds(start, KCHUNK)
            scores = [dot(kcat[j, here, :], qcat[j], NT) for j in range(fold)]
            slopes = [dot(vcat[j, here, :], docat[j], NT) for j in range(fold)]
            out = []
            for j in range(fold):
                p = jnp.exp(scores[j])
                ds = (p * slopes[j]).astype(bf16)
                dv[j, here, :] += dot(p.astype(bf16), docat[j][:, :PAIR], NN)
                dk[j, here, :] += dot(ds, qcat[j][:, :PAIR], NN)
                out.append(dq[j] + dot(kt[j, :, here], ds, NN))
            return tuple(out)

        dq = lax.fori_loop(
            0, bounds[1, i], step, (jnp.zeros((PAIR, 2 * QBLK), f32),) * fold
        )

        @pl.when((i >= MAXLEN // QBLK) & (i < (MAXLEN + own) // QBLK))
        def _():
            for j in range(fold):
                gqkv_ref[
                    0, pl.ds(pl.multiple_of(row0 - MAXLEN, QBLK), QBLK), pl.ds(j * PAIR, PAIR)
                ] = (unpair(dq[j]) * HEAD_DIM**-0.5).T.astype(bf16)

        return carry

    lax.fori_loop(0, window // QBLK, block, 0)
    for j in range(fold):
        cols = pl.ds(j * PAIR, PAIR)
        gqkv_ref[1, :, cols] = dk[j, pl.ds(MAXLEN, own), :].astype(bf16)
        gqkv_ref[2, :, cols] = dv[j, pl.ds(MAXLEN, own), :].astype(bf16)


def attend_back(part, fold, bounds, qkv, grads, hot, mask, own):
    window, wide = qkv.shape
    width = wide // 3
    pairs = width // PAIR
    parts = pairs // fold
    column = lambda c: pl.BlockSpec((window, fold * PAIR), lambda g, b: (0, c * parts + part))
    whole = lambda a: pl.BlockSpec(a.shape, lambda g, b: (0, 0))
    side0 = (LSE0 + 6 * fold * part, 6 * pairs)
    return pl.pallas_call(
        functools.partial(attend_back_kernel, side0),
        grid_spec=pltpu.PrefetchScalarGridSpec(
            num_scalar_prefetch=1,
            grid=(1,),
            in_specs=[
                column(0),
                column(1),
                column(2),
                pl.BlockSpec((window, fold * PAIR), lambda g, b: (0, part)),
                pl.BlockSpec((window, SIDE), lambda g, b: (0, pairs)),
                whole(hot),
                whole(mask),
            ],
            out_specs=pl.BlockSpec((3, own, fold * PAIR), lambda g, b: (0, 0, 0)),
            scratch_shapes=[
                pltpu.VMEM((fold, window + PAD, 2 * PAIR), bf16),
                pltpu.VMEM((fold, window + PAD, 2 * PAIR), bf16),
                pltpu.VMEM((fold, PAIR, window + PAD), bf16),
                pltpu.VMEM((fold, window + PAD, PAIR), f32),
                pltpu.VMEM((fold, window + PAD, PAIR), f32),
            ],
        ),
        out_shape=jax.ShapeDtypeStruct((3, own, fold * PAIR), bf16),
        cost_estimate=pl.CostEstimate(
            flops=own * 900 * PAIR * fold * 16,
            bytes_accessed=window * PAIR * fold * 8,
            transcendentals=0,
        ),
        name=f"attend_back{part}",
    )(bounds, qkv, qkv, qkv, grads, grads, hot, mask)


def low3(values):
    high = values.astype(bf16)
    rest = values - high.astype(f32)
    mid = rest.astype(bf16)
    return high, mid, (rest - mid.astype(f32)).astype(bf16)


def dot3(values, chosen, dims):
    return sum(dot(part, chosen, dims) for part in low3(values))


def iota(shape, axis):
    return lax.broadcasted_iota(jnp.int32, shape, axis)


def mean_row(values):
    return jnp.mean(values, axis=-1, keepdims=True)


def col_sum(values):
    return jnp.sum(values, axis=0, keepdims=True)


def norm_back(grad_out, normed, inv_std, gain_vec):
    grad_norm = grad_out * gain_vec
    inner = grad_norm - mean_row(grad_norm) - normed * mean_row(grad_norm * normed)
    return inv_std * inner, col_sum(grad_out * normed), col_sum(grad_out)


ROWS = 256
VECTORS = 24


def middle_kernel(
    heads_part, place, w_in_hbm, w_back_hbm, w_pool_hbm, tok, ctx, lse, cot, w_out, b_out, gain_a, shift_a, b_in,
    b_back, gain_f, shift_f, b_pool, w_class, starts, labels,
    out, gar, gs, act_hbm, gpre_hbm, gffn, mid, gattn, cls, gpool, vec,
    w_in, w_back, w_pool, act, gpre, slope, unit_a, unit_f, inv_a, inv_f, acc, sems,
):
    own, width = tok.shape
    chunks, _, wide = act.shape
    blocks = own // ROWS
    n_class = w_class.shape[0]
    loads = [
        pltpu.make_async_copy(w_in_hbm, w_in, sems.at[0]),
        pltpu.make_async_copy(w_back_hbm, w_back, sems.at[1]),
        pltpu.make_async_copy(w_pool_hbm, w_pool, sems.at[2]),
    ]
    for load in loads:
        load.start()

    def at(b):
        return pl.ds(pl.multiple_of(b * ROWS, ROWS), ROWS)

    def cols(c):
        return pl.ds(pl.multiple_of(c * wide, wide), wide)

    def norm(hidden, rows, unit, inv, gain, shift):
        centred = hidden - mean_row(hidden)
        inv_std = lax.rsqrt(mean_row(centred * centred) + eps)
        normed = centred * inv_std
        unit[rows, :] = normed
        inv[rows, :] = inv_std
        return (normed * gain[...] + shift[...]).astype(bf16)

    def first_norm(b, carry):
        rows = at(b)
        hidden = tok[rows, :].astype(f32) + dot(ctx[rows, :], w_out[...], NN) + b_out[...]
        mid[rows, :] = norm(hidden, rows, unit_a, inv_a, gain_a, shift_a)
        return carry

    lax.fori_loop(0, blocks, first_norm, 0)
    loads[0].wait()
    loads[1].wait()
    acc[...] = jnp.zeros_like(acc)

    def forward(c, carry):
        for b in range(blocks):
            rows = slice(b * ROWS, (b + 1) * ROWS)
            pre = dot(mid[rows, :], w_in[:, cols(c)], NN) + b_in[:, cols(c)]
            cdf = 0.5 * (1.0 + lax.erf(pre * (0.5**0.5)))
            low = (pre * cdf).astype(bf16)
            act[c, rows, :] = low
            slope[c, rows, :] = cdf + pre * (jnp.exp(-0.5 * pre * pre) * 0.3989422804014327)
            acc[rows, :] += dot(low, w_back[cols(c), :], NN)
        pltpu.make_async_copy(act.at[c], act_hbm.at[c], sems.at[3 + c]).start()
        return carry

    lax.fori_loop(0, chunks, forward, 0)

    def second_norm(b, carry):
        rows = at(b)
        hidden = mid[rows, :].astype(f32) + (acc[rows, :] + b_back[...])
        out[rows, :] = norm(hidden, rows, unit_f, inv_f, gain_f, shift_f)
        return carry

    lax.fori_loop(0, blocks, second_norm, 0)

    loads[2].wait()
    seqs = starts.shape[0]
    picked = (iota((seqs, own), 1) + place[0] * own == starts[...]).astype(f32)
    sel = picked.astype(bf16)
    owned = jnp.sum(picked, axis=1, keepdims=True)
    cls_low = dot(sel, out[...], NN).astype(bf16)
    cls[...] = cls_low
    pooled = jnp.tanh(dot(cls_low, w_pool[...], NN) + b_pool[...])
    logits = [jnp.sum(pooled * w_class[c : c + 1, :], axis=1, keepdims=True) for c in range(n_class)]
    peak = functools.reduce(jnp.maximum, logits)
    expo = [jnp.exp(x - peak) for x in logits]
    total = sum(expo)
    probs = [x / total for x in expo]
    terms = owned * (peak + jnp.log(total) - sum(p * x for p, x in zip(probs, logits)))
    entropy = jnp.sum(terms, axis=0, keepdims=True)
    g_logits = [
        (probs[c] - (labels[...] == c).astype(f32)) * owned for c in range(n_class)
    ]
    g_pooled = sum(g_logits[c] * w_class[c : c + 1, :] for c in range(n_class))
    g_low = (g_pooled * (1.0 - pooled * pooled)).astype(bf16)
    gpool[...] = g_low
    grad_cls = dot(g_low, w_pool[...], NT)

    def second_back(b, carry):
        rows = at(b)
        here = (
            iota((seqs, ROWS), 1) + (place[0] * own + b * ROWS) == starts[...]
        ).astype(f32).astype(bf16)
        back = sum(dot(here, part, TN) for part in low3(grad_cls))
        grad_out = cot[rows, :].astype(f32) + back
        res, g_gain, g_shift = norm_back(grad_out, unit_f[rows, :], inv_f[rows, :], gain_f[...])
        low = res.astype(bf16)
        gar[rows, :] = res
        gffn[rows, :] = low
        return carry[0] + g_gain, carry[1] + g_shift, carry[2] + col_sum(low.astype(f32))

    zero = jnp.zeros((1, width), f32)
    sums_f = lax.fori_loop(0, blocks, second_back, (zero, zero, zero))
    acc[...] = jnp.zeros_like(acc)

    def backward(c, carry):
        g_b_in = jnp.zeros((1, wide), f32)
        for b in range(blocks):
            rows = slice(b * ROWS, (b + 1) * ROWS)
            grad_act = dot(gffn[rows, :], w_back[cols(c), :], NT)
            low = (grad_act * slope[c, rows, :]).astype(bf16)
            gpre[c, rows, :] = low
            g_b_in += col_sum(low.astype(f32))
            acc[rows, :] += dot(low, w_in[:, cols(c)], NT)
        vec[pl.ds(8 + c, 1), :] = g_b_in
        pltpu.make_async_copy(gpre.at[c], gpre_hbm.at[c], sems.at[3 + chunks + c]).start()
        return carry

    lax.fori_loop(0, chunks, backward, 0)

    heads = width // HEAD_DIM
    lane = iota((1, SIDE), 1)
    gap = LSE0 + 3 * heads
    feature, flane = iota((width, SIDE), 0), iota((width, SIDE), 1)
    third = flane - gap - 3 * (feature // HEAD_DIM)
    head_sum = ((third >= 0) & (third < 3)).astype(f32).astype(bf16)
    lrow, llane = iota((lse.shape[0], SIDE), 0), iota((lse.shape[0], SIDE), 1)
    lhead = (lrow // 8) * heads_part + lrow % 8
    spread = [
        ((llane == LSE0 + 3 * lhead + p) & (lrow % 8 < heads_part)).astype(f32).astype(bf16)
        for p in range(3)
    ]
    which = lax.rem(lane - gap + 3 * heads, 3)

    def first_back(b, carry):
        rows = at(b)
        grad_mid = gar[rows, :] + acc[rows, :]
        res, g_gain, g_shift = norm_back(grad_mid, unit_a[rows, :], inv_a[rows, :], gain_a[...])
        low = res.astype(bf16)
        gar[rows, :] = res
        gattn[rows, :] = low
        grad_ctx = dot(low, w_out[...], NT).astype(bf16)
        gs[rows, :width] = grad_ctx
        delta = dot3(grad_ctx.astype(f32) * ctx[rows, :].astype(f32), head_sum, NN)
        high, mid_part, rest = low3(-delta)
        side = jnp.where(which == 0, high, jnp.where(which == 1, mid_part, rest))
        lse_parts = low3(-lse[:, rows])
        side_lse = sum(dot(part, spread[p], TN) for p, part in enumerate(lse_parts))
        gs[rows, width:] = side + side_lse.astype(bf16)
        return carry[0] + g_gain, carry[1] + g_shift, carry[2] + col_sum(low.astype(f32))

    sums_a = lax.fori_loop(0, blocks, first_back, (zero, zero, zero))
    for row, value in enumerate((sums_a[2], sums_a[0], sums_a[1], sums_f[2], sums_f[0], sums_f[1])):
        vec[row : row + 1, :] = value
    vec[6:7, :] = col_sum(g_low.astype(f32))
    vec[7:8, :] = jnp.broadcast_to(entropy, (1, width))
    for c in range(n_class):
        vec[8 + chunks + c : 9 + chunks + c, :] = col_sum(pooled * g_logits[c])
    done = 8 + chunks + n_class
    vec[done:, :] = jnp.zeros((VECTORS - done, width), f32)
    for c in range(chunks):
        pltpu.make_async_copy(act.at[c], act_hbm.at[c], sems.at[3 + c]).wait()
        pltpu.make_async_copy(gpre.at[c], gpre_hbm.at[c], sems.at[3 + chunks + c]).wait()


def middle_layer(heads_part, place, w_in, w_back, w_pool, tok, ctx, lse, cot, w_out, rest, starts, labels):
    own, width = tok.shape
    ff = w_in.shape[1]
    chunks = ff // width
    seqs = starts.shape[0]
    vmem = pl.BlockSpec(memory_space=pltpu.VMEM)
    hbm = pl.BlockSpec(memory_space=pl.ANY)
    shape = jax.ShapeDtypeStruct
    flops = 2 * own * width * (6 * width + 4 * ff)
    return pl.pallas_call(
        functools.partial(middle_kernel, heads_part),
        in_specs=[pl.BlockSpec(memory_space=pltpu.SMEM), hbm, hbm, hbm] + [vmem] * (5 + len(rest) + 2),
        out_specs=[vmem, vmem, vmem, hbm, hbm] + [vmem] * 6,
        out_shape=[
            shape((own, width), bf16),
            shape((own, width), f32),
            shape((own, width + SIDE), bf16),
            shape((chunks, own, width), bf16),
            shape((chunks, own, width), bf16),
            shape((own, width), bf16),
            shape((own, width), bf16),
            shape((own, width), bf16),
            shape((seqs, width), bf16),
            shape((seqs, width), bf16),
            shape((VECTORS, width), f32),
        ],
        scratch_shapes=[
            pltpu.VMEM(w_in.shape, bf16),
            pltpu.VMEM(w_back.shape, bf16),
            pltpu.VMEM(w_pool.shape, bf16),
            pltpu.VMEM((chunks, own, width), bf16),
            pltpu.VMEM((chunks, own, width), bf16),
            pltpu.VMEM((chunks, own, width), f32),
            pltpu.VMEM((own, width), f32),
            pltpu.VMEM((own, width), f32),
            pltpu.VMEM((own, 1), f32),
            pltpu.VMEM((own, 1), f32),
            pltpu.VMEM((own, width), f32),
            pltpu.SemaphoreType.DMA((3 + 2 * chunks,)),
        ],
        compiler_params=pltpu.CompilerParams(vmem_limit_bytes=62 * 2**20),
        cost_estimate=pl.CostEstimate(flops=flops, bytes_accessed=30 * 2**20, transcendentals=0),
        name="middle_layer",
    )(place, w_in, w_back, w_pool, tok, ctx, lse, cot, w_out, *rest, starts, labels)


def split_core(tile, core, half, keep, send, first):
    for n in range(tile.shape[0] // (2 * half)):
        even = tile[2 * n * half : (2 * n + 1) * half, :]
        odd = tile[(2 * n + 1) * half : (2 * n + 2) * half, :]
        keep[first + n, :, :] = jnp.where(core == 0, even, odd).astype(bf16)
        send[first + n, :, :] = jnp.where(core == 0, odd, even).astype(bf16)


def weight_grads_kernel(
    core, act, gpre, gffn, mid, ctx, gattn, cls, gpool,
    back_keep, back_send, in_keep, in_send, out_keep, out_send, mid_t,
):
    y = pl.program_id(0)

    @pl.when(y == 0)
    def _():
        mid_t[...] = mid[...].T
        split_core(dot(ctx[...], gattn[...], TN), core[0], out_keep.shape[1], out_keep, out_send, 0)

    @pl.when(y == 1)
    def _():
        split_core(dot(cls[...], gpool[...], TN), core[0], out_keep.shape[1], out_keep, out_send, 0)

    split_core(dot(act[0], gffn[...], TN), core[0], back_keep.shape[1], back_keep, back_send, 0)
    split_core(dot(mid_t[...], gpre[0], NN), core[0], in_keep.shape[1], in_keep, in_send, 0)


def weight_grads(core, n_seq, act, gpre, gffn, mid, ctx, gattn, cls, gpool):
    chunks, own, width = act.shape
    groups = n_seq // 2
    half_b, half_w = chunks * width // n_seq, width // n_seq
    shape = jax.ShapeDtypeStruct
    whole = lambda a: pl.BlockSpec(a.shape, lambda y, c: (0, 0))
    tile = pl.BlockSpec((1, own, width), lambda y, c: (y, 0, 0))
    back = pl.BlockSpec((groups // chunks, half_b, width), lambda y, c: (y, 0, 0))
    inner = pl.BlockSpec((groups, half_w, width), lambda y, c: (0, 0, y))
    outer = pl.BlockSpec((groups, half_w, width), lambda y, c: (0, 0, jnp.minimum(y, 1)))
    return pl.pallas_call(
        weight_grads_kernel,
        grid_spec=pltpu.PrefetchScalarGridSpec(
            num_scalar_prefetch=1,
            grid=(chunks,),
            in_specs=[tile, tile] + [whole(a) for a in (gffn, mid, ctx, gattn, cls, gpool)],
            out_specs=[back, back, inner, inner, outer, outer],
            scratch_shapes=[pltpu.VMEM((width, own), bf16)],
        ),
        out_shape=[shape((groups, half_b, width), bf16)] * 2
        + [shape((groups, half_w, chunks * width), bf16)] * 2
        + [shape((groups, half_w, 2 * width), bf16)] * 2,
        compiler_params=pltpu.CompilerParams(vmem_limit_bytes=48 * 2**20),
        cost_estimate=pl.CostEstimate(
            flops=2 * own * width * width * (2 * chunks + 1), bytes_accessed=30 * 2**20, transcendentals=0
        ),
        name="weight_grads",
    )(core, act, gpre, gffn, mid, ctx, gattn, cls, gpool)


def last_kernel(n_parts, core, *refs):
    tok, gar, w_qkv = refs[:3]
    parts = refs[3 : 3 + n_parts]
    gtok, vec = refs[3 + n_parts : 5 + n_parts]
    pairs = refs[5 + n_parts : 11 + n_parts]
    tok_t = refs[11 + n_parts]
    c = pl.program_id(0)

    @pl.when(c == 0)
    def _():
        tok_t[...] = tok[...].T
        gtok[...] = gar[...]
        vec[...] = jnp.zeros_like(vec)

    grads = jnp.concatenate([p[0] for p in parts], axis=1)
    gtok[...] += dot(grads, w_qkv[...], NT)
    vec[pl.ds(c, 1), :] = col_sum(grads.astype(f32))
    tile = dot(tok_t[...], grads, NN)
    for n in range(3):

        @pl.when(c == n)
        def _():
            keep, send = pairs[2 * n], pairs[2 * n + 1]
            split_core(tile, core[0], keep.shape[1], keep, send, 0)


def last_layer(core, n_seq, tok, gar, w_qkv, parts):
    own, width = tok.shape
    groups, half = n_seq // 2, width // n_seq
    shape = jax.ShapeDtypeStruct
    whole = lambda a: pl.BlockSpec(a.shape, lambda c, k: (0,) * len(a.shape))
    pair = pl.BlockSpec((groups, half, width), lambda c, k: (0, 0, 0))
    return pl.pallas_call(
        functools.partial(last_kernel, len(parts)),
        grid_spec=pltpu.PrefetchScalarGridSpec(
            num_scalar_prefetch=1,
            grid=(3,),
            in_specs=[whole(tok), whole(gar), pl.BlockSpec((width, width), lambda c, k: (0, c))]
            + [pl.BlockSpec((1,) + p.shape[1:], lambda c, k: (c, 0, 0)) for p in parts],
            out_specs=[whole(gar), pl.BlockSpec((8, width), lambda c, k: (0, 0))] + [pair] * 6,
            scratch_shapes=[pltpu.VMEM((width, own), bf16)],
        ),
        out_shape=[shape((own, width), f32), shape((8, width), f32)]
        + [shape((groups, half, width), bf16)] * 6,
        compiler_params=pltpu.CompilerParams(vmem_limit_bytes=40 * 2**20),
        cost_estimate=pl.CostEstimate(
            flops=12 * own * width * width, bytes_accessed=12 * 2**20, transcendentals=0
        ),
        name="last_layer",
    )(core, tok, gar, w_qkv, *parts)


MESH = pl.DeviceIdType.MESH
OTHER_CORE, NEAR = 1, (2, 4, 6)


class Sends:
    def __init__(self, send_sems, recv_sems):
        self.sems, self.copies, self.at = (send_sems, recv_sems), {}, 0

    def plan(self, name, src, dst, **device):
        self.copies[name] = pltpu.make_async_remote_copy(
            src_ref=src,
            dst_ref=dst,
            send_sem=self.sems[0].at[self.at],
            recv_sem=self.sems[1].at[self.at],
            device_id=device,
            device_id_type=MESH,
        )
        self.at += 1

    def start(self, *names):
        for name in names:
            self.copies[name].start()

    def arrived(self, *names):
        for name in names:
            self.copies[name].wait_recv()

    def drain(self):
        for copy in self.copies.values():
            copy.wait_send()


def greet(devices):
    barrier = pltpu.get_barrier_semaphore()
    for device in devices:
        pl.semaphore_signal(barrier, inc=1, device_id=device, device_id_type=MESH)
    pl.semaphore_wait(barrier, len(devices))


def halves(tile, core, half):
    even = [tile[2 * n * half : (2 * n + 1) * half] for n in range(tile.shape[0] // (2 * half))]
    odd = [tile[(2 * n + 1) * half : (2 * n + 2) * half] for n in range(tile.shape[0] // (2 * half))]
    keep = [jnp.where(core == 0, e, o).astype(bf16) for e, o in zip(even, odd)]
    send = [jnp.where(core == 0, o, e).astype(bf16) for e, o in zip(even, odd)]
    return keep, send


def grads_kernel(
    act_hbm, gpre_hbm, gs, gffn, mid, ctx, gattn, cls, gpool,
    gsw, *refs,
):
    outs, refs = refs[:12], refs[12:]
    (act, gpre, mid_t, keep_a, send_a, got_a, keep_b, send_b, got_b, keep_c, send_c, got_c,
     loads, send_sems, recv_sems, halo_sems) = refs
    seq, head = lax.axis_index("seq"), lax.axis_index("head")
    n_head = lax.axis_size("head")
    core = lax.rem(seq, 2)
    chunks, own, width = act.shape
    half_b, half_w = keep_a.shape[1], keep_b.shape[2]
    for c in range(chunks):
        pltpu.make_async_copy(act_hbm.at[c], act.at[c], loads.at[c]).start()
        pltpu.make_async_copy(gpre_hbm.at[c], gpre.at[c], loads.at[chunks + c]).start()

    barrier = pltpu.get_barrier_semaphore()
    pl.semaphore_signal(barrier, inc=1, device_id={"seq": seq ^ OTHER_CORE}, device_id_type=MESH)

    @pl.when(head > 0)
    def _():
        pl.semaphore_signal(barrier, inc=1, device_id={"head": head - 1}, device_id_type=MESH)

    @pl.when(head < n_head - 1)
    def _():
        pl.semaphore_signal(barrier, inc=1, device_id={"head": head + 1}, device_id_type=MESH)

    pl.semaphore_wait(barrier, 1 + (head > 0).astype(jnp.int32) + (head < n_head - 1).astype(jnp.int32))

    up = pltpu.make_async_remote_copy(
        src_ref=gs.at[pl.ds(own - MAXLEN, MAXLEN)], dst_ref=gsw.at[pl.ds(0, MAXLEN)],
        send_sem=halo_sems.at[0], recv_sem=halo_sems.at[1],
        device_id={"head": lax.rem(head + 1, n_head)}, device_id_type=MESH,
    )
    down = pltpu.make_async_remote_copy(
        src_ref=gs.at[pl.ds(0, MAXLEN)], dst_ref=gsw.at[pl.ds(own + MAXLEN, MAXLEN)],
        send_sem=halo_sems.at[2], recv_sem=halo_sems.at[3],
        device_id={"head": lax.rem(head + n_head - 1, n_head)}, device_id_type=MESH,
    )
    stay = pltpu.make_async_copy(gs, gsw.at[pl.ds(MAXLEN, own)], halo_sems.at[4])

    @pl.when(head < n_head - 1)
    def _():
        up.start()

    @pl.when(head > 0)
    def _():
        down.start()

    stay.start()

    sends = Sends(send_sems, recv_sems)
    partner = {"seq": seq ^ OTHER_CORE}
    for c in range(chunks):
        sends.plan(("a", c), send_a.at[c], got_a.at[c], **partner)
        sends.plan(("b", c), send_b.at[c], got_b.at[c], **partner)
    for n in range(2):
        sends.plan(("c", n), send_c.at[n], got_c.at[n], **partner)

    def put(tile, half, keep, send):
        mine, theirs = halves(tile, core, half)
        for g in range(len(mine)):
            keep[g] = mine[g]
            send[g] = theirs[g]

    mid_t[...] = mid[...].T
    put(dot(ctx[...], gattn[...], TN), half_w, keep_c.at[0], send_c.at[0])
    put(dot(cls[...], gpool[...], TN), half_w, keep_c.at[1], send_c.at[1])
    waiting = [("c", 0), ("c", 1)]
    for c in range(chunks):
        pltpu.make_async_copy(act_hbm.at[c], act.at[c], loads.at[c]).wait()
        mine, theirs = halves(dot(act[c], gffn[...], TN), core, half_b)
        keep_a[c], send_a[c] = mine[0], theirs[0]
        sends.start(*waiting)
        pltpu.make_async_copy(gpre_hbm.at[c], gpre.at[c], loads.at[chunks + c]).wait()
        put(dot(mid_t[...], gpre[c], NN), half_w, keep_b.at[c], send_b.at[c])
        sends.start(("a", c))
        waiting = [("b", c)]

    place = seq // 2
    quarter = half_w // 4
    sends.arrived(("c", 0), ("c", 1))
    for n in range(2):
        cols = pl.ds(n * width, width)
        total = [keep_c[n, g].astype(f32) + got_c[n, g].astype(f32) for g in range(4)]
        for r in range(4):
            for g in range(4):
                rows = [total[g][h * quarter : (h + 1) * quarter] for h in range(4)]
                value = rows[r]
                for h in range(4):
                    if h != r:
                        value = jnp.where((head ^ r) == h, rows[h], value)
                value = jnp.where((head ^ r) == r, rows[r], value)
                outs[8 + r][g, :, cols] = value.astype(outs[8 + r].dtype)
    sends.start(*waiting)
    for c in range(chunks):
        sends.arrived(("a", c))
    for r in (1, 2, 3, 0):
        g = place ^ r
        total = keep_a[g].astype(f32) + got_a[g].astype(f32)
        outs[r][...] = total.astype(outs[r].dtype)
    for c in range(chunks):
        sends.arrived(("b", c))
        for r in (1, 2, 3, 0):
            g = place ^ r
            total = keep_b[c, g].astype(f32) + got_b[c, g].astype(f32)
            outs[4 + r][:, pl.ds(c * width, width)] = total.astype(outs[4 + r].dtype)
    sends.drain()
    stay.wait()

    @pl.when(head < n_head - 1)
    def _():
        up.wait_send()
        down.wait_recv()

    @pl.when(head > 0)
    def _():
        up.wait_recv()
        down.wait_send()


def send_grads(act, gpre, gs, gffn, mid, ctx, gattn, cls, gpool):
    chunks, own, width = act.shape
    half_b, half_w = chunks * width // 8, width // 8
    window = own + 2 * MAXLEN
    shape = jax.ShapeDtypeStruct
    vmem, hbm = pl.BlockSpec(memory_space=pltpu.VMEM), pl.BlockSpec(memory_space=pl.ANY)
    kinds = (f32, bf16, bf16, bf16)
    return pl.pallas_call(
        grads_kernel,
        in_specs=[hbm, hbm] + [vmem] * 7,
        out_specs=[hbm] + [vmem] * 12,
        out_shape=[shape((window, width + SIDE), bf16)]
        + [shape((half_b, width), k) for k in kinds]
        + [shape((half_w, chunks * width), k) for k in kinds]
        + [shape((4, half_w // 4, 2 * width), k) for k in kinds],
        scratch_shapes=[
            pltpu.VMEM((chunks, own, width), bf16),
            pltpu.VMEM((chunks, own, width), bf16),
            pltpu.VMEM((width, own), bf16),
        ]
        + [pltpu.VMEM((chunks, half_b, width), bf16)] * 3
        + [pltpu.VMEM((chunks, 4, half_w, width), bf16)] * 3
        + [pltpu.VMEM((2, 4, half_w, width), bf16)] * 3
        + [
            pltpu.SemaphoreType.DMA((2 * chunks,)),
            pltpu.SemaphoreType.DMA((2 * chunks + 2,)),
            pltpu.SemaphoreType.DMA((2 * chunks + 2,)),
            pltpu.SemaphoreType.DMA((5,)),
        ],
        compiler_params=pltpu.CompilerParams(
            vmem_limit_bytes=60 * 2**20, collective_id=0, has_side_effects=True
        ),
        cost_estimate=pl.CostEstimate(
            flops=2 * own * width * width * (2 * chunks + 1), bytes_accessed=30 * 2**20, transcendentals=0
        ),
        name="send_grads",
    )(act, gpre, gs, gffn, mid, ctx, gattn, cls, gpool)


def finish_kernel(n_parts, *refs):
    tok, gar, w_qkv, vec = refs[:4]
    parts, refs = refs[4 : 4 + n_parts], refs[4 + n_parts :]
    own_a, near_a = refs[0], refs[1:4]
    own_b, near_b = refs[4], refs[5:8]
    own_c, near_c = refs[8], refs[9:12]
    gtok, sum_a, sum_b, sum_c, sum_q, sum_v = refs[12:18]
    (tok_t, all_a, send_a, got_a, all_b, send_b, got_b, all_c, send_c, got_c,
     keep_q, send_q, got_q, own_q, send_n, got_n, all_q, send_z, got_z,
     vecs, got_v, send_sems, recv_sems) = refs[18:]
    seq, head = lax.axis_index("seq"), lax.axis_index("head")
    core, place = lax.rem(seq, 2), seq // 2
    own, width = tok.shape
    half_w = width // 8
    quarter = half_w // 4
    line = (1, 2, 3)
    greet(
        [{"seq": seq ^ OTHER_CORE}]
        + [{"seq": seq ^ near} for near in NEAR]
        + [{"head": head ^ r} for r in line]
    )
    sends = Sends(send_sems, recv_sems)
    for r in line:
        sends.plan(("a", r), send_a.at[r - 1], got_a.at[r - 1], head=head ^ r)
        sends.plan(("b", r), send_b.at[r - 1], got_b.at[r - 1], head=head ^ r)
        sends.plan(("c", r), send_c.at[r - 1], got_c.at[r - 1], seq=seq ^ NEAR[r - 1])
    for c in range(3):
        sends.plan(("core", c), send_q.at[c], got_q.at[c], seq=seq ^ OTHER_CORE)
        for r in line:
            sends.plan(("near", c, r), send_n.at[c, r - 1], got_n.at[c, r - 1], seq=seq ^ NEAR[r - 1])
            sends.plan(("line", c, r), send_z.at[c, r - 1], got_z.at[c, r - 1], head=head ^ r)
    sends.plan(("core", "v"), vecs.at[0], got_v.at[0], seq=seq ^ OTHER_CORE)
    for r in line:
        sends.plan(("near", "v", r), vecs.at[1], got_v.at[r], seq=seq ^ NEAR[r - 1])
        sends.plan(("line", "v", r), vecs.at[2], got_v.at[3 + r], head=head ^ r)

    rows_a = sum_a.shape[0]
    for h in range(4):
        rows = slice(h * rows_a, (h + 1) * rows_a)
        all_a[h] = (own_a[rows, :] + near_a[0][rows, :].astype(f32)) + (
            near_a[1][rows, :].astype(f32) + near_a[2][rows, :].astype(f32)
        )
        rows = slice(h * quarter, (h + 1) * quarter)
        all_b[h] = (own_b[rows, :] + near_b[0][rows, :].astype(f32)) + (
            near_b[1][rows, :].astype(f32) + near_b[2][rows, :].astype(f32)
        )
        all_c[h] = (own_c[h] + near_c[0][h].astype(f32)) + (
            near_c[1][h].astype(f32) + near_c[2][h].astype(f32)
        )
    for r in line:
        send_a[r - 1] = all_a[head ^ r].astype(bf16)
        send_b[r - 1] = all_b[head ^ r].astype(bf16)
        send_c[r - 1] = all_c[place ^ r].astype(bf16)
    tok_t[...] = tok[...].T

    grads = [jnp.concatenate([p[c] for p in parts], axis=1) for c in range(3)]
    vecs[0, : vec.shape[0], :] = vec[...]
    vecs[0, vec.shape[0] :, :] = jnp.concatenate(
        [col_sum(g.astype(f32)) for g in grads] + [jnp.zeros((5, width), f32)], axis=0
    )
    for c in range(3):
        mine, theirs = halves(dot(tok_t[...], grads[c], NN), core, half_w)
        for g in range(4):
            keep_q[c, g] = mine[g]
            send_q[c, g] = theirs[g]
        if c == 0:
            sends.start(*[("a", r) for r in line])
            sends.start(*[("b", r) for r in line])
            sends.start(*[("c", r) for r in line])
            sends.start(("core", "v"))
        else:
            sends.start(("core", c - 1))
    gtok[...] = gar[...] + dot(grads[0], w_qkv[:, :width], NT)
    sends.start(("core", 2))

    for c in range(3):
        sends.arrived(("core", c))
        for r in line:
            g = place ^ r
            send_n[c, r - 1] = (keep_q[c, g].astype(f32) + got_q[c, g].astype(f32)).astype(bf16)
        own_q[c] = keep_q[c, place].astype(f32) + got_q[c, place].astype(f32)
        if c == 0:
            sends.arrived(("core", "v"))
            vecs[1] = vecs[0] + got_v[0]
        else:
            sends.start(*[("near", c - 1, r) for r in line])
    gtok[...] += dot(grads[1], w_qkv[:, width : 2 * width], NT)
    sends.start(*[("near", 2, r) for r in line])
    sends.start(*[("near", "v", r) for r in line])
    gtok[...] += dot(grads[2], w_qkv[:, 2 * width :], NT)

    for c in range(3):
        sends.arrived(*[("near", c, r) for r in line])
        for h in range(4):
            rows = slice(h * quarter, (h + 1) * quarter)
            all_q[c, h] = (own_q[c, rows, :] + got_n[c, 0, rows, :].astype(f32)) + (
                got_n[c, 1, rows, :].astype(f32) + got_n[c, 2, rows, :].astype(f32)
            )
        for r in line:
            send_z[c, r - 1] = all_q[c, head ^ r].astype(bf16)
        if c == 0:
            sends.arrived(*[("c", r) for r in line])
            sum_c[...] = (all_c[place] + got_c[0].astype(f32)) + (
                got_c[1].astype(f32) + got_c[2].astype(f32)
            )
        else:
            sends.start(*[("line", c - 1, r) for r in line])
    sends.arrived(*[("near", "v", r) for r in line])
    vecs[2] = (vecs[1] + got_v[1]) + (got_v[2] + got_v[3])
    sends.arrived(*[("a", r) for r in line])
    sends.start(*[("line", 2, r) for r in line])
    sum_a[...] = (all_a[head] + got_a[0].astype(f32)) + (got_a[1].astype(f32) + got_a[2].astype(f32))
    sends.start(*[("line", "v", r) for r in line])
    sends.arrived(*[("b", r) for r in line])
    sum_b[...] = (all_b[head] + got_b[0].astype(f32)) + (got_b[1].astype(f32) + got_b[2].astype(f32))
    for c in range(3):
        sends.arrived(*[("line", c, r) for r in line])
        sum_q[:, c * width : (c + 1) * width] = (all_q[c, head] + got_z[c, 0].astype(f32)) + (
            got_z[c, 1].astype(f32) + got_z[c, 2].astype(f32)
        )
    sends.arrived(*[("line", "v", r) for r in line])
    sum_v[...] = (vecs[2] + got_v[4]) + (got_v[5] + got_v[6])
    sends.drain()


def finish(tok, gar, w_qkv, vec, parts, a, b, c):
    own, width = tok.shape
    half_w = width // 8
    quarter = half_w // 4
    rows_a, ff = a[0].shape[0] // 4, b[0].shape[1]
    n_vec = vec.shape[0] + 8
    shape = jax.ShapeDtypeStruct
    vmem = pl.BlockSpec(memory_space=pltpu.VMEM)
    n_copies = 9 + 3 * 7 + 7
    return pl.pallas_call(
        functools.partial(finish_kernel, len(parts)),
        in_specs=[vmem] * (4 + len(parts) + 12),
        out_specs=[vmem] * 6,
        out_shape=[
            shape((own, width), f32),
            shape((rows_a, width), f32),
            shape((quarter, ff), f32),
            shape((quarter, 2 * width), f32),
            shape((quarter, 3 * width), f32),
            shape((n_vec, width), f32),
        ],
        scratch_shapes=[
            pltpu.VMEM((width, own), bf16),
            pltpu.VMEM((4, rows_a, width), f32),
            pltpu.VMEM((3, rows_a, width), bf16),
            pltpu.VMEM((3, rows_a, width), bf16),
            pltpu.VMEM((4, quarter, ff), f32),
            pltpu.VMEM((3, quarter, ff), bf16),
            pltpu.VMEM((3, quarter, ff), bf16),
            pltpu.VMEM((4, quarter, 2 * width), f32),
            pltpu.VMEM((3, quarter, 2 * width), bf16),
            pltpu.VMEM((3, quarter, 2 * width), bf16),
            pltpu.VMEM((3, 4, half_w, width), bf16),
            pltpu.VMEM((3, 4, half_w, width), bf16),
            pltpu.VMEM((3, 4, half_w, width), bf16),
            pltpu.VMEM((3, half_w, width), f32),
            pltpu.VMEM((3, 3, half_w, width), bf16),
            pltpu.VMEM((3, 3, half_w, width), bf16),
            pltpu.VMEM((3, 4, quarter, width), f32),
            pltpu.VMEM((3, 3, quarter, width), bf16),
            pltpu.VMEM((3, 3, quarter, width), bf16),
            pltpu.VMEM((3, n_vec, width), f32),
            pltpu.VMEM((7, n_vec, width), f32),
            pltpu.SemaphoreType.DMA((n_copies,)),
            pltpu.SemaphoreType.DMA((n_copies,)),
        ],
        compiler_params=pltpu.CompilerParams(
            vmem_limit_bytes=56 * 2**20, collective_id=1, has_side_effects=True
        ),
        cost_estimate=pl.CostEstimate(
            flops=12 * own * width * width, bytes_accessed=12 * 2**20, transcendentals=0
        ),
        name="finish",
    )(tok, gar, w_qkv, vec, *parts, *a, *b, *c)


def halo(rows, left_axis, n_head):
    up = [(i, i + 1) for i in range(n_head - 1)]
    down = [(i + 1, i) for i in range(n_head - 1)]
    from_left = lax.ppermute(rows[-MAXLEN:], left_axis, up)
    from_right = lax.ppermute(rows[:MAXLEN], left_axis, down)
    return jnp.concatenate([from_left, rows, from_right], axis=0)


def pick(values, axis, index):
    return lax.dynamic_index_in_dim(values, index, axis, keepdims=False)


class Sums:
    def __init__(self, pairs, orders, n_seq, n_head, vectors):
        self.count = {"seq": n_seq, "head": n_head}
        self.bits = {"seq": n_seq.bit_length() - 1, "head": n_head.bit_length() - 1}
        self.stages = sum(self.bits.values())
        self.orders = orders
        self.vectors = vectors
        self.axes = [[n for n in range(self.stages) if n != self.bits["seq"] - 1] for _ in pairs]
        shape = lambda a: a.reshape(
            (2,) * (self.stages - 1) + (a.shape[1] // n_head,) + a.shape[2:]
        )
        self.kept = [shape(keep) for keep, _ in pairs]
        self.sent = [shape(send) for _, send in pairs]
        self.stage = 0
        self.send()

    def send(self):
        self.got = [
            self.swap(v, *self.orders[n][self.stage]) for n, v in enumerate(self.sent)
        ]
        self.vectors = self.vectors + self.swap(self.vectors, *self.orders[0][self.stage])

    def swap(self, values, name, bit):
        return lax.ppermute(values, name, [(i, i ^ (1 << bit)) for i in range(self.count[name])])

    def split(self):
        self.stage += 1
        kept, sent = [], []
        for n, (keep, got) in enumerate(zip(self.kept, self.got)):
            name, bit = self.orders[n][self.stage]
            where = (self.stages if name == "head" else self.bits["seq"]) - 1 - bit
            at = self.axes[n].index(where)
            self.axes[n].pop(at)
            mine = (lax.axis_index(name) >> bit) & 1
            half = lambda m: pick(keep, at, m).astype(f32) + pick(got, at, m).astype(f32)
            sent.append(half(1 - mine).astype(bf16))
            kept.append(half(mine))
        self.kept, self.sent = kept, sent

    def rest(self):
        while self.stage < self.stages - 1:
            self.split()
            self.send()
        return [k.astype(f32) + g.astype(f32) for k, g in zip(self.kept, self.got)]


def after(value, *others):
    return lax.optimization_barrier((value, *others))[0]


def orders(n_seq, n_head):
    seq_bits, head_bits = n_seq.bit_length() - 1, n_head.bit_length() - 1
    core = [("seq", 0)]
    planar = [("seq", b) for b in range(1, seq_bits)]
    along = [("head", b) for b in range(head_bits)]
    return (
        core + planar + along,
        core + planar[::-1] + along,
        core + along + planar,
    )


def local(
    tokens, cotangent, lengths, labels, w_qkv, b_query, b_value, w_out, b_out, gain_attn,
    shift_attn, w_in, b_in, w_back, b_back, gain_ffn, shift_ffn, w_pool, b_pool, w_class,
):
    n_head = lax.axis_size("head")
    n_seq = lax.axis_size("seq")
    head_index = lax.axis_index("head")
    own, width = tokens.shape
    window = own + 2 * MAXLEN
    group = own * n_head

    seq_lengths = lengths[0]
    ends = jnp.cumsum(seq_lengths)
    starts = ends - seq_lengths
    base = head_index * own - MAXLEN
    pos = base + jnp.arange(window, dtype=jnp.int32)
    n_in_group = seq_lengths.shape[0]
    lane_pad = (0, SIDE - n_in_group)
    starts_w = jnp.pad(starts, lane_pad, constant_values=group + MAXLEN)
    ends_w = jnp.pad(ends, lane_pad, constant_values=-MAXLEN)
    inside = (starts_w[None, :] <= pos[:, None]) & (pos[:, None] < ends_w[None, :])
    hot = inside.astype(bf16)
    lane = jnp.arange(SIDE, dtype=jnp.int32)[None, :]
    mask = jnp.where(lane < n_in_group, jnp.where(inside, 0.0, -BIG), 1.0).astype(bf16)
    mask = jnp.concatenate(
        [mask, jnp.broadcast_to(jnp.where(lane < n_in_group, -BIG, 1.0).astype(bf16), (PAD, SIDE))]
    )
    blk = base + QBLK * jnp.arange(window // QBLK, dtype=jnp.int32)
    low = jnp.max(jnp.where(starts[None, :] <= blk[:, None], starts[None, :], -1), axis=1)
    high = jnp.min(
        jnp.where(ends[None, :] > blk[:, None] + QBLK - 1, ends[None, :], group), axis=1
    )
    is_own = (blk >= base + MAXLEN) & (blk < base + MAXLEN + own)
    low = jnp.where(is_own, low - base, jnp.maximum(low - base, MAXLEN))
    high = jnp.where(is_own, high - base, jnp.minimum(high - base, MAXLEN + own))
    valid = (blk >= 0) & (blk < group)
    low = low // 128 * 128
    steps = jnp.where(valid, jnp.maximum((high - low + KCHUNK - 1) // KCHUNK, 0), 0)
    bounds = jnp.stack([low, steps]).astype(jnp.int32)
    own_bounds = bounds[:, MAXLEN // QBLK : (MAXLEN + own) // QBLK]

    tokens_w = halo(tokens, "head", n_head)
    bias = jnp.concatenate([b_query, jnp.zeros_like(b_query), b_value])[None, :]
    qscale = jnp.where(jnp.arange(3 * width) < width, HEAD_DIM**-0.5, 1.0).astype(f32)[None, :]
    qkv = ((dot(tokens_w, w_qkv, NN) + bias) * qscale).astype(bf16)
    context, lse = attend(own_bounds, qkv, hot, mask, own)

    shards = n_seq * n_head
    shard = head_index + n_head * lax.axis_index("seq")
    core = (lax.axis_index("seq") & 1).reshape(1)
    row = lambda v: v.reshape(1, -1)
    seq_pad = (0, -n_in_group % 16)
    column = lambda v, fill: jnp.pad(v, seq_pad, constant_values=fill).reshape(-1, 1)
    rest = [
        row(v) for v in (b_out, gain_attn, shift_attn, b_in, b_back, gain_ffn, shift_ffn, b_pool)
    ] + [w_class.T]
    (output, gar, gs, act, gpre, gffn, mid, gattn, cls, gpool, vec) = middle_layer(
        2 * fold_of(width // PAIR, 3), head_index.reshape(1), w_in, w_back, w_pool, tokens, context, lse, cotangent, w_out,
        rest, column(starts, -1), column(labels[0], 0),
    )
    pairs = width // PAIR
    fold = fold_of(pairs, 2)
    parts = pairs // fold
    gqkv = []
    if (n_seq, n_head) == (8, 4):
        grads_w, *pieces = send_grads(act, gpre, gs, gffn, mid, context, gattn, cls, gpool)
        to = lambda v, axis, count, x: lax.ppermute(v, axis, [(i, i ^ x) for i in range(count)])
        a = [pieces[0]] + [to(pieces[r], "seq", 8, NEAR[r - 1]) for r in (1, 2, 3)]
        b = [pieces[4]] + [to(pieces[4 + r], "seq", 8, NEAR[r - 1]) for r in (1, 2, 3)]
        c = [pieces[8]] + [to(pieces[8 + r], "head", 4, r) for r in (1, 2, 3)]
        for part in range(parts):
            gqkv.append(attend_back(part, fold, bounds, qkv, grads_w, hot, mask, own))
        grad_tokens, sum_wback, sum_win, sum_c, sum_wqkv, summed = finish(
            tokens, gar, w_qkv, vec, gqkv, a, b, c
        )
        vectors, vectors_qkv = summed[: vec.shape[0]], summed[vec.shape[0] :]
        sum_wout, sum_pool = sum_c[:, :width], sum_c[:, width:]
    else:
        grads_w = halo(gs, "head", n_head)

        pieces = weight_grads(core, n_seq, act, gpre, gffn, mid, context, gattn, cls, gpool)
        orders_all = orders(n_seq, n_head)
        first = Sums(
            [pieces[0:2], pieces[2:4], pieces[4:6]], orders_all, n_seq, n_head, vec
        )
        for part in range(parts):
            gqkv.append(attend_back(part, fold, bounds, qkv, grads_w, hot, mask, own))
            bounds = after(bounds, gqkv[-1][0, :8, :128])
            if part + 1 < parts:
                first.split()
                sums = lax.optimization_barrier(tuple(first.sent) + (bounds, first.vectors))
                first.sent, bounds, first.vectors = list(sums[:3]), sums[3], sums[4]
                first.send()
        last_out = last_layer(core, n_seq, tokens, gar, w_qkv, gqkv)
        grad_tokens, vec_qkv = last_out[:2]
        last = Sums(
            [last_out[2:4], last_out[4:6], last_out[6:8]], orders_all, n_seq, n_head, vec_qkv
        )
        sum_wback, sum_win, sum_c = first.rest()
        sum_wout, sum_pool = sum_c[:, :width], sum_c[:, width:]
        sum_q, sum_k, sum_v = last.rest()
        sum_wqkv = jnp.concatenate([sum_q, sum_k, sum_v], axis=1)

        vectors, vectors_qkv = first.vectors, last.vectors
    size = width // shards
    mine = lax.dynamic_slice_in_dim(vectors, shard * size, size, 1)
    mine_qkv = lax.dynamic_slice_in_dim(vectors_qkv, shard * size, size, 1)
    chunks = w_in.shape[1] // width
    n_class = w_class.shape[1]
    grad_bin = lax.dynamic_slice_in_dim(
        vectors[8 : 8 + chunks].reshape(-1), shard * size * chunks, size * chunks, 0
    )
    grad_class = mine[8 + chunks : 8 + chunks + n_class].T
    entropy_mean = vectors[7, 0] / (n_seq * labels.shape[1])
    return (
        output, grad_tokens, sum_wqkv, mine_qkv[0], mine_qkv[2], sum_wout, mine[0], mine[1], mine[2],
        sum_win, grad_bin, sum_wback, mine[3], mine[4], mine[5], sum_pool, mine[6], grad_class,
        entropy_mean,
    )


def solution(mesh):
    rows = P(("seq", "head"), None)
    vec = P(("seq", "head"))
    return jax.shard_map(
        local,
        mesh=mesh,
        in_specs=(rows, rows, P("seq", None), P("seq", None)) + (P(),) * 16,
        out_specs=(
            rows, rows, rows, vec, vec, rows, vec, vec, vec, rows, vec, rows, vec, vec, vec, rows,
            vec, rows, P(),
        ),
        check_vma=False,
    )
```

```python
import functools

import jax
import jax.numpy as jnp
from jax import lax
from jax.experimental import pallas as pl
from jax.experimental.pallas import tpu as pltpu
from jax.sharding import PartitionSpec as P

HEAD_DIM = 64
MAXLEN = 512
PAIR = 2 * HEAD_DIM
QBLK = 128
KCHUNK = 256
PAD = KCHUNK - 128
LSE0 = 32
SIDE = 128

eps = 1e-05
BIG = 1e30
highest = lax.Precision.HIGHEST
f32 = jnp.float32
bf16 = jnp.bfloat16
NT = (((1,), (1,)), ((), ()))
NN = (((1,), (0,)), ((), ()))
TN = (((0,), (0,)), ((), ()))


def dot(left, right, dims):
    return lax.dot_general(left, right, dims, preferred_element_type=f32)


def pair_rows(rows, side):
    lane = lax.broadcasted_iota(jnp.int32, rows.shape, 1)
    zero = jnp.zeros_like(rows)
    first = jnp.where(lane < HEAD_DIM, rows, zero)
    second = jnp.where(lane >= HEAD_DIM, rows, zero)
    return jnp.concatenate(
        [jnp.concatenate([first, side[0]], axis=1), jnp.concatenate([second, side[1]], axis=1)],
        axis=0,
    )


def unpair(both):
    row = lax.broadcasted_iota(jnp.int32, (PAIR, QBLK), 0)
    return jnp.where(row < HEAD_DIM, both[:, :QBLK], both[:, QBLK:])


def attend_kernel(bounds, q_ref, k_ref, v_ref, hot_ref, mask_ref, ctx_ref, lse_ref, kcat, vt):
    window = k_ref.shape[0]
    own = ctx_ref.shape[0]
    fold = kcat.shape[0]
    skip = MAXLEN // QBLK

    @pl.when(pl.program_id(0) == 0)
    def _():
        for j in range(fold):
            kcat[j, :, PAIR:] = mask_ref[...]
            kcat[j, pl.ds(window, PAD), :PAIR] = jnp.zeros((PAD, PAIR), bf16)
            vt[j, :, pl.ds(window, PAD)] = jnp.zeros((PAIR, PAD), bf16)

    lse_ref[...] = jnp.zeros_like(lse_ref)
    for j in range(fold):
        cols = pl.ds(j * PAIR, PAIR)
        kcat[j, pl.ds(0, window), :PAIR] = k_ref[:, cols]
        for at in range(0, window, 256):
            vt[j, :, pl.ds(at, 256)] = v_ref[pl.ds(at, 256), cols].T

    def block(i, carry):
        row0 = pl.multiple_of(i * QBLK, QBLK)
        hot = hot_ref[pl.ds(MAXLEN + row0, QBLK), :]
        rows = q_ref[pl.ds(MAXLEN + row0, QBLK), :]
        qcat = [pair_rows(rows[:, j * PAIR : (j + 1) * PAIR], (hot, hot)) for j in range(fold)]
        first = bounds[skip + i, 0]

        def step(c, state):
            start = pl.multiple_of(first + c * KCHUNK, 128)
            scores = [dot(kcat[j, pl.ds(start, KCHUNK), :], qcat[j], NT) for j in range(fold)]
            out = []
            for j, s in enumerate(scores):
                peak, total, acc = state[j]
                new_peak = jnp.maximum(peak, jnp.max(s, axis=0, keepdims=True))
                scale = jnp.exp(peak - new_peak)
                p = jnp.exp(s - new_peak)
                total = total * scale + jnp.sum(p, axis=0, keepdims=True)
                acc = acc * scale + dot(vt[j, :, pl.ds(start, KCHUNK)], p.astype(bf16), NN)
                out.append((new_peak, total, acc))
            return tuple(out)

        empty = (
            jnp.full((1, 2 * QBLK), -BIG, f32),
            jnp.zeros((1, 2 * QBLK), f32),
            jnp.zeros((PAIR, 2 * QBLK), f32),
        )
        state = lax.fori_loop(0, bounds[skip + i, 1], step, (empty,) * fold)
        for j, (peak, total, acc) in enumerate(state):
            ctx_ref[pl.ds(row0, QBLK), pl.ds(j * PAIR, PAIR)] = unpair(acc / total).T.astype(bf16)
            lse = peak + jnp.log(total)
            lse_ref[2 * j : 2 * j + 1, pl.ds(row0, QBLK)] = lse[:, :QBLK]
            lse_ref[2 * j + 1 : 2 * j + 2, pl.ds(row0, QBLK)] = lse[:, QBLK:]
        return carry

    lax.fori_loop(0, own // QBLK, block, 0)


def fold_of(pairs, most):
    return max(n for n in range(1, most + 1) if pairs % n == 0)


def attend(bounds, qkv, hot, mask, own):
    window, wide = qkv.shape
    width = wide // 3
    pairs = width // PAIR
    fold = fold_of(pairs, 3)
    parts = pairs // fold
    column = lambda part: pl.BlockSpec((window, fold * PAIR), lambda g, b: (0, part * parts + g))
    whole = lambda a: pl.BlockSpec(a.shape, lambda g, b: (0, 0))
    return pl.pallas_call(
        attend_kernel,
        grid_spec=pltpu.PrefetchScalarGridSpec(
            num_scalar_prefetch=1,
            grid=(parts,),
            in_specs=[column(0), column(1), column(2), whole(hot), whole(mask)],
            out_specs=[
                pl.BlockSpec((own, fold * PAIR), lambda g, b: (0, g)),
                pl.BlockSpec((8, own), lambda g, b: (g, 0)),
            ],
            scratch_shapes=[
                pltpu.VMEM((fold, window + PAD, 2 * PAIR), bf16),
                pltpu.VMEM((fold, PAIR, window + PAD), bf16),
            ],
        ),
        out_shape=[
            jax.ShapeDtypeStruct((own, width), bf16),
            jax.ShapeDtypeStruct((8 * parts, own), f32),
        ],
        cost_estimate=pl.CostEstimate(
            flops=own * 600 * width * 4, bytes_accessed=window * wide * 2, transcendentals=0
        ),
        name="attend",
    )(bounds, qkv, qkv, qkv, hot, mask)


def attend_back_kernel(side0, more, bounds, q_ref, k_ref, v_ref, do_ref, side_ref, hot_ref, mask_ref, *refs):
    extra, refs = refs[:more], refs[more:]
    gqkv_ref, (kcat, vcat, kt, dk, dv) = refs[0], refs[-5:]
    window = k_ref.shape[0]
    own = gqkv_ref.shape[1]
    fold = kcat.shape[0]
    low0, gap = side0

    for j in range(fold):
        cols = pl.ds(j * PAIR, PAIR)
        kcat[j, :, PAIR:] = mask_ref[...]
        vcat[j, :, PAIR:] = jnp.ones((window + PAD, SIDE), bf16)
        kcat[j, pl.ds(window, PAD), :PAIR] = jnp.zeros((PAD, PAIR), bf16)
        vcat[j, pl.ds(window, PAD), :PAIR] = jnp.zeros((PAD, PAIR), bf16)
        kt[j, :, pl.ds(window, PAD)] = jnp.zeros((PAIR, PAD), bf16)
        kcat[j, pl.ds(0, window), :PAIR] = k_ref[:, cols]
        vcat[j, pl.ds(0, window), :PAIR] = v_ref[:, cols]
        for at in range(0, window, 256):
            kt[j, :, pl.ds(at, 256)] = k_ref[pl.ds(at, 256), cols].T
    dk[...] = jnp.zeros_like(dk)
    dv[...] = jnp.zeros_like(dv)
    lane = lax.broadcasted_iota(jnp.int32, (QBLK, SIDE), 1)

    def side_lanes(side, first):
        return jnp.where((lane >= first) & (lane < first + 3), side, jnp.zeros_like(side))

    def block(i, carry):
        row0 = pl.multiple_of(i * QBLK, QBLK)
        hot = hot_ref[pl.ds(row0, QBLK), :]
        side = side_ref[pl.ds(row0, QBLK), :]
        rows = q_ref[pl.ds(row0, QBLK), :]
        grads = do_ref[pl.ds(row0, QBLK), :]
        qcat, docat = [], []
        for j in range(fold):
            cols = slice(j * PAIR, (j + 1) * PAIR)
            low = low0 + 6 * j
            qcat.append(
                pair_rows(
                    rows[:, cols],
                    (hot + side_lanes(side, low), hot + side_lanes(side, low + 3)),
                )
            )
            docat.append(
                pair_rows(
                    grads[:, cols],
                    (side_lanes(side, low + gap), side_lanes(side, low + gap + 3)),
                )
            )
        first = bounds[i, 0]

        def step(c, dq):
            start = pl.multiple_of(first + c * KCHUNK, 128)
            here = pl.ds(start, KCHUNK)
            scores = [dot(kcat[j, here, :], qcat[j], NT) for j in range(fold)]
            slopes = [dot(vcat[j, here, :], docat[j], NT) for j in range(fold)]
            out = []
            for j in range(fold):
                p = jnp.exp(scores[j])
                ds = (p * slopes[j]).astype(bf16)
                dv[j, here, :] += dot(p.astype(bf16), docat[j][:, :PAIR], NN)
                dk[j, here, :] += dot(ds, qcat[j][:, :PAIR], NN)
                out.append(dq[j] + dot(kt[j, :, here], ds, NN))
            return tuple(out)

        dq = lax.fori_loop(
            0, bounds[i, 1], step, (jnp.zeros((PAIR, 2 * QBLK), f32),) * fold
        )

        @pl.when((i >= MAXLEN // QBLK) & (i < (MAXLEN + own) // QBLK))
        def _():
            for j in range(fold):
                gqkv_ref[
                    0, pl.ds(pl.multiple_of(row0 - MAXLEN, QBLK), QBLK), pl.ds(j * PAIR, PAIR)
                ] = (unpair(dq[j]) * HEAD_DIM**-0.5).T.astype(bf16)

        return carry

    lax.fori_loop(0, window // QBLK, block, 0)
    for j in range(fold):
        cols = pl.ds(j * PAIR, PAIR)
        gqkv_ref[1, :, cols] = dk[j, pl.ds(MAXLEN, own), :].astype(bf16)
        gqkv_ref[2, :, cols] = dv[j, pl.ds(MAXLEN, own), :].astype(bf16)

    if more:
        tok_t, place = extra[:2]
        keep, send, sums = refs[1:4]
        sums[...] = jnp.zeros_like(sums)

        def third(n, carry):
            grads = gqkv_ref[n]
            sums[pl.ds(n, 1), :] = col_sum(grads.astype(f32))
            mine, theirs = halves(dot(tok_t[...], grads, NN), place[0], keep.shape[2])
            for g in range(len(mine)):
                keep[n, g] = mine[g]
                send[n, g] = theirs[g]
            return carry

        lax.fori_loop(0, 3, third, 0)


def attend_back(part, fold, bounds, qkv, grads, hot, mask, own, extra=()):
    window, wide = qkv.shape
    width = wide // 3
    pairs = width // PAIR
    parts = pairs // fold
    column = lambda c: pl.BlockSpec((window, fold * PAIR), lambda g, b: (0, c * parts + part))
    whole = lambda a: pl.BlockSpec(a.shape, lambda g, b: (0, 0))
    side0 = (LSE0 + 6 * fold * part, 6 * pairs)
    shape = jax.ShapeDtypeStruct
    cols = fold * PAIR
    more_in, more_out = [], []
    if extra:
        more_in = [whole(extra[0]), pl.BlockSpec(memory_space=pltpu.SMEM)]
        more_out = [shape((3, 4, width // 8, cols), bf16)] * 2 + [shape((8, cols), f32)]
    block = lambda a: pl.BlockSpec(a.shape, lambda g, b: (0,) * len(a.shape))
    outs = [shape((3, own, cols), bf16)] + more_out
    results = pl.pallas_call(
        functools.partial(attend_back_kernel, side0, len(extra)),
        grid_spec=pltpu.PrefetchScalarGridSpec(
            num_scalar_prefetch=1,
            grid=(1,),
            in_specs=[
                column(0),
                column(1),
                column(2),
                pl.BlockSpec((window, fold * PAIR), lambda g, b: (0, part)),
                pl.BlockSpec((window, SIDE), lambda g, b: (0, pairs)),
                whole(hot),
                whole(mask),
            ]
            + more_in,
            out_specs=[block(o) for o in outs],
            scratch_shapes=[
                pltpu.VMEM((fold, window + PAD, 2 * PAIR), bf16),
                pltpu.VMEM((fold, window + PAD, 2 * PAIR), bf16),
                pltpu.VMEM((fold, PAIR, window + PAD), bf16),
                pltpu.VMEM((fold, window + PAD, PAIR), f32),
                pltpu.VMEM((fold, window + PAD, PAIR), f32),
            ],
        ),
        out_shape=outs,
        cost_estimate=pl.CostEstimate(
            flops=own * 900 * PAIR * fold * 16,
            bytes_accessed=window * PAIR * fold * 8,
            transcendentals=0,
        ),
        name=f"attend_back{part}",
    )(bounds, qkv, qkv, qkv, grads, grads, hot, mask, *extra)
    return results if extra else results[0]


def low3(values):
    high = values.astype(bf16)
    rest = values - high.astype(f32)
    mid = rest.astype(bf16)
    return high, mid, (rest - mid.astype(f32)).astype(bf16)


def dot3(values, chosen, dims):
    return sum(dot(part, chosen, dims) for part in low3(values))


def iota(shape, axis):
    return lax.broadcasted_iota(jnp.int32, shape, axis)


def mean_row(values):
    return jnp.mean(values, axis=-1, keepdims=True)


def col_sum(values):
    return jnp.sum(values, axis=0, keepdims=True)


def norm_back(grad_out, normed, inv_std, gain_vec):
    grad_norm = grad_out * gain_vec
    inner = grad_norm - mean_row(grad_norm) - normed * mean_row(grad_norm * normed)
    return inv_std * inner, col_sum(grad_out * normed), col_sum(grad_out)


ROWS = 256
VECTORS = 24


def middle_kernel(
    heads_part, place, w_in_hbm, w_back_hbm, w_pool_hbm, tok, ctx, lse, cot, w_out, b_in, w_class, small, seqs_of,
    out, gar, gs, act_hbm, gpre_hbm, gffn, mid, gattn, cls, gpool, vec,
    w_in, w_back, w_pool, act, gpre, slope, unit_a, unit_f, inv_a, inv_f, acc, sems,
):
    own, width = tok.shape
    b_out, gain_a, shift_a, b_back, gain_f, shift_f, b_pool = (small[n : n + 1, :] for n in range(7))
    starts, labels = seqs_of[:, 0:1], seqs_of[:, 1:2]
    chunks, _, wide = act.shape
    blocks = own // ROWS
    n_class = w_class.shape[0]
    loads = [
        pltpu.make_async_copy(w_in_hbm, w_in, sems.at[0]),
        pltpu.make_async_copy(w_back_hbm, w_back, sems.at[1]),
        pltpu.make_async_copy(w_pool_hbm, w_pool, sems.at[2]),
    ]
    for load in loads:
        load.start()

    def at(b):
        return pl.ds(pl.multiple_of(b * ROWS, ROWS), ROWS)

    def cols(c):
        return pl.ds(pl.multiple_of(c * wide, wide), wide)

    def norm(hidden, rows, unit, inv, gain, shift):
        centred = hidden - mean_row(hidden)
        inv_std = lax.rsqrt(mean_row(centred * centred) + eps)
        normed = centred * inv_std
        unit[rows, :] = normed
        inv[rows, :] = inv_std
        return (normed * gain[...] + shift[...]).astype(bf16)

    def first_norm(b, carry):
        rows = at(b)
        hidden = tok[rows, :].astype(f32) + dot(ctx[rows, :], w_out[...], NN) + b_out[...]
        mid[rows, :] = norm(hidden, rows, unit_a, inv_a, gain_a, shift_a)
        return carry

    lax.fori_loop(0, blocks, first_norm, 0)
    loads[0].wait()
    loads[1].wait()
    acc[...] = jnp.zeros_like(acc)

    def forward(c, carry):
        for b in range(blocks):
            rows = slice(b * ROWS, (b + 1) * ROWS)
            pre = dot(mid[rows, :], w_in[:, cols(c)], NN) + b_in[:, cols(c)]
            cdf = 0.5 * (1.0 + lax.erf(pre * (0.5**0.5)))
            low = (pre * cdf).astype(bf16)
            act[c, rows, :] = low
            slope[c, rows, :] = cdf + pre * (jnp.exp(-0.5 * pre * pre) * 0.3989422804014327)
            acc[rows, :] += dot(low, w_back[cols(c), :], NN)
        pltpu.make_async_copy(act.at[c], act_hbm.at[c], sems.at[3 + c]).start()
        return carry

    lax.fori_loop(0, chunks, forward, 0)

    def second_norm(b, carry):
        rows = at(b)
        hidden = mid[rows, :].astype(f32) + (acc[rows, :] + b_back[...])
        out[rows, :] = norm(hidden, rows, unit_f, inv_f, gain_f, shift_f)
        return carry

    lax.fori_loop(0, blocks, second_norm, 0)

    loads[2].wait()
    seqs = starts.shape[0]
    picked = (iota((seqs, own), 1) + place[0] * own == starts[...]).astype(f32)
    sel = picked.astype(bf16)
    owned = jnp.sum(picked, axis=1, keepdims=True)
    cls_low = dot(sel, out[...], NN).astype(bf16)
    cls[...] = cls_low
    pooled = jnp.tanh(dot(cls_low, w_pool[...], NN) + b_pool[...])
    logits = [jnp.sum(pooled * w_class[c : c + 1, :], axis=1, keepdims=True) for c in range(n_class)]
    peak = functools.reduce(jnp.maximum, logits)
    expo = [jnp.exp(x - peak) for x in logits]
    total = sum(expo)
    probs = [x / total for x in expo]
    terms = owned * (peak + jnp.log(total) - sum(p * x for p, x in zip(probs, logits)))
    entropy = jnp.sum(terms, axis=0, keepdims=True)
    g_logits = [
        (probs[c] - (labels[...] == c).astype(f32)) * owned for c in range(n_class)
    ]
    g_pooled = sum(g_logits[c] * w_class[c : c + 1, :] for c in range(n_class))
    g_low = (g_pooled * (1.0 - pooled * pooled)).astype(bf16)
    gpool[...] = g_low
    grad_cls = dot(g_low, w_pool[...], NT)

    def second_back(b, carry):
        rows = at(b)
        here = (
            iota((seqs, ROWS), 1) + (place[0] * own + b * ROWS) == starts[...]
        ).astype(f32).astype(bf16)
        back = sum(dot(here, part, TN) for part in low3(grad_cls))
        grad_out = cot[rows, :].astype(f32) + back
        res, g_gain, g_shift = norm_back(grad_out, unit_f[rows, :], inv_f[rows, :], gain_f[...])
        low = res.astype(bf16)
        gar[rows, :] = res
        gffn[rows, :] = low
        return carry[0] + g_gain, carry[1] + g_shift, carry[2] + col_sum(low.astype(f32))

    zero = jnp.zeros((1, width), f32)
    sums_f = lax.fori_loop(0, blocks, second_back, (zero, zero, zero))
    acc[...] = jnp.zeros_like(acc)

    def backward(c, carry):
        g_b_in = jnp.zeros((1, wide), f32)
        for b in range(blocks):
            rows = slice(b * ROWS, (b + 1) * ROWS)
            grad_act = dot(gffn[rows, :], w_back[cols(c), :], NT)
            low = (grad_act * slope[c, rows, :]).astype(bf16)
            gpre[c, rows, :] = low
            g_b_in += col_sum(low.astype(f32))
            acc[rows, :] += dot(low, w_in[:, cols(c)], NT)
        vec[pl.ds(8 + c, 1), :] = g_b_in
        pltpu.make_async_copy(gpre.at[c], gpre_hbm.at[c], sems.at[3 + chunks + c]).start()
        return carry

    lax.fori_loop(0, chunks, backward, 0)

    heads = width // HEAD_DIM
    lane = iota((1, SIDE), 1)
    gap = LSE0 + 3 * heads
    feature, flane = iota((width, SIDE), 0), iota((width, SIDE), 1)
    third = flane - gap - 3 * (feature // HEAD_DIM)
    head_sum = ((third >= 0) & (third < 3)).astype(f32).astype(bf16)
    lrow, llane = iota((lse.shape[0], SIDE), 0), iota((lse.shape[0], SIDE), 1)
    lhead = (lrow // 8) * heads_part + lrow % 8
    spread = [
        ((llane == LSE0 + 3 * lhead + p) & (lrow % 8 < heads_part)).astype(f32).astype(bf16)
        for p in range(3)
    ]
    which = lax.rem(lane - gap + 3 * heads, 3)

    def first_back(b, carry):
        rows = at(b)
        grad_mid = gar[rows, :] + acc[rows, :]
        res, g_gain, g_shift = norm_back(grad_mid, unit_a[rows, :], inv_a[rows, :], gain_a[...])
        low = res.astype(bf16)
        gar[rows, :] = res
        gattn[rows, :] = low
        grad_ctx = dot(low, w_out[...], NT).astype(bf16)
        gs[rows, :width] = grad_ctx
        delta = dot3(grad_ctx.astype(f32) * ctx[rows, :].astype(f32), head_sum, NN)
        high, mid_part, rest = low3(-delta)
        side = jnp.where(which == 0, high, jnp.where(which == 1, mid_part, rest))
        lse_parts = low3(-lse[:, rows])
        side_lse = sum(dot(part, spread[p], TN) for p, part in enumerate(lse_parts))
        gs[rows, width:] = side + side_lse.astype(bf16)
        return carry[0] + g_gain, carry[1] + g_shift, carry[2] + col_sum(low.astype(f32))

    sums_a = lax.fori_loop(0, blocks, first_back, (zero, zero, zero))
    for row, value in enumerate((sums_a[2], sums_a[0], sums_a[1], sums_f[2], sums_f[0], sums_f[1])):
        vec[row : row + 1, :] = value
    vec[6:7, :] = col_sum(g_low.astype(f32))
    vec[7:8, :] = jnp.broadcast_to(entropy, (1, width))
    for c in range(n_class):
        vec[8 + chunks + c : 9 + chunks + c, :] = col_sum(pooled * g_logits[c])
    done = 8 + chunks + n_class
    vec[done:, :] = jnp.zeros((VECTORS - done, width), f32)
    for c in range(chunks):
        pltpu.make_async_copy(act.at[c], act_hbm.at[c], sems.at[3 + c]).wait()
        pltpu.make_async_copy(gpre.at[c], gpre_hbm.at[c], sems.at[3 + chunks + c]).wait()


def middle_layer(heads_part, place, w_in, w_back, w_pool, tok, ctx, lse, cot, w_out, b_in, w_class, small, seqs_of):
    own, width = tok.shape
    ff = w_in.shape[1]
    chunks = ff // width
    seqs = seqs_of.shape[0]
    vmem = pl.BlockSpec(memory_space=pltpu.VMEM)
    hbm = pl.BlockSpec(memory_space=pl.ANY)
    shape = jax.ShapeDtypeStruct
    flops = 2 * own * width * (6 * width + 4 * ff)
    return pl.pallas_call(
        functools.partial(middle_kernel, heads_part),
        in_specs=[pl.BlockSpec(memory_space=pltpu.SMEM), hbm, hbm, hbm] + [vmem] * 9,
        out_specs=[vmem, vmem, vmem, hbm, hbm] + [vmem] * 6,
        out_shape=[
            shape((own, width), bf16),
            shape((own, width), f32),
            shape((own, width + SIDE), bf16),
            shape((chunks, own, width), bf16),
            shape((chunks, own, width), bf16),
            shape((own, width), bf16),
            shape((own, width), bf16),
            shape((own, width), bf16),
            shape((seqs, width), bf16),
            shape((seqs, width), bf16),
            shape((VECTORS, width), f32),
        ],
        scratch_shapes=[
            pltpu.VMEM(w_in.shape, bf16),
            pltpu.VMEM(w_back.shape, bf16),
            pltpu.VMEM(w_pool.shape, bf16),
            pltpu.VMEM((chunks, own, width), bf16),
            pltpu.VMEM((chunks, own, width), bf16),
            pltpu.VMEM((chunks, own, width), f32),
            pltpu.VMEM((own, width), f32),
            pltpu.VMEM((own, width), f32),
            pltpu.VMEM((own, 1), f32),
            pltpu.VMEM((own, 1), f32),
            pltpu.VMEM((own, width), f32),
            pltpu.SemaphoreType.DMA((3 + 2 * chunks,)),
        ],
        compiler_params=pltpu.CompilerParams(vmem_limit_bytes=62 * 2**20),
        cost_estimate=pl.CostEstimate(flops=flops, bytes_accessed=30 * 2**20, transcendentals=0),
        name="middle_layer",
    )(place, w_in, w_back, w_pool, tok, ctx, lse, cot, w_out, b_in, w_class, small, seqs_of)


def split_core(tile, core, half, keep, send, first):
    for n in range(tile.shape[0] // (2 * half)):
        even = tile[2 * n * half : (2 * n + 1) * half, :]
        odd = tile[(2 * n + 1) * half : (2 * n + 2) * half, :]
        keep[first + n, :, :] = jnp.where(core == 0, even, odd).astype(bf16)
        send[first + n, :, :] = jnp.where(core == 0, odd, even).astype(bf16)


def weight_grads_kernel(
    core, act, gpre, gffn, mid, ctx, gattn, cls, gpool,
    back_keep, back_send, in_keep, in_send, out_keep, out_send, mid_t,
):
    y = pl.program_id(0)

    @pl.when(y == 0)
    def _():
        mid_t[...] = mid[...].T
        split_core(dot(ctx[...], gattn[...], TN), core[0], out_keep.shape[1], out_keep, out_send, 0)

    @pl.when(y == 1)
    def _():
        split_core(dot(cls[...], gpool[...], TN), core[0], out_keep.shape[1], out_keep, out_send, 0)

    split_core(dot(act[0], gffn[...], TN), core[0], back_keep.shape[1], back_keep, back_send, 0)
    split_core(dot(mid_t[...], gpre[0], NN), core[0], in_keep.shape[1], in_keep, in_send, 0)


def weight_grads(core, n_seq, act, gpre, gffn, mid, ctx, gattn, cls, gpool):
    chunks, own, width = act.shape
    groups = n_seq // 2
    half_b, half_w = chunks * width // n_seq, width // n_seq
    shape = jax.ShapeDtypeStruct
    whole = lambda a: pl.BlockSpec(a.shape, lambda y, c: (0, 0))
    tile = pl.BlockSpec((1, own, width), lambda y, c: (y, 0, 0))
    back = pl.BlockSpec((groups // chunks, half_b, width), lambda y, c: (y, 0, 0))
    inner = pl.BlockSpec((groups, half_w, width), lambda y, c: (0, 0, y))
    outer = pl.BlockSpec((groups, half_w, width), lambda y, c: (0, 0, jnp.minimum(y, 1)))
    return pl.pallas_call(
        weight_grads_kernel,
        grid_spec=pltpu.PrefetchScalarGridSpec(
            num_scalar_prefetch=1,
            grid=(chunks,),
            in_specs=[tile, tile] + [whole(a) for a in (gffn, mid, ctx, gattn, cls, gpool)],
            out_specs=[back, back, inner, inner, outer, outer],
            scratch_shapes=[pltpu.VMEM((width, own), bf16)],
        ),
        out_shape=[shape((groups, half_b, width), bf16)] * 2
        + [shape((groups, half_w, chunks * width), bf16)] * 2
        + [shape((groups, half_w, 2 * width), bf16)] * 2,
        compiler_params=pltpu.CompilerParams(vmem_limit_bytes=48 * 2**20),
        cost_estimate=pl.CostEstimate(
            flops=2 * own * width * width * (2 * chunks + 1), bytes_accessed=30 * 2**20, transcendentals=0
        ),
        name="weight_grads",
    )(core, act, gpre, gffn, mid, ctx, gattn, cls, gpool)


def last_kernel(n_parts, core, *refs):
    tok, gar, w_qkv = refs[:3]
    parts = refs[3 : 3 + n_parts]
    gtok, vec = refs[3 + n_parts : 5 + n_parts]
    pairs = refs[5 + n_parts : 11 + n_parts]
    tok_t = refs[11 + n_parts]
    c = pl.program_id(0)

    @pl.when(c == 0)
    def _():
        tok_t[...] = tok[...].T
        gtok[...] = gar[...]
        vec[...] = jnp.zeros_like(vec)

    grads = jnp.concatenate([p[0] for p in parts], axis=1)
    gtok[...] += dot(grads, w_qkv[...], NT)
    vec[pl.ds(c, 1), :] = col_sum(grads.astype(f32))
    tile = dot(tok_t[...], grads, NN)
    for n in range(3):

        @pl.when(c == n)
        def _():
            keep, send = pairs[2 * n], pairs[2 * n + 1]
            split_core(tile, core[0], keep.shape[1], keep, send, 0)


def last_layer(core, n_seq, tok, gar, w_qkv, parts):
    own, width = tok.shape
    groups, half = n_seq // 2, width // n_seq
    shape = jax.ShapeDtypeStruct
    whole = lambda a: pl.BlockSpec(a.shape, lambda c, k: (0,) * len(a.shape))
    pair = pl.BlockSpec((groups, half, width), lambda c, k: (0, 0, 0))
    return pl.pallas_call(
        functools.partial(last_kernel, len(parts)),
        grid_spec=pltpu.PrefetchScalarGridSpec(
            num_scalar_prefetch=1,
            grid=(3,),
            in_specs=[whole(tok), whole(gar), pl.BlockSpec((width, width), lambda c, k: (0, c))]
            + [pl.BlockSpec((1,) + p.shape[1:], lambda c, k: (c, 0, 0)) for p in parts],
            out_specs=[whole(gar), pl.BlockSpec((8, width), lambda c, k: (0, 0))] + [pair] * 6,
            scratch_shapes=[pltpu.VMEM((width, own), bf16)],
        ),
        out_shape=[shape((own, width), f32), shape((8, width), f32)]
        + [shape((groups, half, width), bf16)] * 6,
        compiler_params=pltpu.CompilerParams(vmem_limit_bytes=40 * 2**20),
        cost_estimate=pl.CostEstimate(
            flops=12 * own * width * width, bytes_accessed=12 * 2**20, transcendentals=0
        ),
        name="last_layer",
    )(core, tok, gar, w_qkv, *parts)


MESH = pl.DeviceIdType.MESH
OTHER_CORE, NEAR = 1, (2, 4, 6)


class Sends:
    def __init__(self, send_sems, recv_sems):
        self.sems, self.copies, self.at = (send_sems, recv_sems), {}, 0

    def plan(self, name, src, dst, **device):
        self.copies[name] = pltpu.make_async_remote_copy(
            src_ref=src,
            dst_ref=dst,
            send_sem=self.sems[0].at[self.at],
            recv_sem=self.sems[1].at[self.at],
            device_id=device,
            device_id_type=MESH,
        )
        self.at += 1

    def start(self, *names):
        for name in names:
            self.copies[name].start()

    def arrived(self, *names):
        for name in names:
            self.copies[name].wait_recv()

    def drain(self):
        for copy in self.copies.values():
            copy.wait_send()


def greet(devices):
    barrier = pltpu.get_barrier_semaphore()
    for device in devices:
        pl.semaphore_signal(barrier, inc=1, device_id=device, device_id_type=MESH)
    pl.semaphore_wait(barrier, len(devices))


def halves(tile, core, half):
    even = [tile[2 * n * half : (2 * n + 1) * half] for n in range(tile.shape[0] // (2 * half))]
    odd = [tile[(2 * n + 1) * half : (2 * n + 2) * half] for n in range(tile.shape[0] // (2 * half))]
    keep = [jnp.where(core == 0, e, o).astype(bf16) for e, o in zip(even, odd)]
    send = [jnp.where(core == 0, o, e).astype(bf16) for e, o in zip(even, odd)]
    return keep, send


def front_kernel(
    tok, w_hbm, small, lens, labels, qkv_hbm, hot, mask, bounds, seqs_of,
    sides, w, work, rows_of, load_sem, out_sems, send_sems, recv_sems,
):
    head, n_head = lax.axis_index("head"), lax.axis_size("head")
    own, width = tok.shape
    window = hot.shape[0]
    load = pltpu.make_async_copy(w_hbm, w, load_sem)
    load.start()
    not_first, not_last = head > 0, head < n_head - 1
    barrier = pltpu.get_barrier_semaphore()

    @pl.when(not_first)
    def _():
        pl.semaphore_signal(barrier, inc=1, device_id={"head": head - 1}, device_id_type=MESH)

    @pl.when(not_last)
    def _():
        pl.semaphore_signal(barrier, inc=1, device_id={"head": head + 1}, device_id_type=MESH)

    pl.semaphore_wait(barrier, not_first.astype(jnp.int32) + not_last.astype(jnp.int32))
    pieces = MAXLEN // ROWS
    here = lambda n: pl.ds(n * ROWS, ROWS)
    up, down = [], []
    for n in range(pieces):
        for copies, first, side, device in (
            (up, own - MAXLEN, 0, lax.rem(head + 1, n_head)),
            (down, 0, 1, lax.rem(head + n_head - 1, n_head)),
        ):
            copies.append(
                pltpu.make_async_remote_copy(
                    src_ref=tok.at[pl.ds(first + n * ROWS, ROWS)], dst_ref=sides.at[side, here(n)],
                    send_sem=send_sems.at[side, n], recv_sem=recv_sems.at[side, n],
                    device_id={"head": device}, device_id_type=MESH,
                )
            )

    @pl.when(not_last)
    def _():
        for copy in up:
            copy.start()

    @pl.when(not_first)
    def _():
        for copy in down:
            copy.start()

    @pl.when(head == 0)
    def _():
        sides[0] = jnp.zeros((MAXLEN, width), bf16)

    @pl.when(head == n_head - 1)
    def _():
        sides[1] = jnp.zeros((MAXLEN, width), bf16)

    def stored(at, n):
        return pltpu.make_async_copy(
            work.at[pl.ds(at, ROWS)], qkv_hbm.at[pl.ds(at, ROWS)], out_sems.at[n]
        )

    def project(rows, at, n):
        into = pl.ds(at, ROWS)
        query = (dot(rows, w[:, :width], NN) + small[7:8, :]) * HEAD_DIM**-0.5
        work[into, :width] = query.astype(bf16)
        work[into, width : 2 * width] = dot(rows, w[:, width : 2 * width], NN).astype(bf16)
        value = dot(rows, w[:, 2 * width :], NN) + small[8:9, :]
        work[into, 2 * width :] = value.astype(bf16)
        stored(at, n).start()

    load.wait()

    def own_rows(n, carry):
        at = pl.multiple_of(n * ROWS, ROWS)
        project(tok[pl.ds(at, ROWS), :], pl.multiple_of(MAXLEN + at, ROWS), n)
        return carry

    lax.fori_loop(0, own // ROWS, own_rows, 0)

    n_seqs = lens.shape[1]
    rows_of[...] = jnp.zeros_like(rows_of)
    rows_of[0:1, :n_seqs] = lens[...]
    rows_of[1:2, :n_seqs] = labels[...]
    i, j = iota((SIDE, SIDE), 0), iota((SIDE, SIDE), 1)
    length, label = rows_of[0:1, :].astype(f32), rows_of[1:2, :].astype(f32)
    to_col = lambda row, chosen: jnp.sum(jnp.where(chosen, row, 0.0), axis=1, keepdims=True)
    length_col, ends_col = to_col(length, i == j), to_col(length, j <= i)
    ends = jnp.sum(jnp.where(i <= j, length_col, 0.0), axis=0, keepdims=True)
    starts = ends - length
    group = float(own * n_head)
    n_rows = seqs_of.shape[0]
    row, lane = i[:n_rows], j[:n_rows]
    first_col = jnp.where(row < n_seqs, (ends_col - length_col)[:n_rows], -1.0)
    label_col = to_col(label, i == j)[:n_rows]
    seqs_of[...] = jnp.where(lane == 0, first_col, jnp.where(lane == 1, label_col, 0.0)).astype(jnp.int32)

    base = head * own - MAXLEN
    row, lane = i[:16], j[:16]
    blk = (base + row * QBLK).astype(f32)
    taken = lane < n_seqs
    low = jnp.max(jnp.where(taken & (starts <= blk), starts, -1.0), axis=1, keepdims=True)
    high = jnp.min(
        jnp.where(taken & (ends > blk + (QBLK - 1)), ends, group), axis=1, keepdims=True
    )
    at = row * QBLK
    is_own = (at >= MAXLEN) & (at < MAXLEN + own)
    low = jnp.broadcast_to(low.astype(jnp.int32), at.shape) - base
    high = jnp.broadcast_to(high.astype(jnp.int32), at.shape) - base
    low = jnp.where(is_own, low, jnp.maximum(low, MAXLEN))
    high = jnp.where(is_own, high, jnp.minimum(high, MAXLEN + own))
    low = (low >> 7) << 7
    valid = (blk >= 0.0) & (blk < group)
    steps = jnp.where(valid, jnp.maximum((high - low + KCHUNK - 1) >> (KCHUNK.bit_length() - 1), 0), 0)
    bounds[...] = jnp.where(lane == 0, low, jnp.where(lane == 1, steps, 0))

    lane = iota((QBLK, SIDE), 1)

    def masks(n, carry):
        at = pl.multiple_of(n * QBLK, QBLK)
        pos = (iota((QBLK, SIDE), 0) + (base + at)).astype(f32)
        inside = ((starts <= pos) & (pos < ends)).astype(f32)
        hot[pl.ds(at, QBLK), :] = inside.astype(bf16)
        mask[pl.ds(at, QBLK), :] = jnp.where(lane < n_seqs, (inside - 1.0) * BIG, 1.0).astype(bf16)
        return carry

    lax.fori_loop(0, window // QBLK, masks, 0)
    mask[pl.ds(window, PAD), :] = jnp.where(iota((PAD, SIDE), 1) < n_seqs, -BIG, 1.0).astype(bf16)

    for n in range(pieces):

        @pl.when(not_first)
        def _():
            up[n].wait_recv()

        @pl.when(not_last)
        def _():
            down[n].wait_recv()

        def side_rows(side, carry):
            at = pl.multiple_of(side * (MAXLEN + own) + n * ROWS, ROWS)
            project(sides[side, here(n), :], at, own // ROWS + 2 * n + side)
            return carry

        lax.fori_loop(0, 2, side_rows, 0)

    for n in range(own // ROWS):
        stored(MAXLEN + n * ROWS, n).wait()
    for n in range(pieces):
        for side in range(2):
            stored(side * (MAXLEN + own) + n * ROWS, own // ROWS + 2 * n + side).wait()

    @pl.when(not_last)
    def _():
        for copy in up:
            copy.wait_send()

    @pl.when(not_first)
    def _():
        for copy in down:
            copy.wait_send()


def front(tok, w_qkv, small, lens, labels):
    own, width = tok.shape
    window = own + 2 * MAXLEN
    seqs = lens.shape[1] + -lens.shape[1] % 16
    pieces = MAXLEN // ROWS
    shape = jax.ShapeDtypeStruct
    vmem, hbm = pl.BlockSpec(memory_space=pltpu.VMEM), pl.BlockSpec(memory_space=pl.ANY)
    return pl.pallas_call(
        front_kernel,
        in_specs=[vmem, hbm, vmem, vmem, vmem],
        out_specs=[hbm] + [vmem] * 4,
        out_shape=[
            shape((window, 3 * width), bf16),
            shape((window, SIDE), bf16),
            shape((window + PAD, SIDE), bf16),
            shape((16, SIDE), jnp.int32),
            shape((seqs, SIDE), jnp.int32),
        ],
        scratch_shapes=[
            pltpu.VMEM((2, MAXLEN, width), bf16),
            pltpu.VMEM(w_qkv.shape, bf16),
            pltpu.VMEM((window, 3 * width), bf16),
            pltpu.VMEM((8, SIDE), jnp.int32),
            pltpu.SemaphoreType.DMA,
            pltpu.SemaphoreType.DMA((own // ROWS + 2 * pieces,)),
            pltpu.SemaphoreType.DMA((2, pieces)),
            pltpu.SemaphoreType.DMA((2, pieces)),
        ],
        compiler_params=pltpu.CompilerParams(
            vmem_limit_bytes=40 * 2**20, collective_id=2, has_side_effects=True
        ),
        cost_estimate=pl.CostEstimate(
            flops=6 * window * width * width, bytes_accessed=16 * 2**20, transcendentals=0
        ),
        name="front",
    )(tok, w_qkv, small, lens, labels)


def grads_kernel(
    act_hbm, gpre_hbm, gs, gffn, mid, ctx, gattn, cls, gpool, tok,
    gsw, tok_t, *refs,
):
    outs, refs = refs[:7], refs[7:]
    outs = (*outs[:6], outs[6].at[0], outs[6].at[1])
    (act, gpre, mid_t, keep_a, send_a, got_a, keep_b, send_b, got_b, keep_c, send_c, got_c, split,
     loads, send_sems, recv_sems, halo_sems) = refs
    seq, head = lax.axis_index("seq"), lax.axis_index("head")
    n_head = lax.axis_size("head")
    core = lax.rem(seq, 2)
    chunks, own, width = act.shape
    half_b, half_w = keep_a.shape[1], keep_b.shape[2]
    for c in range(chunks):
        pltpu.make_async_copy(act_hbm.at[c], act.at[c], loads.at[c]).start()
        pltpu.make_async_copy(gpre_hbm.at[c], gpre.at[c], loads.at[chunks + c]).start()

    barrier = pltpu.get_barrier_semaphore()
    pl.semaphore_signal(barrier, inc=1, device_id={"seq": seq ^ OTHER_CORE}, device_id_type=MESH)

    @pl.when(head > 0)
    def _():
        pl.semaphore_signal(barrier, inc=1, device_id={"head": head - 1}, device_id_type=MESH)

    @pl.when(head < n_head - 1)
    def _():
        pl.semaphore_signal(barrier, inc=1, device_id={"head": head + 1}, device_id_type=MESH)

    pl.semaphore_wait(barrier, 1 + (head > 0).astype(jnp.int32) + (head < n_head - 1).astype(jnp.int32))

    up = pltpu.make_async_remote_copy(
        src_ref=gs.at[pl.ds(own - MAXLEN, MAXLEN)], dst_ref=gsw.at[pl.ds(0, MAXLEN)],
        send_sem=halo_sems.at[0], recv_sem=halo_sems.at[1],
        device_id={"head": lax.rem(head + 1, n_head)}, device_id_type=MESH,
    )
    down = pltpu.make_async_remote_copy(
        src_ref=gs.at[pl.ds(0, MAXLEN)], dst_ref=gsw.at[pl.ds(own + MAXLEN, MAXLEN)],
        send_sem=halo_sems.at[2], recv_sem=halo_sems.at[3],
        device_id={"head": lax.rem(head + n_head - 1, n_head)}, device_id_type=MESH,
    )
    stay = pltpu.make_async_copy(gs, gsw.at[pl.ds(MAXLEN, own)], halo_sems.at[4])

    @pl.when(head < n_head - 1)
    def _():
        up.start()

    @pl.when(head > 0)
    def _():
        down.start()

    stay.start()

    def to_core(send, got, first, n):
        return pltpu.make_async_remote_copy(
            src_ref=send.at[n], dst_ref=got.at[n],
            send_sem=send_sems.at[first + n], recv_sem=recv_sems.at[first + n],
            device_id={"seq": seq ^ OTHER_CORE}, device_id_type=MESH,
        )

    copy_a = lambda n: to_core(send_a, got_a, 0, n)
    copy_b = lambda n: to_core(send_b, got_b, chunks, n)
    copy_c = lambda n: to_core(send_c, got_c, 2 * chunks, n)

    def put(tile, half, keep, send):
        mine, theirs = halves(tile, core, half)
        for g in range(len(mine)):
            keep[g] = mine[g]
            send[g] = theirs[g]

    mid_t[...] = mid[...].T
    put(dot(ctx[...], gattn[...], TN), half_w, keep_c.at[0], send_c.at[0])
    put(dot(cls[...], gpool[...], TN), half_w, keep_c.at[1], send_c.at[1])

    def chunk(c, carry):
        pltpu.make_async_copy(gpre_hbm.at[c], gpre.at[c], loads.at[chunks + c]).wait()
        put(dot(mid_t[...], gpre[c], NN), half_w, keep_b.at[c], send_b.at[c])

        @pl.when(c == 0)
        def _():
            copy_c(0).start()
            copy_c(1).start()

        @pl.when(c > 0)
        def _():
            copy_a(jnp.maximum(c - 1, 0)).start()

        pltpu.make_async_copy(act_hbm.at[c], act.at[c], loads.at[c]).wait()
        mine, theirs = halves(dot(act[c], gffn[...], TN), core, half_b)
        keep_a[c], send_a[c] = mine[0], theirs[0]
        copy_b(c).start()
        return carry

    lax.fori_loop(0, chunks, chunk, 0)

    tok_t[...] = tok[...].T

    place = seq // 2
    quarter = half_w // 4
    rows_a = half_b // 4
    turns = (1, 2, 3, 0)
    for n in range(2):
        copy_c(n).wait_recv()
        for r in turns:
            total = keep_c[n, place ^ r].astype(f32) + got_c[n, place ^ r].astype(f32)
            for h in range(4):
                outs[r][h, rows_a + n * quarter : rows_a + (n + 1) * quarter, :] = total[
                    h * quarter : (h + 1) * quarter
                ].astype(outs[r].dtype)
    copy_a(chunks - 1).start()

    def sum_b(c, carry):
        copy_b(c).wait_recv()
        for g in range(4):
            total = keep_b[c, g].astype(f32) + got_b[c, g].astype(f32)
            for h in range(4):
                split[h, g] = total[h * quarter : (h + 1) * quarter]
        cols = pl.ds(pl.multiple_of(c * width, width), width)
        for r in range(4):
            for g in range(4):
                outs[4 + r][g, :, cols] = split[head ^ r, g].astype(outs[4 + r].dtype)
        return carry

    lax.fori_loop(0, chunks, sum_b, 0)
    for c in range(chunks):
        copy_a(c).wait_recv()
    for r in turns:
        total = keep_a[place ^ r].astype(f32) + got_a[place ^ r].astype(f32)
        for h in range(4):
            outs[r][h, :rows_a, :] = total[h * rows_a : (h + 1) * rows_a].astype(outs[r].dtype)
    for c in range(chunks):
        copy_a(c).wait_send()
        copy_b(c).wait_send()
    for n in range(2):
        copy_c(n).wait_send()
    stay.wait()

    @pl.when(head < n_head - 1)
    def _():
        up.wait_send()
        down.wait_recv()

    @pl.when(head > 0)
    def _():
        up.wait_recv()
        down.wait_send()


def send_grads(act, gpre, gs, gffn, mid, ctx, gattn, cls, gpool, tok):
    chunks, own, width = act.shape
    half_b, half_w = chunks * width // 8, width // 8
    window = own + 2 * MAXLEN
    shape = jax.ShapeDtypeStruct
    vmem, hbm = pl.BlockSpec(memory_space=pltpu.VMEM), pl.BlockSpec(memory_space=pl.ANY)
    kinds = (f32, bf16, bf16, bf16)
    return pl.pallas_call(
        grads_kernel,
        in_specs=[hbm, hbm] + [vmem] * 8,
        out_specs=[hbm] + [vmem] * 8,
        out_shape=[shape((window, width + SIDE), bf16), shape((width, own), bf16)]
        + [shape((4, half_b // 4 + half_w // 2, width), k) for k in kinds]
        + [shape((4, half_w // 4, chunks * width), k) for k in kinds[:2]]
        + [shape((2, 4, half_w // 4, chunks * width), bf16)],
        scratch_shapes=[
            pltpu.VMEM((chunks, own, width), bf16),
            pltpu.VMEM((chunks, own, width), bf16),
            pltpu.VMEM((width, own), bf16),
        ]
        + [pltpu.VMEM((chunks, half_b, width), bf16)] * 3
        + [pltpu.VMEM((chunks, 4, half_w, width), bf16)] * 3
        + [pltpu.VMEM((2, 4, half_w, width), bf16)] * 3
        + [
            pltpu.VMEM((4, 4, half_w // 4, width), f32),
            pltpu.SemaphoreType.DMA((2 * chunks,)),
            pltpu.SemaphoreType.DMA((2 * chunks + 2,)),
            pltpu.SemaphoreType.DMA((2 * chunks + 2,)),
            pltpu.SemaphoreType.DMA((5,)),
        ],
        compiler_params=pltpu.CompilerParams(
            vmem_limit_bytes=60 * 2**20, collective_id=0, has_side_effects=True
        ),
        cost_estimate=pl.CostEstimate(
            flops=2 * own * width * width * (2 * chunks + 1), bytes_accessed=30 * 2**20, transcendentals=0
        ),
        name="send_grads",
    )(act, gpre, gs, gffn, mid, ctx, gattn, cls, gpool, tok)


def finish_kernel(n_parts, *refs):
    inputs, refs = refs[: 10 + 4 * n_parts], refs[10 + 4 * n_parts :]
    sends_q = inputs[9 : 9 + n_parts]
    gtok, sum_a, sum_b, sum_out, sum_pool, sum_q, sum_v = refs[:7]
    n_held = 8 + 3 * n_parts
    held, refs = refs[7 : 7 + n_held], refs[7 + n_held :]
    own_a, near_a, own_b, near_b, vec = held[0], held[1:4], held[4], (held[5], held[6].at[0]), held[7]
    keeps, vec_parts, parts = (held[8 + n * n_parts : 8 + (n + 1) * n_parts] for n in range(3))
    (w_qkv, all_a, send_a, got_a, all_b, send_b, got_b, got_f, got_q, own_q, send_n, got_n, all_q, send_z, got_z,
     vecs, got_v, loads, send_sems, recv_sems) = refs
    wanted = inputs[:8] + inputs[9 + n_parts : -1] + (inputs[8], inputs[-1])
    copies = [
        pltpu.make_async_copy(src, dst, loads.at[n])
        for n, (src, dst) in enumerate(zip(wanted, held + (w_qkv, gtok)))
    ]
    for copy in copies:
        copy.start()
    seq, head = lax.axis_index("seq"), lax.axis_index("head")
    place = seq // 2
    width = gtok.shape[1]
    quarter = width // 32
    cols = width // n_parts
    line = (1, 2, 3)
    greet(
        [{"seq": seq ^ OTHER_CORE}]
        + [{"seq": seq ^ near} for near in NEAR]
        + [{"head": head ^ r} for r in line]
    )
    sends = Sends(send_sems, recv_sems)
    for r in line:
        sends.plan(("a", r), send_a.at[r - 1], got_a.at[r - 1], head=head ^ r)
        sends.plan(("b", r), send_b.at[r - 1], got_b.at[r - 1], seq=seq ^ NEAR[r - 1])
    for p in range(n_parts):
        sends.plan(("core", p), sends_q[p], got_q.at[p], seq=seq ^ OTHER_CORE)
        for r in line:
            sends.plan(("near", p, r), send_n.at[p, r - 1], got_n.at[p, r - 1], seq=seq ^ NEAR[r - 1])
            sends.plan(("line", p, r), send_z.at[p, r - 1], got_z.at[p, r - 1], head=head ^ r)
    sends.plan(("core", "v"), vecs.at[0], got_v.at[0], seq=seq ^ OTHER_CORE)
    for r in line:
        sends.plan(("near", "v", r), vecs.at[1], got_v.at[r], seq=seq ^ NEAR[r - 1])
        sends.plan(("line", "v", r), vecs.at[2], got_v.at[3 + r], head=head ^ r)
    sends.plan("pass", inputs[6].at[1], got_f, head=head ^ 1)
    sends.start(*[("core", p) for p in range(n_parts)])
    sends.start("pass")

    for copy in copies[: 8 + 2 * n_parts]:
        copy.wait()
    rows_v = vec.shape[0]
    vecs[0, :rows_v, :] = vec[...]
    for p in range(n_parts):
        vecs[0, rows_v:, p * cols : (p + 1) * cols] = vec_parts[p][...]
    for h in range(4):
        all_a[h] = (own_a[h] + near_a[0][h].astype(f32)) + (
            near_a[1][h].astype(f32) + near_a[2][h].astype(f32)
        )
    for r in line:
        send_a[r - 1] = all_a[head ^ r].astype(bf16)
    sends.start(("core", "v"))

    def start_near(p):
        sends.start(*[("near", p, r) for r in line])

    for p in range(n_parts):
        sends.arrived(("core", p))
        for r in line:
            for n in range(3):
                send_n[p, r - 1, n] = (
                    keeps[p][n, place ^ r].astype(f32) + got_q[p, n, place ^ r].astype(f32)
                ).astype(bf16)
        for n in range(3):
            own_q[p, n] = keeps[p][n, place].astype(f32) + got_q[p, n, place].astype(f32)
        if p == 0:
            sends.start(*[("a", r) for r in line])
        else:
            start_near(p - 1)
    start_near(n_parts - 1)
    sends.arrived(("core", "v"))
    vecs[1] = vecs[0] + got_v[0]
    sends.arrived("pass")
    for g in range(4):
        all_b[g] = (own_b[g] + near_b[0][g].astype(f32)) + (
            near_b[1][g].astype(f32) + got_f[g].astype(f32)
        )
    for r in line:
        send_b[r - 1] = all_b[place ^ r].astype(bf16)
    for copy in copies[8 + 2 * n_parts :]:
        copy.wait()

    def back(n, carry):
        here = pl.ds(pl.multiple_of(n * width, width), width)
        gtok[...] += dot(jnp.concatenate([p[n] for p in parts], axis=1), w_qkv[:, here], NT)

        @pl.when(n == 0)
        def _():
            sends.start(*[("near", "v", r) for r in line])
            sends.start(*[("b", r) for r in line])

        return carry

    lax.fori_loop(0, 3, back, 0)

    for p in range(n_parts):
        sends.arrived(*[("near", p, r) for r in line])
        for h in range(4):
            rows = slice(h * quarter, (h + 1) * quarter)
            for n in range(3):
                all_q[p, h, n] = (own_q[p, n, rows, :] + got_n[p, 0, n, rows, :].astype(f32)) + (
                    got_n[p, 1, n, rows, :].astype(f32) + got_n[p, 2, n, rows, :].astype(f32)
                )
        for r in line:
            send_z[p, r - 1] = all_q[p, head ^ r].astype(bf16)
        if p > 0:
            sends.start(*[("line", p - 1, r) for r in line])
    sends.arrived(*[("near", "v", r) for r in line])
    vecs[2] = (vecs[1] + got_v[1]) + (got_v[2] + got_v[3])
    sends.start(*[("line", n_parts - 1, r) for r in line])
    sends.arrived(*[("a", r) for r in line])
    total = (all_a[head] + got_a[0].astype(f32)) + (got_a[1].astype(f32) + got_a[2].astype(f32))
    rows_a = sum_a.shape[0]
    sum_a[...] = total[:rows_a]
    sum_out[...] = total[rows_a : rows_a + quarter]
    sum_pool[...] = total[rows_a + quarter :]
    sends.start(*[("line", "v", r) for r in line])
    sends.arrived(*[("b", r) for r in line])
    sum_b[...] = (all_b[place] + got_b[0].astype(f32)) + (got_b[1].astype(f32) + got_b[2].astype(f32))
    for p in range(n_parts):
        sends.arrived(*[("line", p, r) for r in line])
        for n in range(3):
            at = n * width + p * cols
            sum_q[:, at : at + cols] = (all_q[p, head, n] + got_z[p, 0, n].astype(f32)) + (
                got_z[p, 1, n].astype(f32) + got_z[p, 2, n].astype(f32)
            )
    sends.arrived(*[("line", "v", r) for r in line])
    sum_v[...] = (vecs[2] + got_v[4]) + (got_v[5] + got_v[6])
    sends.drain()


def finish(gar, w_qkv, vec, parts, a, b):
    own, width = gar.shape
    half_w = width // 8
    quarter = half_w // 4
    n_parts = len(parts)
    cols = width // n_parts
    rows_z, ff = a[0].shape[1], b[0].shape[2]
    n_vec = vec.shape[0] + 8
    shape = jax.ShapeDtypeStruct
    vmem, hbm = pl.BlockSpec(memory_space=pltpu.VMEM), pl.BlockSpec(memory_space=pl.ANY)
    n_copies = 6 + 7 * n_parts + 7 + 1
    grads, keeps, sends, sums = ([p[n] for p in parts] for n in range(4))
    held = [*a, *b, vec, *keeps, *sums, *grads]
    return pl.pallas_call(
        functools.partial(finish_kernel, n_parts),
        in_specs=[hbm] * (10 + 4 * n_parts),
        out_specs=[vmem] * 7,
        out_shape=[
            shape((own, width), f32),
            shape((rows_z - 2 * quarter, width), f32),
            shape((quarter, ff), f32),
            shape((quarter, width), f32),
            shape((quarter, width), f32),
            shape((quarter, 3 * width), f32),
            shape((n_vec, width), f32),
        ],
        scratch_shapes=[pltpu.VMEM(h.shape, h.dtype) for h in held]
        + [
            pltpu.VMEM(w_qkv.shape, bf16),
            pltpu.VMEM((4, rows_z, width), f32),
            pltpu.VMEM((3, rows_z, width), bf16),
            pltpu.VMEM((3, rows_z, width), bf16),
            pltpu.VMEM((4, quarter, ff), f32),
            pltpu.VMEM((3, quarter, ff), bf16),
            pltpu.VMEM((3, quarter, ff), bf16),
            pltpu.VMEM((4, quarter, ff), bf16),
            pltpu.VMEM((n_parts, 3, 4, half_w, cols), bf16),
            pltpu.VMEM((n_parts, 3, half_w, cols), f32),
            pltpu.VMEM((n_parts, 3, 3, half_w, cols), bf16),
            pltpu.VMEM((n_parts, 3, 3, half_w, cols), bf16),
            pltpu.VMEM((n_parts, 4, 3, quarter, cols), f32),
            pltpu.VMEM((n_parts, 3, 3, quarter, cols), bf16),
            pltpu.VMEM((n_parts, 3, 3, quarter, cols), bf16),
            pltpu.VMEM((3, n_vec, width), f32),
            pltpu.VMEM((7, n_vec, width), f32),
            pltpu.SemaphoreType.DMA((len(held) + 2,)),
            pltpu.SemaphoreType.DMA((n_copies,)),
            pltpu.SemaphoreType.DMA((n_copies,)),
        ],
        compiler_params=pltpu.CompilerParams(
            vmem_limit_bytes=56 * 2**20, collective_id=1, has_side_effects=True
        ),
        cost_estimate=pl.CostEstimate(
            flops=12 * own * width * width, bytes_accessed=12 * 2**20, transcendentals=0
        ),
        name="finish",
    )(*a, *b, vec, w_qkv, *sends, *keeps, *sums, *grads, gar)


def halo(rows, left_axis, n_head):
    up = [(i, i + 1) for i in range(n_head - 1)]
    down = [(i + 1, i) for i in range(n_head - 1)]
    from_left = lax.ppermute(rows[-MAXLEN:], left_axis, up)
    from_right = lax.ppermute(rows[:MAXLEN], left_axis, down)
    return jnp.concatenate([from_left, rows, from_right], axis=0)


def pick(values, axis, index):
    return lax.dynamic_index_in_dim(values, index, axis, keepdims=False)


class Sums:
    def __init__(self, pairs, orders, n_seq, n_head, vectors):
        self.count = {"seq": n_seq, "head": n_head}
        self.bits = {"seq": n_seq.bit_length() - 1, "head": n_head.bit_length() - 1}
        self.stages = sum(self.bits.values())
        self.orders = orders
        self.vectors = vectors
        self.axes = [[n for n in range(self.stages) if n != self.bits["seq"] - 1] for _ in pairs]
        shape = lambda a: a.reshape(
            (2,) * (self.stages - 1) + (a.shape[1] // n_head,) + a.shape[2:]
        )
        self.kept = [shape(keep) for keep, _ in pairs]
        self.sent = [shape(send) for _, send in pairs]
        self.stage = 0
        self.send()

    def send(self):
        self.got = [
            self.swap(v, *self.orders[n][self.stage]) for n, v in enumerate(self.sent)
        ]
        self.vectors = self.vectors + self.swap(self.vectors, *self.orders[0][self.stage])

    def swap(self, values, name, bit):
        return lax.ppermute(values, name, [(i, i ^ (1 << bit)) for i in range(self.count[name])])

    def split(self):
        self.stage += 1
        kept, sent = [], []
        for n, (keep, got) in enumerate(zip(self.kept, self.got)):
            name, bit = self.orders[n][self.stage]
            where = (self.stages if name == "head" else self.bits["seq"]) - 1 - bit
            at = self.axes[n].index(where)
            self.axes[n].pop(at)
            mine = (lax.axis_index(name) >> bit) & 1
            half = lambda m: pick(keep, at, m).astype(f32) + pick(got, at, m).astype(f32)
            sent.append(half(1 - mine).astype(bf16))
            kept.append(half(mine))
        self.kept, self.sent = kept, sent

    def rest(self):
        while self.stage < self.stages - 1:
            self.split()
            self.send()
        return [k.astype(f32) + g.astype(f32) for k, g in zip(self.kept, self.got)]


def after(value, *others):
    return lax.optimization_barrier((value, *others))[0]


def orders(n_seq, n_head):
    seq_bits, head_bits = n_seq.bit_length() - 1, n_head.bit_length() - 1
    core = [("seq", 0)]
    planar = [("seq", b) for b in range(1, seq_bits)]
    along = [("head", b) for b in range(head_bits)]
    return (
        core + planar + along,
        core + planar[::-1] + along,
        core + along + planar,
    )


def local(
    tokens, cotangent, lengths, labels, w_qkv, b_query, b_value, w_out, b_out, gain_attn,
    shift_attn, w_in, b_in, w_back, b_back, gain_ffn, shift_ffn, w_pool, b_pool, w_class,
):
    n_head = lax.axis_size("head")
    n_seq = lax.axis_size("seq")
    head_index = lax.axis_index("head")
    own, width = tokens.shape
    window = own + 2 * MAXLEN
    group = own * n_head

    small = jnp.stack(
        [b_out, gain_attn, shift_attn, b_back, gain_ffn, shift_ffn, b_pool, b_query, b_value]
    )
    if (n_seq, n_head) == (8, 4):
        qkv, hot, mask, bounds, seqs_of = front(tokens, w_qkv, small, lengths, labels)
    else:
        seq_lengths = lengths[0]
        ends = jnp.cumsum(seq_lengths)
        starts = ends - seq_lengths
        base = head_index * own - MAXLEN
        pos = base + jnp.arange(window, dtype=jnp.int32)
        n_in_group = seq_lengths.shape[0]
        lane_pad = (0, SIDE - n_in_group)
        starts_w = jnp.pad(starts, lane_pad, constant_values=group + MAXLEN)
        ends_w = jnp.pad(ends, lane_pad, constant_values=-MAXLEN)
        inside = (starts_w[None, :] <= pos[:, None]) & (pos[:, None] < ends_w[None, :])
        hot = inside.astype(bf16)
        lane = jnp.arange(SIDE, dtype=jnp.int32)[None, :]
        mask = jnp.where(lane < n_in_group, jnp.where(inside, 0.0, -BIG), 1.0).astype(bf16)
        mask = jnp.concatenate(
            [mask, jnp.broadcast_to(jnp.where(lane < n_in_group, -BIG, 1.0).astype(bf16), (PAD, SIDE))]
        )
        blk = base + QBLK * jnp.arange(window // QBLK, dtype=jnp.int32)
        low = jnp.max(jnp.where(starts[None, :] <= blk[:, None], starts[None, :], -1), axis=1)
        high = jnp.min(
            jnp.where(ends[None, :] > blk[:, None] + QBLK - 1, ends[None, :], group), axis=1
        )
        is_own = (blk >= base + MAXLEN) & (blk < base + MAXLEN + own)
        low = jnp.where(is_own, low - base, jnp.maximum(low - base, MAXLEN))
        high = jnp.where(is_own, high - base, jnp.minimum(high - base, MAXLEN + own))
        valid = (blk >= 0) & (blk < group)
        low = low // 128 * 128
        steps = jnp.where(valid, jnp.maximum((high - low + KCHUNK - 1) // KCHUNK, 0), 0)
        bounds = jnp.stack([low, steps], axis=1).astype(jnp.int32)
        seq_pad = (0, -n_in_group % 16)
        seqs_of = jnp.stack(
            [jnp.pad(starts, seq_pad, constant_values=-1), jnp.pad(labels[0], seq_pad)], axis=1
        )
        tokens_w = halo(tokens, "head", n_head)
        bias = jnp.concatenate([b_query, jnp.zeros_like(b_query), b_value])[None, :]
        qscale = jnp.where(jnp.arange(3 * width) < width, HEAD_DIM**-0.5, 1.0).astype(f32)[None, :]
        qkv = ((dot(tokens_w, w_qkv, NN) + bias) * qscale).astype(bf16)
    context, lse = attend(bounds, qkv, hot, mask, own)

    shards = n_seq * n_head
    shard = head_index + n_head * lax.axis_index("seq")
    core = (lax.axis_index("seq") & 1).reshape(1)
    (output, gar, gs, act, gpre, gffn, mid, gattn, cls, gpool, vec) = middle_layer(
        2 * fold_of(width // PAIR, 3), head_index.reshape(1), w_in, w_back, w_pool, tokens, context, lse,
        cotangent, w_out, b_in.reshape(1, -1), w_class.T, small, seqs_of,
    )
    pairs = width // PAIR
    fold = fold_of(pairs, 2)
    parts = pairs // fold
    gqkv = []
    if (n_seq, n_head) == (8, 4):
        grads_w, tok_t, *pieces = send_grads(act, gpre, gs, gffn, mid, context, gattn, cls, gpool, tokens)
        to = lambda v, axis, count, x: lax.ppermute(v, axis, [(i, i ^ x) for i in range(count)])
        a = [pieces[0]] + [to(pieces[r], "seq", 8, NEAR[r - 1]) for r in (1, 2, 3)]
        b = [pieces[4], to(pieces[5], "head", 4, 1), to(pieces[6], "head", 4, 2)]
        for part in range(parts):
            gqkv.append(attend_back(part, fold, bounds, qkv, grads_w, hot, mask, own, (tok_t, core)))
        grad_tokens, sum_wback, sum_win, sum_wout, sum_pool, sum_wqkv, summed = finish(
            gar, w_qkv, vec, gqkv, a, b
        )
        vectors, vectors_qkv = summed[: vec.shape[0]], summed[vec.shape[0] :]
    else:
        grads_w = halo(gs, "head", n_head)

        pieces = weight_grads(core, n_seq, act, gpre, gffn, mid, context, gattn, cls, gpool)
        orders_all = orders(n_seq, n_head)
        first = Sums(
            [pieces[0:2], pieces[2:4], pieces[4:6]], orders_all, n_seq, n_head, vec
        )
        for part in range(parts):
            gqkv.append(attend_back(part, fold, bounds, qkv, grads_w, hot, mask, own))
            bounds = after(bounds, gqkv[-1][0, :8, :128])
            if part + 1 < parts:
                first.split()
                sums = lax.optimization_barrier(tuple(first.sent) + (bounds, first.vectors))
                first.sent, bounds, first.vectors = list(sums[:3]), sums[3], sums[4]
                first.send()
        last_out = last_layer(core, n_seq, tokens, gar, w_qkv, gqkv)
        grad_tokens, vec_qkv = last_out[:2]
        last = Sums(
            [last_out[2:4], last_out[4:6], last_out[6:8]], orders_all, n_seq, n_head, vec_qkv
        )
        sum_wback, sum_win, sum_c = first.rest()
        sum_wout, sum_pool = sum_c[:, :width], sum_c[:, width:]
        sum_q, sum_k, sum_v = last.rest()
        sum_wqkv = jnp.concatenate([sum_q, sum_k, sum_v], axis=1)

        vectors, vectors_qkv = first.vectors, last.vectors
    size = width // shards
    mine = lax.dynamic_slice_in_dim(vectors, shard * size, size, 1)
    mine_qkv = lax.dynamic_slice_in_dim(vectors_qkv, shard * size, size, 1)
    chunks = w_in.shape[1] // width
    n_class = w_class.shape[1]
    grad_bin = lax.dynamic_slice_in_dim(
        vectors[8 : 8 + chunks].reshape(-1), shard * size * chunks, size * chunks, 0
    )
    grad_class = mine[8 + chunks : 8 + chunks + n_class].T
    entropy_mean = vectors[7, 0] / (n_seq * labels.shape[1])
    return (
        output, grad_tokens, sum_wqkv, mine_qkv[0], mine_qkv[2], sum_wout, mine[0], mine[1], mine[2],
        sum_win, grad_bin, sum_wback, mine[3], mine[4], mine[5], sum_pool, mine[6], grad_class,
        entropy_mean,
    )


def solution(mesh):
    rows = P(("seq", "head"), None)
    vec = P(("seq", "head"))
    return jax.shard_map(
        local,
        mesh=mesh,
        in_specs=(rows, rows, P("seq", None), P("seq", None)) + (P(),) * 16,
        out_specs=(
            rows, rows, rows, vec, vec, rows, vec, vec, vec, rows, vec, rows, vec, vec, vec, rows,
            vec, rows, P(),
        ),
        check_vma=False,
    )
```

```python
import functools

import jax
import jax.numpy as jnp
from jax import lax
from jax.experimental import pallas as pl
from jax.experimental.pallas import tpu as pltpu
from jax.sharding import PartitionSpec as P

HEAD_DIM = 64
MAXLEN = 512
PAIR = 2 * HEAD_DIM
QBLK = 128
KCHUNK = 256
PAD = KCHUNK - 128
LSE0 = 32
SIDE = 128

eps = 1e-05
BIG = 1e30
highest = lax.Precision.HIGHEST
f32 = jnp.float32
bf16 = jnp.bfloat16
NT = (((1,), (1,)), ((), ()))
NN = (((1,), (0,)), ((), ()))
TN = (((0,), (0,)), ((), ()))


def dot(left, right, dims):
    return lax.dot_general(left, right, dims, preferred_element_type=f32)


def pair_rows(rows, side):
    lane = lax.broadcasted_iota(jnp.int32, rows.shape, 1)
    zero = jnp.zeros_like(rows)
    first = jnp.where(lane < HEAD_DIM, rows, zero)
    second = jnp.where(lane >= HEAD_DIM, rows, zero)
    return jnp.concatenate(
        [jnp.concatenate([first, side[0]], axis=1), jnp.concatenate([second, side[1]], axis=1)],
        axis=0,
    )


def unpair(both):
    row = lax.broadcasted_iota(jnp.int32, (PAIR, QBLK), 0)
    return jnp.where(row < HEAD_DIM, both[:, :QBLK], both[:, QBLK:])


def attend_kernel(bounds, q_ref, k_ref, v_ref, hot_ref, mask_ref, ctx_ref, lse_ref, kcat, vt):
    window = k_ref.shape[0]
    own = ctx_ref.shape[0]
    fold = kcat.shape[0]
    skip = MAXLEN // QBLK

    @pl.when(pl.program_id(0) == 0)
    def _():
        for j in range(fold):
            kcat[j, :, PAIR:] = mask_ref[...]
            kcat[j, pl.ds(window, PAD), :PAIR] = jnp.zeros((PAD, PAIR), bf16)
            vt[j, :, pl.ds(window, PAD)] = jnp.zeros((PAIR, PAD), bf16)

    lse_ref[...] = jnp.zeros_like(lse_ref)
    for j in range(fold):
        cols = pl.ds(j * PAIR, PAIR)
        kcat[j, pl.ds(0, window), :PAIR] = k_ref[:, cols]
        for at in range(0, window, 256):
            vt[j, :, pl.ds(at, 256)] = v_ref[pl.ds(at, 256), cols].T

    def block(i, carry):
        row0 = pl.multiple_of(i * QBLK, QBLK)
        hot = hot_ref[pl.ds(MAXLEN + row0, QBLK), :]
        rows = q_ref[pl.ds(MAXLEN + row0, QBLK), :]
        qcat = [pair_rows(rows[:, j * PAIR : (j + 1) * PAIR], (hot, hot)) for j in range(fold)]
        first = bounds[skip + i, 0]

        def step(c, state):
            start = pl.multiple_of(first + c * KCHUNK, 128)
            scores = [dot(kcat[j, pl.ds(start, KCHUNK), :], qcat[j], NT) for j in range(fold)]
            out = []
            for j, s in enumerate(scores):
                peak, total, acc = state[j]
                new_peak = jnp.maximum(peak, jnp.max(s, axis=0, keepdims=True))
                scale = jnp.exp(peak - new_peak)
                p = jnp.exp(s - new_peak)
                total = total * scale + jnp.sum(p, axis=0, keepdims=True)
                acc = acc * scale + dot(vt[j, :, pl.ds(start, KCHUNK)], p.astype(bf16), NN)
                out.append((new_peak, total, acc))
            return tuple(out)

        empty = (
            jnp.full((1, 2 * QBLK), -BIG, f32),
            jnp.zeros((1, 2 * QBLK), f32),
            jnp.zeros((PAIR, 2 * QBLK), f32),
        )
        state = lax.fori_loop(0, bounds[skip + i, 1], step, (empty,) * fold)
        for j, (peak, total, acc) in enumerate(state):
            ctx_ref[pl.ds(row0, QBLK), pl.ds(j * PAIR, PAIR)] = unpair(acc / total).T.astype(bf16)
            lse = peak + jnp.log(total)
            lse_ref[2 * j : 2 * j + 1, pl.ds(row0, QBLK)] = lse[:, :QBLK]
            lse_ref[2 * j + 1 : 2 * j + 2, pl.ds(row0, QBLK)] = lse[:, QBLK:]
        return carry

    lax.fori_loop(0, own // QBLK, block, 0)


def fold_of(pairs, most):
    return max(n for n in range(1, most + 1) if pairs % n == 0)


def attend(bounds, qkv, hot, mask, own):
    window, wide = qkv.shape
    width = wide // 3
    pairs = width // PAIR
    fold = fold_of(pairs, 3)
    parts = pairs // fold
    column = lambda part: pl.BlockSpec((window, fold * PAIR), lambda g, b: (0, part * parts + g))
    whole = lambda a: pl.BlockSpec(a.shape, lambda g, b: (0, 0))
    return pl.pallas_call(
        attend_kernel,
        grid_spec=pltpu.PrefetchScalarGridSpec(
            num_scalar_prefetch=1,
            grid=(parts,),
            in_specs=[column(0), column(1), column(2), whole(hot), whole(mask)],
            out_specs=[
                pl.BlockSpec((own, fold * PAIR), lambda g, b: (0, g)),
                pl.BlockSpec((8, own), lambda g, b: (g, 0)),
            ],
            scratch_shapes=[
                pltpu.VMEM((fold, window + PAD, 2 * PAIR), bf16),
                pltpu.VMEM((fold, PAIR, window + PAD), bf16),
            ],
        ),
        out_shape=[
            jax.ShapeDtypeStruct((own, width), bf16),
            jax.ShapeDtypeStruct((8 * parts, own), f32),
        ],
        cost_estimate=pl.CostEstimate(
            flops=own * 600 * width * 4, bytes_accessed=window * wide * 2, transcendentals=0
        ),
        name="attend",
    )(bounds, qkv, qkv, qkv, hot, mask)


def attend_back_kernel(side0, more, bounds, q_ref, k_ref, v_ref, do_ref, side_ref, hot_ref, mask_ref, *refs):
    extra, refs = refs[:more], refs[more:]
    gqkv_ref, (kcat, vcat, kt, dk, dv) = refs[0].at[0], refs[-5:]
    window = k_ref.shape[0]
    own = gqkv_ref.shape[1]
    fold = kcat.shape[0]
    lanes, gap = side0
    part = pl.program_id(0)
    low0 = LSE0 + lanes * part

    @pl.when(part == 0)
    def _():
        for j in range(fold):
            kcat[j, :, PAIR:] = mask_ref[...]
            vcat[j, :, PAIR:] = jnp.ones((window + PAD, SIDE), bf16)
            kcat[j, pl.ds(window, PAD), :PAIR] = jnp.zeros((PAD, PAIR), bf16)
            vcat[j, pl.ds(window, PAD), :PAIR] = jnp.zeros((PAD, PAIR), bf16)
            kt[j, :, pl.ds(window, PAD)] = jnp.zeros((PAIR, PAD), bf16)

    for j in range(fold):
        cols = pl.ds(j * PAIR, PAIR)
        kcat[j, pl.ds(0, window), :PAIR] = k_ref[:, cols]
        vcat[j, pl.ds(0, window), :PAIR] = v_ref[:, cols]
        for at in range(0, window, 256):
            kt[j, :, pl.ds(at, 256)] = k_ref[pl.ds(at, 256), cols].T
    dk[...] = jnp.zeros_like(dk)
    dv[...] = jnp.zeros_like(dv)
    lane = lax.broadcasted_iota(jnp.int32, (QBLK, SIDE), 1)

    def side_lanes(side, first):
        return jnp.where((lane >= first) & (lane < first + 3), side, jnp.zeros_like(side))

    def block(i, carry):
        row0 = pl.multiple_of(i * QBLK, QBLK)
        hot = hot_ref[pl.ds(row0, QBLK), :]
        side = side_ref[pl.ds(row0, QBLK), :]
        rows = q_ref[pl.ds(row0, QBLK), :]
        grads = do_ref[pl.ds(row0, QBLK), :]
        qcat, docat = [], []
        for j in range(fold):
            cols = slice(j * PAIR, (j + 1) * PAIR)
            low = low0 + 6 * j
            qcat.append(
                pair_rows(
                    rows[:, cols],
                    (hot + side_lanes(side, low), hot + side_lanes(side, low + 3)),
                )
            )
            docat.append(
                pair_rows(
                    grads[:, cols],
                    (side_lanes(side, low + gap), side_lanes(side, low + gap + 3)),
                )
            )
        first = bounds[i, 0]

        def step(c, dq):
            start = pl.multiple_of(first + c * KCHUNK, 128)
            here = pl.ds(start, KCHUNK)
            scores = [dot(kcat[j, here, :], qcat[j], NT) for j in range(fold)]
            slopes = [dot(vcat[j, here, :], docat[j], NT) for j in range(fold)]
            out = []
            for j in range(fold):
                p = jnp.exp(scores[j])
                ds = (p * slopes[j]).astype(bf16)
                dv[j, here, :] += dot(p.astype(bf16), docat[j][:, :PAIR], NN)
                dk[j, here, :] += dot(ds, qcat[j][:, :PAIR], NN)
                out.append(dq[j] + dot(kt[j, :, here], ds, NN))
            return tuple(out)

        dq = lax.fori_loop(
            0, bounds[i, 1], step, (jnp.zeros((PAIR, 2 * QBLK), f32),) * fold
        )

        @pl.when((i >= MAXLEN // QBLK) & (i < (MAXLEN + own) // QBLK))
        def _():
            for j in range(fold):
                gqkv_ref[
                    0, pl.ds(pl.multiple_of(row0 - MAXLEN, QBLK), QBLK), pl.ds(j * PAIR, PAIR)
                ] = (unpair(dq[j]) * HEAD_DIM**-0.5).T.astype(bf16)

        return carry

    lax.fori_loop(0, window // QBLK, block, 0)
    for j in range(fold):
        cols = pl.ds(j * PAIR, PAIR)
        gqkv_ref[1, :, cols] = dk[j, pl.ds(MAXLEN, own), :].astype(bf16)
        gqkv_ref[2, :, cols] = dv[j, pl.ds(MAXLEN, own), :].astype(bf16)

    if more:
        tok_t, place = extra[:2]
        keep, send, sums = (ref.at[0] for ref in refs[1:4])
        sums[...] = jnp.zeros_like(sums)

        def third(n, carry):
            grads = gqkv_ref[n]
            sums[pl.ds(n, 1), :] = col_sum(grads.astype(f32))
            mine, theirs = halves(dot(tok_t[...], grads, NN), place[0], keep.shape[2])
            for g in range(len(mine)):
                keep[n, g] = mine[g]
                send[n, g] = theirs[g]
            return carry

        lax.fori_loop(0, 3, third, 0)


def attend_back(bounds, qkv, grads, hot, mask, own, extra=()):
    window, wide = qkv.shape
    width = wide // 3
    pairs = width // PAIR
    fold = fold_of(pairs, 2)
    parts = pairs // fold
    cols = fold * PAIR
    column = lambda c: pl.BlockSpec((window, cols), lambda g, b: (0, c * parts + g))
    whole = lambda a: pl.BlockSpec(a.shape, lambda g, b: (0, 0))
    shape = jax.ShapeDtypeStruct
    more_in, more_out = [], []
    if extra:
        more_in = [whole(extra[0]), pl.BlockSpec(memory_space=pltpu.SMEM)]
        more_out = [shape((parts, 3, 4, width // 8, cols), bf16)] * 2 + [shape((parts, 8, cols), f32)]
    block = lambda a: pl.BlockSpec((1,) + a.shape[1:], lambda g, b: (g,) + (0,) * (len(a.shape) - 1))
    outs = [shape((parts, 3, own, cols), bf16)] + more_out
    results = pl.pallas_call(
        functools.partial(attend_back_kernel, (6 * fold, 6 * pairs), len(extra)),
        grid_spec=pltpu.PrefetchScalarGridSpec(
            num_scalar_prefetch=1,
            grid=(parts,),
            in_specs=[
                column(0),
                column(1),
                column(2),
                pl.BlockSpec((window, cols), lambda g, b: (0, g)),
                pl.BlockSpec((window, SIDE), lambda g, b: (0, pairs)),
                whole(hot),
                whole(mask),
            ]
            + more_in,
            out_specs=[block(o) for o in outs],
            scratch_shapes=[
                pltpu.VMEM((fold, window + PAD, 2 * PAIR), bf16),
                pltpu.VMEM((fold, window + PAD, 2 * PAIR), bf16),
                pltpu.VMEM((fold, PAIR, window + PAD), bf16),
                pltpu.VMEM((fold, window + PAD, PAIR), f32),
                pltpu.VMEM((fold, window + PAD, PAIR), f32),
            ],
        ),
        out_shape=outs,
        cost_estimate=pl.CostEstimate(
            flops=own * 900 * width * 16, bytes_accessed=window * width * 8, transcendentals=0
        ),
        name="attend_back",
    )(bounds, qkv, qkv, qkv, grads, grads, hot, mask, *extra)
    return results if extra else results[0]


def low3(values):
    high = values.astype(bf16)
    rest = values - high.astype(f32)
    mid = rest.astype(bf16)
    return high, mid, (rest - mid.astype(f32)).astype(bf16)


def dot3(values, chosen, dims):
    return sum(dot(part, chosen, dims) for part in low3(values))


def iota(shape, axis):
    return lax.broadcasted_iota(jnp.int32, shape, axis)


def mean_row(values):
    return jnp.mean(values, axis=-1, keepdims=True)


def col_sum(values):
    return jnp.sum(values, axis=0, keepdims=True)


def norm_back(grad_out, normed, inv_std, gain_vec):
    grad_norm = grad_out * gain_vec
    inner = grad_norm - mean_row(grad_norm) - normed * mean_row(grad_norm * normed)
    return inv_std * inner, col_sum(grad_out * normed), col_sum(grad_out)


ROWS = 256
VECTORS = 24


def middle_kernel(
    heads_part, place, w_in_hbm, w_back_hbm, w_pool_hbm, lse_hbm, cot_hbm, tok, ctx, w_out, b_in, w_class, small, seqs_of,
    out_hbm, gar_hbm, gs_hbm, act_hbm, gpre_hbm, gffn_hbm, mid_hbm, gattn_hbm, cls, gpool, vec,
    out, gar, gs, gffn, mid, gattn, lse, cot, more_sems, w_in, w_back, w_pool, act, gpre, slope, unit_a, unit_f, inv_a, inv_f, acc, sems,
):
    own, width = tok.shape
    b_out, gain_a, shift_a, b_back, gain_f, shift_f, b_pool = (small[:, n * width : (n + 1) * width] for n in range(7))
    starts, labels = seqs_of[:, 0:1], seqs_of[:, 1:2]
    chunks, _, wide = act.shape
    blocks = own // ROWS
    n_class = w_class.shape[0]
    loads = [
        pltpu.make_async_copy(w_in_hbm, w_in, sems.at[0]),
        pltpu.make_async_copy(w_back_hbm, w_back, sems.at[1]),
        pltpu.make_async_copy(w_pool_hbm, w_pool, sems.at[2]),
        pltpu.make_async_copy(cot_hbm, cot, more_sems.at[0]),
        pltpu.make_async_copy(lse_hbm, lse, more_sems.at[1]),
    ]
    store_mid, store_out, store_gffn = (
        pltpu.make_async_copy(src, dst, more_sems.at[2 + n])
        for n, (src, dst) in enumerate(((mid, mid_hbm), (out, out_hbm), (gffn, gffn_hbm)))
    )

    def last_stores(b):
        return [
            pltpu.make_async_copy(src.at[at(b)], dst.at[at(b)], more_sems.at[5 + 3 * b + n])
            for n, (src, dst) in enumerate(((gar, gar_hbm), (gs, gs_hbm), (gattn, gattn_hbm)))
        ]

    for load in loads:
        load.start()

    def at(b):
        return pl.ds(pl.multiple_of(b * ROWS, ROWS), ROWS)

    def cols(c):
        return pl.ds(pl.multiple_of(c * wide, wide), wide)

    def norm(hidden, rows, unit, inv, gain, shift):
        centred = hidden - mean_row(hidden)
        inv_std = lax.rsqrt(mean_row(centred * centred) + eps)
        normed = centred * inv_std
        unit[rows, :] = normed
        inv[rows, :] = inv_std
        return (normed * gain[...] + shift[...]).astype(bf16)

    def first_norm(b, carry):
        rows = at(b)
        hidden = tok[rows, :].astype(f32) + dot(ctx[rows, :], w_out[...], NN) + b_out[...]
        mid[rows, :] = norm(hidden, rows, unit_a, inv_a, gain_a, shift_a)
        return carry

    lax.fori_loop(0, blocks, first_norm, 0)
    store_mid.start()
    loads[0].wait()
    loads[1].wait()
    acc[...] = jnp.zeros_like(acc)

    def forward(c, carry):
        for b in range(blocks):
            rows = slice(b * ROWS, (b + 1) * ROWS)
            pre = dot(mid[rows, :], w_in[:, cols(c)], NN) + b_in[:, cols(c)]
            cdf = 0.5 * (1.0 + lax.erf(pre * (0.5**0.5)))
            low = (pre * cdf).astype(bf16)
            act[c, rows, :] = low
            slope[c, rows, :] = cdf + pre * (jnp.exp(-0.5 * pre * pre) * 0.3989422804014327)
            acc[rows, :] += dot(low, w_back[cols(c), :], NN)
        pltpu.make_async_copy(act.at[c], act_hbm.at[c], sems.at[3 + c]).start()
        return carry

    lax.fori_loop(0, chunks, forward, 0)

    def second_norm(b, carry):
        rows = at(b)
        hidden = mid[rows, :].astype(f32) + (acc[rows, :] + b_back[...])
        out[rows, :] = norm(hidden, rows, unit_f, inv_f, gain_f, shift_f)
        return carry

    lax.fori_loop(0, blocks, second_norm, 0)
    store_out.start()
    loads[3].wait()
    loads[4].wait()

    loads[2].wait()
    seqs = starts.shape[0]
    picked = (iota((seqs, own), 1) + place[0] * own == starts[...]).astype(f32)
    sel = picked.astype(bf16)
    owned = jnp.sum(picked, axis=1, keepdims=True)
    cls_low = dot(sel, out[...], NN).astype(bf16)
    cls[...] = cls_low
    pooled = jnp.tanh(dot(cls_low, w_pool[...], NN) + b_pool[...])
    logits = [jnp.sum(pooled * w_class[c : c + 1, :], axis=1, keepdims=True) for c in range(n_class)]
    peak = functools.reduce(jnp.maximum, logits)
    expo = [jnp.exp(x - peak) for x in logits]
    total = sum(expo)
    probs = [x / total for x in expo]
    terms = owned * (peak + jnp.log(total) - sum(p * x for p, x in zip(probs, logits)))
    entropy = jnp.sum(terms, axis=0, keepdims=True)
    g_logits = [
        (probs[c] - (labels[...] == c).astype(f32)) * owned for c in range(n_class)
    ]
    g_pooled = sum(g_logits[c] * w_class[c : c + 1, :] for c in range(n_class))
    g_low = (g_pooled * (1.0 - pooled * pooled)).astype(bf16)
    gpool[...] = g_low
    grad_cls = dot(g_low, w_pool[...], NT)

    def second_back(b, carry):
        rows = at(b)
        here = (
            iota((seqs, ROWS), 1) + (place[0] * own + b * ROWS) == starts[...]
        ).astype(f32).astype(bf16)
        back = sum(dot(here, part, TN) for part in low3(grad_cls))
        grad_out = cot[rows, :].astype(f32) + back
        res, g_gain, g_shift = norm_back(grad_out, unit_f[rows, :], inv_f[rows, :], gain_f[...])
        low = res.astype(bf16)
        gar[rows, :] = res
        gffn[rows, :] = low
        return carry[0] + g_gain, carry[1] + g_shift, carry[2] + col_sum(low.astype(f32))

    zero = jnp.zeros((1, width), f32)
    sums_f = lax.fori_loop(0, blocks, second_back, (zero, zero, zero))
    store_gffn.start()
    acc[...] = jnp.zeros_like(acc)

    def backward(c, carry):
        g_b_in = jnp.zeros((1, wide), f32)
        for b in range(blocks):
            rows = slice(b * ROWS, (b + 1) * ROWS)
            grad_act = dot(gffn[rows, :], w_back[cols(c), :], NT)
            low = (grad_act * slope[c, rows, :]).astype(bf16)
            gpre[c, rows, :] = low
            g_b_in += col_sum(low.astype(f32))
            acc[rows, :] += dot(low, w_in[:, cols(c)], NT)
        vec[pl.ds(8 + c, 1), :] = g_b_in
        pltpu.make_async_copy(gpre.at[c], gpre_hbm.at[c], sems.at[3 + chunks + c]).start()
        return carry

    lax.fori_loop(0, chunks, backward, 0)

    heads = width // HEAD_DIM
    lane = iota((1, SIDE), 1)
    gap = LSE0 + 3 * heads
    feature, flane = iota((width, SIDE), 0), iota((width, SIDE), 1)
    third = flane - gap - 3 * (feature // HEAD_DIM)
    head_sum = ((third >= 0) & (third < 3)).astype(f32).astype(bf16)
    lrow, llane = iota((lse.shape[0], SIDE), 0), iota((lse.shape[0], SIDE), 1)
    lhead = (lrow // 8) * heads_part + lrow % 8
    spread = [
        ((llane == LSE0 + 3 * lhead + p) & (lrow % 8 < heads_part)).astype(f32).astype(bf16)
        for p in range(3)
    ]
    which = lax.rem(lane - gap + 3 * heads, 3)

    def first_back(b, carry):
        rows = at(b)
        grad_mid = gar[rows, :] + acc[rows, :]
        res, g_gain, g_shift = norm_back(grad_mid, unit_a[rows, :], inv_a[rows, :], gain_a[...])
        low = res.astype(bf16)
        gar[rows, :] = res
        gattn[rows, :] = low
        grad_ctx = dot(low, w_out[...], NT).astype(bf16)
        gs[rows, :width] = grad_ctx
        delta = dot3(grad_ctx.astype(f32) * ctx[rows, :].astype(f32), head_sum, NN)
        high, mid_part, rest = low3(-delta)
        side = jnp.where(which == 0, high, jnp.where(which == 1, mid_part, rest))
        lse_parts = low3(-lse[:, rows])
        side_lse = sum(dot(part, spread[p], TN) for p, part in enumerate(lse_parts))
        gs[rows, width:] = side + side_lse.astype(bf16)
        for copy in last_stores(b):
            copy.start()
        return carry[0] + g_gain, carry[1] + g_shift, carry[2] + col_sum(low.astype(f32))

    sums_a = lax.fori_loop(0, blocks, first_back, (zero, zero, zero))
    for row, value in enumerate((sums_a[2], sums_a[0], sums_a[1], sums_f[2], sums_f[0], sums_f[1])):
        vec[row : row + 1, :] = value
    vec[6:7, :] = col_sum(g_low.astype(f32))
    vec[7:8, :] = jnp.broadcast_to(entropy, (1, width))
    for c in range(n_class):
        vec[8 + chunks + c : 9 + chunks + c, :] = col_sum(pooled * g_logits[c])
    done = 8 + chunks + n_class
    vec[done:, :] = jnp.zeros((VECTORS - done, width), f32)
    for c in range(chunks):
        pltpu.make_async_copy(act.at[c], act_hbm.at[c], sems.at[3 + c]).wait()
        pltpu.make_async_copy(gpre.at[c], gpre_hbm.at[c], sems.at[3 + chunks + c]).wait()
    for copy in (store_mid, store_out, store_gffn):
        copy.wait()
    for b in range(blocks):
        for copy in last_stores(b):
            copy.wait()


def middle_layer(heads_part, place, w_in, w_back, w_pool, tok, ctx, lse, cot, w_out, b_in, w_class, small, seqs_of):
    own, width = tok.shape
    ff = w_in.shape[1]
    chunks = ff // width
    seqs = seqs_of.shape[0]
    vmem = pl.BlockSpec(memory_space=pltpu.VMEM)
    hbm = pl.BlockSpec(memory_space=pl.ANY)
    shape = jax.ShapeDtypeStruct
    flops = 2 * own * width * (6 * width + 4 * ff)
    return pl.pallas_call(
        functools.partial(middle_kernel, heads_part),
        in_specs=[pl.BlockSpec(memory_space=pltpu.SMEM)] + [hbm] * 5 + [vmem] * 7,
        out_specs=[hbm] * 8 + [vmem] * 3,
        out_shape=[
            shape((own, width), bf16),
            shape((own, width), f32),
            shape((own, width + SIDE), bf16),
            shape((chunks, own, width), bf16),
            shape((chunks, own, width), bf16),
            shape((own, width), bf16),
            shape((own, width), bf16),
            shape((own, width), bf16),
            shape((seqs, width), bf16),
            shape((seqs, width), bf16),
            shape((VECTORS, width), f32),
        ],
        scratch_shapes=[
            pltpu.VMEM((own, width), bf16),
            pltpu.VMEM((own, width), f32),
            pltpu.VMEM((own, width + SIDE), bf16),
            pltpu.VMEM((own, width), bf16),
            pltpu.VMEM((own, width), bf16),
            pltpu.VMEM((own, width), bf16),
            pltpu.VMEM(lse.shape, f32),
            pltpu.VMEM(cot.shape, bf16),
            pltpu.SemaphoreType.DMA((5 + 3 * (own // ROWS),)),
            pltpu.VMEM(w_in.shape, bf16),
            pltpu.VMEM(w_back.shape, bf16),
            pltpu.VMEM(w_pool.shape, bf16),
            pltpu.VMEM((chunks, own, width), bf16),
            pltpu.VMEM((chunks, own, width), bf16),
            pltpu.VMEM((chunks, own, width), f32),
            pltpu.VMEM((own, width), f32),
            pltpu.VMEM((own, width), f32),
            pltpu.VMEM((own, 1), f32),
            pltpu.VMEM((own, 1), f32),
            pltpu.VMEM((own, width), f32),
            pltpu.SemaphoreType.DMA((3 + 2 * chunks,)),
        ],
        compiler_params=pltpu.CompilerParams(vmem_limit_bytes=62 * 2**20),
        cost_estimate=pl.CostEstimate(flops=flops, bytes_accessed=30 * 2**20, transcendentals=0),
        name="middle_layer",
    )(place, w_in, w_back, w_pool, lse, cot, tok, ctx, w_out, b_in, w_class, small, seqs_of)


def split_core(tile, core, half, keep, send, first):
    for n in range(tile.shape[0] // (2 * half)):
        even = tile[2 * n * half : (2 * n + 1) * half, :]
        odd = tile[(2 * n + 1) * half : (2 * n + 2) * half, :]
        keep[first + n, :, :] = jnp.where(core == 0, even, odd).astype(bf16)
        send[first + n, :, :] = jnp.where(core == 0, odd, even).astype(bf16)


def weight_grads_kernel(
    core, act, gpre, gffn, mid, ctx, gattn, cls, gpool,
    back_keep, back_send, in_keep, in_send, out_keep, out_send, mid_t,
):
    y = pl.program_id(0)

    @pl.when(y == 0)
    def _():
        mid_t[...] = mid[...].T
        split_core(dot(ctx[...], gattn[...], TN), core[0], out_keep.shape[1], out_keep, out_send, 0)

    @pl.when(y == 1)
    def _():
        split_core(dot(cls[...], gpool[...], TN), core[0], out_keep.shape[1], out_keep, out_send, 0)

    split_core(dot(act[0], gffn[...], TN), core[0], back_keep.shape[1], back_keep, back_send, 0)
    split_core(dot(mid_t[...], gpre[0], NN), core[0], in_keep.shape[1], in_keep, in_send, 0)


def weight_grads(core, n_seq, act, gpre, gffn, mid, ctx, gattn, cls, gpool):
    chunks, own, width = act.shape
    groups = n_seq // 2
    half_b, half_w = chunks * width // n_seq, width // n_seq
    shape = jax.ShapeDtypeStruct
    whole = lambda a: pl.BlockSpec(a.shape, lambda y, c: (0, 0))
    tile = pl.BlockSpec((1, own, width), lambda y, c: (y, 0, 0))
    back = pl.BlockSpec((groups // chunks, half_b, width), lambda y, c: (y, 0, 0))
    inner = pl.BlockSpec((groups, half_w, width), lambda y, c: (0, 0, y))
    outer = pl.BlockSpec((groups, half_w, width), lambda y, c: (0, 0, jnp.minimum(y, 1)))
    return pl.pallas_call(
        weight_grads_kernel,
        grid_spec=pltpu.PrefetchScalarGridSpec(
            num_scalar_prefetch=1,
            grid=(chunks,),
            in_specs=[tile, tile] + [whole(a) for a in (gffn, mid, ctx, gattn, cls, gpool)],
            out_specs=[back, back, inner, inner, outer, outer],
            scratch_shapes=[pltpu.VMEM((width, own), bf16)],
        ),
        out_shape=[shape((groups, half_b, width), bf16)] * 2
        + [shape((groups, half_w, chunks * width), bf16)] * 2
        + [shape((groups, half_w, 2 * width), bf16)] * 2,
        compiler_params=pltpu.CompilerParams(vmem_limit_bytes=48 * 2**20),
        cost_estimate=pl.CostEstimate(
            flops=2 * own * width * width * (2 * chunks + 1), bytes_accessed=30 * 2**20, transcendentals=0
        ),
        name="weight_grads",
    )(core, act, gpre, gffn, mid, ctx, gattn, cls, gpool)


def last_kernel(n_parts, core, *refs):
    tok, gar, w_qkv = refs[:3]
    parts = refs[3 : 3 + n_parts]
    gtok, vec = refs[3 + n_parts : 5 + n_parts]
    pairs = refs[5 + n_parts : 11 + n_parts]
    tok_t = refs[11 + n_parts]
    c = pl.program_id(0)

    @pl.when(c == 0)
    def _():
        tok_t[...] = tok[...].T
        gtok[...] = gar[...]
        vec[...] = jnp.zeros_like(vec)

    grads = jnp.concatenate([p[0] for p in parts], axis=1)
    gtok[...] += dot(grads, w_qkv[...], NT)
    vec[pl.ds(c, 1), :] = col_sum(grads.astype(f32))
    tile = dot(tok_t[...], grads, NN)
    for n in range(3):

        @pl.when(c == n)
        def _():
            keep, send = pairs[2 * n], pairs[2 * n + 1]
            split_core(tile, core[0], keep.shape[1], keep, send, 0)


def last_layer(core, n_seq, tok, gar, w_qkv, parts):
    own, width = tok.shape
    groups, half = n_seq // 2, width // n_seq
    shape = jax.ShapeDtypeStruct
    whole = lambda a: pl.BlockSpec(a.shape, lambda c, k: (0,) * len(a.shape))
    pair = pl.BlockSpec((groups, half, width), lambda c, k: (0, 0, 0))
    return pl.pallas_call(
        functools.partial(last_kernel, len(parts)),
        grid_spec=pltpu.PrefetchScalarGridSpec(
            num_scalar_prefetch=1,
            grid=(3,),
            in_specs=[whole(tok), whole(gar), pl.BlockSpec((width, width), lambda c, k: (0, c))]
            + [pl.BlockSpec((1,) + p.shape[1:], lambda c, k: (c, 0, 0)) for p in parts],
            out_specs=[whole(gar), pl.BlockSpec((8, width), lambda c, k: (0, 0))] + [pair] * 6,
            scratch_shapes=[pltpu.VMEM((width, own), bf16)],
        ),
        out_shape=[shape((own, width), f32), shape((8, width), f32)]
        + [shape((groups, half, width), bf16)] * 6,
        compiler_params=pltpu.CompilerParams(vmem_limit_bytes=40 * 2**20),
        cost_estimate=pl.CostEstimate(
            flops=12 * own * width * width, bytes_accessed=12 * 2**20, transcendentals=0
        ),
        name="last_layer",
    )(core, tok, gar, w_qkv, *parts)


MESH = pl.DeviceIdType.MESH
OTHER_CORE, NEAR = 1, (2, 4, 6)


class Sends:
    def __init__(self, send_sems, recv_sems):
        self.sems, self.copies, self.at = (send_sems, recv_sems), {}, 0

    def plan(self, name, src, dst, **device):
        self.copies[name] = pltpu.make_async_remote_copy(
            src_ref=src,
            dst_ref=dst,
            send_sem=self.sems[0].at[self.at],
            recv_sem=self.sems[1].at[self.at],
            device_id=device,
            device_id_type=MESH,
        )
        self.at += 1

    def start(self, *names):
        for name in names:
            self.copies[name].start()

    def arrived(self, *names):
        for name in names:
            self.copies[name].wait_recv()

    def drain(self):
        for copy in self.copies.values():
            copy.wait_send()


def greet(devices):
    barrier = pltpu.get_barrier_semaphore()
    for device in devices:
        pl.semaphore_signal(barrier, inc=1, device_id=device, device_id_type=MESH)
    pl.semaphore_wait(barrier, len(devices))


def halves(tile, core, half):
    even = [tile[2 * n * half : (2 * n + 1) * half] for n in range(tile.shape[0] // (2 * half))]
    odd = [tile[(2 * n + 1) * half : (2 * n + 2) * half] for n in range(tile.shape[0] // (2 * half))]
    keep = [jnp.where(core == 0, e, o).astype(bf16) for e, o in zip(even, odd)]
    send = [jnp.where(core == 0, o, e).astype(bf16) for e, o in zip(even, odd)]
    return keep, send


def front_kernel(
    tok, w_hbm, small, lens, labels, qkv_hbm, hot, mask, bounds, seqs_of,
    sides, w, work, rows_of, load_sem, out_sems, send_sems, recv_sems,
):
    head, n_head = lax.axis_index("head"), lax.axis_size("head")
    own, width = tok.shape
    window = hot.shape[0]
    load = pltpu.make_async_copy(w_hbm, w, load_sem)
    load.start()
    not_first, not_last = head > 0, head < n_head - 1
    barrier = pltpu.get_barrier_semaphore()

    @pl.when(not_first)
    def _():
        pl.semaphore_signal(barrier, inc=1, device_id={"head": head - 1}, device_id_type=MESH)

    @pl.when(not_last)
    def _():
        pl.semaphore_signal(barrier, inc=1, device_id={"head": head + 1}, device_id_type=MESH)

    pl.semaphore_wait(barrier, not_first.astype(jnp.int32) + not_last.astype(jnp.int32))
    pieces = MAXLEN // ROWS
    here = lambda n: pl.ds(n * ROWS, ROWS)
    up, down = [], []
    for n in range(pieces):
        for copies, first, side, device in (
            (up, own - MAXLEN, 0, lax.rem(head + 1, n_head)),
            (down, 0, 1, lax.rem(head + n_head - 1, n_head)),
        ):
            copies.append(
                pltpu.make_async_remote_copy(
                    src_ref=tok.at[pl.ds(first + n * ROWS, ROWS)], dst_ref=sides.at[side, here(n)],
                    send_sem=send_sems.at[side, n], recv_sem=recv_sems.at[side, n],
                    device_id={"head": device}, device_id_type=MESH,
                )
            )

    @pl.when(not_last)
    def _():
        for copy in up:
            copy.start()

    @pl.when(not_first)
    def _():
        for copy in down:
            copy.start()

    @pl.when(head == 0)
    def _():
        sides[0] = jnp.zeros((MAXLEN, width), bf16)

    @pl.when(head == n_head - 1)
    def _():
        sides[1] = jnp.zeros((MAXLEN, width), bf16)

    def stored(at, n):
        return pltpu.make_async_copy(
            work.at[pl.ds(at, ROWS)], qkv_hbm.at[pl.ds(at, ROWS)], out_sems.at[n]
        )

    def project(rows, at, n):
        into = pl.ds(at, ROWS)
        query = (dot(rows, w[:, :width], NN) + small[:, 7 * width : 8 * width]) * HEAD_DIM**-0.5
        work[into, :width] = query.astype(bf16)
        work[into, width : 2 * width] = dot(rows, w[:, width : 2 * width], NN).astype(bf16)
        value = dot(rows, w[:, 2 * width :], NN) + small[:, 8 * width : 9 * width]
        work[into, 2 * width :] = value.astype(bf16)
        stored(at, n).start()

    load.wait()

    def own_rows(n, carry):
        at = pl.multiple_of(n * ROWS, ROWS)
        project(tok[pl.ds(at, ROWS), :], pl.multiple_of(MAXLEN + at, ROWS), n)
        return carry

    lax.fori_loop(0, own // ROWS, own_rows, 0)

    n_seqs = lens.shape[1]
    rows_of[...] = jnp.zeros_like(rows_of)
    rows_of[0:1, :n_seqs] = lens[...]
    rows_of[1:2, :n_seqs] = labels[...]
    i, j = iota((SIDE, SIDE), 0), iota((SIDE, SIDE), 1)
    length, label = rows_of[0:1, :].astype(f32), rows_of[1:2, :].astype(f32)
    to_col = lambda row, chosen: jnp.sum(jnp.where(chosen, row, 0.0), axis=1, keepdims=True)
    length_col, ends_col = to_col(length, i == j), to_col(length, j <= i)
    ends = jnp.sum(jnp.where(i <= j, length_col, 0.0), axis=0, keepdims=True)
    starts = ends - length
    group = float(own * n_head)
    n_rows = seqs_of.shape[0]
    row, lane = i[:n_rows], j[:n_rows]
    first_col = jnp.where(row < n_seqs, (ends_col - length_col)[:n_rows], -1.0)
    label_col = to_col(label, i == j)[:n_rows]
    seqs_of[...] = jnp.where(lane == 0, first_col, jnp.where(lane == 1, label_col, 0.0)).astype(jnp.int32)

    base = head * own - MAXLEN
    row, lane = i[:16], j[:16]
    blk = (base + row * QBLK).astype(f32)
    taken = lane < n_seqs
    low = jnp.max(jnp.where(taken & (starts <= blk), starts, -1.0), axis=1, keepdims=True)
    high = jnp.min(
        jnp.where(taken & (ends > blk + (QBLK - 1)), ends, group), axis=1, keepdims=True
    )
    at = row * QBLK
    is_own = (at >= MAXLEN) & (at < MAXLEN + own)
    low = jnp.broadcast_to(low.astype(jnp.int32), at.shape) - base
    high = jnp.broadcast_to(high.astype(jnp.int32), at.shape) - base
    low = jnp.where(is_own, low, jnp.maximum(low, MAXLEN))
    high = jnp.where(is_own, high, jnp.minimum(high, MAXLEN + own))
    low = (low >> 7) << 7
    valid = (blk >= 0.0) & (blk < group)
    steps = jnp.where(valid, jnp.maximum((high - low + KCHUNK - 1) >> (KCHUNK.bit_length() - 1), 0), 0)
    bounds[...] = jnp.where(lane == 0, low, jnp.where(lane == 1, steps, 0))

    lane = iota((QBLK, SIDE), 1)

    def masks(n, carry):
        at = pl.multiple_of(n * QBLK, QBLK)
        pos = (iota((QBLK, SIDE), 0) + (base + at)).astype(f32)
        inside = ((starts <= pos) & (pos < ends)).astype(f32)
        hot[pl.ds(at, QBLK), :] = inside.astype(bf16)
        mask[pl.ds(at, QBLK), :] = jnp.where(lane < n_seqs, (inside - 1.0) * BIG, 1.0).astype(bf16)
        return carry

    lax.fori_loop(0, window // QBLK, masks, 0)
    mask[pl.ds(window, PAD), :] = jnp.where(iota((PAD, SIDE), 1) < n_seqs, -BIG, 1.0).astype(bf16)

    for n in range(pieces):

        @pl.when(not_first)
        def _():
            up[n].wait_recv()

        @pl.when(not_last)
        def _():
            down[n].wait_recv()

        def side_rows(side, carry):
            at = pl.multiple_of(side * (MAXLEN + own) + n * ROWS, ROWS)
            project(sides[side, here(n), :], at, own // ROWS + 2 * n + side)
            return carry

        lax.fori_loop(0, 2, side_rows, 0)

    for n in range(own // ROWS):
        stored(MAXLEN + n * ROWS, n).wait()
    for n in range(pieces):
        for side in range(2):
            stored(side * (MAXLEN + own) + n * ROWS, own // ROWS + 2 * n + side).wait()

    @pl.when(not_last)
    def _():
        for copy in up:
            copy.wait_send()

    @pl.when(not_first)
    def _():
        for copy in down:
            copy.wait_send()


def front(tok, w_qkv, small, lens, labels):
    own, width = tok.shape
    window = own + 2 * MAXLEN
    seqs = lens.shape[1] + -lens.shape[1] % 16
    pieces = MAXLEN // ROWS
    shape = jax.ShapeDtypeStruct
    vmem, hbm = pl.BlockSpec(memory_space=pltpu.VMEM), pl.BlockSpec(memory_space=pl.ANY)
    return pl.pallas_call(
        front_kernel,
        in_specs=[vmem, hbm, vmem, vmem, vmem],
        out_specs=[hbm] + [vmem] * 4,
        out_shape=[
            shape((window, 3 * width), bf16),
            shape((window, SIDE), bf16),
            shape((window + PAD, SIDE), bf16),
            shape((16, SIDE), jnp.int32),
            shape((seqs, SIDE), jnp.int32),
        ],
        scratch_shapes=[
            pltpu.VMEM((2, MAXLEN, width), bf16),
            pltpu.VMEM(w_qkv.shape, bf16),
            pltpu.VMEM((window, 3 * width), bf16),
            pltpu.VMEM((8, SIDE), jnp.int32),
            pltpu.SemaphoreType.DMA,
            pltpu.SemaphoreType.DMA((own // ROWS + 2 * pieces,)),
            pltpu.SemaphoreType.DMA((2, pieces)),
            pltpu.SemaphoreType.DMA((2, pieces)),
        ],
        compiler_params=pltpu.CompilerParams(
            vmem_limit_bytes=62 * 2**20, collective_id=2, has_side_effects=True
        ),
        cost_estimate=pl.CostEstimate(
            flops=6 * window * width * width, bytes_accessed=16 * 2**20, transcendentals=0
        ),
        name="front",
    )(tok, w_qkv, small, lens, labels)


def grads_kernel(
    ctx_hbm, gattn_hbm, mid_hbm, gffn_hbm, tok_hbm, gs_hbm, act_hbm, gpre_hbm, cls, gpool,
    gsw, *refs,
):
    stores, outs, held, refs = refs[:8], refs[8:16], refs[16:22], refs[22:]
    tok_t, (ctx, gattn, mid, gffn, tok, gs) = outs[7], held
    store = [
        pltpu.make_async_copy(src, dst, refs[-1].at[6 + n])
        for n, (src, dst) in enumerate(zip(outs, stores))
    ]
    load = [
        pltpu.make_async_copy(src, dst, refs[-1].at[n])
        for n, (src, dst) in enumerate(
            zip((ctx_hbm, gattn_hbm, mid_hbm, gffn_hbm, tok_hbm, gs_hbm), held)
        )
    ]
    outs = (*outs[:6], outs[6].at[0], outs[6].at[1])
    (act, gpre, mid_t, keep_a, send_a, got_a, keep_b, send_b, got_b, keep_c, send_c, got_c, split,
     loads, send_sems, recv_sems, halo_sems, _) = refs
    seq, head = lax.axis_index("seq"), lax.axis_index("head")
    n_head = lax.axis_size("head")
    core = lax.rem(seq, 2)
    chunks, own, width = act.shape
    half_b, half_w = keep_a.shape[1], keep_b.shape[2]
    for n in range(3):
        load[n].start()
    for c in range(chunks):
        pltpu.make_async_copy(gpre_hbm.at[c], gpre.at[c], loads.at[chunks + c]).start()
        if c == 0:
            load[3].start()
        pltpu.make_async_copy(act_hbm.at[c], act.at[c], loads.at[c]).start()
    load[5].start()
    load[4].start()

    barrier = pltpu.get_barrier_semaphore()
    pl.semaphore_signal(barrier, inc=1, device_id={"seq": seq ^ OTHER_CORE}, device_id_type=MESH)

    @pl.when(head > 0)
    def _():
        pl.semaphore_signal(barrier, inc=1, device_id={"head": head - 1}, device_id_type=MESH)

    @pl.when(head < n_head - 1)
    def _():
        pl.semaphore_signal(barrier, inc=1, device_id={"head": head + 1}, device_id_type=MESH)

    pl.semaphore_wait(barrier, 1 + (head > 0).astype(jnp.int32) + (head < n_head - 1).astype(jnp.int32))

    up = pltpu.make_async_remote_copy(
        src_ref=gs_hbm.at[pl.ds(own - MAXLEN, MAXLEN)], dst_ref=gsw.at[pl.ds(0, MAXLEN)],
        send_sem=halo_sems.at[0], recv_sem=halo_sems.at[1],
        device_id={"head": lax.rem(head + 1, n_head)}, device_id_type=MESH,
    )
    down = pltpu.make_async_remote_copy(
        src_ref=gs_hbm.at[pl.ds(0, MAXLEN)], dst_ref=gsw.at[pl.ds(own + MAXLEN, MAXLEN)],
        send_sem=halo_sems.at[2], recv_sem=halo_sems.at[3],
        device_id={"head": lax.rem(head + n_head - 1, n_head)}, device_id_type=MESH,
    )
    stay = pltpu.make_async_copy(gs, gsw.at[pl.ds(MAXLEN, own)], halo_sems.at[4])

    @pl.when(head < n_head - 1)
    def _():
        up.start()

    @pl.when(head > 0)
    def _():
        down.start()

    def to_core(send, got, first, n):
        return pltpu.make_async_remote_copy(
            src_ref=send.at[n], dst_ref=got.at[n],
            send_sem=send_sems.at[first + n], recv_sem=recv_sems.at[first + n],
            device_id={"seq": seq ^ OTHER_CORE}, device_id_type=MESH,
        )

    copy_a = lambda n: to_core(send_a, got_a, 0, n)
    copy_b = lambda n: to_core(send_b, got_b, chunks, n)
    copy_c = lambda n: to_core(send_c, got_c, 2 * chunks, n)

    def put(tile, half, keep, send):
        mine, theirs = halves(tile, core, half)
        for g in range(len(mine)):
            keep[g] = mine[g]
            send[g] = theirs[g]

    put(dot(cls[...], gpool[...], TN), half_w, keep_c.at[1], send_c.at[1])
    load[0].wait()
    load[1].wait()
    put(dot(ctx[...], gattn[...], TN), half_w, keep_c.at[0], send_c.at[0])
    load[2].wait()
    mid_t[...] = mid[...].T
    load[3].wait()

    def chunk(c, carry):
        pltpu.make_async_copy(gpre_hbm.at[c], gpre.at[c], loads.at[chunks + c]).wait()
        put(dot(mid_t[...], gpre[c], NN), half_w, keep_b.at[c], send_b.at[c])

        @pl.when(c == 0)
        def _():
            copy_c(0).start()
            copy_c(1).start()

        @pl.when(c > 0)
        def _():
            copy_a(jnp.maximum(c - 1, 0)).start()

        pltpu.make_async_copy(act_hbm.at[c], act.at[c], loads.at[c]).wait()
        mine, theirs = halves(dot(act[c], gffn[...], TN), core, half_b)
        keep_a[c], send_a[c] = mine[0], theirs[0]
        copy_b(c).start()
        return carry

    lax.fori_loop(0, chunks, chunk, 0)

    load[5].wait()
    stay.start()
    load[4].wait()
    tok_t[...] = tok[...].T

    place = seq // 2
    quarter = half_w // 4
    rows_a = half_b // 4
    turns = (1, 2, 3, 0)
    for n in range(2):
        copy_c(n).wait_recv()
        for r in turns:
            total = keep_c[n, place ^ r].astype(f32) + got_c[n, place ^ r].astype(f32)
            for h in range(4):
                outs[r][h, rows_a + n * quarter : rows_a + (n + 1) * quarter, :] = total[
                    h * quarter : (h + 1) * quarter
                ].astype(outs[r].dtype)
    copy_a(chunks - 1).start()
    store[7].start()

    def sum_b(c, carry):
        copy_b(c).wait_recv()
        for g in range(4):
            total = keep_b[c, g].astype(f32) + got_b[c, g].astype(f32)
            for h in range(4):
                split[h, g] = total[h * quarter : (h + 1) * quarter]
        cols = pl.ds(pl.multiple_of(c * width, width), width)
        for r in range(4):
            for g in range(4):
                outs[4 + r][g, :, cols] = split[head ^ r, g].astype(outs[4 + r].dtype)
        return carry

    lax.fori_loop(0, chunks, sum_b, 0)
    for n in (5, 6, 4):
        store[n].start()
    for c in range(chunks):
        copy_a(c).wait_recv()
    for r in turns:
        total = keep_a[place ^ r].astype(f32) + got_a[place ^ r].astype(f32)
        for h in range(4):
            outs[r][h, :rows_a, :] = total[h * rows_a : (h + 1) * rows_a].astype(outs[r].dtype)
        store[r].start()
    for c in range(chunks):
        copy_a(c).wait_send()
        copy_b(c).wait_send()
    for n in range(2):
        copy_c(n).wait_send()
    stay.wait()
    for copy in store:
        copy.wait()

    @pl.when(head < n_head - 1)
    def _():
        up.wait_send()
        down.wait_recv()

    @pl.when(head > 0)
    def _():
        up.wait_recv()
        down.wait_send()


def send_grads(act, gpre, gs, gffn, mid, ctx, gattn, cls, gpool, tok):
    chunks, own, width = act.shape
    half_b, half_w = chunks * width // 8, width // 8
    window = own + 2 * MAXLEN
    shape = jax.ShapeDtypeStruct
    vmem, hbm = pl.BlockSpec(memory_space=pltpu.VMEM), pl.BlockSpec(memory_space=pl.ANY)
    kinds = (f32, bf16, bf16, bf16)
    outs = (
        [shape((4, half_b // 4 + half_w // 2, width), k) for k in kinds]
        + [shape((4, half_w // 4, chunks * width), k) for k in kinds[:2]]
        + [shape((2, 4, half_w // 4, chunks * width), bf16), shape((width, own), bf16)]
    )
    held = (ctx, gattn, mid, gffn, tok, gs)
    gsw, *pieces, tok_t = pl.pallas_call(
        grads_kernel,
        in_specs=[hbm] * 8 + [vmem] * 2,
        out_specs=[hbm] * 9,
        out_shape=[shape((window, width + SIDE), bf16)] + outs,
        scratch_shapes=[pltpu.VMEM(o.shape, o.dtype) for o in [*outs, *held]]
        + [
            pltpu.VMEM((chunks, own, width), bf16),
            pltpu.VMEM((chunks, own, width), bf16),
            pltpu.VMEM((width, own), bf16),
        ]
        + [pltpu.VMEM((chunks, half_b, width), bf16)] * 3
        + [pltpu.VMEM((chunks, 4, half_w, width), bf16)] * 3
        + [pltpu.VMEM((2, 4, half_w, width), bf16)] * 3
        + [
            pltpu.VMEM((4, 4, half_w // 4, width), f32),
            pltpu.SemaphoreType.DMA((2 * chunks,)),
            pltpu.SemaphoreType.DMA((2 * chunks + 2,)),
            pltpu.SemaphoreType.DMA((2 * chunks + 2,)),
            pltpu.SemaphoreType.DMA((5,)),
            pltpu.SemaphoreType.DMA((14,)),
        ],
        compiler_params=pltpu.CompilerParams(
            vmem_limit_bytes=62 * 2**20, collective_id=0, has_side_effects=True
        ),
        cost_estimate=pl.CostEstimate(
            flops=2 * own * width * width * (2 * chunks + 1), bytes_accessed=30 * 2**20, transcendentals=0
        ),
        name="send_grads",
    )(*held, act, gpre, cls, gpool)
    return gsw, tok_t, *pieces


def finish_kernel(n_parts, *refs):
    inputs, refs = refs[:14], refs[14:]
    sends_q = inputs[9]
    gtok, sum_a, sum_b, sum_out, sum_pool, sum_q, sum_v = refs[:7]
    n_held = 11
    held, refs = refs[7 : 7 + n_held], refs[7 + n_held :]
    own_a, near_a, own_b, near_b, vec = held[0], held[1:4], held[4], (held[5], held[6].at[0]), held[7]
    keeps, vec_parts, parts = held[8:]
    (w_qkv, all_a, send_a, got_a, all_b, send_b, got_b, got_f, got_q, own_q, send_n, got_n, all_q, send_z, got_z,
     vecs, got_v, loads, send_sems, recv_sems) = refs
    wanted = inputs[:8] + inputs[10:-1] + (inputs[8], inputs[-1])
    copies = [
        pltpu.make_async_copy(src, dst, loads.at[n])
        for n, (src, dst) in enumerate(zip(wanted, held + (w_qkv, gtok)))
    ]
    for copy in copies:
        copy.start()
    seq, head = lax.axis_index("seq"), lax.axis_index("head")
    place = seq // 2
    width = gtok.shape[1]
    quarter = width // 32
    cols = width // n_parts
    line = (1, 2, 3)
    greet(
        [{"seq": seq ^ OTHER_CORE}]
        + [{"seq": seq ^ near} for near in NEAR]
        + [{"head": head ^ r} for r in line]
    )
    sends = Sends(send_sems, recv_sems)
    for r in line:
        sends.plan(("a", r), send_a.at[r - 1], got_a.at[r - 1], head=head ^ r)
        sends.plan(("b", r), send_b.at[r - 1], got_b.at[r - 1], seq=seq ^ NEAR[r - 1])
    for p in range(n_parts):
        sends.plan(("core", p), sends_q.at[p], got_q.at[p], seq=seq ^ OTHER_CORE)
        for r in line:
            sends.plan(("near", p, r), send_n.at[p, r - 1], got_n.at[p, r - 1], seq=seq ^ NEAR[r - 1])
            sends.plan(("line", p, r), send_z.at[p, r - 1], got_z.at[p, r - 1], head=head ^ r)
    sends.plan(("core", "v"), vecs.at[0], got_v.at[0], seq=seq ^ OTHER_CORE)
    for r in line:
        sends.plan(("near", "v", r), vecs.at[1], got_v.at[r], seq=seq ^ NEAR[r - 1])
        sends.plan(("line", "v", r), vecs.at[2], got_v.at[3 + r], head=head ^ r)
    sends.plan("pass", inputs[6].at[1], got_f, head=head ^ 1)
    sends.start(*[("core", p) for p in range(n_parts)])
    sends.start("pass")

    for copy in copies[:10]:
        copy.wait()
    rows_v = vec.shape[0]
    vecs[0, :rows_v, :] = vec[...]
    for p in range(n_parts):
        vecs[0, rows_v:, p * cols : (p + 1) * cols] = vec_parts[p]
    for h in range(4):
        all_a[h] = (own_a[h] + near_a[0][h].astype(f32)) + (
            near_a[1][h].astype(f32) + near_a[2][h].astype(f32)
        )
    for r in line:
        send_a[r - 1] = all_a[head ^ r].astype(bf16)
    sends.start(("core", "v"))

    def start_near(p):
        sends.start(*[("near", p, r) for r in line])

    for p in range(n_parts):
        sends.arrived(("core", p))
        for r in line:
            for n in range(3):
                send_n[p, r - 1, n] = (
                    keeps[p, n, place ^ r].astype(f32) + got_q[p, n, place ^ r].astype(f32)
                ).astype(bf16)
        for n in range(3):
            own_q[p, n] = keeps[p, n, place].astype(f32) + got_q[p, n, place].astype(f32)
        if p == 0:
            sends.start(*[("a", r) for r in line])
        else:
            start_near(p - 1)
    start_near(n_parts - 1)
    sends.arrived(("core", "v"))
    vecs[1] = vecs[0] + got_v[0]
    sends.arrived("pass")
    for g in range(4):
        all_b[g] = (own_b[g] + near_b[0][g].astype(f32)) + (
            near_b[1][g].astype(f32) + got_f[g].astype(f32)
        )
    for r in line:
        send_b[r - 1] = all_b[place ^ r].astype(bf16)
    for copy in copies[10:]:
        copy.wait()

    def back(n, carry):
        here = pl.ds(pl.multiple_of(n * width, width), width)
        gtok[...] += dot(jnp.concatenate([parts[p, n] for p in range(n_parts)], axis=1), w_qkv[:, here], NT)

        @pl.when(n == 0)
        def _():
            sends.start(*[("near", "v", r) for r in line])
            sends.start(*[("b", r) for r in line])

        return carry

    lax.fori_loop(0, 3, back, 0)

    for p in range(n_parts):
        sends.arrived(*[("near", p, r) for r in line])
        for h in range(4):
            rows = slice(h * quarter, (h + 1) * quarter)
            for n in range(3):
                all_q[p, h, n] = (own_q[p, n, rows, :] + got_n[p, 0, n, rows, :].astype(f32)) + (
                    got_n[p, 1, n, rows, :].astype(f32) + got_n[p, 2, n, rows, :].astype(f32)
                )
        for r in line:
            send_z[p, r - 1] = all_q[p, head ^ r].astype(bf16)
        if p > 0:
            sends.start(*[("line", p - 1, r) for r in line])
    sends.arrived(*[("near", "v", r) for r in line])
    vecs[2] = (vecs[1] + got_v[1]) + (got_v[2] + got_v[3])
    sends.start(*[("line", n_parts - 1, r) for r in line])
    sends.arrived(*[("a", r) for r in line])
    total = (all_a[head] + got_a[0].astype(f32)) + (got_a[1].astype(f32) + got_a[2].astype(f32))
    rows_a = sum_a.shape[0]
    sum_a[...] = total[:rows_a]
    sum_out[...] = total[rows_a : rows_a + quarter]
    sum_pool[...] = total[rows_a + quarter :]
    sends.start(*[("line", "v", r) for r in line])
    sends.arrived(*[("b", r) for r in line])
    sum_b[...] = (all_b[place] + got_b[0].astype(f32)) + (got_b[1].astype(f32) + got_b[2].astype(f32))
    for p in range(n_parts):
        sends.arrived(*[("line", p, r) for r in line])
        for n in range(3):
            at = n * width + p * cols
            sum_q[:, at : at + cols] = (all_q[p, head, n] + got_z[p, 0, n].astype(f32)) + (
                got_z[p, 1, n].astype(f32) + got_z[p, 2, n].astype(f32)
            )
    sends.arrived(*[("line", "v", r) for r in line])
    sum_v[...] = (vecs[2] + got_v[4]) + (got_v[5] + got_v[6])
    sends.drain()


def finish(gar, w_qkv, vec, parts, a, b):
    own, width = gar.shape
    half_w = width // 8
    quarter = half_w // 4
    n_parts = parts[0].shape[0]
    cols = width // n_parts
    rows_z, ff = a[0].shape[1], b[0].shape[2]
    n_vec = vec.shape[0] + 8
    shape = jax.ShapeDtypeStruct
    vmem, hbm = pl.BlockSpec(memory_space=pltpu.VMEM), pl.BlockSpec(memory_space=pl.ANY)
    n_copies = 6 + 7 * n_parts + 7 + 1
    grads, keeps, sends, sums = parts
    held = [*a, *b, vec, keeps, sums, grads]
    return pl.pallas_call(
        functools.partial(finish_kernel, n_parts),
        in_specs=[hbm] * 14,
        out_specs=[vmem] * 7,
        out_shape=[
            shape((own, width), f32),
            shape((rows_z - 2 * quarter, width), f32),
            shape((quarter, ff), f32),
            shape((quarter, width), f32),
            shape((quarter, width), f32),
            shape((quarter, 3 * width), f32),
            shape((n_vec, width), f32),
        ],
        scratch_shapes=[pltpu.VMEM(h.shape, h.dtype) for h in held]
        + [
            pltpu.VMEM(w_qkv.shape, bf16),
            pltpu.VMEM((4, rows_z, width), f32),
            pltpu.VMEM((3, rows_z, width), bf16),
            pltpu.VMEM((3, rows_z, width), bf16),
            pltpu.VMEM((4, quarter, ff), f32),
            pltpu.VMEM((3, quarter, ff), bf16),
            pltpu.VMEM((3, quarter, ff), bf16),
            pltpu.VMEM((4, quarter, ff), bf16),
            pltpu.VMEM((n_parts, 3, 4, half_w, cols), bf16),
            pltpu.VMEM((n_parts, 3, half_w, cols), f32),
            pltpu.VMEM((n_parts, 3, 3, half_w, cols), bf16),
            pltpu.VMEM((n_parts, 3, 3, half_w, cols), bf16),
            pltpu.VMEM((n_parts, 4, 3, quarter, cols), f32),
            pltpu.VMEM((n_parts, 3, 3, quarter, cols), bf16),
            pltpu.VMEM((n_parts, 3, 3, quarter, cols), bf16),
            pltpu.VMEM((3, n_vec, width), f32),
            pltpu.VMEM((7, n_vec, width), f32),
            pltpu.SemaphoreType.DMA((len(held) + 2,)),
            pltpu.SemaphoreType.DMA((n_copies,)),
            pltpu.SemaphoreType.DMA((n_copies,)),
        ],
        compiler_params=pltpu.CompilerParams(
            vmem_limit_bytes=62 * 2**20, collective_id=1, has_side_effects=True
        ),
        cost_estimate=pl.CostEstimate(
            flops=12 * own * width * width, bytes_accessed=12 * 2**20, transcendentals=0
        ),
        name="finish",
    )(*a, *b, vec, w_qkv, sends, keeps, sums, grads, gar)


def halo(rows, left_axis, n_head):
    up = [(i, i + 1) for i in range(n_head - 1)]
    down = [(i + 1, i) for i in range(n_head - 1)]
    from_left = lax.ppermute(rows[-MAXLEN:], left_axis, up)
    from_right = lax.ppermute(rows[:MAXLEN], left_axis, down)
    return jnp.concatenate([from_left, rows, from_right], axis=0)


def pick(values, axis, index):
    return lax.dynamic_index_in_dim(values, index, axis, keepdims=False)


class Sums:
    def __init__(self, pairs, orders, n_seq, n_head, vectors):
        self.count = {"seq": n_seq, "head": n_head}
        self.bits = {"seq": n_seq.bit_length() - 1, "head": n_head.bit_length() - 1}
        self.stages = sum(self.bits.values())
        self.orders = orders
        self.vectors = vectors
        self.axes = [[n for n in range(self.stages) if n != self.bits["seq"] - 1] for _ in pairs]
        shape = lambda a: a.reshape(
            (2,) * (self.stages - 1) + (a.shape[1] // n_head,) + a.shape[2:]
        )
        self.kept = [shape(keep) for keep, _ in pairs]
        self.sent = [shape(send) for _, send in pairs]
        self.stage = 0
        self.send()

    def send(self):
        self.got = [
            self.swap(v, *self.orders[n][self.stage]) for n, v in enumerate(self.sent)
        ]
        self.vectors = self.vectors + self.swap(self.vectors, *self.orders[0][self.stage])

    def swap(self, values, name, bit):
        return lax.ppermute(values, name, [(i, i ^ (1 << bit)) for i in range(self.count[name])])

    def split(self):
        self.stage += 1
        kept, sent = [], []
        for n, (keep, got) in enumerate(zip(self.kept, self.got)):
            name, bit = self.orders[n][self.stage]
            where = (self.stages if name == "head" else self.bits["seq"]) - 1 - bit
            at = self.axes[n].index(where)
            self.axes[n].pop(at)
            mine = (lax.axis_index(name) >> bit) & 1
            half = lambda m: pick(keep, at, m).astype(f32) + pick(got, at, m).astype(f32)
            sent.append(half(1 - mine).astype(bf16))
            kept.append(half(mine))
        self.kept, self.sent = kept, sent

    def rest(self):
        while self.stage < self.stages - 1:
            self.split()
            self.send()
        return [k.astype(f32) + g.astype(f32) for k, g in zip(self.kept, self.got)]


def after(value, *others):
    return lax.optimization_barrier((value, *others))[0]


def orders(n_seq, n_head):
    seq_bits, head_bits = n_seq.bit_length() - 1, n_head.bit_length() - 1
    core = [("seq", 0)]
    planar = [("seq", b) for b in range(1, seq_bits)]
    along = [("head", b) for b in range(head_bits)]
    return (
        core + planar + along,
        core + planar[::-1] + along,
        core + along + planar,
    )


def local(
    tokens, cotangent, lengths, labels, w_qkv, b_query, b_value, w_out, b_out, gain_attn,
    shift_attn, w_in, b_in, w_back, b_back, gain_ffn, shift_ffn, w_pool, b_pool, w_class,
):
    n_head = lax.axis_size("head")
    n_seq = lax.axis_size("seq")
    head_index = lax.axis_index("head")
    own, width = tokens.shape
    window = own + 2 * MAXLEN
    group = own * n_head

    vectors = (b_out, gain_attn, shift_attn, b_back, gain_ffn, shift_ffn, b_pool, b_query, b_value)
    small = jnp.concatenate([*vectors, jnp.zeros((-9 * width % 1024,), f32)]).reshape(1, -1)
    if (n_seq, n_head) == (8, 4):
        qkv, hot, mask, bounds, seqs_of = front(tokens, w_qkv, small, lengths, labels)
    else:
        seq_lengths = lengths[0]
        ends = jnp.cumsum(seq_lengths)
        starts = ends - seq_lengths
        base = head_index * own - MAXLEN
        pos = base + jnp.arange(window, dtype=jnp.int32)
        n_in_group = seq_lengths.shape[0]
        lane_pad = (0, SIDE - n_in_group)
        starts_w = jnp.pad(starts, lane_pad, constant_values=group + MAXLEN)
        ends_w = jnp.pad(ends, lane_pad, constant_values=-MAXLEN)
        inside = (starts_w[None, :] <= pos[:, None]) & (pos[:, None] < ends_w[None, :])
        hot = inside.astype(bf16)
        lane = jnp.arange(SIDE, dtype=jnp.int32)[None, :]
        mask = jnp.where(lane < n_in_group, jnp.where(inside, 0.0, -BIG), 1.0).astype(bf16)
        mask = jnp.concatenate(
            [mask, jnp.broadcast_to(jnp.where(lane < n_in_group, -BIG, 1.0).astype(bf16), (PAD, SIDE))]
        )
        blk = base + QBLK * jnp.arange(window // QBLK, dtype=jnp.int32)
        low = jnp.max(jnp.where(starts[None, :] <= blk[:, None], starts[None, :], -1), axis=1)
        high = jnp.min(
            jnp.where(ends[None, :] > blk[:, None] + QBLK - 1, ends[None, :], group), axis=1
        )
        is_own = (blk >= base + MAXLEN) & (blk < base + MAXLEN + own)
        low = jnp.where(is_own, low - base, jnp.maximum(low - base, MAXLEN))
        high = jnp.where(is_own, high - base, jnp.minimum(high - base, MAXLEN + own))
        valid = (blk >= 0) & (blk < group)
        low = low // 128 * 128
        steps = jnp.where(valid, jnp.maximum((high - low + KCHUNK - 1) // KCHUNK, 0), 0)
        bounds = jnp.stack([low, steps], axis=1).astype(jnp.int32)
        seq_pad = (0, -n_in_group % 16)
        seqs_of = jnp.stack(
            [jnp.pad(starts, seq_pad, constant_values=-1), jnp.pad(labels[0], seq_pad)], axis=1
        )
        tokens_w = halo(tokens, "head", n_head)
        bias = jnp.concatenate([b_query, jnp.zeros_like(b_query), b_value])[None, :]
        qscale = jnp.where(jnp.arange(3 * width) < width, HEAD_DIM**-0.5, 1.0).astype(f32)[None, :]
        qkv = ((dot(tokens_w, w_qkv, NN) + bias) * qscale).astype(bf16)
    context, lse = attend(bounds, qkv, hot, mask, own)

    shards = n_seq * n_head
    shard = head_index + n_head * lax.axis_index("seq")
    core = (lax.axis_index("seq") & 1).reshape(1)
    (output, gar, gs, act, gpre, gffn, mid, gattn, cls, gpool, vec) = middle_layer(
        2 * fold_of(width // PAIR, 3), head_index.reshape(1), w_in, w_back, w_pool, tokens, context, lse,
        cotangent, w_out, b_in.reshape(1, -1), w_class.T, small, seqs_of,
    )
    if (n_seq, n_head) == (8, 4):
        grads_w, tok_t, *pieces = send_grads(act, gpre, gs, gffn, mid, context, gattn, cls, gpool, tokens)
        to = lambda v, axis, count, x: lax.ppermute(v, axis, [(i, i ^ x) for i in range(count)])
        a = [pieces[0]] + [to(pieces[r], "seq", 8, NEAR[r - 1]) for r in (1, 2, 3)]
        b = [pieces[4], to(pieces[5], "head", 4, 1), to(pieces[6], "head", 4, 2)]
        gqkv = attend_back(bounds, qkv, grads_w, hot, mask, own, (tok_t, core))
        grad_tokens, sum_wback, sum_win, sum_wout, sum_pool, sum_wqkv, summed = finish(
            gar, w_qkv, vec, gqkv, a, b
        )
    else:
        grads_w = halo(gs, "head", n_head)

        pieces = weight_grads(core, n_seq, act, gpre, gffn, mid, context, gattn, cls, gpool)
        orders_all = orders(n_seq, n_head)
        first = Sums(
            [pieces[0:2], pieces[2:4], pieces[4:6]], orders_all, n_seq, n_head, vec
        )
        gqkv = attend_back(bounds, qkv, grads_w, hot, mask, own)
        last_out = last_layer(core, n_seq, tokens, gar, w_qkv, list(gqkv))
        grad_tokens, vec_qkv = last_out[:2]
        last = Sums(
            [last_out[2:4], last_out[4:6], last_out[6:8]], orders_all, n_seq, n_head, vec_qkv
        )
        sum_wback, sum_win, sum_c = first.rest()
        sum_wout, sum_pool = sum_c[:, :width], sum_c[:, width:]
        sum_q, sum_k, sum_v = last.rest()
        sum_wqkv = jnp.concatenate([sum_q, sum_k, sum_v], axis=1)

        summed = jnp.concatenate([first.vectors, last.vectors])
    size = width // shards
    chunks = w_in.shape[1] // width
    n_class = w_class.shape[1]
    n_vec = vec.shape[0]
    mine = lax.dynamic_slice(summed, (0, shard * size), (summed.shape[0], size))
    row_shards = shards // chunks
    grad_bin = lax.dynamic_slice(
        summed, (8 + shard // row_shards, shard % row_shards * (size * chunks)), (1, size * chunks)
    )[0]
    grad_class = mine[8 + chunks : 8 + chunks + n_class].T
    entropy_mean = summed[7, 0] / (n_seq * labels.shape[1])
    return (
        output, grad_tokens, sum_wqkv, mine[n_vec], mine[n_vec + 2], sum_wout, mine[0], mine[1], mine[2],
        sum_win, grad_bin, sum_wback, mine[3], mine[4], mine[5], sum_pool, mine[6], grad_class,
        entropy_mean,
    )


def solution(mesh):
    rows = P(("seq", "head"), None)
    vec = P(("seq", "head"))
    return jax.shard_map(
        local,
        mesh=mesh,
        in_specs=(rows, rows, P("seq", None), P("seq", None)) + (P(),) * 16,
        out_specs=(
            rows, rows, rows, vec, vec, rows, vec, vec, vec, rows, vec, rows, vec, vec, vec, rows,
            vec, rows, P(),
        ),
        check_vma=False,
    )
```

```python
import functools

import jax
import jax.numpy as jnp
from jax import lax
from jax.experimental import pallas as pl
from jax.experimental.pallas import tpu as pltpu
from jax.sharding import PartitionSpec as P

HEAD_DIM = 64
MAXLEN = 512
PAIR = 2 * HEAD_DIM
QBLK = 128
KCHUNK = 256
PAD = KCHUNK - 128
LSE0 = 32
SIDE = 128

eps = 1e-05
BIG = 1e30
highest = lax.Precision.HIGHEST
f32 = jnp.float32
bf16 = jnp.bfloat16
NT = (((1,), (1,)), ((), ()))
NN = (((1,), (0,)), ((), ()))
TN = (((0,), (0,)), ((), ()))


def dot(left, right, dims):
    return lax.dot_general(left, right, dims, preferred_element_type=f32)


def pair_rows(rows, side):
    lane = lax.broadcasted_iota(jnp.int32, rows.shape, 1)
    zero = jnp.zeros_like(rows)
    first = jnp.where(lane < HEAD_DIM, rows, zero)
    second = jnp.where(lane >= HEAD_DIM, rows, zero)
    return jnp.concatenate(
        [jnp.concatenate([first, side[0]], axis=1), jnp.concatenate([second, side[1]], axis=1)],
        axis=0,
    )


def unpair(both):
    row = lax.broadcasted_iota(jnp.int32, (PAIR, QBLK), 0)
    return jnp.where(row < HEAD_DIM, both[:, :QBLK], both[:, QBLK:])


def attend_kernel(bounds, q_ref, k_ref, v_ref, hot_ref, mask_ref, ctx_ref, lse_ref, kcat, vt):
    window = k_ref.shape[0]
    own = ctx_ref.shape[0]
    fold = kcat.shape[0]
    skip = MAXLEN // QBLK

    @pl.when(pl.program_id(0) == 0)
    def _():
        for j in range(fold):
            kcat[j, :, PAIR:] = mask_ref[...]
            kcat[j, pl.ds(window, PAD), :PAIR] = jnp.zeros((PAD, PAIR), bf16)
            vt[j, :, pl.ds(window, PAD)] = jnp.zeros((PAIR, PAD), bf16)

    lse_ref[...] = jnp.zeros_like(lse_ref)
    for j in range(fold):
        cols = pl.ds(j * PAIR, PAIR)
        kcat[j, pl.ds(0, window), :PAIR] = k_ref[:, cols]
        for at in range(0, window, 256):
            vt[j, :, pl.ds(at, 256)] = v_ref[pl.ds(at, 256), cols].T

    def block(i, carry):
        row0 = pl.multiple_of(i * QBLK, QBLK)
        hot = hot_ref[pl.ds(MAXLEN + row0, QBLK), :]
        rows = q_ref[pl.ds(MAXLEN + row0, QBLK), :]
        qcat = [pair_rows(rows[:, j * PAIR : (j + 1) * PAIR], (hot, hot)) for j in range(fold)]
        first = bounds[skip + i, 0]

        def step(c, state):
            start = pl.multiple_of(first + c * KCHUNK, 128)
            scores = [dot(kcat[j, pl.ds(start, KCHUNK), :], qcat[j], NT) for j in range(fold)]
            out = []
            for j, s in enumerate(scores):
                peak, total, acc = state[j]
                new_peak = jnp.maximum(peak, jnp.max(s, axis=0, keepdims=True))
                scale = jnp.exp(peak - new_peak)
                p = jnp.exp(s - new_peak)
                total = total * scale + jnp.sum(p, axis=0, keepdims=True)
                acc = acc * scale + dot(vt[j, :, pl.ds(start, KCHUNK)], p.astype(bf16), NN)
                out.append((new_peak, total, acc))
            return tuple(out)

        empty = (
            jnp.full((1, 2 * QBLK), -BIG, f32),
            jnp.zeros((1, 2 * QBLK), f32),
            jnp.zeros((PAIR, 2 * QBLK), f32),
        )
        state = lax.fori_loop(0, bounds[skip + i, 1], step, (empty,) * fold)
        for j, (peak, total, acc) in enumerate(state):
            ctx_ref[pl.ds(row0, QBLK), pl.ds(j * PAIR, PAIR)] = unpair(acc / total).T.astype(bf16)
            lse = peak + jnp.log(total)
            lse_ref[2 * j : 2 * j + 1, pl.ds(row0, QBLK)] = lse[:, :QBLK]
            lse_ref[2 * j + 1 : 2 * j + 2, pl.ds(row0, QBLK)] = lse[:, QBLK:]
        return carry

    lax.fori_loop(0, own // QBLK, block, 0)


def fold_of(pairs, most):
    return max(n for n in range(1, most + 1) if pairs % n == 0)


def attend(bounds, qkv, hot, mask, own):
    window, wide = qkv.shape
    width = wide // 3
    pairs = width // PAIR
    fold = fold_of(pairs, 3)
    parts = pairs // fold
    column = lambda part: pl.BlockSpec((window, fold * PAIR), lambda g, b: (0, part * parts + g))
    whole = lambda a: pl.BlockSpec(a.shape, lambda g, b: (0, 0))
    return pl.pallas_call(
        attend_kernel,
        grid_spec=pltpu.PrefetchScalarGridSpec(
            num_scalar_prefetch=1,
            grid=(parts,),
            in_specs=[column(0), column(1), column(2), whole(hot), whole(mask)],
            out_specs=[
                pl.BlockSpec((own, fold * PAIR), lambda g, b: (0, g)),
                pl.BlockSpec((8, own), lambda g, b: (g, 0)),
            ],
            scratch_shapes=[
                pltpu.VMEM((fold, window + PAD, 2 * PAIR), bf16),
                pltpu.VMEM((fold, PAIR, window + PAD), bf16),
            ],
        ),
        out_shape=[
            jax.ShapeDtypeStruct((own, width), bf16),
            jax.ShapeDtypeStruct((8 * parts, own), f32),
        ],
        cost_estimate=pl.CostEstimate(
            flops=own * 600 * width * 4, bytes_accessed=window * wide * 2, transcendentals=0
        ),
        name="attend",
    )(bounds, qkv, qkv, qkv, hot, mask)


def attend_back_kernel(side0, more, bounds, q_ref, k_ref, v_ref, do_ref, side_ref, hot_ref, mask_ref, *refs):
    extra, refs = refs[:more], refs[more:]
    gqkv_ref, (kcat, vcat, kt, dk, dv) = refs[0].at[0], refs[-5:]
    window = k_ref.shape[0]
    own = gqkv_ref.shape[1]
    fold = kcat.shape[0]
    lanes, gap = side0
    part = pl.program_id(0)
    low0 = LSE0 + lanes * part

    @pl.when(part == 0)
    def _():
        for j in range(fold):
            kcat[j, :, PAIR:] = mask_ref[...]
            vcat[j, :, PAIR:] = jnp.ones((window + PAD, SIDE), bf16)
            kcat[j, pl.ds(window, PAD), :PAIR] = jnp.zeros((PAD, PAIR), bf16)
            vcat[j, pl.ds(window, PAD), :PAIR] = jnp.zeros((PAD, PAIR), bf16)
            kt[j, :, pl.ds(window, PAD)] = jnp.zeros((PAIR, PAD), bf16)

    for j in range(fold):
        cols = pl.ds(j * PAIR, PAIR)
        kcat[j, pl.ds(0, window), :PAIR] = k_ref[:, cols]
        vcat[j, pl.ds(0, window), :PAIR] = v_ref[:, cols]
        for at in range(0, window, 256):
            kt[j, :, pl.ds(at, 256)] = k_ref[pl.ds(at, 256), cols].T
    dk[...] = jnp.zeros_like(dk)
    dv[...] = jnp.zeros_like(dv)
    lane = lax.broadcasted_iota(jnp.int32, (QBLK, SIDE), 1)

    def side_lanes(side, first):
        return jnp.where((lane >= first) & (lane < first + 3), side, jnp.zeros_like(side))

    def block(i, carry):
        row0 = pl.multiple_of(i * QBLK, QBLK)
        hot = hot_ref[pl.ds(row0, QBLK), :]
        side = side_ref[pl.ds(row0, QBLK), :]
        rows = q_ref[pl.ds(row0, QBLK), :]
        grads = do_ref[pl.ds(row0, QBLK), :]
        qcat, docat = [], []
        for j in range(fold):
            cols = slice(j * PAIR, (j + 1) * PAIR)
            low = low0 + 6 * j
            qcat.append(
                pair_rows(
                    rows[:, cols],
                    (hot + side_lanes(side, low), hot + side_lanes(side, low + 3)),
                )
            )
            docat.append(
                pair_rows(
                    grads[:, cols],
                    (side_lanes(side, low + gap), side_lanes(side, low + gap + 3)),
                )
            )
        first = bounds[i, 0]

        def step(c, dq):
            start = pl.multiple_of(first + c * KCHUNK, 128)
            here = pl.ds(start, KCHUNK)
            scores = [dot(kcat[j, here, :], qcat[j], NT) for j in range(fold)]
            slopes = [dot(vcat[j, here, :], docat[j], NT) for j in range(fold)]
            out = []
            for j in range(fold):
                p = jnp.exp(scores[j])
                ds = (p * slopes[j]).astype(bf16)
                dv[j, here, :] += dot(p.astype(bf16), docat[j][:, :PAIR], NN)
                dk[j, here, :] += dot(ds, qcat[j][:, :PAIR], NN)
                out.append(dq[j] + dot(kt[j, :, here], ds, NN))
            return tuple(out)

        dq = lax.fori_loop(
            0, bounds[i, 1], step, (jnp.zeros((PAIR, 2 * QBLK), f32),) * fold
        )

        @pl.when((i >= MAXLEN // QBLK) & (i < (MAXLEN + own) // QBLK))
        def _():
            for j in range(fold):
                gqkv_ref[
                    0, pl.ds(pl.multiple_of(row0 - MAXLEN, QBLK), QBLK), pl.ds(j * PAIR, PAIR)
                ] = (unpair(dq[j]) * HEAD_DIM**-0.5).T.astype(bf16)

        return carry

    lax.fori_loop(0, window // QBLK, block, 0)
    for j in range(fold):
        cols = pl.ds(j * PAIR, PAIR)
        gqkv_ref[1, :, cols] = dk[j, pl.ds(MAXLEN, own), :].astype(bf16)
        gqkv_ref[2, :, cols] = dv[j, pl.ds(MAXLEN, own), :].astype(bf16)

    if more:
        tok_t, place = extra[:2]
        keep, send, sums = (ref.at[0] for ref in refs[1:4])
        sums[...] = jnp.zeros_like(sums)

        def third(n, carry):
            grads = gqkv_ref[n]
            sums[pl.ds(n, 1), :] = col_sum(grads.astype(f32))
            mine, theirs = halves(dot(tok_t[...], grads, NN), place[0], keep.shape[2])
            for g in range(len(mine)):
                keep[n, g] = mine[g]
                send[n, g] = theirs[g]
            return carry

        lax.fori_loop(0, 3, third, 0)


def attend_back(bounds, qkv, grads, hot, mask, own, extra=()):
    window, wide = qkv.shape
    width = wide // 3
    pairs = width // PAIR
    fold = fold_of(pairs, 2)
    parts = pairs // fold
    cols = fold * PAIR
    column = lambda c: pl.BlockSpec((window, cols), lambda g, b: (0, c * parts + g))
    whole = lambda a: pl.BlockSpec(a.shape, lambda g, b: (0, 0))
    shape = jax.ShapeDtypeStruct
    more_in, more_out = [], []
    if extra:
        more_in = [whole(extra[0]), pl.BlockSpec(memory_space=pltpu.SMEM)]
        more_out = [shape((parts, 3, 4, width // 8, cols), bf16)] * 2 + [shape((parts, 8, cols), f32)]
    block = lambda a: pl.BlockSpec((1,) + a.shape[1:], lambda g, b: (g,) + (0,) * (len(a.shape) - 1))
    outs = [shape((parts, 3, own, cols), bf16)] + more_out
    results = pl.pallas_call(
        functools.partial(attend_back_kernel, (6 * fold, 6 * pairs), len(extra)),
        grid_spec=pltpu.PrefetchScalarGridSpec(
            num_scalar_prefetch=1,
            grid=(parts,),
            in_specs=[
                column(0),
                column(1),
                column(2),
                pl.BlockSpec((window, cols), lambda g, b: (0, g)),
                pl.BlockSpec((window, SIDE), lambda g, b: (0, pairs)),
                whole(hot),
                whole(mask),
            ]
            + more_in,
            out_specs=[block(o) for o in outs],
            scratch_shapes=[
                pltpu.VMEM((fold, window + PAD, 2 * PAIR), bf16),
                pltpu.VMEM((fold, window + PAD, 2 * PAIR), bf16),
                pltpu.VMEM((fold, PAIR, window + PAD), bf16),
                pltpu.VMEM((fold, window + PAD, PAIR), f32),
                pltpu.VMEM((fold, window + PAD, PAIR), f32),
            ],
        ),
        out_shape=outs,
        cost_estimate=pl.CostEstimate(
            flops=own * 900 * width * 16, bytes_accessed=window * width * 8, transcendentals=0
        ),
        name="attend_back",
    )(bounds, qkv, qkv, qkv, grads, grads, hot, mask, *extra)
    return results if extra else results[0]


def low3(values):
    high = values.astype(bf16)
    rest = values - high.astype(f32)
    mid = rest.astype(bf16)
    return high, mid, (rest - mid.astype(f32)).astype(bf16)


def dot3(values, chosen, dims):
    return sum(dot(part, chosen, dims) for part in low3(values))


def iota(shape, axis):
    return lax.broadcasted_iota(jnp.int32, shape, axis)


def mean_row(values):
    return jnp.mean(values, axis=-1, keepdims=True)


def col_sum(values):
    return jnp.sum(values, axis=0, keepdims=True)


def norm_back(grad_out, normed, inv_std, gain_vec):
    grad_norm = grad_out * gain_vec
    inner = grad_norm - mean_row(grad_norm) - normed * mean_row(grad_norm * normed)
    return inv_std * inner, col_sum(grad_out * normed), col_sum(grad_out)


ROWS = 256
VECTORS = 24


def middle_kernel(
    heads_part, place, w_in_hbm, w_back_hbm, w_pool_hbm, lse_hbm, cot_hbm, tok, ctx, w_out, b_in, w_class, seqs_of, *refs,
):
    vectors, refs = refs[:7], refs[7:]
    (out_hbm, gar_hbm, gs_hbm, act_hbm, gpre_hbm, gffn_hbm, mid_hbm, gattn_hbm, cls, gpool, vec,
    out, gar, gs, gffn, mid, gattn, lse, cot, more_sems, w_in, w_back, w_pool, act, gpre, slope, unit_a, unit_f, inv_a, inv_f, acc, sems) = refs
    own, width = tok.shape
    b_out, gain_a, shift_a, b_back, gain_f, shift_f, b_pool = (v[...].reshape(1, -1) for v in vectors)
    starts, labels = seqs_of[:, 0:1], seqs_of[:, 1:2]
    chunks, _, wide = act.shape
    blocks = own // ROWS
    n_class = w_class.shape[0]
    loads = [
        pltpu.make_async_copy(w_in_hbm, w_in, sems.at[0]),
        pltpu.make_async_copy(w_back_hbm, w_back, sems.at[1]),
        pltpu.make_async_copy(w_pool_hbm, w_pool, sems.at[2]),
        pltpu.make_async_copy(cot_hbm, cot, more_sems.at[0]),
        pltpu.make_async_copy(lse_hbm, lse, more_sems.at[1]),
    ]
    store_mid, store_out, store_gffn = (
        pltpu.make_async_copy(src, dst, more_sems.at[2 + n])
        for n, (src, dst) in enumerate(((mid, mid_hbm), (out, out_hbm), (gffn, gffn_hbm)))
    )

    def last_stores(b):
        return [
            pltpu.make_async_copy(src.at[at(b)], dst.at[at(b)], more_sems.at[5 + 3 * b + n])
            for n, (src, dst) in enumerate(((gar, gar_hbm), (gs, gs_hbm), (gattn, gattn_hbm)))
        ]

    for load in loads:
        load.start()

    def at(b):
        return pl.ds(pl.multiple_of(b * ROWS, ROWS), ROWS)

    def cols(c):
        return pl.ds(pl.multiple_of(c * wide, wide), wide)

    def norm(hidden, rows, unit, inv, gain, shift):
        centred = hidden - mean_row(hidden)
        inv_std = lax.rsqrt(mean_row(centred * centred) + eps)
        normed = centred * inv_std
        unit[rows, :] = normed
        inv[rows, :] = inv_std
        return (normed * gain[...] + shift[...]).astype(bf16)

    def first_norm(b, carry):
        rows = at(b)
        hidden = tok[rows, :].astype(f32) + dot(ctx[rows, :], w_out[...], NN) + b_out[...]
        mid[rows, :] = norm(hidden, rows, unit_a, inv_a, gain_a, shift_a)
        return carry

    lax.fori_loop(0, blocks, first_norm, 0)
    store_mid.start()
    loads[0].wait()
    loads[1].wait()
    acc[...] = jnp.zeros_like(acc)

    def forward(c, carry):
        for b in range(blocks):
            rows = slice(b * ROWS, (b + 1) * ROWS)
            pre = dot(mid[rows, :], w_in[:, cols(c)], NN) + b_in[:, cols(c)]
            cdf = 0.5 * (1.0 + lax.erf(pre * (0.5**0.5)))
            low = (pre * cdf).astype(bf16)
            act[c, rows, :] = low
            slope[c, rows, :] = cdf + pre * (jnp.exp(-0.5 * pre * pre) * 0.3989422804014327)
            acc[rows, :] += dot(low, w_back[cols(c), :], NN)
        pltpu.make_async_copy(act.at[c], act_hbm.at[c], sems.at[3 + c]).start()
        return carry

    lax.fori_loop(0, chunks, forward, 0)

    def second_norm(b, carry):
        rows = at(b)
        hidden = mid[rows, :].astype(f32) + (acc[rows, :] + b_back[...])
        out[rows, :] = norm(hidden, rows, unit_f, inv_f, gain_f, shift_f)
        return carry

    lax.fori_loop(0, blocks, second_norm, 0)
    store_out.start()
    loads[3].wait()
    loads[4].wait()

    loads[2].wait()
    seqs = starts.shape[0]
    picked = (iota((seqs, own), 1) + place[0] * own == starts[...]).astype(f32)
    sel = picked.astype(bf16)
    owned = jnp.sum(picked, axis=1, keepdims=True)
    cls_low = dot(sel, out[...], NN).astype(bf16)
    cls[...] = cls_low
    pooled = jnp.tanh(dot(cls_low, w_pool[...], NN) + b_pool[...])
    logits = [jnp.sum(pooled * w_class[c : c + 1, :], axis=1, keepdims=True) for c in range(n_class)]
    peak = functools.reduce(jnp.maximum, logits)
    expo = [jnp.exp(x - peak) for x in logits]
    total = sum(expo)
    probs = [x / total for x in expo]
    terms = owned * (peak + jnp.log(total) - sum(p * x for p, x in zip(probs, logits)))
    entropy = jnp.sum(terms, axis=0, keepdims=True)
    g_logits = [
        (probs[c] - (labels[...] == c).astype(f32)) * owned for c in range(n_class)
    ]
    g_pooled = sum(g_logits[c] * w_class[c : c + 1, :] for c in range(n_class))
    g_low = (g_pooled * (1.0 - pooled * pooled)).astype(bf16)
    gpool[...] = g_low
    grad_cls = dot(g_low, w_pool[...], NT)

    def second_back(b, carry):
        rows = at(b)
        here = (
            iota((seqs, ROWS), 1) + (place[0] * own + b * ROWS) == starts[...]
        ).astype(f32).astype(bf16)
        back = sum(dot(here, part, TN) for part in low3(grad_cls))
        grad_out = cot[rows, :].astype(f32) + back
        res, g_gain, g_shift = norm_back(grad_out, unit_f[rows, :], inv_f[rows, :], gain_f[...])
        low = res.astype(bf16)
        gar[rows, :] = res
        gffn[rows, :] = low
        return carry[0] + g_gain, carry[1] + g_shift, carry[2] + col_sum(low.astype(f32))

    zero = jnp.zeros((1, width), f32)
    sums_f = lax.fori_loop(0, blocks, second_back, (zero, zero, zero))
    store_gffn.start()
    acc[...] = jnp.zeros_like(acc)

    def backward(c, carry):
        g_b_in = jnp.zeros((1, wide), f32)
        for b in range(blocks):
            rows = slice(b * ROWS, (b + 1) * ROWS)
            grad_act = dot(gffn[rows, :], w_back[cols(c), :], NT)
            low = (grad_act * slope[c, rows, :]).astype(bf16)
            gpre[c, rows, :] = low
            g_b_in += col_sum(low.astype(f32))
            acc[rows, :] += dot(low, w_in[:, cols(c)], NT)
        vec[pl.ds(8 + c, 1), :] = g_b_in
        pltpu.make_async_copy(gpre.at[c], gpre_hbm.at[c], sems.at[3 + chunks + c]).start()
        return carry

    lax.fori_loop(0, chunks, backward, 0)

    heads = width // HEAD_DIM
    lane = iota((1, SIDE), 1)
    gap = LSE0 + 3 * heads
    feature, flane = iota((width, SIDE), 0), iota((width, SIDE), 1)
    third = flane - gap - 3 * (feature // HEAD_DIM)
    head_sum = ((third >= 0) & (third < 3)).astype(f32).astype(bf16)
    lrow, llane = iota((lse.shape[0], SIDE), 0), iota((lse.shape[0], SIDE), 1)
    lhead = (lrow // 8) * heads_part + lrow % 8
    spread = [
        ((llane == LSE0 + 3 * lhead + p) & (lrow % 8 < heads_part)).astype(f32).astype(bf16)
        for p in range(3)
    ]
    which = lax.rem(lane - gap + 3 * heads, 3)

    def first_back(b, carry):
        rows = at(b)
        grad_mid = gar[rows, :] + acc[rows, :]
        res, g_gain, g_shift = norm_back(grad_mid, unit_a[rows, :], inv_a[rows, :], gain_a[...])
        low = res.astype(bf16)
        gar[rows, :] = res
        gattn[rows, :] = low
        grad_ctx = dot(low, w_out[...], NT).astype(bf16)
        gs[rows, :width] = grad_ctx
        delta = dot3(grad_ctx.astype(f32) * ctx[rows, :].astype(f32), head_sum, NN)
        high, mid_part, rest = low3(-delta)
        side = jnp.where(which == 0, high, jnp.where(which == 1, mid_part, rest))
        lse_parts = low3(-lse[:, rows])
        side_lse = sum(dot(part, spread[p], TN) for p, part in enumerate(lse_parts))
        gs[rows, width:] = side + side_lse.astype(bf16)
        for copy in last_stores(b):
            copy.start()
        return carry[0] + g_gain, carry[1] + g_shift, carry[2] + col_sum(low.astype(f32))

    sums_a = lax.fori_loop(0, blocks, first_back, (zero, zero, zero))
    for row, value in enumerate((sums_a[2], sums_a[0], sums_a[1], sums_f[2], sums_f[0], sums_f[1])):
        vec[row : row + 1, :] = value
    vec[6:7, :] = col_sum(g_low.astype(f32))
    vec[7:8, :] = jnp.broadcast_to(entropy, (1, width))
    for c in range(n_class):
        vec[8 + chunks + c : 9 + chunks + c, :] = col_sum(pooled * g_logits[c])
    done = 8 + chunks + n_class
    vec[done:, :] = jnp.zeros((VECTORS - done, width), f32)
    for c in range(chunks):
        pltpu.make_async_copy(act.at[c], act_hbm.at[c], sems.at[3 + c]).wait()
        pltpu.make_async_copy(gpre.at[c], gpre_hbm.at[c], sems.at[3 + chunks + c]).wait()
    for copy in (store_mid, store_out, store_gffn):
        copy.wait()
    for b in range(blocks):
        for copy in last_stores(b):
            copy.wait()


def middle_layer(heads_part, place, w_in, w_back, w_pool, tok, ctx, lse, cot, w_out, b_in, w_class, seqs_of, vectors):
    own, width = tok.shape
    ff = w_in.shape[1]
    chunks = ff // width
    seqs = seqs_of.shape[0]
    vmem = pl.BlockSpec(memory_space=pltpu.VMEM)
    hbm = pl.BlockSpec(memory_space=pl.ANY)
    shape = jax.ShapeDtypeStruct
    flops = 2 * own * width * (6 * width + 4 * ff)
    return pl.pallas_call(
        functools.partial(middle_kernel, heads_part),
        in_specs=[pl.BlockSpec(memory_space=pltpu.SMEM)] + [hbm] * 5 + [vmem] * 13,
        out_specs=[hbm] * 8 + [vmem] * 3,
        out_shape=[
            shape((own, width), bf16),
            shape((own, width), f32),
            shape((own, width + SIDE), bf16),
            shape((chunks, own, width), bf16),
            shape((chunks, own, width), bf16),
            shape((own, width), bf16),
            shape((own, width), bf16),
            shape((own, width), bf16),
            shape((seqs, width), bf16),
            shape((seqs, width), bf16),
            shape((VECTORS, width), f32),
        ],
        scratch_shapes=[
            pltpu.VMEM((own, width), bf16),
            pltpu.VMEM((own, width), f32),
            pltpu.VMEM((own, width + SIDE), bf16),
            pltpu.VMEM((own, width), bf16),
            pltpu.VMEM((own, width), bf16),
            pltpu.VMEM((own, width), bf16),
            pltpu.VMEM(lse.shape, f32),
            pltpu.VMEM(cot.shape, bf16),
            pltpu.SemaphoreType.DMA((5 + 3 * (own // ROWS),)),
            pltpu.VMEM(w_in.shape, bf16),
            pltpu.VMEM(w_back.shape, bf16),
            pltpu.VMEM(w_pool.shape, bf16),
            pltpu.VMEM((chunks, own, width), bf16),
            pltpu.VMEM((chunks, own, width), bf16),
            pltpu.VMEM((chunks, own, width), f32),
            pltpu.VMEM((own, width), f32),
            pltpu.VMEM((own, width), f32),
            pltpu.VMEM((own, 1), f32),
            pltpu.VMEM((own, 1), f32),
            pltpu.VMEM((own, width), f32),
            pltpu.SemaphoreType.DMA((3 + 2 * chunks,)),
        ],
        compiler_params=pltpu.CompilerParams(vmem_limit_bytes=62 * 2**20),
        cost_estimate=pl.CostEstimate(flops=flops, bytes_accessed=30 * 2**20, transcendentals=0),
        name="middle_layer",
    )(place, w_in, w_back, w_pool, lse, cot, tok, ctx, w_out, b_in, w_class, seqs_of, *vectors)


def split_core(tile, core, half, keep, send, first):
    for n in range(tile.shape[0] // (2 * half)):
        even = tile[2 * n * half : (2 * n + 1) * half, :]
        odd = tile[(2 * n + 1) * half : (2 * n + 2) * half, :]
        keep[first + n, :, :] = jnp.where(core == 0, even, odd).astype(bf16)
        send[first + n, :, :] = jnp.where(core == 0, odd, even).astype(bf16)


def weight_grads_kernel(
    core, act, gpre, gffn, mid, ctx, gattn, cls, gpool,
    back_keep, back_send, in_keep, in_send, out_keep, out_send, mid_t,
):
    y = pl.program_id(0)

    @pl.when(y == 0)
    def _():
        mid_t[...] = mid[...].T
        split_core(dot(ctx[...], gattn[...], TN), core[0], out_keep.shape[1], out_keep, out_send, 0)

    @pl.when(y == 1)
    def _():
        split_core(dot(cls[...], gpool[...], TN), core[0], out_keep.shape[1], out_keep, out_send, 0)

    split_core(dot(act[0], gffn[...], TN), core[0], back_keep.shape[1], back_keep, back_send, 0)
    split_core(dot(mid_t[...], gpre[0], NN), core[0], in_keep.shape[1], in_keep, in_send, 0)


def weight_grads(core, n_seq, act, gpre, gffn, mid, ctx, gattn, cls, gpool):
    chunks, own, width = act.shape
    groups = n_seq // 2
    half_b, half_w = chunks * width // n_seq, width // n_seq
    shape = jax.ShapeDtypeStruct
    whole = lambda a: pl.BlockSpec(a.shape, lambda y, c: (0, 0))
    tile = pl.BlockSpec((1, own, width), lambda y, c: (y, 0, 0))
    back = pl.BlockSpec((groups // chunks, half_b, width), lambda y, c: (y, 0, 0))
    inner = pl.BlockSpec((groups, half_w, width), lambda y, c: (0, 0, y))
    outer = pl.BlockSpec((groups, half_w, width), lambda y, c: (0, 0, jnp.minimum(y, 1)))
    return pl.pallas_call(
        weight_grads_kernel,
        grid_spec=pltpu.PrefetchScalarGridSpec(
            num_scalar_prefetch=1,
            grid=(chunks,),
            in_specs=[tile, tile] + [whole(a) for a in (gffn, mid, ctx, gattn, cls, gpool)],
            out_specs=[back, back, inner, inner, outer, outer],
            scratch_shapes=[pltpu.VMEM((width, own), bf16)],
        ),
        out_shape=[shape((groups, half_b, width), bf16)] * 2
        + [shape((groups, half_w, chunks * width), bf16)] * 2
        + [shape((groups, half_w, 2 * width), bf16)] * 2,
        compiler_params=pltpu.CompilerParams(vmem_limit_bytes=48 * 2**20),
        cost_estimate=pl.CostEstimate(
            flops=2 * own * width * width * (2 * chunks + 1), bytes_accessed=30 * 2**20, transcendentals=0
        ),
        name="weight_grads",
    )(core, act, gpre, gffn, mid, ctx, gattn, cls, gpool)


def last_kernel(n_parts, core, *refs):
    tok, gar, w_qkv = refs[:3]
    parts = refs[3 : 3 + n_parts]
    gtok, vec = refs[3 + n_parts : 5 + n_parts]
    pairs = refs[5 + n_parts : 11 + n_parts]
    tok_t = refs[11 + n_parts]
    c = pl.program_id(0)

    @pl.when(c == 0)
    def _():
        tok_t[...] = tok[...].T
        gtok[...] = gar[...]
        vec[...] = jnp.zeros_like(vec)

    grads = jnp.concatenate([p[0] for p in parts], axis=1)
    gtok[...] += dot(grads, w_qkv[...], NT)
    vec[pl.ds(c, 1), :] = col_sum(grads.astype(f32))
    tile = dot(tok_t[...], grads, NN)
    for n in range(3):

        @pl.when(c == n)
        def _():
            keep, send = pairs[2 * n], pairs[2 * n + 1]
            split_core(tile, core[0], keep.shape[1], keep, send, 0)


def last_layer(core, n_seq, tok, gar, w_qkv, parts):
    own, width = tok.shape
    groups, half = n_seq // 2, width // n_seq
    shape = jax.ShapeDtypeStruct
    whole = lambda a: pl.BlockSpec(a.shape, lambda c, k: (0,) * len(a.shape))
    pair = pl.BlockSpec((groups, half, width), lambda c, k: (0, 0, 0))
    return pl.pallas_call(
        functools.partial(last_kernel, len(parts)),
        grid_spec=pltpu.PrefetchScalarGridSpec(
            num_scalar_prefetch=1,
            grid=(3,),
            in_specs=[whole(tok), whole(gar), pl.BlockSpec((width, width), lambda c, k: (0, c))]
            + [pl.BlockSpec((1,) + p.shape[1:], lambda c, k: (c, 0, 0)) for p in parts],
            out_specs=[whole(gar), pl.BlockSpec((8, width), lambda c, k: (0, 0))] + [pair] * 6,
            scratch_shapes=[pltpu.VMEM((width, own), bf16)],
        ),
        out_shape=[shape((own, width), f32), shape((8, width), f32)]
        + [shape((groups, half, width), bf16)] * 6,
        compiler_params=pltpu.CompilerParams(vmem_limit_bytes=40 * 2**20),
        cost_estimate=pl.CostEstimate(
            flops=12 * own * width * width, bytes_accessed=12 * 2**20, transcendentals=0
        ),
        name="last_layer",
    )(core, tok, gar, w_qkv, *parts)


MESH = pl.DeviceIdType.MESH
OTHER_CORE, NEAR = 1, (2, 4, 6)


class Sends:
    def __init__(self, send_sems, recv_sems):
        self.sems, self.copies, self.at = (send_sems, recv_sems), {}, 0

    def plan(self, name, src, dst, **device):
        self.copies[name] = pltpu.make_async_remote_copy(
            src_ref=src,
            dst_ref=dst,
            send_sem=self.sems[0].at[self.at],
            recv_sem=self.sems[1].at[self.at],
            device_id=device,
            device_id_type=MESH,
        )
        self.at += 1

    def start(self, *names):
        for name in names:
            self.copies[name].start()

    def arrived(self, *names):
        for name in names:
            self.copies[name].wait_recv()

    def drain(self):
        for copy in self.copies.values():
            copy.wait_send()


def greet(devices):
    barrier = pltpu.get_barrier_semaphore()
    for device in devices:
        pl.semaphore_signal(barrier, inc=1, device_id=device, device_id_type=MESH)
    pl.semaphore_wait(barrier, len(devices))


def halves(tile, core, half):
    even = [tile[2 * n * half : (2 * n + 1) * half] for n in range(tile.shape[0] // (2 * half))]
    odd = [tile[(2 * n + 1) * half : (2 * n + 2) * half] for n in range(tile.shape[0] // (2 * half))]
    keep = [jnp.where(core == 0, e, o).astype(bf16) for e, o in zip(even, odd)]
    send = [jnp.where(core == 0, o, e).astype(bf16) for e, o in zip(even, odd)]
    return keep, send


def front_kernel(
    tok, w_hbm, bias_q, bias_v, lens, labels, qkv_hbm, hot, mask, bounds, seqs_of,
    sides, w, work, rows_of, load_sem, out_sems, send_sems, recv_sems,
):
    head, n_head = lax.axis_index("head"), lax.axis_size("head")
    own, width = tok.shape
    window = hot.shape[0]
    load = pltpu.make_async_copy(w_hbm, w, load_sem)
    load.start()
    not_first, not_last = head > 0, head < n_head - 1
    barrier = pltpu.get_barrier_semaphore()

    @pl.when(not_first)
    def _():
        pl.semaphore_signal(barrier, inc=1, device_id={"head": head - 1}, device_id_type=MESH)

    @pl.when(not_last)
    def _():
        pl.semaphore_signal(barrier, inc=1, device_id={"head": head + 1}, device_id_type=MESH)

    pl.semaphore_wait(barrier, not_first.astype(jnp.int32) + not_last.astype(jnp.int32))
    pieces = MAXLEN // ROWS
    here = lambda n: pl.ds(n * ROWS, ROWS)
    up, down = [], []
    for n in range(pieces):
        for copies, first, side, device in (
            (up, own - MAXLEN, 0, lax.rem(head + 1, n_head)),
            (down, 0, 1, lax.rem(head + n_head - 1, n_head)),
        ):
            copies.append(
                pltpu.make_async_remote_copy(
                    src_ref=tok.at[pl.ds(first + n * ROWS, ROWS)], dst_ref=sides.at[side, here(n)],
                    send_sem=send_sems.at[side, n], recv_sem=recv_sems.at[side, n],
                    device_id={"head": device}, device_id_type=MESH,
                )
            )

    @pl.when(not_last)
    def _():
        for copy in up:
            copy.start()

    @pl.when(not_first)
    def _():
        for copy in down:
            copy.start()

    @pl.when(head == 0)
    def _():
        sides[0] = jnp.zeros((MAXLEN, width), bf16)

    @pl.when(head == n_head - 1)
    def _():
        sides[1] = jnp.zeros((MAXLEN, width), bf16)

    def stored(at, n):
        return pltpu.make_async_copy(
            work.at[pl.ds(at, ROWS)], qkv_hbm.at[pl.ds(at, ROWS)], out_sems.at[n]
        )

    def project(rows, at, n):
        into = pl.ds(at, ROWS)
        query = (dot(rows, w[:, :width], NN) + bias_q[...].reshape(1, -1)) * HEAD_DIM**-0.5
        work[into, :width] = query.astype(bf16)
        work[into, width : 2 * width] = dot(rows, w[:, width : 2 * width], NN).astype(bf16)
        value = dot(rows, w[:, 2 * width :], NN) + bias_v[...].reshape(1, -1)
        work[into, 2 * width :] = value.astype(bf16)
        stored(at, n).start()

    load.wait()

    def own_rows(n, carry):
        at = pl.multiple_of(n * ROWS, ROWS)
        project(tok[pl.ds(at, ROWS), :], pl.multiple_of(MAXLEN + at, ROWS), n)
        return carry

    lax.fori_loop(0, own // ROWS, own_rows, 0)

    n_seqs = lens.shape[1]
    rows_of[...] = jnp.zeros_like(rows_of)
    rows_of[0:1, :n_seqs] = lens[...]
    rows_of[1:2, :n_seqs] = labels[...]
    i, j = iota((SIDE, SIDE), 0), iota((SIDE, SIDE), 1)
    length, label = rows_of[0:1, :].astype(f32), rows_of[1:2, :].astype(f32)
    to_col = lambda row, chosen: jnp.sum(jnp.where(chosen, row, 0.0), axis=1, keepdims=True)
    length_col, ends_col = to_col(length, i == j), to_col(length, j <= i)
    ends = jnp.sum(jnp.where(i <= j, length_col, 0.0), axis=0, keepdims=True)
    starts = ends - length
    group = float(own * n_head)
    n_rows = seqs_of.shape[0]
    row, lane = i[:n_rows], j[:n_rows]
    first_col = jnp.where(row < n_seqs, (ends_col - length_col)[:n_rows], -1.0)
    label_col = to_col(label, i == j)[:n_rows]
    seqs_of[...] = jnp.where(lane == 0, first_col, jnp.where(lane == 1, label_col, 0.0)).astype(jnp.int32)

    base = head * own - MAXLEN
    row, lane = i[:16], j[:16]
    blk = (base + row * QBLK).astype(f32)
    taken = lane < n_seqs
    low = jnp.max(jnp.where(taken & (starts <= blk), starts, -1.0), axis=1, keepdims=True)
    high = jnp.min(
        jnp.where(taken & (ends > blk + (QBLK - 1)), ends, group), axis=1, keepdims=True
    )
    at = row * QBLK
    is_own = (at >= MAXLEN) & (at < MAXLEN + own)
    low = jnp.broadcast_to(low.astype(jnp.int32), at.shape) - base
    high = jnp.broadcast_to(high.astype(jnp.int32), at.shape) - base
    low = jnp.where(is_own, low, jnp.maximum(low, MAXLEN))
    high = jnp.where(is_own, high, jnp.minimum(high, MAXLEN + own))
    low = (low >> 7) << 7
    valid = (blk >= 0.0) & (blk < group)
    steps = jnp.where(valid, jnp.maximum((high - low + KCHUNK - 1) >> (KCHUNK.bit_length() - 1), 0), 0)
    bounds[...] = jnp.where(lane == 0, low, jnp.where(lane == 1, steps, 0))

    lane = iota((QBLK, SIDE), 1)

    def masks(n, carry):
        at = pl.multiple_of(n * QBLK, QBLK)
        pos = (iota((QBLK, SIDE), 0) + (base + at)).astype(f32)
        inside = ((starts <= pos) & (pos < ends)).astype(f32)
        hot[pl.ds(at, QBLK), :] = inside.astype(bf16)
        mask[pl.ds(at, QBLK), :] = jnp.where(lane < n_seqs, (inside - 1.0) * BIG, 1.0).astype(bf16)
        return carry

    lax.fori_loop(0, window // QBLK, masks, 0)
    mask[pl.ds(window, PAD), :] = jnp.where(iota((PAD, SIDE), 1) < n_seqs, -BIG, 1.0).astype(bf16)

    for n in range(pieces):

        @pl.when(not_first)
        def _():
            up[n].wait_recv()

        @pl.when(not_last)
        def _():
            down[n].wait_recv()

        def side_rows(side, carry):
            at = pl.multiple_of(side * (MAXLEN + own) + n * ROWS, ROWS)
            project(sides[side, here(n), :], at, own // ROWS + 2 * n + side)
            return carry

        lax.fori_loop(0, 2, side_rows, 0)

    for n in range(own // ROWS):
        stored(MAXLEN + n * ROWS, n).wait()
    for n in range(pieces):
        for side in range(2):
            stored(side * (MAXLEN + own) + n * ROWS, own // ROWS + 2 * n + side).wait()

    @pl.when(not_last)
    def _():
        for copy in up:
            copy.wait_send()

    @pl.when(not_first)
    def _():
        for copy in down:
            copy.wait_send()


def front(tok, w_qkv, bias_q, bias_v, lens, labels):
    own, width = tok.shape
    window = own + 2 * MAXLEN
    seqs = lens.shape[1] + -lens.shape[1] % 16
    pieces = MAXLEN // ROWS
    shape = jax.ShapeDtypeStruct
    vmem, hbm = pl.BlockSpec(memory_space=pltpu.VMEM), pl.BlockSpec(memory_space=pl.ANY)
    return pl.pallas_call(
        front_kernel,
        in_specs=[vmem, hbm] + [vmem] * 4,
        out_specs=[hbm] + [vmem] * 4,
        out_shape=[
            shape((window, 3 * width), bf16),
            shape((window, SIDE), bf16),
            shape((window + PAD, SIDE), bf16),
            shape((16, SIDE), jnp.int32),
            shape((seqs, SIDE), jnp.int32),
        ],
        scratch_shapes=[
            pltpu.VMEM((2, MAXLEN, width), bf16),
            pltpu.VMEM(w_qkv.shape, bf16),
            pltpu.VMEM((window, 3 * width), bf16),
            pltpu.VMEM((8, SIDE), jnp.int32),
            pltpu.SemaphoreType.DMA,
            pltpu.SemaphoreType.DMA((own // ROWS + 2 * pieces,)),
            pltpu.SemaphoreType.DMA((2, pieces)),
            pltpu.SemaphoreType.DMA((2, pieces)),
        ],
        compiler_params=pltpu.CompilerParams(
            vmem_limit_bytes=62 * 2**20, collective_id=2, has_side_effects=True
        ),
        cost_estimate=pl.CostEstimate(
            flops=6 * window * width * width, bytes_accessed=16 * 2**20, transcendentals=0
        ),
        name="front",
    )(tok, w_qkv, bias_q, bias_v, lens, labels)


def grads_kernel(
    ctx_hbm, gattn_hbm, mid_hbm, gffn_hbm, tok_hbm, gs_hbm, act_hbm, gpre_hbm, cls, gpool,
    gsw, *refs,
):
    stores, outs, held, refs = refs[:8], refs[8:16], refs[16:22], refs[22:]
    tok_t, (ctx, gattn, mid, gffn, tok, gs) = outs[7], held
    store = [
        pltpu.make_async_copy(src, dst, refs[-1].at[6 + n])
        for n, (src, dst) in enumerate(zip(outs, stores))
    ]
    load = [
        pltpu.make_async_copy(src, dst, refs[-1].at[n])
        for n, (src, dst) in enumerate(
            zip((ctx_hbm, gattn_hbm, mid_hbm, gffn_hbm, tok_hbm, gs_hbm), held)
        )
    ]
    outs = (*outs[:6], outs[6].at[0], outs[6].at[1])
    (act, gpre, mid_t, keep_a, send_a, got_a, keep_b, send_b, got_b, keep_c, send_c, got_c, split,
     loads, send_sems, recv_sems, halo_sems, _) = refs
    seq, head = lax.axis_index("seq"), lax.axis_index("head")
    n_head = lax.axis_size("head")
    core = lax.rem(seq, 2)
    chunks, own, width = act.shape
    half_b, half_w = keep_a.shape[1], keep_b.shape[2]
    for n in range(3):
        load[n].start()
    for c in range(chunks):
        pltpu.make_async_copy(gpre_hbm.at[c], gpre.at[c], loads.at[chunks + c]).start()
        if c == 0:
            load[3].start()
        pltpu.make_async_copy(act_hbm.at[c], act.at[c], loads.at[c]).start()
    load[5].start()
    load[4].start()

    barrier = pltpu.get_barrier_semaphore()
    pl.semaphore_signal(barrier, inc=1, device_id={"seq": seq ^ OTHER_CORE}, device_id_type=MESH)

    @pl.when(head > 0)
    def _():
        pl.semaphore_signal(barrier, inc=1, device_id={"head": head - 1}, device_id_type=MESH)

    @pl.when(head < n_head - 1)
    def _():
        pl.semaphore_signal(barrier, inc=1, device_id={"head": head + 1}, device_id_type=MESH)

    pl.semaphore_wait(barrier, 1 + (head > 0).astype(jnp.int32) + (head < n_head - 1).astype(jnp.int32))

    up = pltpu.make_async_remote_copy(
        src_ref=gs_hbm.at[pl.ds(own - MAXLEN, MAXLEN)], dst_ref=gsw.at[pl.ds(0, MAXLEN)],
        send_sem=halo_sems.at[0], recv_sem=halo_sems.at[1],
        device_id={"head": lax.rem(head + 1, n_head)}, device_id_type=MESH,
    )
    down = pltpu.make_async_remote_copy(
        src_ref=gs_hbm.at[pl.ds(0, MAXLEN)], dst_ref=gsw.at[pl.ds(own + MAXLEN, MAXLEN)],
        send_sem=halo_sems.at[2], recv_sem=halo_sems.at[3],
        device_id={"head": lax.rem(head + n_head - 1, n_head)}, device_id_type=MESH,
    )
    stay = pltpu.make_async_copy(gs, gsw.at[pl.ds(MAXLEN, own)], halo_sems.at[4])

    @pl.when(head < n_head - 1)
    def _():
        up.start()

    @pl.when(head > 0)
    def _():
        down.start()

    def to_core(send, got, first, n):
        return pltpu.make_async_remote_copy(
            src_ref=send.at[n], dst_ref=got.at[n],
            send_sem=send_sems.at[first + n], recv_sem=recv_sems.at[first + n],
            device_id={"seq": seq ^ OTHER_CORE}, device_id_type=MESH,
        )

    copy_a = lambda n: to_core(send_a, got_a, 0, n)
    copy_b = lambda n: to_core(send_b, got_b, chunks, n)
    copy_c = lambda n: to_core(send_c, got_c, 2 * chunks, n)

    def put(tile, half, keep, send):
        mine, theirs = halves(tile, core, half)
        for g in range(len(mine)):
            keep[g] = mine[g]
            send[g] = theirs[g]

    put(dot(cls[...], gpool[...], TN), half_w, keep_c.at[1], send_c.at[1])
    load[0].wait()
    load[1].wait()
    put(dot(ctx[...], gattn[...], TN), half_w, keep_c.at[0], send_c.at[0])
    load[2].wait()
    mid_t[...] = mid[...].T
    load[3].wait()

    def chunk(c, carry):
        pltpu.make_async_copy(gpre_hbm.at[c], gpre.at[c], loads.at[chunks + c]).wait()
        put(dot(mid_t[...], gpre[c], NN), half_w, keep_b.at[c], send_b.at[c])

        @pl.when(c == 0)
        def _():
            copy_c(0).start()
            copy_c(1).start()

        @pl.when(c > 0)
        def _():
            copy_a(jnp.maximum(c - 1, 0)).start()

        pltpu.make_async_copy(act_hbm.at[c], act.at[c], loads.at[c]).wait()
        mine, theirs = halves(dot(act[c], gffn[...], TN), core, half_b)
        keep_a[c], send_a[c] = mine[0], theirs[0]
        copy_b(c).start()
        return carry

    lax.fori_loop(0, chunks, chunk, 0)

    load[5].wait()
    stay.start()
    load[4].wait()
    tok_t[...] = tok[...].T

    place = seq // 2
    quarter = half_w // 4
    rows_a = half_b // 4
    turns = (1, 2, 3, 0)
    for n in range(2):
        copy_c(n).wait_recv()
        for r in turns:
            total = keep_c[n, place ^ r].astype(f32) + got_c[n, place ^ r].astype(f32)
            for h in range(4):
                outs[r][h, rows_a + n * quarter : rows_a + (n + 1) * quarter, :] = total[
                    h * quarter : (h + 1) * quarter
                ].astype(outs[r].dtype)
    copy_a(chunks - 1).start()
    store[7].start()

    def sum_b(c, carry):
        copy_b(c).wait_recv()
        for g in range(4):
            total = keep_b[c, g].astype(f32) + got_b[c, g].astype(f32)
            for h in range(4):
                split[h, g] = total[h * quarter : (h + 1) * quarter]
        cols = pl.ds(pl.multiple_of(c * width, width), width)
        for r in range(4):
            for g in range(4):
                outs[4 + r][g, :, cols] = split[head ^ r, g].astype(outs[4 + r].dtype)
        return carry

    lax.fori_loop(0, chunks, sum_b, 0)
    for n in (5, 6, 4):
        store[n].start()
    for c in range(chunks):
        copy_a(c).wait_recv()
    for r in turns:
        total = keep_a[place ^ r].astype(f32) + got_a[place ^ r].astype(f32)
        for h in range(4):
            outs[r][h, :rows_a, :] = total[h * rows_a : (h + 1) * rows_a].astype(outs[r].dtype)
        store[r].start()
    for c in range(chunks):
        copy_a(c).wait_send()
        copy_b(c).wait_send()
    for n in range(2):
        copy_c(n).wait_send()
    stay.wait()
    for copy in store:
        copy.wait()

    @pl.when(head < n_head - 1)
    def _():
        up.wait_send()
        down.wait_recv()

    @pl.when(head > 0)
    def _():
        up.wait_recv()
        down.wait_send()


def send_grads(act, gpre, gs, gffn, mid, ctx, gattn, cls, gpool, tok):
    chunks, own, width = act.shape
    half_b, half_w = chunks * width // 8, width // 8
    window = own + 2 * MAXLEN
    shape = jax.ShapeDtypeStruct
    vmem, hbm = pl.BlockSpec(memory_space=pltpu.VMEM), pl.BlockSpec(memory_space=pl.ANY)
    kinds = (f32, bf16, bf16, bf16)
    outs = (
        [shape((4, half_b // 4 + half_w // 2, width), k) for k in kinds]
        + [shape((4, half_w // 4, chunks * width), k) for k in kinds[:2]]
        + [shape((2, 4, half_w // 4, chunks * width), bf16), shape((width, own), bf16)]
    )
    held = (ctx, gattn, mid, gffn, tok, gs)
    gsw, *pieces, tok_t = pl.pallas_call(
        grads_kernel,
        in_specs=[hbm] * 8 + [vmem] * 2,
        out_specs=[hbm] * 9,
        out_shape=[shape((window, width + SIDE), bf16)] + outs,
        scratch_shapes=[pltpu.VMEM(o.shape, o.dtype) for o in [*outs, *held]]
        + [
            pltpu.VMEM((chunks, own, width), bf16),
            pltpu.VMEM((chunks, own, width), bf16),
            pltpu.VMEM((width, own), bf16),
        ]
        + [pltpu.VMEM((chunks, half_b, width), bf16)] * 3
        + [pltpu.VMEM((chunks, 4, half_w, width), bf16)] * 3
        + [pltpu.VMEM((2, 4, half_w, width), bf16)] * 3
        + [
            pltpu.VMEM((4, 4, half_w // 4, width), f32),
            pltpu.SemaphoreType.DMA((2 * chunks,)),
            pltpu.SemaphoreType.DMA((2 * chunks + 2,)),
            pltpu.SemaphoreType.DMA((2 * chunks + 2,)),
            pltpu.SemaphoreType.DMA((5,)),
            pltpu.SemaphoreType.DMA((14,)),
        ],
        compiler_params=pltpu.CompilerParams(
            vmem_limit_bytes=62 * 2**20, collective_id=0, has_side_effects=True
        ),
        cost_estimate=pl.CostEstimate(
            flops=2 * own * width * width * (2 * chunks + 1), bytes_accessed=30 * 2**20, transcendentals=0
        ),
        name="send_grads",
    )(*held, act, gpre, cls, gpool)
    return gsw, tok_t, *pieces


def finish_kernel(n_parts, *refs):
    inputs, refs = refs[:14], refs[14:]
    sends_q = inputs[9]
    gtok, sum_a, sum_b, sum_out, sum_pool, sum_q, sum_v = refs[:7]
    n_held = 11
    held, refs = refs[7 : 7 + n_held], refs[7 + n_held :]
    own_a, near_a, own_b, near_b, vec = held[0], held[1:4], held[4], (held[5], held[6].at[0]), held[7]
    keeps, vec_parts, parts = held[8:]
    (w_qkv, all_a, send_a, got_a, all_b, send_b, got_b, got_f, got_q, own_q, send_n, got_n, all_q, send_z, got_z,
     vecs, got_v, loads, send_sems, recv_sems) = refs
    wanted = inputs[:8] + inputs[10:-1] + (inputs[8], inputs[-1])
    copies = [
        pltpu.make_async_copy(src, dst, loads.at[n])
        for n, (src, dst) in enumerate(zip(wanted, held + (w_qkv, gtok)))
    ]
    for copy in copies:
        copy.start()
    seq, head = lax.axis_index("seq"), lax.axis_index("head")
    place = seq // 2
    width = gtok.shape[1]
    quarter = width // 32
    cols = width // n_parts
    line = (1, 2, 3)
    greet(
        [{"seq": seq ^ OTHER_CORE}]
        + [{"seq": seq ^ near} for near in NEAR]
        + [{"head": head ^ r} for r in line]
    )
    sends = Sends(send_sems, recv_sems)
    for r in line:
        sends.plan(("a", r), send_a.at[r - 1], got_a.at[r - 1], head=head ^ r)
        sends.plan(("b", r), send_b.at[r - 1], got_b.at[r - 1], seq=seq ^ NEAR[r - 1])
    for p in range(n_parts):
        sends.plan(("core", p), sends_q.at[p], got_q.at[p], seq=seq ^ OTHER_CORE)
        for r in line:
            sends.plan(("near", p, r), send_n.at[p, r - 1], got_n.at[p, r - 1], seq=seq ^ NEAR[r - 1])
            sends.plan(("line", p, r), send_z.at[p, r - 1], got_z.at[p, r - 1], head=head ^ r)
    sends.plan(("core", "v"), vecs.at[0], got_v.at[0], seq=seq ^ OTHER_CORE)
    for r in line:
        sends.plan(("near", "v", r), vecs.at[1], got_v.at[r], seq=seq ^ NEAR[r - 1])
        sends.plan(("line", "v", r), vecs.at[2], got_v.at[3 + r], head=head ^ r)
    sends.plan("pass", inputs[6].at[1], got_f, head=head ^ 1)
    sends.start(*[("core", p) for p in range(n_parts)])
    sends.start("pass")

    for copy in copies[:10]:
        copy.wait()
    rows_v = vec.shape[0]
    vecs[0, :rows_v, :] = vec[...]
    for p in range(n_parts):
        vecs[0, rows_v:, p * cols : (p + 1) * cols] = vec_parts[p]
    for h in range(4):
        all_a[h] = (own_a[h] + near_a[0][h].astype(f32)) + (
            near_a[1][h].astype(f32) + near_a[2][h].astype(f32)
        )
    for r in line:
        send_a[r - 1] = all_a[head ^ r].astype(bf16)
    sends.start(("core", "v"))

    def start_near(p):
        sends.start(*[("near", p, r) for r in line])

    for p in range(n_parts):
        sends.arrived(("core", p))
        for r in line:
            for n in range(3):
                send_n[p, r - 1, n] = (
                    keeps[p, n, place ^ r].astype(f32) + got_q[p, n, place ^ r].astype(f32)
                ).astype(bf16)
        for n in range(3):
            own_q[p, n] = keeps[p, n, place].astype(f32) + got_q[p, n, place].astype(f32)
        if p == 0:
            sends.start(*[("a", r) for r in line])
        else:
            start_near(p - 1)
    start_near(n_parts - 1)
    sends.arrived(("core", "v"))
    vecs[1] = vecs[0] + got_v[0]
    sends.arrived("pass")
    for g in range(4):
        all_b[g] = (own_b[g] + near_b[0][g].astype(f32)) + (
            near_b[1][g].astype(f32) + got_f[g].astype(f32)
        )
    for r in line:
        send_b[r - 1] = all_b[place ^ r].astype(bf16)
    for copy in copies[10:]:
        copy.wait()

    def back(n, carry):
        here = pl.ds(pl.multiple_of(n * width, width), width)
        gtok[...] += dot(jnp.concatenate([parts[p, n] for p in range(n_parts)], axis=1), w_qkv[:, here], NT)

        @pl.when(n == 0)
        def _():
            sends.start(*[("near", "v", r) for r in line])
            sends.start(*[("b", r) for r in line])

        return carry

    lax.fori_loop(0, 3, back, 0)

    for p in range(n_parts):
        sends.arrived(*[("near", p, r) for r in line])
        for h in range(4):
            rows = slice(h * quarter, (h + 1) * quarter)
            for n in range(3):
                all_q[p, h, n] = (own_q[p, n, rows, :] + got_n[p, 0, n, rows, :].astype(f32)) + (
                    got_n[p, 1, n, rows, :].astype(f32) + got_n[p, 2, n, rows, :].astype(f32)
                )
        for r in line:
            send_z[p, r - 1] = all_q[p, head ^ r].astype(bf16)
        if p > 0:
            sends.start(*[("line", p - 1, r) for r in line])
    sends.arrived(*[("near", "v", r) for r in line])
    vecs[2] = (vecs[1] + got_v[1]) + (got_v[2] + got_v[3])
    sends.start(*[("line", n_parts - 1, r) for r in line])
    sends.arrived(*[("a", r) for r in line])
    total = (all_a[head] + got_a[0].astype(f32)) + (got_a[1].astype(f32) + got_a[2].astype(f32))
    rows_a = sum_a.shape[0]
    sum_a[...] = total[:rows_a]
    sum_out[...] = total[rows_a : rows_a + quarter]
    sum_pool[...] = total[rows_a + quarter :]
    sends.start(*[("line", "v", r) for r in line])
    sends.arrived(*[("b", r) for r in line])
    sum_b[...] = (all_b[place] + got_b[0].astype(f32)) + (got_b[1].astype(f32) + got_b[2].astype(f32))
    for p in range(n_parts):
        sends.arrived(*[("line", p, r) for r in line])
        for n in range(3):
            at = n * width + p * cols
            sum_q[:, at : at + cols] = (all_q[p, head, n] + got_z[p, 0, n].astype(f32)) + (
                got_z[p, 1, n].astype(f32) + got_z[p, 2, n].astype(f32)
            )
    sends.arrived(*[("line", "v", r) for r in line])
    sum_v[...] = (vecs[2] + got_v[4]) + (got_v[5] + got_v[6])
    sends.drain()


def finish(gar, w_qkv, vec, parts, a, b):
    own, width = gar.shape
    half_w = width // 8
    quarter = half_w // 4
    n_parts = parts[0].shape[0]
    cols = width // n_parts
    rows_z, ff = a[0].shape[1], b[0].shape[2]
    n_vec = vec.shape[0] + 8
    shape = jax.ShapeDtypeStruct
    vmem, hbm = pl.BlockSpec(memory_space=pltpu.VMEM), pl.BlockSpec(memory_space=pl.ANY)
    n_copies = 6 + 7 * n_parts + 7 + 1
    grads, keeps, sends, sums = parts
    held = [*a, *b, vec, keeps, sums, grads]
    return pl.pallas_call(
        functools.partial(finish_kernel, n_parts),
        in_specs=[hbm] * 14,
        out_specs=[vmem] * 7,
        out_shape=[
            shape((own, width), f32),
            shape((rows_z - 2 * quarter, width), f32),
            shape((quarter, ff), f32),
            shape((quarter, width), f32),
            shape((quarter, width), f32),
            shape((quarter, 3 * width), f32),
            shape((n_vec, width), f32),
        ],
        scratch_shapes=[pltpu.VMEM(h.shape, h.dtype) for h in held]
        + [
            pltpu.VMEM(w_qkv.shape, bf16),
            pltpu.VMEM((4, rows_z, width), f32),
            pltpu.VMEM((3, rows_z, width), bf16),
            pltpu.VMEM((3, rows_z, width), bf16),
            pltpu.VMEM((4, quarter, ff), f32),
            pltpu.VMEM((3, quarter, ff), bf16),
            pltpu.VMEM((3, quarter, ff), bf16),
            pltpu.VMEM((4, quarter, ff), bf16),
            pltpu.VMEM((n_parts, 3, 4, half_w, cols), bf16),
            pltpu.VMEM((n_parts, 3, half_w, cols), f32),
            pltpu.VMEM((n_parts, 3, 3, half_w, cols), bf16),
            pltpu.VMEM((n_parts, 3, 3, half_w, cols), bf16),
            pltpu.VMEM((n_parts, 4, 3, quarter, cols), f32),
            pltpu.VMEM((n_parts, 3, 3, quarter, cols), bf16),
            pltpu.VMEM((n_parts, 3, 3, quarter, cols), bf16),
            pltpu.VMEM((3, n_vec, width), f32),
            pltpu.VMEM((7, n_vec, width), f32),
            pltpu.SemaphoreType.DMA((len(held) + 2,)),
            pltpu.SemaphoreType.DMA((n_copies,)),
            pltpu.SemaphoreType.DMA((n_copies,)),
        ],
        compiler_params=pltpu.CompilerParams(
            vmem_limit_bytes=62 * 2**20, collective_id=1, has_side_effects=True
        ),
        cost_estimate=pl.CostEstimate(
            flops=12 * own * width * width, bytes_accessed=12 * 2**20, transcendentals=0
        ),
        name="finish",
    )(*a, *b, vec, w_qkv, sends, keeps, sums, grads, gar)


def own_vectors_kernel(chunks, n_class, count, n_through, shard, summed, *refs):
    through, outs, refs = refs[:n_through], refs[n_through:][: 12 + n_through], refs[12 + 2 * n_through :]
    loads, stores = [], []
    for src, dst, held in zip(through, outs[12:], refs):
        step = ROWS if src.shape[0] > ROWS else src.shape[0]
        for first in range(0, src.shape[0], step):
            rows, n = pl.ds(first, step), len(loads)
            loads.append(pltpu.make_async_copy(src.at[rows], held.at[rows], refs[-1].at[0, n]))
            stores.append(pltpu.make_async_copy(held.at[rows], dst.at[rows], refs[-1].at[1, n]))
    for copy in loads:
        copy.start()
    *rows_of, outs_bin, outs_class, entropy = outs[:12]
    width = summed.shape[1]
    size, size_bin = outs_class.shape[1], outs_bin.shape[1]
    here = shard[0]

    def columns(values, first, n):
        chosen = iota((width, n), 0) == first + iota((width, n), 1)
        return dot3(values, chosen.astype(f32).astype(bf16), NN)

    mine = columns(summed[...], here * size, size)
    n_vec = summed.shape[0] - 8
    for n, out in zip((n_vec, n_vec + 2, 0, 1, 2, 3, 4, 5, 6), rows_of):
        out[...] = mine[n : n + 1]
    outs_class[...] = mine[8 + chunks : 8 + chunks + n_class]
    rows = summed[8:16, :]
    per_row = width // size_bin
    rows = jnp.where(iota(rows.shape, 0) == lax.div(here, per_row), rows, 0.0)
    line = jnp.broadcast_to(col_sum(rows), rows.shape)
    outs_bin[...] = columns(line, lax.rem(here, per_row) * size_bin, size_bin)[0:1]
    entropy[...] = summed[7:8, 0:1] * (1.0 / count)
    for load, store in zip(loads, stores):
        load.wait()
        store.start()
    for store in stores:
        store.wait()


def own_vectors(summed, shard, shards, chunks, n_class, count, through=()):
    size = summed.shape[1] // shards
    shape = jax.ShapeDtypeStruct
    vmem = pl.BlockSpec(memory_space=pltpu.VMEM)
    outs = [(1, size)] * 9 + [(1, size * chunks), (n_class, size), (1, 1)]
    n_copies = sum(-(-t.shape[0] // ROWS) for t in through)
    results = pl.pallas_call(
        functools.partial(own_vectors_kernel, chunks, n_class, count, len(through)),
        in_specs=[pl.BlockSpec(memory_space=pltpu.SMEM), vmem]
        + [pl.BlockSpec(memory_space=pl.ANY)] * len(through),
        out_specs=[vmem] * len(outs) + [pl.BlockSpec(memory_space=pl.ANY)] * len(through),
        out_shape=[shape(o, f32) for o in outs] + [shape(t.shape, t.dtype) for t in through],
        scratch_shapes=[pltpu.VMEM(t.shape, t.dtype) for t in through]
        + [pltpu.SemaphoreType.DMA((2, max(n_copies, 1)))],
        compiler_params=pltpu.CompilerParams(vmem_limit_bytes=62 * 2**20),
        name="own_vectors",
    )(shard.reshape(1), summed, *through)
    rows_of, (outs_class, entropy) = results[:10], results[10:12]
    return [r.reshape(-1) for r in rows_of], outs_class.T, entropy.reshape(()), results[12:]


def halo(rows, left_axis, n_head):
    up = [(i, i + 1) for i in range(n_head - 1)]
    down = [(i + 1, i) for i in range(n_head - 1)]
    from_left = lax.ppermute(rows[-MAXLEN:], left_axis, up)
    from_right = lax.ppermute(rows[:MAXLEN], left_axis, down)
    return jnp.concatenate([from_left, rows, from_right], axis=0)


def pick(values, axis, index):
    return lax.dynamic_index_in_dim(values, index, axis, keepdims=False)


class Sums:
    def __init__(self, pairs, orders, n_seq, n_head, vectors):
        self.count = {"seq": n_seq, "head": n_head}
        self.bits = {"seq": n_seq.bit_length() - 1, "head": n_head.bit_length() - 1}
        self.stages = sum(self.bits.values())
        self.orders = orders
        self.vectors = vectors
        self.axes = [[n for n in range(self.stages) if n != self.bits["seq"] - 1] for _ in pairs]
        shape = lambda a: a.reshape(
            (2,) * (self.stages - 1) + (a.shape[1] // n_head,) + a.shape[2:]
        )
        self.kept = [shape(keep) for keep, _ in pairs]
        self.sent = [shape(send) for _, send in pairs]
        self.stage = 0
        self.send()

    def send(self):
        self.got = [
            self.swap(v, *self.orders[n][self.stage]) for n, v in enumerate(self.sent)
        ]
        self.vectors = self.vectors + self.swap(self.vectors, *self.orders[0][self.stage])

    def swap(self, values, name, bit):
        return lax.ppermute(values, name, [(i, i ^ (1 << bit)) for i in range(self.count[name])])

    def split(self):
        self.stage += 1
        kept, sent = [], []
        for n, (keep, got) in enumerate(zip(self.kept, self.got)):
            name, bit = self.orders[n][self.stage]
            where = (self.stages if name == "head" else self.bits["seq"]) - 1 - bit
            at = self.axes[n].index(where)
            self.axes[n].pop(at)
            mine = (lax.axis_index(name) >> bit) & 1
            half = lambda m: pick(keep, at, m).astype(f32) + pick(got, at, m).astype(f32)
            sent.append(half(1 - mine).astype(bf16))
            kept.append(half(mine))
        self.kept, self.sent = kept, sent

    def rest(self):
        while self.stage < self.stages - 1:
            self.split()
            self.send()
        return [k.astype(f32) + g.astype(f32) for k, g in zip(self.kept, self.got)]


def after(value, *others):
    return lax.optimization_barrier((value, *others))[0]


def orders(n_seq, n_head):
    seq_bits, head_bits = n_seq.bit_length() - 1, n_head.bit_length() - 1
    core = [("seq", 0)]
    planar = [("seq", b) for b in range(1, seq_bits)]
    along = [("head", b) for b in range(head_bits)]
    return (
        core + planar + along,
        core + planar[::-1] + along,
        core + along + planar,
    )


def local(
    tokens, cotangent, lengths, labels, w_qkv, b_query, b_value, w_out, b_out, gain_attn,
    shift_attn, w_in, b_in, w_back, b_back, gain_ffn, shift_ffn, w_pool, b_pool, w_class,
):
    n_head = lax.axis_size("head")
    n_seq = lax.axis_size("seq")
    head_index = lax.axis_index("head")
    own, width = tokens.shape
    window = own + 2 * MAXLEN
    group = own * n_head

    if (n_seq, n_head) == (8, 4):
        qkv, hot, mask, bounds, seqs_of = front(tokens, w_qkv, b_query, b_value, lengths, labels)
    else:
        seq_lengths = lengths[0]
        ends = jnp.cumsum(seq_lengths)
        starts = ends - seq_lengths
        base = head_index * own - MAXLEN
        pos = base + jnp.arange(window, dtype=jnp.int32)
        n_in_group = seq_lengths.shape[0]
        lane_pad = (0, SIDE - n_in_group)
        starts_w = jnp.pad(starts, lane_pad, constant_values=group + MAXLEN)
        ends_w = jnp.pad(ends, lane_pad, constant_values=-MAXLEN)
        inside = (starts_w[None, :] <= pos[:, None]) & (pos[:, None] < ends_w[None, :])
        hot = inside.astype(bf16)
        lane = jnp.arange(SIDE, dtype=jnp.int32)[None, :]
        mask = jnp.where(lane < n_in_group, jnp.where(inside, 0.0, -BIG), 1.0).astype(bf16)
        mask = jnp.concatenate(
            [mask, jnp.broadcast_to(jnp.where(lane < n_in_group, -BIG, 1.0).astype(bf16), (PAD, SIDE))]
        )
        blk = base + QBLK * jnp.arange(window // QBLK, dtype=jnp.int32)
        low = jnp.max(jnp.where(starts[None, :] <= blk[:, None], starts[None, :], -1), axis=1)
        high = jnp.min(
            jnp.where(ends[None, :] > blk[:, None] + QBLK - 1, ends[None, :], group), axis=1
        )
        is_own = (blk >= base + MAXLEN) & (blk < base + MAXLEN + own)
        low = jnp.where(is_own, low - base, jnp.maximum(low - base, MAXLEN))
        high = jnp.where(is_own, high - base, jnp.minimum(high - base, MAXLEN + own))
        valid = (blk >= 0) & (blk < group)
        low = low // 128 * 128
        steps = jnp.where(valid, jnp.maximum((high - low + KCHUNK - 1) // KCHUNK, 0), 0)
        bounds = jnp.stack([low, steps], axis=1).astype(jnp.int32)
        seq_pad = (0, -n_in_group % 16)
        seqs_of = jnp.stack(
            [jnp.pad(starts, seq_pad, constant_values=-1), jnp.pad(labels[0], seq_pad)], axis=1
        )
        tokens_w = halo(tokens, "head", n_head)
        bias = jnp.concatenate([b_query, jnp.zeros_like(b_query), b_value])[None, :]
        qscale = jnp.where(jnp.arange(3 * width) < width, HEAD_DIM**-0.5, 1.0).astype(f32)[None, :]
        qkv = ((dot(tokens_w, w_qkv, NN) + bias) * qscale).astype(bf16)
    context, lse = attend(bounds, qkv, hot, mask, own)

    shards = n_seq * n_head
    shard = head_index + n_head * lax.axis_index("seq")
    core = (lax.axis_index("seq") & 1).reshape(1)
    (output, gar, gs, act, gpre, gffn, mid, gattn, cls, gpool, vec) = middle_layer(
        2 * fold_of(width // PAIR, 3), head_index.reshape(1), w_in, w_back, w_pool, tokens, context, lse,
        cotangent, w_out, b_in.reshape(1, -1), w_class.T, seqs_of,
        (b_out, gain_attn, shift_attn, b_back, gain_ffn, shift_ffn, b_pool),
    )
    if (n_seq, n_head) == (8, 4):
        grads_w, tok_t, *pieces = send_grads(act, gpre, gs, gffn, mid, context, gattn, cls, gpool, tokens)
        to = lambda v, axis, count, x: lax.ppermute(v, axis, [(i, i ^ x) for i in range(count)])
        a = [pieces[0]] + [to(pieces[r], "seq", 8, NEAR[r - 1]) for r in (1, 2, 3)]
        b = [pieces[4], to(pieces[5], "head", 4, 1), to(pieces[6], "head", 4, 2)]
        gqkv = attend_back(bounds, qkv, grads_w, hot, mask, own, (tok_t, core))
        grad_tokens, sum_wback, sum_win, sum_wout, sum_pool, sum_wqkv, summed = finish(
            gar, w_qkv, vec, gqkv, a, b
        )
    else:
        grads_w = halo(gs, "head", n_head)

        pieces = weight_grads(core, n_seq, act, gpre, gffn, mid, context, gattn, cls, gpool)
        orders_all = orders(n_seq, n_head)
        first = Sums(
            [pieces[0:2], pieces[2:4], pieces[4:6]], orders_all, n_seq, n_head, vec
        )
        gqkv = attend_back(bounds, qkv, grads_w, hot, mask, own)
        last_out = last_layer(core, n_seq, tokens, gar, w_qkv, list(gqkv))
        grad_tokens, vec_qkv = last_out[:2]
        last = Sums(
            [last_out[2:4], last_out[4:6], last_out[6:8]], orders_all, n_seq, n_head, vec_qkv
        )
        sum_wback, sum_win, sum_c = first.rest()
        sum_wout, sum_pool = sum_c[:, :width], sum_c[:, width:]
        sum_q, sum_k, sum_v = last.rest()
        sum_wqkv = jnp.concatenate([sum_q, sum_k, sum_v], axis=1)

        summed = jnp.concatenate([first.vectors, last.vectors])
    sums = (grad_tokens, sum_wback, sum_win, sum_wout, sum_pool, sum_wqkv)
    (grad_bq, grad_bv, *mine, grad_bin), grad_class, entropy_mean, sums = own_vectors(
        summed, shard, shards, w_in.shape[1] // width, w_class.shape[1], n_seq * labels.shape[1], sums
    )
    grad_tokens, sum_wback, sum_win, sum_wout, sum_pool, sum_wqkv = sums
    return (
        output, grad_tokens, sum_wqkv, grad_bq, grad_bv, sum_wout, mine[0], mine[1], mine[2],
        sum_win, grad_bin, sum_wback, mine[3], mine[4], mine[5], sum_pool, mine[6], grad_class,
        entropy_mean,
    )


def solution(mesh):
    rows = P(("seq", "head"), None)
    vec = P(("seq", "head"))
    return jax.shard_map(
        local,
        mesh=mesh,
        in_specs=(rows, rows, P("seq", None), P("seq", None)) + (P(),) * 16,
        out_specs=(
            rows, rows, rows, vec, vec, rows, vec, vec, vec, rows, vec, rows, vec, vec, vec, rows,
            vec, rows, P(),
        ),
        check_vma=False,
    )
```

```python
import functools

import jax
import jax.numpy as jnp
from jax import lax
from jax.experimental import pallas as pl
from jax.experimental.pallas import tpu as pltpu
from jax.sharding import PartitionSpec as P

HEAD_DIM = 64
MAXLEN = 512
PAIR = 2 * HEAD_DIM
QBLK = 128
KCHUNK = 256
PAD = KCHUNK - 128
LSE0 = 32
SIDE = 128

eps = 1e-05
BIG = 1e30
highest = lax.Precision.HIGHEST
f32 = jnp.float32
bf16 = jnp.bfloat16
NT = (((1,), (1,)), ((), ()))
NN = (((1,), (0,)), ((), ()))
TN = (((0,), (0,)), ((), ()))


def dot(left, right, dims):
    return lax.dot_general(left, right, dims, preferred_element_type=f32)


def pair_rows(rows, side):
    lane = lax.broadcasted_iota(jnp.int32, rows.shape, 1)
    zero = jnp.zeros_like(rows)
    first = jnp.where(lane < HEAD_DIM, rows, zero)
    second = jnp.where(lane >= HEAD_DIM, rows, zero)
    return jnp.concatenate(
        [jnp.concatenate([first, side[0]], axis=1), jnp.concatenate([second, side[1]], axis=1)],
        axis=0,
    )


def unpair(both):
    row = lax.broadcasted_iota(jnp.int32, (PAIR, QBLK), 0)
    return jnp.where(row < HEAD_DIM, both[:, :QBLK], both[:, QBLK:])


def attend_kernel(bounds, q_ref, k_ref, v_ref, hot_ref, mask_ref, ctx_ref, lse_ref, kcat, vt):
    window = k_ref.shape[0]
    own = ctx_ref.shape[0]
    fold = kcat.shape[0]
    skip = MAXLEN // QBLK

    @pl.when(pl.program_id(0) == 0)
    def _():
        for j in range(fold):
            kcat[j, :, PAIR:] = mask_ref[...]
            kcat[j, pl.ds(window, PAD), :PAIR] = jnp.zeros((PAD, PAIR), bf16)
            vt[j, :, pl.ds(window, PAD)] = jnp.zeros((PAIR, PAD), bf16)

    lse_ref[...] = jnp.zeros_like(lse_ref)
    for j in range(fold):
        cols = pl.ds(j * PAIR, PAIR)
        kcat[j, pl.ds(0, window), :PAIR] = k_ref[:, cols]
        for at in range(0, window, 256):
            vt[j, :, pl.ds(at, 256)] = v_ref[pl.ds(at, 256), cols].T

    def block(i, carry):
        row0 = pl.multiple_of(i * QBLK, QBLK)
        hot = hot_ref[pl.ds(MAXLEN + row0, QBLK), :]
        rows = q_ref[pl.ds(MAXLEN + row0, QBLK), :]
        qcat = [pair_rows(rows[:, j * PAIR : (j + 1) * PAIR], (hot, hot)) for j in range(fold)]
        first = bounds[skip + i, 0]

        def step(c, state):
            start = pl.multiple_of(first + c * KCHUNK, 128)
            scores = [dot(kcat[j, pl.ds(start, KCHUNK), :], qcat[j], NT) for j in range(fold)]
            out = []
            for j, s in enumerate(scores):
                peak, total, acc = state[j]
                new_peak = jnp.maximum(peak, jnp.max(s, axis=0, keepdims=True))
                scale = jnp.exp(peak - new_peak)
                p = jnp.exp(s - new_peak)
                total = total * scale + jnp.sum(p, axis=0, keepdims=True)
                acc = acc * scale + dot(vt[j, :, pl.ds(start, KCHUNK)], p.astype(bf16), NN)
                out.append((new_peak, total, acc))
            return tuple(out)

        empty = (
            jnp.full((1, 2 * QBLK), -BIG, f32),
            jnp.zeros((1, 2 * QBLK), f32),
            jnp.zeros((PAIR, 2 * QBLK), f32),
        )
        state = lax.fori_loop(0, bounds[skip + i, 1], step, (empty,) * fold)
        for j, (peak, total, acc) in enumerate(state):
            ctx_ref[pl.ds(row0, QBLK), pl.ds(j * PAIR, PAIR)] = unpair(acc / total).T.astype(bf16)
            lse = peak + jnp.log(total)
            lse_ref[2 * j : 2 * j + 1, pl.ds(row0, QBLK)] = lse[:, :QBLK]
            lse_ref[2 * j + 1 : 2 * j + 2, pl.ds(row0, QBLK)] = lse[:, QBLK:]
        return carry

    lax.fori_loop(0, own // QBLK, block, 0)


def fold_of(pairs, most):
    return max(n for n in range(1, most + 1) if pairs % n == 0)


def attend(bounds, qkv, hot, mask, own):
    window, wide = qkv.shape
    width = wide // 3
    pairs = width // PAIR
    fold = fold_of(pairs, 3)
    parts = pairs // fold
    column = lambda part: pl.BlockSpec((window, fold * PAIR), lambda g, b: (0, part * parts + g))
    whole = lambda a: pl.BlockSpec(a.shape, lambda g, b: (0, 0))
    return pl.pallas_call(
        attend_kernel,
        grid_spec=pltpu.PrefetchScalarGridSpec(
            num_scalar_prefetch=1,
            grid=(parts,),
            in_specs=[column(0), column(1), column(2), whole(hot), whole(mask)],
            out_specs=[
                pl.BlockSpec((own, fold * PAIR), lambda g, b: (0, g)),
                pl.BlockSpec((8, own), lambda g, b: (g, 0)),
            ],
            scratch_shapes=[
                pltpu.VMEM((fold, window + PAD, 2 * PAIR), bf16),
                pltpu.VMEM((fold, PAIR, window + PAD), bf16),
            ],
        ),
        out_shape=[
            jax.ShapeDtypeStruct((own, width), bf16),
            jax.ShapeDtypeStruct((8 * parts, own), f32),
        ],
        cost_estimate=pl.CostEstimate(
            flops=own * 600 * width * 4, bytes_accessed=window * wide * 2, transcendentals=0
        ),
        name="attend",
    )(bounds, qkv, qkv, qkv, hot, mask)


def attend_back_kernel(side0, more, bounds, q_ref, k_ref, v_ref, do_ref, side_ref, hot_ref, mask_ref, *refs):
    extra, refs = refs[:more], refs[more:]
    gqkv_ref, (kcat, vcat, kt, dk, dv) = refs[0].at[0], refs[-5:]
    window = k_ref.shape[0]
    own = gqkv_ref.shape[1]
    fold = kcat.shape[0]
    lanes, gap = side0
    part = pl.program_id(0)
    low0 = LSE0 + lanes * part

    @pl.when(part == 0)
    def _():
        for j in range(fold):
            kcat[j, :, PAIR:] = mask_ref[...]
            vcat[j, :, PAIR:] = jnp.ones((window + PAD, SIDE), bf16)
            kcat[j, pl.ds(window, PAD), :PAIR] = jnp.zeros((PAD, PAIR), bf16)
            vcat[j, pl.ds(window, PAD), :PAIR] = jnp.zeros((PAD, PAIR), bf16)
            kt[j, :, pl.ds(window, PAD)] = jnp.zeros((PAIR, PAD), bf16)

    for j in range(fold):
        cols = pl.ds(j * PAIR, PAIR)
        kcat[j, pl.ds(0, window), :PAIR] = k_ref[:, cols]
        vcat[j, pl.ds(0, window), :PAIR] = v_ref[:, cols]
        for at in range(0, window, 256):
            kt[j, :, pl.ds(at, 256)] = k_ref[pl.ds(at, 256), cols].T
    dk[...] = jnp.zeros_like(dk)
    dv[...] = jnp.zeros_like(dv)
    lane = lax.broadcasted_iota(jnp.int32, (QBLK, SIDE), 1)

    def side_lanes(side, first):
        return jnp.where((lane >= first) & (lane < first + 3), side, jnp.zeros_like(side))

    def block(i, carry):
        row0 = pl.multiple_of(i * QBLK, QBLK)
        hot = hot_ref[pl.ds(row0, QBLK), :]
        side = side_ref[pl.ds(row0, QBLK), :]
        rows = q_ref[pl.ds(row0, QBLK), :]
        grads = do_ref[pl.ds(row0, QBLK), :]
        qcat, docat = [], []
        for j in range(fold):
            cols = slice(j * PAIR, (j + 1) * PAIR)
            low = low0 + 6 * j
            qcat.append(
                pair_rows(
                    rows[:, cols],
                    (hot + side_lanes(side, low), hot + side_lanes(side, low + 3)),
                )
            )
            docat.append(
                pair_rows(
                    grads[:, cols],
                    (side_lanes(side, low + gap), side_lanes(side, low + gap + 3)),
                )
            )
        first = bounds[i, 0]

        def step(c, dq):
            start = pl.multiple_of(first + c * KCHUNK, 128)
            here = pl.ds(start, KCHUNK)
            scores = [dot(kcat[j, here, :], qcat[j], NT) for j in range(fold)]
            slopes = [dot(vcat[j, here, :], docat[j], NT) for j in range(fold)]
            out = []
            for j in range(fold):
                p = jnp.exp(scores[j])
                ds = (p * slopes[j]).astype(bf16)
                dv[j, here, :] += dot(p.astype(bf16), docat[j][:, :PAIR], NN)
                dk[j, here, :] += dot(ds, qcat[j][:, :PAIR], NN)
                out.append(dq[j] + dot(kt[j, :, here], ds, NN))
            return tuple(out)

        dq = lax.fori_loop(
            0, bounds[i, 1], step, (jnp.zeros((PAIR, 2 * QBLK), f32),) * fold
        )

        @pl.when((i >= MAXLEN // QBLK) & (i < (MAXLEN + own) // QBLK))
        def _():
            for j in range(fold):
                gqkv_ref[
                    0, pl.ds(pl.multiple_of(row0 - MAXLEN, QBLK), QBLK), pl.ds(j * PAIR, PAIR)
                ] = (unpair(dq[j]) * HEAD_DIM**-0.5).T.astype(bf16)

        return carry

    lax.fori_loop(0, window // QBLK, block, 0)
    for j in range(fold):
        cols = pl.ds(j * PAIR, PAIR)
        gqkv_ref[1, :, cols] = dk[j, pl.ds(MAXLEN, own), :].astype(bf16)
        gqkv_ref[2, :, cols] = dv[j, pl.ds(MAXLEN, own), :].astype(bf16)

    if more:
        tok_t, place = extra[:2]
        keep, send, sums = (ref.at[0] for ref in refs[1:4])
        sums[...] = jnp.zeros_like(sums)

        def third(n, carry):
            grads = gqkv_ref[n]
            sums[pl.ds(n, 1), :] = col_sum(grads.astype(f32))
            mine, theirs = halves(dot(tok_t[...], grads, NN), place[0], keep.shape[2])
            for g in range(len(mine)):
                keep[n, g] = mine[g]
                send[n, g] = theirs[g]
            return carry

        lax.fori_loop(0, 3, third, 0)


def attend_back(bounds, qkv, grads, hot, mask, own, extra=()):
    window, wide = qkv.shape
    width = wide // 3
    pairs = width // PAIR
    fold = fold_of(pairs, 3)
    parts = pairs // fold
    cols = fold * PAIR
    column = lambda c: pl.BlockSpec((window, cols), lambda g, b: (0, c * parts + g))
    whole = lambda a: pl.BlockSpec(a.shape, lambda g, b: (0, 0))
    shape = jax.ShapeDtypeStruct
    more_in, more_out = [], []
    if extra:
        more_in = [whole(extra[0]), pl.BlockSpec(memory_space=pltpu.SMEM)]
        more_out = [shape((parts, 3, 4, width // 8, cols), bf16)] * 2 + [shape((parts, 8, cols), f32)]
    block = lambda a: pl.BlockSpec((1,) + a.shape[1:], lambda g, b: (g,) + (0,) * (len(a.shape) - 1))
    outs = [shape((parts, 3, own, cols), bf16)] + more_out
    results = pl.pallas_call(
        functools.partial(attend_back_kernel, (6 * fold, 6 * pairs), len(extra)),
        grid_spec=pltpu.PrefetchScalarGridSpec(
            num_scalar_prefetch=1,
            grid=(parts,),
            in_specs=[
                column(0),
                column(1),
                column(2),
                pl.BlockSpec((window, cols), lambda g, b: (0, g)),
                pl.BlockSpec((window, SIDE), lambda g, b: (0, pairs)),
                whole(hot),
                whole(mask),
            ]
            + more_in,
            out_specs=[block(o) for o in outs],
            scratch_shapes=[
                pltpu.VMEM((fold, window + PAD, 2 * PAIR), bf16),
                pltpu.VMEM((fold, window + PAD, 2 * PAIR), bf16),
                pltpu.VMEM((fold, PAIR, window + PAD), bf16),
                pltpu.VMEM((fold, window + PAD, PAIR), f32),
                pltpu.VMEM((fold, window + PAD, PAIR), f32),
            ],
        ),
        out_shape=outs,
        cost_estimate=pl.CostEstimate(
            flops=own * 900 * width * 16, bytes_accessed=window * width * 8, transcendentals=0
        ),
        name="attend_back",
    )(bounds, qkv, qkv, qkv, grads, grads, hot, mask, *extra)
    return results if extra else results[0]


def low3(values):
    high = values.astype(bf16)
    rest = values - high.astype(f32)
    mid = rest.astype(bf16)
    return high, mid, (rest - mid.astype(f32)).astype(bf16)


def dot3(values, chosen, dims):
    return sum(dot(part, chosen, dims) for part in low3(values))


def iota(shape, axis):
    return lax.broadcasted_iota(jnp.int32, shape, axis)


def mean_row(values):
    return jnp.mean(values, axis=-1, keepdims=True)


def col_sum(values):
    return jnp.sum(values, axis=0, keepdims=True)


def norm_back(grad_out, normed, inv_std, gain_vec):
    grad_norm = grad_out * gain_vec
    inner = grad_norm - mean_row(grad_norm) - normed * mean_row(grad_norm * normed)
    return inv_std * inner, col_sum(grad_out * normed), col_sum(grad_out)


ROWS = 256
VECTORS = 24


def middle_kernel(
    heads_part, place, w_in_hbm, w_back_hbm, w_pool_hbm, lse_hbm, cot_hbm, tok, ctx, w_out, b_in, w_class, seqs_of, *refs,
):
    vectors, refs = refs[:7], refs[7:]
    (out_hbm, gar_hbm, gs_hbm, act_hbm, gpre_hbm, gffn_hbm, mid_hbm, gattn_hbm, cls, gpool, vec,
    out, gar, gs, gffn, mid, gattn, lse, cot, more_sems, w_in, w_back, w_pool, act, gpre, slope, unit_a, unit_f, inv_a, inv_f, acc, sems) = refs
    own, width = tok.shape
    b_out, gain_a, shift_a, b_back, gain_f, shift_f, b_pool = (v[...].reshape(1, -1) for v in vectors)
    starts, labels = seqs_of[:, 0:1], seqs_of[:, 1:2]
    chunks, _, wide = act.shape
    blocks = own // ROWS
    n_class = w_class.shape[0]
    loads = [
        pltpu.make_async_copy(w_in_hbm, w_in, sems.at[0]),
        pltpu.make_async_copy(w_back_hbm, w_back, sems.at[1]),
        pltpu.make_async_copy(w_pool_hbm, w_pool, sems.at[2]),
        pltpu.make_async_copy(cot_hbm, cot, more_sems.at[0]),
        pltpu.make_async_copy(lse_hbm, lse, more_sems.at[1]),
    ]
    store_mid, store_out, store_gffn = (
        pltpu.make_async_copy(src, dst, more_sems.at[2 + n])
        for n, (src, dst) in enumerate(((mid, mid_hbm), (out, out_hbm), (gffn, gffn_hbm)))
    )

    def last_stores(b):
        return [
            pltpu.make_async_copy(src.at[at(b)], dst.at[at(b)], more_sems.at[5 + 3 * b + n])
            for n, (src, dst) in enumerate(((gar, gar_hbm), (gs, gs_hbm), (gattn, gattn_hbm)))
        ]

    for load in loads:
        load.start()

    def at(b):
        return pl.ds(pl.multiple_of(b * ROWS, ROWS), ROWS)

    def cols(c):
        return pl.ds(pl.multiple_of(c * wide, wide), wide)

    def norm(hidden, rows, unit, inv, gain, shift):
        centred = hidden - mean_row(hidden)
        inv_std = lax.rsqrt(mean_row(centred * centred) + eps)
        normed = centred * inv_std
        unit[rows, :] = normed
        inv[rows, :] = inv_std
        return (normed * gain[...] + shift[...]).astype(bf16)

    def first_norm(b, carry):
        rows = at(b)
        hidden = tok[rows, :].astype(f32) + dot(ctx[rows, :], w_out[...], NN) + b_out[...]
        mid[rows, :] = norm(hidden, rows, unit_a, inv_a, gain_a, shift_a)
        return carry

    lax.fori_loop(0, blocks, first_norm, 0)
    store_mid.start()
    loads[0].wait()
    loads[1].wait()
    acc[...] = jnp.zeros_like(acc)

    def forward(c, carry):
        for b in range(blocks):
            rows = slice(b * ROWS, (b + 1) * ROWS)
            pre = dot(mid[rows, :], w_in[:, cols(c)], NN) + b_in[:, cols(c)]
            cdf = 0.5 * (1.0 + lax.erf(pre * (0.5**0.5)))
            low = (pre * cdf).astype(bf16)
            act[c, rows, :] = low
            slope[c, rows, :] = cdf + pre * (jnp.exp(-0.5 * pre * pre) * 0.3989422804014327)
            acc[rows, :] += dot(low, w_back[cols(c), :], NN)
        pltpu.make_async_copy(act.at[c], act_hbm.at[c], sems.at[3 + c]).start()
        return carry

    lax.fori_loop(0, chunks, forward, 0)

    def second_norm(b, carry):
        rows = at(b)
        hidden = mid[rows, :].astype(f32) + (acc[rows, :] + b_back[...])
        out[rows, :] = norm(hidden, rows, unit_f, inv_f, gain_f, shift_f)
        return carry

    lax.fori_loop(0, blocks, second_norm, 0)
    store_out.start()
    loads[3].wait()
    loads[4].wait()

    loads[2].wait()
    seqs = starts.shape[0]
    picked = (iota((seqs, own), 1) + place[0] * own == starts[...]).astype(f32)
    sel = picked.astype(bf16)
    owned = jnp.sum(picked, axis=1, keepdims=True)
    cls_low = dot(sel, out[...], NN).astype(bf16)
    cls[...] = cls_low
    pooled = jnp.tanh(dot(cls_low, w_pool[...], NN) + b_pool[...])
    logits = [jnp.sum(pooled * w_class[c : c + 1, :], axis=1, keepdims=True) for c in range(n_class)]
    peak = functools.reduce(jnp.maximum, logits)
    expo = [jnp.exp(x - peak) for x in logits]
    total = sum(expo)
    probs = [x / total for x in expo]
    terms = owned * (peak + jnp.log(total) - sum(p * x for p, x in zip(probs, logits)))
    entropy = jnp.sum(terms, axis=0, keepdims=True)
    g_logits = [
        (probs[c] - (labels[...] == c).astype(f32)) * owned for c in range(n_class)
    ]
    g_pooled = sum(g_logits[c] * w_class[c : c + 1, :] for c in range(n_class))
    g_low = (g_pooled * (1.0 - pooled * pooled)).astype(bf16)
    gpool[...] = g_low
    grad_cls = dot(g_low, w_pool[...], NT)

    def second_back(b, carry):
        rows = at(b)
        here = (
            iota((seqs, ROWS), 1) + (place[0] * own + b * ROWS) == starts[...]
        ).astype(f32).astype(bf16)
        back = sum(dot(here, part, TN) for part in low3(grad_cls))
        grad_out = cot[rows, :].astype(f32) + back
        res, g_gain, g_shift = norm_back(grad_out, unit_f[rows, :], inv_f[rows, :], gain_f[...])
        low = res.astype(bf16)
        gar[rows, :] = res
        gffn[rows, :] = low
        return carry[0] + g_gain, carry[1] + g_shift, carry[2] + col_sum(low.astype(f32))

    zero = jnp.zeros((1, width), f32)
    sums_f = lax.fori_loop(0, blocks, second_back, (zero, zero, zero))
    store_gffn.start()
    acc[...] = jnp.zeros_like(acc)

    def backward(c, carry):
        g_b_in = jnp.zeros((1, wide), f32)
        for b in range(blocks):
            rows = slice(b * ROWS, (b + 1) * ROWS)
            grad_act = dot(gffn[rows, :], w_back[cols(c), :], NT)
            low = (grad_act * slope[c, rows, :]).astype(bf16)
            gpre[c, rows, :] = low
            g_b_in += col_sum(low.astype(f32))
            acc[rows, :] += dot(low, w_in[:, cols(c)], NT)
        vec[pl.ds(8 + c, 1), :] = g_b_in
        pltpu.make_async_copy(gpre.at[c], gpre_hbm.at[c], sems.at[3 + chunks + c]).start()
        return carry

    lax.fori_loop(0, chunks, backward, 0)

    heads = width // HEAD_DIM
    lane = iota((1, SIDE), 1)
    gap = LSE0 + 3 * heads
    feature, flane = iota((width, SIDE), 0), iota((width, SIDE), 1)
    third = flane - gap - 3 * (feature // HEAD_DIM)
    head_sum = ((third >= 0) & (third < 3)).astype(f32).astype(bf16)
    lrow, llane = iota((lse.shape[0], SIDE), 0), iota((lse.shape[0], SIDE), 1)
    lhead = (lrow // 8) * heads_part + lrow % 8
    spread = [
        ((llane == LSE0 + 3 * lhead + p) & (lrow % 8 < heads_part)).astype(f32).astype(bf16)
        for p in range(3)
    ]
    which = lax.rem(lane - gap + 3 * heads, 3)

    def first_back(b, carry):
        rows = at(b)
        grad_mid = gar[rows, :] + acc[rows, :]
        res, g_gain, g_shift = norm_back(grad_mid, unit_a[rows, :], inv_a[rows, :], gain_a[...])
        low = res.astype(bf16)
        gar[rows, :] = res
        gattn[rows, :] = low
        grad_ctx = dot(low, w_out[...], NT).astype(bf16)
        gs[rows, :width] = grad_ctx
        delta = dot3(grad_ctx.astype(f32) * ctx[rows, :].astype(f32), head_sum, NN)
        high, mid_part, rest = low3(-delta)
        side = jnp.where(which == 0, high, jnp.where(which == 1, mid_part, rest))
        lse_parts = low3(-lse[:, rows])
        side_lse = sum(dot(part, spread[p], TN) for p, part in enumerate(lse_parts))
        gs[rows, width:] = side + side_lse.astype(bf16)
        for copy in last_stores(b):
            copy.start()
        return carry[0] + g_gain, carry[1] + g_shift, carry[2] + col_sum(low.astype(f32))

    sums_a = lax.fori_loop(0, blocks, first_back, (zero, zero, zero))
    for row, value in enumerate((sums_a[2], sums_a[0], sums_a[1], sums_f[2], sums_f[0], sums_f[1])):
        vec[row : row + 1, :] = value
    vec[6:7, :] = col_sum(g_low.astype(f32))
    vec[7:8, :] = jnp.broadcast_to(entropy, (1, width))
    for c in range(n_class):
        vec[8 + chunks + c : 9 + chunks + c, :] = col_sum(pooled * g_logits[c])
    done = 8 + chunks + n_class
    vec[done:, :] = jnp.zeros((VECTORS - done, width), f32)
    for c in range(chunks):
        pltpu.make_async_copy(act.at[c], act_hbm.at[c], sems.at[3 + c]).wait()
        pltpu.make_async_copy(gpre.at[c], gpre_hbm.at[c], sems.at[3 + chunks + c]).wait()
    for copy in (store_mid, store_out, store_gffn):
        copy.wait()
    for b in range(blocks):
        for copy in last_stores(b):
            copy.wait()


def middle_layer(heads_part, place, w_in, w_back, w_pool, tok, ctx, lse, cot, w_out, b_in, w_class, seqs_of, vectors):
    own, width = tok.shape
    ff = w_in.shape[1]
    chunks = ff // width
    seqs = seqs_of.shape[0]
    vmem = pl.BlockSpec(memory_space=pltpu.VMEM)
    hbm = pl.BlockSpec(memory_space=pl.ANY)
    shape = jax.ShapeDtypeStruct
    flops = 2 * own * width * (6 * width + 4 * ff)
    return pl.pallas_call(
        functools.partial(middle_kernel, heads_part),
        in_specs=[pl.BlockSpec(memory_space=pltpu.SMEM)] + [hbm] * 5 + [vmem] * 13,
        out_specs=[hbm] * 8 + [vmem] * 3,
        out_shape=[
            shape((own, width), bf16),
            shape((own, width), f32),
            shape((own, width + SIDE), bf16),
            shape((chunks, own, width), bf16),
            shape((chunks, own, width), bf16),
            shape((own, width), bf16),
            shape((own, width), bf16),
            shape((own, width), bf16),
            shape((seqs, width), bf16),
            shape((seqs, width), bf16),
            shape((VECTORS, width), f32),
        ],
        scratch_shapes=[
            pltpu.VMEM((own, width), bf16),
            pltpu.VMEM((own, width), f32),
            pltpu.VMEM((own, width + SIDE), bf16),
            pltpu.VMEM((own, width), bf16),
            pltpu.VMEM((own, width), bf16),
            pltpu.VMEM((own, width), bf16),
            pltpu.VMEM(lse.shape, f32),
            pltpu.VMEM(cot.shape, bf16),
            pltpu.SemaphoreType.DMA((5 + 3 * (own // ROWS),)),
            pltpu.VMEM(w_in.shape, bf16),
            pltpu.VMEM(w_back.shape, bf16),
            pltpu.VMEM(w_pool.shape, bf16),
            pltpu.VMEM((chunks, own, width), bf16),
            pltpu.VMEM((chunks, own, width), bf16),
            pltpu.VMEM((chunks, own, width), f32),
            pltpu.VMEM((own, width), f32),
            pltpu.VMEM((own, width), f32),
            pltpu.VMEM((own, 1), f32),
            pltpu.VMEM((own, 1), f32),
            pltpu.VMEM((own, width), f32),
            pltpu.SemaphoreType.DMA((3 + 2 * chunks,)),
        ],
        compiler_params=pltpu.CompilerParams(vmem_limit_bytes=62 * 2**20),
        cost_estimate=pl.CostEstimate(flops=flops, bytes_accessed=30 * 2**20, transcendentals=0),
        name="middle_layer",
    )(place, w_in, w_back, w_pool, lse, cot, tok, ctx, w_out, b_in, w_class, seqs_of, *vectors)


def split_core(tile, core, half, keep, send, first):
    for n in range(tile.shape[0] // (2 * half)):
        even = tile[2 * n * half : (2 * n + 1) * half, :]
        odd = tile[(2 * n + 1) * half : (2 * n + 2) * half, :]
        keep[first + n, :, :] = jnp.where(core == 0, even, odd).astype(bf16)
        send[first + n, :, :] = jnp.where(core == 0, odd, even).astype(bf16)


def weight_grads_kernel(
    core, act, gpre, gffn, mid, ctx, gattn, cls, gpool,
    back_keep, back_send, in_keep, in_send, out_keep, out_send, mid_t,
):
    y = pl.program_id(0)

    @pl.when(y == 0)
    def _():
        mid_t[...] = mid[...].T
        split_core(dot(ctx[...], gattn[...], TN), core[0], out_keep.shape[1], out_keep, out_send, 0)

    @pl.when(y == 1)
    def _():
        split_core(dot(cls[...], gpool[...], TN), core[0], out_keep.shape[1], out_keep, out_send, 0)

    split_core(dot(act[0], gffn[...], TN), core[0], back_keep.shape[1], back_keep, back_send, 0)
    split_core(dot(mid_t[...], gpre[0], NN), core[0], in_keep.shape[1], in_keep, in_send, 0)


def weight_grads(core, n_seq, act, gpre, gffn, mid, ctx, gattn, cls, gpool):
    chunks, own, width = act.shape
    groups = n_seq // 2
    half_b, half_w = chunks * width // n_seq, width // n_seq
    shape = jax.ShapeDtypeStruct
    whole = lambda a: pl.BlockSpec(a.shape, lambda y, c: (0, 0))
    tile = pl.BlockSpec((1, own, width), lambda y, c: (y, 0, 0))
    back = pl.BlockSpec((groups // chunks, half_b, width), lambda y, c: (y, 0, 0))
    inner = pl.BlockSpec((groups, half_w, width), lambda y, c: (0, 0, y))
    outer = pl.BlockSpec((groups, half_w, width), lambda y, c: (0, 0, jnp.minimum(y, 1)))
    return pl.pallas_call(
        weight_grads_kernel,
        grid_spec=pltpu.PrefetchScalarGridSpec(
            num_scalar_prefetch=1,
            grid=(chunks,),
            in_specs=[tile, tile] + [whole(a) for a in (gffn, mid, ctx, gattn, cls, gpool)],
            out_specs=[back, back, inner, inner, outer, outer],
            scratch_shapes=[pltpu.VMEM((width, own), bf16)],
        ),
        out_shape=[shape((groups, half_b, width), bf16)] * 2
        + [shape((groups, half_w, chunks * width), bf16)] * 2
        + [shape((groups, half_w, 2 * width), bf16)] * 2,
        compiler_params=pltpu.CompilerParams(vmem_limit_bytes=48 * 2**20),
        cost_estimate=pl.CostEstimate(
            flops=2 * own * width * width * (2 * chunks + 1), bytes_accessed=30 * 2**20, transcendentals=0
        ),
        name="weight_grads",
    )(core, act, gpre, gffn, mid, ctx, gattn, cls, gpool)


def last_kernel(n_parts, core, *refs):
    tok, gar, w_qkv = refs[:3]
    parts = refs[3 : 3 + n_parts]
    gtok, vec = refs[3 + n_parts : 5 + n_parts]
    pairs = refs[5 + n_parts : 11 + n_parts]
    tok_t = refs[11 + n_parts]
    c = pl.program_id(0)

    @pl.when(c == 0)
    def _():
        tok_t[...] = tok[...].T
        gtok[...] = gar[...]
        vec[...] = jnp.zeros_like(vec)

    grads = jnp.concatenate([p[0] for p in parts], axis=1)
    gtok[...] += dot(grads, w_qkv[...], NT)
    vec[pl.ds(c, 1), :] = col_sum(grads.astype(f32))
    tile = dot(tok_t[...], grads, NN)
    for n in range(3):

        @pl.when(c == n)
        def _():
            keep, send = pairs[2 * n], pairs[2 * n + 1]
            split_core(tile, core[0], keep.shape[1], keep, send, 0)


def last_layer(core, n_seq, tok, gar, w_qkv, parts):
    own, width = tok.shape
    groups, half = n_seq // 2, width // n_seq
    shape = jax.ShapeDtypeStruct
    whole = lambda a: pl.BlockSpec(a.shape, lambda c, k: (0,) * len(a.shape))
    pair = pl.BlockSpec((groups, half, width), lambda c, k: (0, 0, 0))
    return pl.pallas_call(
        functools.partial(last_kernel, len(parts)),
        grid_spec=pltpu.PrefetchScalarGridSpec(
            num_scalar_prefetch=1,
            grid=(3,),
            in_specs=[whole(tok), whole(gar), pl.BlockSpec((width, width), lambda c, k: (0, c))]
            + [pl.BlockSpec((1,) + p.shape[1:], lambda c, k: (c, 0, 0)) for p in parts],
            out_specs=[whole(gar), pl.BlockSpec((8, width), lambda c, k: (0, 0))] + [pair] * 6,
            scratch_shapes=[pltpu.VMEM((width, own), bf16)],
        ),
        out_shape=[shape((own, width), f32), shape((8, width), f32)]
        + [shape((groups, half, width), bf16)] * 6,
        compiler_params=pltpu.CompilerParams(vmem_limit_bytes=40 * 2**20),
        cost_estimate=pl.CostEstimate(
            flops=12 * own * width * width, bytes_accessed=12 * 2**20, transcendentals=0
        ),
        name="last_layer",
    )(core, tok, gar, w_qkv, *parts)


MESH = pl.DeviceIdType.MESH
OTHER_CORE, NEAR = 1, (2, 4, 6)


class Sends:
    def __init__(self, send_sems, recv_sems):
        self.sems, self.copies, self.at = (send_sems, recv_sems), {}, 0

    def plan(self, name, src, dst, **device):
        self.copies[name] = pltpu.make_async_remote_copy(
            src_ref=src,
            dst_ref=dst,
            send_sem=self.sems[0].at[self.at],
            recv_sem=self.sems[1].at[self.at],
            device_id=device,
            device_id_type=MESH,
        )
        self.at += 1

    def start(self, *names):
        for name in names:
            self.copies[name].start()

    def arrived(self, *names):
        for name in names:
            self.copies[name].wait_recv()

    def drain(self):
        for copy in self.copies.values():
            copy.wait_send()


def greet(devices):
    barrier = pltpu.get_barrier_semaphore()
    for device in devices:
        pl.semaphore_signal(barrier, inc=1, device_id=device, device_id_type=MESH)
    pl.semaphore_wait(barrier, len(devices))


def halves(tile, core, half):
    even = [tile[2 * n * half : (2 * n + 1) * half] for n in range(tile.shape[0] // (2 * half))]
    odd = [tile[(2 * n + 1) * half : (2 * n + 2) * half] for n in range(tile.shape[0] // (2 * half))]
    keep = [jnp.where(core == 0, e, o).astype(bf16) for e, o in zip(even, odd)]
    send = [jnp.where(core == 0, o, e).astype(bf16) for e, o in zip(even, odd)]
    return keep, send


def front_kernel(
    tok, w_hbm, bias_q, bias_v, lens, labels, qkv_hbm, hot, mask, bounds, seqs_of,
    sides, w, work, rows_of, load_sem, out_sems, send_sems, recv_sems,
):
    head, n_head = lax.axis_index("head"), lax.axis_size("head")
    own, width = tok.shape
    window = hot.shape[0]
    load = pltpu.make_async_copy(w_hbm, w, load_sem)
    load.start()
    not_first, not_last = head > 0, head < n_head - 1
    barrier = pltpu.get_barrier_semaphore()

    @pl.when(not_first)
    def _():
        pl.semaphore_signal(barrier, inc=1, device_id={"head": head - 1}, device_id_type=MESH)

    @pl.when(not_last)
    def _():
        pl.semaphore_signal(barrier, inc=1, device_id={"head": head + 1}, device_id_type=MESH)

    pl.semaphore_wait(barrier, not_first.astype(jnp.int32) + not_last.astype(jnp.int32))
    pieces = MAXLEN // ROWS
    here = lambda n: pl.ds(n * ROWS, ROWS)
    up, down = [], []
    for n in range(pieces):
        for copies, first, side, device in (
            (up, own - MAXLEN, 0, lax.rem(head + 1, n_head)),
            (down, 0, 1, lax.rem(head + n_head - 1, n_head)),
        ):
            copies.append(
                pltpu.make_async_remote_copy(
                    src_ref=tok.at[pl.ds(first + n * ROWS, ROWS)], dst_ref=sides.at[side, here(n)],
                    send_sem=send_sems.at[side, n], recv_sem=recv_sems.at[side, n],
                    device_id={"head": device}, device_id_type=MESH,
                )
            )

    @pl.when(not_last)
    def _():
        for copy in up:
            copy.start()

    @pl.when(not_first)
    def _():
        for copy in down:
            copy.start()

    @pl.when(head == 0)
    def _():
        sides[0] = jnp.zeros((MAXLEN, width), bf16)

    @pl.when(head == n_head - 1)
    def _():
        sides[1] = jnp.zeros((MAXLEN, width), bf16)

    def stored(at, n):
        return pltpu.make_async_copy(
            work.at[pl.ds(at, ROWS)], qkv_hbm.at[pl.ds(at, ROWS)], out_sems.at[n]
        )

    def project(rows, at, n):
        into = pl.ds(at, ROWS)
        query = (dot(rows, w[:, :width], NN) + bias_q[...].reshape(1, -1)) * HEAD_DIM**-0.5
        work[into, :width] = query.astype(bf16)
        work[into, width : 2 * width] = dot(rows, w[:, width : 2 * width], NN).astype(bf16)
        value = dot(rows, w[:, 2 * width :], NN) + bias_v[...].reshape(1, -1)
        work[into, 2 * width :] = value.astype(bf16)
        stored(at, n).start()

    load.wait()

    def own_rows(n, carry):
        at = pl.multiple_of(n * ROWS, ROWS)
        project(tok[pl.ds(at, ROWS), :], pl.multiple_of(MAXLEN + at, ROWS), n)
        return carry

    lax.fori_loop(0, own // ROWS, own_rows, 0)

    n_seqs = lens.shape[1]
    rows_of[...] = jnp.zeros_like(rows_of)
    rows_of[0:1, :n_seqs] = lens[...]
    rows_of[1:2, :n_seqs] = labels[...]
    i, j = iota((SIDE, SIDE), 0), iota((SIDE, SIDE), 1)
    length, label = rows_of[0:1, :].astype(f32), rows_of[1:2, :].astype(f32)
    to_col = lambda row, chosen: jnp.sum(jnp.where(chosen, row, 0.0), axis=1, keepdims=True)
    length_col, ends_col = to_col(length, i == j), to_col(length, j <= i)
    ends = jnp.sum(jnp.where(i <= j, length_col, 0.0), axis=0, keepdims=True)
    starts = ends - length
    group = float(own * n_head)
    n_rows = seqs_of.shape[0]
    row, lane = i[:n_rows], j[:n_rows]
    first_col = jnp.where(row < n_seqs, (ends_col - length_col)[:n_rows], -1.0)
    label_col = to_col(label, i == j)[:n_rows]
    seqs_of[...] = jnp.where(lane == 0, first_col, jnp.where(lane == 1, label_col, 0.0)).astype(jnp.int32)

    base = head * own - MAXLEN
    row, lane = i[:16], j[:16]
    blk = (base + row * QBLK).astype(f32)
    taken = lane < n_seqs
    low = jnp.max(jnp.where(taken & (starts <= blk), starts, -1.0), axis=1, keepdims=True)
    high = jnp.min(
        jnp.where(taken & (ends > blk + (QBLK - 1)), ends, group), axis=1, keepdims=True
    )
    at = row * QBLK
    is_own = (at >= MAXLEN) & (at < MAXLEN + own)
    low = jnp.broadcast_to(low.astype(jnp.int32), at.shape) - base
    high = jnp.broadcast_to(high.astype(jnp.int32), at.shape) - base
    low = jnp.where(is_own, low, jnp.maximum(low, MAXLEN))
    high = jnp.where(is_own, high, jnp.minimum(high, MAXLEN + own))
    low = (low >> 7) << 7
    valid = (blk >= 0.0) & (blk < group)
    steps = jnp.where(valid, jnp.maximum((high - low + KCHUNK - 1) >> (KCHUNK.bit_length() - 1), 0), 0)
    bounds[...] = jnp.where(lane == 0, low, jnp.where(lane == 1, steps, 0))

    lane = iota((QBLK, SIDE), 1)

    def masks(n, carry):
        at = pl.multiple_of(n * QBLK, QBLK)
        pos = (iota((QBLK, SIDE), 0) + (base + at)).astype(f32)
        inside = ((starts <= pos) & (pos < ends)).astype(f32)
        hot[pl.ds(at, QBLK), :] = inside.astype(bf16)
        mask[pl.ds(at, QBLK), :] = jnp.where(lane < n_seqs, (inside - 1.0) * BIG, 1.0).astype(bf16)
        return carry

    lax.fori_loop(0, window // QBLK, masks, 0)
    mask[pl.ds(window, PAD), :] = jnp.where(iota((PAD, SIDE), 1) < n_seqs, -BIG, 1.0).astype(bf16)

    for n in range(pieces):

        @pl.when(not_first)
        def _():
            up[n].wait_recv()

        @pl.when(not_last)
        def _():
            down[n].wait_recv()

        def side_rows(side, carry):
            at = pl.multiple_of(side * (MAXLEN + own) + n * ROWS, ROWS)
            project(sides[side, here(n), :], at, own // ROWS + 2 * n + side)
            return carry

        lax.fori_loop(0, 2, side_rows, 0)

    for n in range(own // ROWS):
        stored(MAXLEN + n * ROWS, n).wait()
    for n in range(pieces):
        for side in range(2):
            stored(side * (MAXLEN + own) + n * ROWS, own // ROWS + 2 * n + side).wait()

    @pl.when(not_last)
    def _():
        for copy in up:
            copy.wait_send()

    @pl.when(not_first)
    def _():
        for copy in down:
            copy.wait_send()


def front(tok, w_qkv, bias_q, bias_v, lens, labels):
    own, width = tok.shape
    window = own + 2 * MAXLEN
    seqs = lens.shape[1] + -lens.shape[1] % 16
    pieces = MAXLEN // ROWS
    shape = jax.ShapeDtypeStruct
    vmem, hbm = pl.BlockSpec(memory_space=pltpu.VMEM), pl.BlockSpec(memory_space=pl.ANY)
    return pl.pallas_call(
        front_kernel,
        in_specs=[vmem, hbm] + [vmem] * 4,
        out_specs=[hbm] + [vmem] * 4,
        out_shape=[
            shape((window, 3 * width), bf16),
            shape((window, SIDE), bf16),
            shape((window + PAD, SIDE), bf16),
            shape((16, SIDE), jnp.int32),
            shape((seqs, SIDE), jnp.int32),
        ],
        scratch_shapes=[
            pltpu.VMEM((2, MAXLEN, width), bf16),
            pltpu.VMEM(w_qkv.shape, bf16),
            pltpu.VMEM((window, 3 * width), bf16),
            pltpu.VMEM((8, SIDE), jnp.int32),
            pltpu.SemaphoreType.DMA,
            pltpu.SemaphoreType.DMA((own // ROWS + 2 * pieces,)),
            pltpu.SemaphoreType.DMA((2, pieces)),
            pltpu.SemaphoreType.DMA((2, pieces)),
        ],
        compiler_params=pltpu.CompilerParams(
            vmem_limit_bytes=62 * 2**20, collective_id=2, has_side_effects=True
        ),
        cost_estimate=pl.CostEstimate(
            flops=6 * window * width * width, bytes_accessed=16 * 2**20, transcendentals=0
        ),
        name="front",
    )(tok, w_qkv, bias_q, bias_v, lens, labels)


def grads_kernel(
    ctx_hbm, gattn_hbm, mid_hbm, gffn_hbm, tok_hbm, gs_hbm, act_hbm, gpre_hbm, cls, gpool,
    gsw, *refs,
):
    stores, outs, held, refs = refs[:8], refs[8:16], refs[16:22], refs[22:]
    tok_t, (ctx, gattn, mid, gffn, tok, gs) = outs[7], held
    store = [
        pltpu.make_async_copy(src, dst, refs[-1].at[6 + n])
        for n, (src, dst) in enumerate(zip(outs, stores))
    ]
    load = [
        pltpu.make_async_copy(src, dst, refs[-1].at[n])
        for n, (src, dst) in enumerate(
            zip((ctx_hbm, gattn_hbm, mid_hbm, gffn_hbm, tok_hbm, gs_hbm), held)
        )
    ]
    outs = (*outs[:6], outs[6].at[0], outs[6].at[1])
    (act, gpre, mid_t, keep_a, send_a, got_a, keep_b, send_b, got_b, keep_c, send_c, got_c, split,
     loads, send_sems, recv_sems, halo_sems, _) = refs
    seq, head = lax.axis_index("seq"), lax.axis_index("head")
    n_head = lax.axis_size("head")
    core = lax.rem(seq, 2)
    chunks, own, width = act.shape
    half_b, half_w = keep_a.shape[1], keep_b.shape[2]
    for n in range(3):
        load[n].start()
    for c in range(chunks):
        pltpu.make_async_copy(gpre_hbm.at[c], gpre.at[c], loads.at[chunks + c]).start()
        if c == 0:
            load[3].start()
        pltpu.make_async_copy(act_hbm.at[c], act.at[c], loads.at[c]).start()
    load[5].start()
    load[4].start()

    barrier = pltpu.get_barrier_semaphore()
    pl.semaphore_signal(barrier, inc=1, device_id={"seq": seq ^ OTHER_CORE}, device_id_type=MESH)

    @pl.when(head > 0)
    def _():
        pl.semaphore_signal(barrier, inc=1, device_id={"head": head - 1}, device_id_type=MESH)

    @pl.when(head < n_head - 1)
    def _():
        pl.semaphore_signal(barrier, inc=1, device_id={"head": head + 1}, device_id_type=MESH)

    pl.semaphore_wait(barrier, 1 + (head > 0).astype(jnp.int32) + (head < n_head - 1).astype(jnp.int32))

    up = pltpu.make_async_remote_copy(
        src_ref=gs_hbm.at[pl.ds(own - MAXLEN, MAXLEN)], dst_ref=gsw.at[pl.ds(0, MAXLEN)],
        send_sem=halo_sems.at[0], recv_sem=halo_sems.at[1],
        device_id={"head": lax.rem(head + 1, n_head)}, device_id_type=MESH,
    )
    down = pltpu.make_async_remote_copy(
        src_ref=gs_hbm.at[pl.ds(0, MAXLEN)], dst_ref=gsw.at[pl.ds(own + MAXLEN, MAXLEN)],
        send_sem=halo_sems.at[2], recv_sem=halo_sems.at[3],
        device_id={"head": lax.rem(head + n_head - 1, n_head)}, device_id_type=MESH,
    )
    stay = pltpu.make_async_copy(gs, gsw.at[pl.ds(MAXLEN, own)], halo_sems.at[4])

    @pl.when(head < n_head - 1)
    def _():
        up.start()

    @pl.when(head > 0)
    def _():
        down.start()

    def to_core(send, got, first, n):
        return pltpu.make_async_remote_copy(
            src_ref=send.at[n], dst_ref=got.at[n],
            send_sem=send_sems.at[first + n], recv_sem=recv_sems.at[first + n],
            device_id={"seq": seq ^ OTHER_CORE}, device_id_type=MESH,
        )

    copy_a = lambda n: to_core(send_a, got_a, 0, n)
    copy_b = lambda n: to_core(send_b, got_b, chunks, n)
    copy_c = lambda n: to_core(send_c, got_c, 2 * chunks, n)

    def put(tile, half, keep, send):
        mine, theirs = halves(tile, core, half)
        for g in range(len(mine)):
            keep[g] = mine[g]
            send[g] = theirs[g]

    put(dot(cls[...], gpool[...], TN), half_w, keep_c.at[1], send_c.at[1])
    load[0].wait()
    load[1].wait()
    put(dot(ctx[...], gattn[...], TN), half_w, keep_c.at[0], send_c.at[0])
    load[2].wait()
    mid_t[...] = mid[...].T
    load[3].wait()

    def chunk(c, carry):
        pltpu.make_async_copy(gpre_hbm.at[c], gpre.at[c], loads.at[chunks + c]).wait()
        put(dot(mid_t[...], gpre[c], NN), half_w, keep_b.at[c], send_b.at[c])

        @pl.when(c == 0)
        def _():
            copy_c(0).start()
            copy_c(1).start()

        @pl.when(c > 0)
        def _():
            copy_a(jnp.maximum(c - 1, 0)).start()

        pltpu.make_async_copy(act_hbm.at[c], act.at[c], loads.at[c]).wait()
        mine, theirs = halves(dot(act[c], gffn[...], TN), core, half_b)
        keep_a[c], send_a[c] = mine[0], theirs[0]
        copy_b(c).start()
        return carry

    lax.fori_loop(0, chunks, chunk, 0)

    load[5].wait()
    stay.start()
    load[4].wait()
    tok_t[...] = tok[...].T

    place = seq // 2
    quarter = half_w // 4
    rows_a = half_b // 4
    turns = (1, 2, 3, 0)
    for n in range(2):
        copy_c(n).wait_recv()
        for r in turns:
            total = keep_c[n, place ^ r].astype(f32) + got_c[n, place ^ r].astype(f32)
            for h in range(4):
                outs[r][h, rows_a + n * quarter : rows_a + (n + 1) * quarter, :] = total[
                    h * quarter : (h + 1) * quarter
                ].astype(outs[r].dtype)
    copy_a(chunks - 1).start()
    store[7].start()

    def sum_b(c, carry):
        copy_b(c).wait_recv()
        for g in range(4):
            total = keep_b[c, g].astype(f32) + got_b[c, g].astype(f32)
            for h in range(4):
                split[h, g] = total[h * quarter : (h + 1) * quarter]
        cols = pl.ds(pl.multiple_of(c * width, width), width)
        for r in range(4):
            for g in range(4):
                outs[4 + r][g, :, cols] = split[head ^ r, g].astype(outs[4 + r].dtype)
        return carry

    lax.fori_loop(0, chunks, sum_b, 0)
    for n in (5, 6, 4):
        store[n].start()
    for c in range(chunks):
        copy_a(c).wait_recv()
    for r in turns:
        total = keep_a[place ^ r].astype(f32) + got_a[place ^ r].astype(f32)
        for h in range(4):
            outs[r][h, :rows_a, :] = total[h * rows_a : (h + 1) * rows_a].astype(outs[r].dtype)
        store[r].start()
    for c in range(chunks):
        copy_a(c).wait_send()
        copy_b(c).wait_send()
    for n in range(2):
        copy_c(n).wait_send()
    stay.wait()
    for copy in store:
        copy.wait()

    @pl.when(head < n_head - 1)
    def _():
        up.wait_send()
        down.wait_recv()

    @pl.when(head > 0)
    def _():
        up.wait_recv()
        down.wait_send()


def send_grads(act, gpre, gs, gffn, mid, ctx, gattn, cls, gpool, tok):
    chunks, own, width = act.shape
    half_b, half_w = chunks * width // 8, width // 8
    window = own + 2 * MAXLEN
    shape = jax.ShapeDtypeStruct
    vmem, hbm = pl.BlockSpec(memory_space=pltpu.VMEM), pl.BlockSpec(memory_space=pl.ANY)
    kinds = (f32, bf16, bf16, bf16)
    outs = (
        [shape((4, half_b // 4 + half_w // 2, width), k) for k in kinds]
        + [shape((4, half_w // 4, chunks * width), k) for k in kinds[:2]]
        + [shape((2, 4, half_w // 4, chunks * width), bf16), shape((width, own), bf16)]
    )
    held = (ctx, gattn, mid, gffn, tok, gs)
    gsw, *pieces, tok_t = pl.pallas_call(
        grads_kernel,
        in_specs=[hbm] * 8 + [vmem] * 2,
        out_specs=[hbm] * 9,
        out_shape=[shape((window, width + SIDE), bf16)] + outs,
        scratch_shapes=[pltpu.VMEM(o.shape, o.dtype) for o in [*outs, *held]]
        + [
            pltpu.VMEM((chunks, own, width), bf16),
            pltpu.VMEM((chunks, own, width), bf16),
            pltpu.VMEM((width, own), bf16),
        ]
        + [pltpu.VMEM((chunks, half_b, width), bf16)] * 3
        + [pltpu.VMEM((chunks, 4, half_w, width), bf16)] * 3
        + [pltpu.VMEM((2, 4, half_w, width), bf16)] * 3
        + [
            pltpu.VMEM((4, 4, half_w // 4, width), f32),
            pltpu.SemaphoreType.DMA((2 * chunks,)),
            pltpu.SemaphoreType.DMA((2 * chunks + 2,)),
            pltpu.SemaphoreType.DMA((2 * chunks + 2,)),
            pltpu.SemaphoreType.DMA((5,)),
            pltpu.SemaphoreType.DMA((14,)),
        ],
        compiler_params=pltpu.CompilerParams(
            vmem_limit_bytes=62 * 2**20, collective_id=0, has_side_effects=True
        ),
        cost_estimate=pl.CostEstimate(
            flops=2 * own * width * width * (2 * chunks + 1), bytes_accessed=30 * 2**20, transcendentals=0
        ),
        name="send_grads",
    )(*held, act, gpre, cls, gpool)
    return gsw, tok_t, *pieces


def finish_kernel(n_parts, *refs):
    inputs, refs = refs[:14], refs[14:]
    sends_q = inputs[9]
    gtok, sum_a, sum_b, sum_out, sum_pool, sum_q, sum_v = refs[:7]
    n_held = 11
    held, refs = refs[7 : 7 + n_held], refs[7 + n_held :]
    own_a, near_a, own_b, near_b, vec = held[0], held[1:4], held[4], (held[5], held[6].at[0]), held[7]
    keeps, vec_parts, parts = held[8:]
    (w_qkv, all_a, send_a, got_a, all_b, send_b, got_b, got_f, got_q, own_q, send_n, got_n, all_q, send_z, got_z,
     vecs, got_v, loads, send_sems, recv_sems) = refs
    wanted = inputs[:8] + inputs[10:-1] + (inputs[8], inputs[-1])
    copies = [
        pltpu.make_async_copy(src, dst, loads.at[n])
        for n, (src, dst) in enumerate(zip(wanted, held + (w_qkv, gtok)))
    ]
    for copy in copies:
        copy.start()
    seq, head = lax.axis_index("seq"), lax.axis_index("head")
    place = seq // 2
    width = gtok.shape[1]
    quarter = width // 32
    cols = width // n_parts
    line = (1, 2, 3)
    greet(
        [{"seq": seq ^ OTHER_CORE}]
        + [{"seq": seq ^ near} for near in NEAR]
        + [{"head": head ^ r} for r in line]
    )
    sends = Sends(send_sems, recv_sems)
    for r in line:
        sends.plan(("a", r), send_a.at[r - 1], got_a.at[r - 1], head=head ^ r)
        sends.plan(("b", r), send_b.at[r - 1], got_b.at[r - 1], seq=seq ^ NEAR[r - 1])
    for p in range(n_parts):
        sends.plan(("core", p), sends_q.at[p], got_q.at[p], seq=seq ^ OTHER_CORE)
        for r in line:
            sends.plan(("near", p, r), send_n.at[p, r - 1], got_n.at[p, r - 1], seq=seq ^ NEAR[r - 1])
            sends.plan(("line", p, r), send_z.at[p, r - 1], got_z.at[p, r - 1], head=head ^ r)
    sends.plan(("core", "v"), vecs.at[0], got_v.at[0], seq=seq ^ OTHER_CORE)
    for r in line:
        sends.plan(("near", "v", r), vecs.at[1], got_v.at[r], seq=seq ^ NEAR[r - 1])
        sends.plan(("line", "v", r), vecs.at[2], got_v.at[3 + r], head=head ^ r)
    sends.plan("pass", inputs[6].at[1], got_f, head=head ^ 1)
    sends.start(*[("core", p) for p in range(n_parts)])
    sends.start("pass")

    for copy in copies[:10]:
        copy.wait()
    rows_v = vec.shape[0]
    vecs[0, :rows_v, :] = vec[...]
    for p in range(n_parts):
        vecs[0, rows_v:, p * cols : (p + 1) * cols] = vec_parts[p]
    for h in range(4):
        all_a[h] = (own_a[h] + near_a[0][h].astype(f32)) + (
            near_a[1][h].astype(f32) + near_a[2][h].astype(f32)
        )
    for r in line:
        send_a[r - 1] = all_a[head ^ r].astype(bf16)
    sends.start(("core", "v"))

    def start_near(p):
        sends.start(*[("near", p, r) for r in line])

    for p in range(n_parts):
        sends.arrived(("core", p))
        for r in line:
            for n in range(3):
                send_n[p, r - 1, n] = (
                    keeps[p, n, place ^ r].astype(f32) + got_q[p, n, place ^ r].astype(f32)
                ).astype(bf16)
        for n in range(3):
            own_q[p, n] = keeps[p, n, place].astype(f32) + got_q[p, n, place].astype(f32)
        if p == 0:
            sends.start(*[("a", r) for r in line])
        else:
            start_near(p - 1)
    start_near(n_parts - 1)
    sends.arrived(("core", "v"))
    vecs[1] = vecs[0] + got_v[0]
    sends.arrived("pass")
    for g in range(4):
        all_b[g] = (own_b[g] + near_b[0][g].astype(f32)) + (
            near_b[1][g].astype(f32) + got_f[g].astype(f32)
        )
    for r in line:
        send_b[r - 1] = all_b[place ^ r].astype(bf16)
    for copy in copies[10:]:
        copy.wait()

    def back(n, carry):
        here = pl.ds(pl.multiple_of(n * width, width), width)
        gtok[...] += dot(jnp.concatenate([parts[p, n] for p in range(n_parts)], axis=1), w_qkv[:, here], NT)

        @pl.when(n == 0)
        def _():
            sends.start(*[("near", "v", r) for r in line])
            sends.start(*[("b", r) for r in line])

        return carry

    lax.fori_loop(0, 3, back, 0)

    for p in range(n_parts):
        sends.arrived(*[("near", p, r) for r in line])
        for h in range(4):
            rows = slice(h * quarter, (h + 1) * quarter)
            for n in range(3):
                all_q[p, h, n] = (own_q[p, n, rows, :] + got_n[p, 0, n, rows, :].astype(f32)) + (
                    got_n[p, 1, n, rows, :].astype(f32) + got_n[p, 2, n, rows, :].astype(f32)
                )
        for r in line:
            send_z[p, r - 1] = all_q[p, head ^ r].astype(bf16)
        if p > 0:
            sends.start(*[("line", p - 1, r) for r in line])
    sends.arrived(*[("near", "v", r) for r in line])
    vecs[2] = (vecs[1] + got_v[1]) + (got_v[2] + got_v[3])
    sends.start(*[("line", n_parts - 1, r) for r in line])
    sends.arrived(*[("a", r) for r in line])
    total = (all_a[head] + got_a[0].astype(f32)) + (got_a[1].astype(f32) + got_a[2].astype(f32))
    rows_a = sum_a.shape[0]
    sum_a[...] = total[:rows_a]
    sum_out[...] = total[rows_a : rows_a + quarter]
    sum_pool[...] = total[rows_a + quarter :]
    sends.start(*[("line", "v", r) for r in line])
    sends.arrived(*[("b", r) for r in line])
    sum_b[...] = (all_b[place] + got_b[0].astype(f32)) + (got_b[1].astype(f32) + got_b[2].astype(f32))
    for p in range(n_parts):
        sends.arrived(*[("line", p, r) for r in line])
        for n in range(3):
            at = n * width + p * cols
            sum_q[:, at : at + cols] = (all_q[p, head, n] + got_z[p, 0, n].astype(f32)) + (
                got_z[p, 1, n].astype(f32) + got_z[p, 2, n].astype(f32)
            )
    sends.arrived(*[("line", "v", r) for r in line])
    sum_v[...] = (vecs[2] + got_v[4]) + (got_v[5] + got_v[6])
    sends.drain()


def finish(gar, w_qkv, vec, parts, a, b):
    own, width = gar.shape
    half_w = width // 8
    quarter = half_w // 4
    n_parts = parts[0].shape[0]
    cols = width // n_parts
    rows_z, ff = a[0].shape[1], b[0].shape[2]
    n_vec = vec.shape[0] + 8
    shape = jax.ShapeDtypeStruct
    vmem, hbm = pl.BlockSpec(memory_space=pltpu.VMEM), pl.BlockSpec(memory_space=pl.ANY)
    n_copies = 6 + 7 * n_parts + 7 + 1
    grads, keeps, sends, sums = parts
    held = [*a, *b, vec, keeps, sums, grads]
    return pl.pallas_call(
        functools.partial(finish_kernel, n_parts),
        in_specs=[hbm] * 14,
        out_specs=[vmem] * 7,
        out_shape=[
            shape((own, width), f32),
            shape((rows_z - 2 * quarter, width), f32),
            shape((quarter, ff), f32),
            shape((quarter, width), f32),
            shape((quarter, width), f32),
            shape((quarter, 3 * width), f32),
            shape((n_vec, width), f32),
        ],
        scratch_shapes=[pltpu.VMEM(h.shape, h.dtype) for h in held]
        + [
            pltpu.VMEM(w_qkv.shape, bf16),
            pltpu.VMEM((4, rows_z, width), f32),
            pltpu.VMEM((3, rows_z, width), bf16),
            pltpu.VMEM((3, rows_z, width), bf16),
            pltpu.VMEM((4, quarter, ff), f32),
            pltpu.VMEM((3, quarter, ff), bf16),
            pltpu.VMEM((3, quarter, ff), bf16),
            pltpu.VMEM((4, quarter, ff), bf16),
            pltpu.VMEM((n_parts, 3, 4, half_w, cols), bf16),
            pltpu.VMEM((n_parts, 3, half_w, cols), f32),
            pltpu.VMEM((n_parts, 3, 3, half_w, cols), bf16),
            pltpu.VMEM((n_parts, 3, 3, half_w, cols), bf16),
            pltpu.VMEM((n_parts, 4, 3, quarter, cols), f32),
            pltpu.VMEM((n_parts, 3, 3, quarter, cols), bf16),
            pltpu.VMEM((n_parts, 3, 3, quarter, cols), bf16),
            pltpu.VMEM((3, n_vec, width), f32),
            pltpu.VMEM((7, n_vec, width), f32),
            pltpu.SemaphoreType.DMA((len(held) + 2,)),
            pltpu.SemaphoreType.DMA((n_copies,)),
            pltpu.SemaphoreType.DMA((n_copies,)),
        ],
        compiler_params=pltpu.CompilerParams(
            vmem_limit_bytes=62 * 2**20, collective_id=1, has_side_effects=True
        ),
        cost_estimate=pl.CostEstimate(
            flops=12 * own * width * width, bytes_accessed=12 * 2**20, transcendentals=0
        ),
        name="finish",
    )(*a, *b, vec, w_qkv, sends, keeps, sums, grads, gar)


def own_vectors_kernel(chunks, n_class, count, n_through, shard, summed, *refs):
    through, outs, refs = refs[:n_through], refs[n_through:][: 12 + n_through], refs[12 + 2 * n_through :]
    loads, stores = [], []
    for src, dst, held in zip(through, outs[12:], refs):
        step = ROWS if src.shape[0] > ROWS else src.shape[0]
        for first in range(0, src.shape[0], step):
            rows, n = pl.ds(first, step), len(loads)
            loads.append(pltpu.make_async_copy(src.at[rows], held.at[rows], refs[-1].at[0, n]))
            stores.append(pltpu.make_async_copy(held.at[rows], dst.at[rows], refs[-1].at[1, n]))
    for copy in loads:
        copy.start()
    *rows_of, outs_bin, outs_class, entropy = outs[:12]
    width = summed.shape[1]
    size, size_bin = outs_class.shape[1], outs_bin.shape[1]
    here = shard[0]

    def columns(values, first, n):
        chosen = iota((width, n), 0) == first + iota((width, n), 1)
        return dot3(values, chosen.astype(f32).astype(bf16), NN)

    mine = columns(summed[...], here * size, size)
    n_vec = summed.shape[0] - 8
    for n, out in zip((n_vec, n_vec + 2, 0, 1, 2, 3, 4, 5, 6), rows_of):
        out[...] = mine[n : n + 1]
    outs_class[...] = mine[8 + chunks : 8 + chunks + n_class]
    rows = summed[8:16, :]
    per_row = width // size_bin
    rows = jnp.where(iota(rows.shape, 0) == lax.div(here, per_row), rows, 0.0)
    line = jnp.broadcast_to(col_sum(rows), rows.shape)
    outs_bin[...] = columns(line, lax.rem(here, per_row) * size_bin, size_bin)[0:1]
    entropy[...] = summed[7:8, 0:1] * (1.0 / count)
    for load, store in zip(loads, stores):
        load.wait()
        store.start()
    for store in stores:
        store.wait()


def own_vectors(summed, shard, shards, chunks, n_class, count, through=()):
    size = summed.shape[1] // shards
    shape = jax.ShapeDtypeStruct
    vmem = pl.BlockSpec(memory_space=pltpu.VMEM)
    outs = [(1, size)] * 9 + [(1, size * chunks), (n_class, size), (1, 1)]
    n_copies = sum(-(-t.shape[0] // ROWS) for t in through)
    results = pl.pallas_call(
        functools.partial(own_vectors_kernel, chunks, n_class, count, len(through)),
        in_specs=[pl.BlockSpec(memory_space=pltpu.SMEM), vmem]
        + [pl.BlockSpec(memory_space=pl.ANY)] * len(through),
        out_specs=[vmem] * len(outs) + [pl.BlockSpec(memory_space=pl.ANY)] * len(through),
        out_shape=[shape(o, f32) for o in outs] + [shape(t.shape, t.dtype) for t in through],
        scratch_shapes=[pltpu.VMEM(t.shape, t.dtype) for t in through]
        + [pltpu.SemaphoreType.DMA((2, max(n_copies, 1)))],
        compiler_params=pltpu.CompilerParams(vmem_limit_bytes=62 * 2**20),
        name="own_vectors",
    )(shard.reshape(1), summed, *through)
    rows_of, (outs_class, entropy) = results[:10], results[10:12]
    return [r.reshape(-1) for r in rows_of], outs_class.T, entropy.reshape(()), results[12:]


def halo(rows, left_axis, n_head):
    up = [(i, i + 1) for i in range(n_head - 1)]
    down = [(i + 1, i) for i in range(n_head - 1)]
    from_left = lax.ppermute(rows[-MAXLEN:], left_axis, up)
    from_right = lax.ppermute(rows[:MAXLEN], left_axis, down)
    return jnp.concatenate([from_left, rows, from_right], axis=0)


def pick(values, axis, index):
    return lax.dynamic_index_in_dim(values, index, axis, keepdims=False)


class Sums:
    def __init__(self, pairs, orders, n_seq, n_head, vectors):
        self.count = {"seq": n_seq, "head": n_head}
        self.bits = {"seq": n_seq.bit_length() - 1, "head": n_head.bit_length() - 1}
        self.stages = sum(self.bits.values())
        self.orders = orders
        self.vectors = vectors
        self.axes = [[n for n in range(self.stages) if n != self.bits["seq"] - 1] for _ in pairs]
        shape = lambda a: a.reshape(
            (2,) * (self.stages - 1) + (a.shape[1] // n_head,) + a.shape[2:]
        )
        self.kept = [shape(keep) for keep, _ in pairs]
        self.sent = [shape(send) for _, send in pairs]
        self.stage = 0
        self.send()

    def send(self):
        self.got = [
            self.swap(v, *self.orders[n][self.stage]) for n, v in enumerate(self.sent)
        ]
        self.vectors = self.vectors + self.swap(self.vectors, *self.orders[0][self.stage])

    def swap(self, values, name, bit):
        return lax.ppermute(values, name, [(i, i ^ (1 << bit)) for i in range(self.count[name])])

    def split(self):
        self.stage += 1
        kept, sent = [], []
        for n, (keep, got) in enumerate(zip(self.kept, self.got)):
            name, bit = self.orders[n][self.stage]
            where = (self.stages if name == "head" else self.bits["seq"]) - 1 - bit
            at = self.axes[n].index(where)
            self.axes[n].pop(at)
            mine = (lax.axis_index(name) >> bit) & 1
            half = lambda m: pick(keep, at, m).astype(f32) + pick(got, at, m).astype(f32)
            sent.append(half(1 - mine).astype(bf16))
            kept.append(half(mine))
        self.kept, self.sent = kept, sent

    def rest(self):
        while self.stage < self.stages - 1:
            self.split()
            self.send()
        return [k.astype(f32) + g.astype(f32) for k, g in zip(self.kept, self.got)]


def after(value, *others):
    return lax.optimization_barrier((value, *others))[0]


def orders(n_seq, n_head):
    seq_bits, head_bits = n_seq.bit_length() - 1, n_head.bit_length() - 1
    core = [("seq", 0)]
    planar = [("seq", b) for b in range(1, seq_bits)]
    along = [("head", b) for b in range(head_bits)]
    return (
        core + planar + along,
        core + planar[::-1] + along,
        core + along + planar,
    )


def local(
    tokens, cotangent, lengths, labels, w_qkv, b_query, b_value, w_out, b_out, gain_attn,
    shift_attn, w_in, b_in, w_back, b_back, gain_ffn, shift_ffn, w_pool, b_pool, w_class,
):
    n_head = lax.axis_size("head")
    n_seq = lax.axis_size("seq")
    head_index = lax.axis_index("head")
    own, width = tokens.shape
    window = own + 2 * MAXLEN
    group = own * n_head

    if (n_seq, n_head) == (8, 4):
        qkv, hot, mask, bounds, seqs_of = front(tokens, w_qkv, b_query, b_value, lengths, labels)
    else:
        seq_lengths = lengths[0]
        ends = jnp.cumsum(seq_lengths)
        starts = ends - seq_lengths
        base = head_index * own - MAXLEN
        pos = base + jnp.arange(window, dtype=jnp.int32)
        n_in_group = seq_lengths.shape[0]
        lane_pad = (0, SIDE - n_in_group)
        starts_w = jnp.pad(starts, lane_pad, constant_values=group + MAXLEN)
        ends_w = jnp.pad(ends, lane_pad, constant_values=-MAXLEN)
        inside = (starts_w[None, :] <= pos[:, None]) & (pos[:, None] < ends_w[None, :])
        hot = inside.astype(bf16)
        lane = jnp.arange(SIDE, dtype=jnp.int32)[None, :]
        mask = jnp.where(lane < n_in_group, jnp.where(inside, 0.0, -BIG), 1.0).astype(bf16)
        mask = jnp.concatenate(
            [mask, jnp.broadcast_to(jnp.where(lane < n_in_group, -BIG, 1.0).astype(bf16), (PAD, SIDE))]
        )
        blk = base + QBLK * jnp.arange(window // QBLK, dtype=jnp.int32)
        low = jnp.max(jnp.where(starts[None, :] <= blk[:, None], starts[None, :], -1), axis=1)
        high = jnp.min(
            jnp.where(ends[None, :] > blk[:, None] + QBLK - 1, ends[None, :], group), axis=1
        )
        is_own = (blk >= base + MAXLEN) & (blk < base + MAXLEN + own)
        low = jnp.where(is_own, low - base, jnp.maximum(low - base, MAXLEN))
        high = jnp.where(is_own, high - base, jnp.minimum(high - base, MAXLEN + own))
        valid = (blk >= 0) & (blk < group)
        low = low // 128 * 128
        steps = jnp.where(valid, jnp.maximum((high - low + KCHUNK - 1) // KCHUNK, 0), 0)
        bounds = jnp.stack([low, steps], axis=1).astype(jnp.int32)
        seq_pad = (0, -n_in_group % 16)
        seqs_of = jnp.stack(
            [jnp.pad(starts, seq_pad, constant_values=-1), jnp.pad(labels[0], seq_pad)], axis=1
        )
        tokens_w = halo(tokens, "head", n_head)
        bias = jnp.concatenate([b_query, jnp.zeros_like(b_query), b_value])[None, :]
        qscale = jnp.where(jnp.arange(3 * width) < width, HEAD_DIM**-0.5, 1.0).astype(f32)[None, :]
        qkv = ((dot(tokens_w, w_qkv, NN) + bias) * qscale).astype(bf16)
    context, lse = attend(bounds, qkv, hot, mask, own)

    shards = n_seq * n_head
    shard = head_index + n_head * lax.axis_index("seq")
    core = (lax.axis_index("seq") & 1).reshape(1)
    (output, gar, gs, act, gpre, gffn, mid, gattn, cls, gpool, vec) = middle_layer(
        2 * fold_of(width // PAIR, 3), head_index.reshape(1), w_in, w_back, w_pool, tokens, context, lse,
        cotangent, w_out, b_in.reshape(1, -1), w_class.T, seqs_of,
        (b_out, gain_attn, shift_attn, b_back, gain_ffn, shift_ffn, b_pool),
    )
    if (n_seq, n_head) == (8, 4):
        grads_w, tok_t, *pieces = send_grads(act, gpre, gs, gffn, mid, context, gattn, cls, gpool, tokens)
        to = lambda v, axis, count, x: lax.ppermute(v, axis, [(i, i ^ x) for i in range(count)])
        a = [pieces[0]] + [to(pieces[r], "seq", 8, NEAR[r - 1]) for r in (1, 2, 3)]
        b = [pieces[4], to(pieces[5], "head", 4, 1), to(pieces[6], "head", 4, 2)]
        gqkv = attend_back(bounds, qkv, grads_w, hot, mask, own, (tok_t, core))
        grad_tokens, sum_wback, sum_win, sum_wout, sum_pool, sum_wqkv, summed = finish(
            gar, w_qkv, vec, gqkv, a, b
        )
    else:
        grads_w = halo(gs, "head", n_head)

        pieces = weight_grads(core, n_seq, act, gpre, gffn, mid, context, gattn, cls, gpool)
        orders_all = orders(n_seq, n_head)
        first = Sums(
            [pieces[0:2], pieces[2:4], pieces[4:6]], orders_all, n_seq, n_head, vec
        )
        gqkv = attend_back(bounds, qkv, grads_w, hot, mask, own)
        last_out = last_layer(core, n_seq, tokens, gar, w_qkv, list(gqkv))
        grad_tokens, vec_qkv = last_out[:2]
        last = Sums(
            [last_out[2:4], last_out[4:6], last_out[6:8]], orders_all, n_seq, n_head, vec_qkv
        )
        sum_wback, sum_win, sum_c = first.rest()
        sum_wout, sum_pool = sum_c[:, :width], sum_c[:, width:]
        sum_q, sum_k, sum_v = last.rest()
        sum_wqkv = jnp.concatenate([sum_q, sum_k, sum_v], axis=1)

        summed = jnp.concatenate([first.vectors, last.vectors])
    sums = (grad_tokens, sum_wback, sum_win, sum_wout, sum_pool, sum_wqkv)
    (grad_bq, grad_bv, *mine, grad_bin), grad_class, entropy_mean, sums = own_vectors(
        summed, shard, shards, w_in.shape[1] // width, w_class.shape[1], n_seq * labels.shape[1], sums
    )
    grad_tokens, sum_wback, sum_win, sum_wout, sum_pool, sum_wqkv = sums
    return (
        output, grad_tokens, sum_wqkv, grad_bq, grad_bv, sum_wout, mine[0], mine[1], mine[2],
        sum_win, grad_bin, sum_wback, mine[3], mine[4], mine[5], sum_pool, mine[6], grad_class,
        entropy_mean,
    )


def solution(mesh):
    rows = P(("seq", "head"), None)
    vec = P(("seq", "head"))
    return jax.shard_map(
        local,
        mesh=mesh,
        in_specs=(rows, rows, P("seq", None), P("seq", None)) + (P(),) * 16,
        out_specs=(
            rows, rows, rows, vec, vec, rows, vec, vec, vec, rows, vec, rows, vec, vec, vec, rows,
            vec, rows, P(),
        ),
        check_vma=False,
    )
```
